32 devices in a mesh: dp: 8 (over z, x), fsdp: 4 (over y, core).
Axes of the slice: x: 2, y: 2, z: 4, core: 2. Of those that a mesh axis runs over, the one named last changes fastest.
Arguments:
- tokens: bfloat16 [32, 169, 1024], P(('dp', 'fsdp')), may hold values from -6 to 6
- out_grad: bfloat16 [32, 169, 1024], P(('dp', 'fsdp')), may hold values from -6 to 6
- text_len: int32 [32], P(('dp', 'fsdp')), may hold values from 12 to 120
- x_bucket: int32 [32, 169], P(('dp', 'fsdp')), may hold values from 0 to 127
- y_bucket: int32 [32, 169], P(('dp', 'fsdp')), may hold values from 0 to 127
- patch_mask: int32 [32, 49], P(('dp', 'fsdp')), may hold values 0 or 1
- qkv_weight: bfloat16 [1024, 3072], P(('dp', 'fsdp')), may hold values from -0.1875 to 0.1875
- qv_bias: bfloat16 [2048], P(('dp', 'fsdp')), may hold values from -3 to 3
- proj_weight: bfloat16 [1024, 1024], P(('dp', 'fsdp')), may hold values from -1 to 1
- proj_bias: bfloat16 [1024], P(('dp', 'fsdp')), may hold values from -2 to 2
- first_gain: bfloat16 [1024], P(('dp', 'fsdp')), may hold values from 0.5 to 1.5
- first_shift: bfloat16 [1024], P(('dp', 'fsdp')), may hold values from -2 to 2
- rel_tables: bfloat16 [6144], P(('dp', 'fsdp')), may hold values from -4 to 4
- up_weight: bfloat16 [1024, 4096], P(('dp', 'fsdp')), may hold values from -0.1875 to 0.1875
- up_bias: bfloat16 [4096], P(('dp', 'fsdp')), may hold values from -3 to 3
- down_weight: bfloat16 [1024, 4096], P(('dp', 'fsdp')), may hold values from -0.09375 to 0.09375
- down_bias: bfloat16 [1024], P(('dp', 'fsdp')), may hold values from -2 to 2
- second_gain: bfloat16 [1024], P(('dp', 'fsdp')), may hold values from 0.5 to 1.5
- second_shift: bfloat16 [1024], P(('dp', 'fsdp')), may hold values from -2 to 2
Outputs:
- encoded: bfloat16 [32, 169, 1024], P(('dp', 'fsdp'))
- grad_tokens: float32 [32, 169, 1024], P(('dp', 'fsdp'))
- grad_qkv: float32 [1024, 3072], P(('dp', 'fsdp'))
- grad_qvbias: float32 [2048], P(('dp', 'fsdp'))
- grad_proj: float32 [1024, 1024], P(('dp', 'fsdp'))
- grad_projbias: float32 [1024], P(('dp', 'fsdp'))
- grad_firstgain: float32 [1024], P(('dp', 'fsdp'))
- grad_firstshift: float32 [1024], P(('dp', 'fsdp'))
- grad_tables: float32 [6144], P(('dp', 'fsdp'))
- grad_up: float32 [1024, 4096], P(('dp', 'fsdp'))
- grad_upbias: float32 [4096], P(('dp', 'fsdp'))
- grad_down: float32 [1024, 4096], P(('dp', 'fsdp'))
- grad_downbias: float32 [1024], P(('dp', 'fsdp'))
- grad_secondgain: float32 [1024], P(('dp', 'fsdp'))
- grad_secondshift: float32 [1024], P(('dp', 'fsdp'))
The draws below stay inside these ranges and needn't reach their ends.
All inputs are finite; a program needn't handle non-finite values. No bound on the sum of `patch_mask` on one device may be relied on, other than what follows from the above.
Results may differ from the reference program's by a relative error of at most 0.015.
Values may be sent and summed in bfloat16 or wider, within the bound.
No kernel may reach another device: no remote copies, remote signals or barrier semaphores. Data moves between devices by JAX's collectives and lax.ppermute only.
A program may use at most 256 MiB of HBM per device.

```python
import jax
import jax.numpy as jnp
from jax import lax

D = 1024
H = 16
HD = 64
FF = 4096
NB = 128
TEXT = 120
PATCH = 49
SLOTS = 169
DOCS = 32


def set_ends(values, own_key, smallest, top_value):
    dims = values.shape
    place = [jax.random.randint(jax.random.fold_in(own_key, axis), (), 0, dims[axis]) for axis in range(len(dims))]
    values = values.at[tuple(place)].set(smallest)
    longest = dims.index(max(dims))
    place[longest] = (place[longest] + 1) % dims[longest]
    return values.at[tuple(place)].set(top_value)


def level_of(key, dims, cuts, least, top_value):
    loudness, own = 1.0, jax.random.fold_in(key, 6)
    for position, blocks in cuts:
        heights = jnp.exp(jax.random.uniform(jax.random.fold_in(own, position), (blocks,), jnp.float32, least / len(cuts), top_value / len(cuts)))
        loudness = loudness * jnp.repeat(heights, dims[position] // blocks).reshape([-1 if axis == position else 1 for axis in range(len(dims))])
    return loudness


def scatter_about(key, shape, scale, reach, cuts=(), kind=jnp.bfloat16):
    result = scale * jax.random.normal(key, shape, jnp.float32)
    if cuts:
        result = result * level_of(key, shape, cuts, -0.22, 0.18)
    return jnp.clip(result, -reach, reach).astype(kind)


def setup_inputs(seed: int = 0) -> dict:
    key_list = jax.random.split(jax.random.key(seed), 20)
    tokens = scatter_about(key_list[0], (DOCS, SLOTS, D), 1.0, 6.0, ((0, 32),))
    out_grad = scatter_about(key_list[1], (DOCS, SLOTS, D), 1.0, 6.0, ((0, 32),))
    text_len = set_ends(jax.random.randint(key_list[2], (DOCS,), max(1, TEXT // 10), TEXT + 1), jax.random.fold_in(key_list[2], 1), max(1, TEXT // 10), TEXT).astype(jnp.int32)
    x_bucket = set_ends(jax.random.randint(key_list[3], (DOCS, SLOTS), 0, NB), jax.random.fold_in(key_list[3], 1), 0, NB - 1).astype(jnp.int32)
    y_bucket = set_ends(jax.random.randint(key_list[4], (DOCS, SLOTS), 0, NB), jax.random.fold_in(key_list[4], 1), 0, NB - 1).astype(jnp.int32)
    patch_mask = set_ends((jax.random.randint(key_list[5], (DOCS, PATCH), 0, 4) < 3).astype(jnp.int32), jax.random.fold_in(key_list[5], 1), 0, 1)
    qkv_weight = scatter_about(key_list[6], (D, 3 * D), D ** -0.5, 0.1875, ((0, 32),))
    qv_bias = scatter_about(key_list[7], (2 * D,), 0.5, 3.0, ((0, 32),))
    proj_weight = scatter_about(key_list[8], (D, D), (D // 32) ** -0.5, 1.0, ((0, 32),))
    proj_bias = scatter_about(key_list[9], (D,), 0.3, 2.0, ((0, 32),))
    first_gain = jnp.clip(1.0 + 0.1 * jax.random.normal(key_list[10], (D,), jnp.float32), 0.5, 1.5).astype(jnp.bfloat16)
    first_shift = scatter_about(key_list[11], (D,), 0.3, 2.0, ((0, 32),))
    rel_tables = scatter_about(key_list[12], (3 * H * NB,), 0.7, 4.0, ((0, 32),))
    up_weight = scatter_about(key_list[13], (D, FF), D ** -0.5, 0.1875, ((0, 32),))
    up_bias = scatter_about(key_list[14], (FF,), 0.5, 3.0, ((0, 32),))
    down_weight = scatter_about(key_list[15], (D, FF), FF ** -0.5, 0.09375, ((0, 32),))
    down_bias = scatter_about(key_list[16], (D,), 0.3, 2.0, ((0, 32),))
    second_gain = jnp.clip(1.0 + 0.1 * jax.random.normal(key_list[17], (D,), jnp.float32), 0.5, 1.5).astype(jnp.bfloat16)
    second_shift = scatter_about(key_list[18], (D,), 0.3, 2.0, ((0, 32),))
    return {"tokens": tokens, "out_grad": out_grad, "text_len": text_len, "x_bucket": x_bucket, "y_bucket": y_bucket, "patch_mask": patch_mask, "qkv_weight": qkv_weight, "qv_bias": qv_bias, "proj_weight": proj_weight, "proj_bias": proj_bias, "first_gain": first_gain, "first_shift": first_shift, "rel_tables": rel_tables, "up_weight": up_weight, "up_bias": up_bias, "down_weight": down_weight, "down_bias": down_bias, "second_gain": second_gain, "second_shift": second_shift}


HIGHEST = lax.Precision.HIGHEST
NEGATIVE = -1e+30
EPSILON = 1e-05

@jax.custom_vjp
def low(v):
    return lax.optimization_barrier(v.astype(jnp.bfloat16)).astype(jnp.float32)

@jax.custom_vjp
def low_back(v):
    return v

def low_keep(v):
    return (low(v), None)

def low_pass(kept, grad):
    return (grad,)

def back_keep(v):
    return (v, None)

def back_low(kept, grad):
    return (low(grad),)
low.defvjp(low_keep, low_pass)
low_back.defvjp(back_keep, back_low)

def layer_norm(values, norm_gain, norm_shift):
    average = lax.optimization_barrier(jnp.mean(values, axis=-1, keepdims=True))
    centred = values - average
    spread = lax.optimization_barrier(jnp.mean(centred * centred, axis=-1, keepdims=True))
    return centred * lax.rsqrt(spread + EPSILON) * norm_gain + norm_shift

def key_valid(text_len, patch_mask):
    places = jnp.arange(TEXT, dtype=jnp.int32)
    text_part = places[None, :] < text_len[:, None]
    return jnp.concatenate([text_part, patch_mask > 0], axis=1)

def encode_group(params, block_tokens, valid_keys, block_x, block_y):
    qkv_weight, qv_bias, proj_weight, proj_bias, first_gain, first_shift, rel_tables, up_weight, up_bias, down_weight, down_bias, second_gain, second_shift = params
    groups = block_tokens.shape[0]
    rows_in = block_tokens.reshape(groups * SLOTS, D)
    qkv_bias = jnp.concatenate([qv_bias[:D], jnp.zeros((D,), jnp.float32), qv_bias[D:]])
    qkv_rows = jnp.dot(low(rows_in), qkv_weight, precision=HIGHEST) + qkv_bias
    qkv_rows = low(low_back(qkv_rows)).reshape(groups, SLOTS, 3, H, HD)
    queries = qkv_rows[:, :, 0]
    keys_all = qkv_rows[:, :, 1]
    values_all = qkv_rows[:, :, 2]
    content = jnp.einsum('gihe,gjhe->ghij', queries, keys_all, precision=HIGHEST) * 0.125
    table_grid = rel_tables.reshape(3, H, NB)
    half_span = NB // 2
    positions = jnp.arange(SLOTS, dtype=jnp.int32) * NB // SLOTS
    pos_rel = jnp.clip(positions[None, :] - positions[:, None], -half_span, half_span - 1) + half_span
    x_rel = jnp.clip(block_x[:, None, :] - block_x[:, :, None], -half_span, half_span - 1) + half_span
    y_rel = jnp.clip(block_y[:, None, :] - block_y[:, :, None], -half_span, half_span - 1) + half_span
    spatial = table_grid[0][:, pos_rel][None]
    spatial = spatial + jnp.moveaxis(table_grid[1][:, x_rel], 0, 1)
    spatial = spatial + jnp.moveaxis(table_grid[2][:, y_rel], 0, 1)
    scores = low_back(content + spatial)
    scores = jnp.where(valid_keys[:, None, None, :] > 0, scores, NEGATIVE)
    row_peak = lax.optimization_barrier(jnp.max(scores, axis=-1, keepdims=True))
    exponent = jnp.exp(scores - row_peak)
    probability = exponent / lax.optimization_barrier(jnp.sum(exponent, axis=-1, keepdims=True))
    attended = jnp.einsum('ghij,gjhe->gihe', low(probability), values_all, precision=HIGHEST)
    attended = low(low_back(attended.reshape(groups * SLOTS, D)))
    branch = low_back(jnp.dot(attended, proj_weight, precision=HIGHEST) + proj_bias)
    resid_one = rows_in + branch
    normed_one = layer_norm(resid_one, first_gain, first_shift)
    pre_act = low_back(jnp.dot(low(normed_one), up_weight, precision=HIGHEST) + up_bias)
    activated = low(jax.nn.gelu(pre_act, approximate=False))
    ffn_out = low_back(jnp.dot(activated, down_weight.T, precision=HIGHEST) + down_bias)
    resid_two = normed_one + ffn_out
    final_rows = layer_norm(resid_two, second_gain, second_shift) * valid_keys.reshape(groups * SLOTS, 1)
    return final_rows.reshape(groups, SLOTS, D)

def reference(tokens, out_grad, text_len, x_bucket, y_bucket, patch_mask, qkv_weight, qv_bias, proj_weight, proj_bias, first_gain, first_shift, rel_tables, up_weight, up_bias, down_weight, down_bias, second_gain, second_shift):
    params = tuple((weight.astype(jnp.float32) for weight in (qkv_weight, qv_bias, proj_weight, proj_bias, first_gain, first_shift, rel_tables, up_weight, up_bias, down_weight, down_bias, second_gain, second_shift)))
    valid_keys = key_valid(text_len, patch_mask).astype(jnp.float32)
    group_size = 4 if DOCS % 4 == 0 else 1
    blocks = DOCS // group_size

    def run(param_set, tokens_float):

        def one_group(inputs):
            block_tokens, block_valid, block_x, block_y = inputs
            return encode_group(param_set, block_tokens, block_valid, block_x, block_y)
        outputs = lax.map(jax.checkpoint(one_group), (tokens_float.reshape(blocks, group_size, SLOTS, D), valid_keys.reshape(blocks, group_size, SLOTS), x_bucket.reshape(blocks, group_size, SLOTS), y_bucket.reshape(blocks, group_size, SLOTS)))
        return outputs.reshape(DOCS, SLOTS, D)
    encoded, backward = jax.vjp(run, params, tokens.astype(jnp.float32))
    grads, grad_tokens = backward(out_grad.astype(jnp.float32))
    return (encoded.astype(jnp.bfloat16), grad_tokens, grads[0], grads[1], grads[2], grads[3], grads[4], grads[5], grads[6], grads[7], grads[8], grads[9], grads[10], grads[11], grads[12])
```

```python
from functools import partial

import jax
import jax.numpy as jnp
from jax import lax
from jax.experimental import pallas as pl
from jax.experimental.pallas import tpu as pltpu
from jax.sharding import PartitionSpec as P

D = 1024
H = 16
HD = 64
FF = 4096
NB = 128
TEXT = 120
SLOTS = 169
ROWS = 176
NEGATIVE = -1e30
EPSILON = 1e-05

f32 = jnp.float32
bf16 = jnp.bfloat16


def axis_bits(axis):
    bits, b = [], lax.axis_size(axis) // 2
    while b >= 1:
        bits.append((axis, b))
        b //= 2
    return bits


def swap(x, bit):
    axis, b = bit
    return lax.ppermute(x, axis, [(i, i ^ b) for i in range(lax.axis_size(axis))])


def side(bit):
    axis, b = bit
    return (lax.axis_index(axis) // b) % 2


def pair_up(mine, other, bit, pos):
    one = side(bit) == 1
    return jnp.stack([jnp.where(one, other, mine), jnp.where(one, mine, other)], axis=pos)


def halves(x, bit, pos):
    me = side(bit)
    give = lax.dynamic_index_in_dim(x, 1 - me, pos, keepdims=False)
    keep = lax.dynamic_index_in_dim(x, me, pos, keepdims=False)
    return give, keep


def gather_over(x, order, canon):
    tail = x.shape
    have = []
    for bit in order:
        other = swap(x, bit)
        have = sorted(have + [bit], key=canon.index)
        x = pair_up(x, other, bit, have.index(bit))
    return x.reshape((-1,) + tail)


def scatter_sum(x, order, canon):
    tail = x.shape[1:]
    x = x.reshape((2,) * len(canon) + tail)
    have = list(canon)
    for bit in order:
        pos = have.index(bit)
        have.remove(bit)
        give, keep = halves(x, bit, pos)
        x = keep.astype(f32) + swap(give.astype(bf16), bit).astype(f32)
        if have:
            x = x.astype(bf16)
    return x


def exchange(x, canon):
    shape = x.shape
    x = x.reshape((2,) * len(canon) + shape[1:])
    for pos in reversed(range(len(canon))):
        bit = canon[pos]
        give, keep = halves(x, bit, pos)
        x = pair_up(keep, swap(give, bit), bit, pos)
    return x.reshape(shape)


def dot_nt(a, b):
    return lax.dot_general(a, b, (((1,), (1,)), ((), ())), preferred_element_type=f32)


def dot_tn(a, b):
    return lax.dot_general(a, b, (((0,), (0,)), ((), ())), preferred_element_type=f32)


def one_hot_codes(ids):
    buckets = lax.broadcasted_iota(jnp.int32, (ROWS, NB), 1)
    return [(ids[:, k : k + 1] == buckets).astype(f32).astype(bf16) for k in range(3)]


def bias_kernel(heads, ids_ref, live_ref, ext_ref, out_ref):
    hots = one_hot_codes(ids_ref[0])
    live = live_ref[0] > 0.5
    for h in range(heads):
        total = jnp.zeros((ROWS, ROWS), f32)
        for k in range(3):
            row = ext_ref[k * heads + h : k * heads + h + 1, :]
            spread = jnp.broadcast_to(row, (NB, 2 * NB))
            skew = pltpu.roll(spread, NB + 1, 1, stride=1, stride_axis=0)
            codes = jnp.dot(
                hots[k], skew[:, :NB].astype(bf16), preferred_element_type=f32
            ).astype(bf16)
            total = total + dot_nt(codes, hots[k])
        out_ref[0, h] = jnp.where(live, total, NEGATIVE)


def softmax_rows(q, k, bias):
    s = dot_nt(q, k) * 0.125 + bias
    e = jnp.exp(s - jnp.max(s, axis=-1, keepdims=True))
    return e / jnp.sum(e, axis=-1, keepdims=True)


def attend_kernel(heads, qkv_ref, bias_ref, out_ref):
    width = heads * HD
    for h in range(heads):
        at = slice(h * HD, (h + 1) * HD)
        q = qkv_ref[0, :, h * HD : (h + 1) * HD]
        k = qkv_ref[0, :, width + h * HD : width + (h + 1) * HD]
        v = qkv_ref[0, :, 2 * width + h * HD : 2 * width + (h + 1) * HD]
        p = softmax_rows(q, k, bias_ref[0, h]).astype(bf16)
        out_ref[0, :, at] = jnp.dot(p, v, preferred_element_type=f32).astype(bf16)


def attend_back_kernel(
    heads, qkv_ref, bias_ref, grad_ref, ids_ref, dqkv_ref, sums_ref, ext_ref, grid_ref
):
    step = pl.program_id(0)
    width = heads * HD
    hots = one_hot_codes(ids_ref[0])
    flipped = one_hot_codes(NB - 1 - ids_ref[0])

    @pl.when(step == 0)
    def _():
        grid_ref[...] = jnp.zeros_like(grid_ref)
        sums_ref[...] = jnp.zeros_like(sums_ref)

    for h in range(heads):
        q = qkv_ref[0, :, h * HD : (h + 1) * HD]
        k = qkv_ref[0, :, width + h * HD : width + (h + 1) * HD]
        v = qkv_ref[0, :, 2 * width + h * HD : 2 * width + (h + 1) * HD]
        g = grad_ref[0, :, h * HD : (h + 1) * HD]
        p = softmax_rows(q, k, bias_ref[0, h])
        dp = dot_nt(g, v)
        ds = (p * (dp - jnp.sum(p * dp, axis=-1, keepdims=True))).astype(bf16)
        dv = dot_tn(p.astype(bf16), g).astype(bf16)
        dq = (jnp.dot(ds, k, preferred_element_type=f32) * 0.125).astype(bf16)
        dk = (dot_tn(ds, q) * 0.125).astype(bf16)
        dqkv_ref[0, :, h * HD : (h + 1) * HD] = dq
        dqkv_ref[0, :, width + h * HD : width + (h + 1) * HD] = dk
        dqkv_ref[0, :, 2 * width + h * HD : 2 * width + (h + 1) * HD] = dv
        for k3 in range(3):
            part = jnp.dot(ds, hots[k3], preferred_element_type=f32).astype(bf16)
            grid_ref[k3 * heads + h] += dot_tn(flipped[k3], part)
    sums_ref[...] += jnp.sum(dqkv_ref[0].astype(f32), axis=0, keepdims=True)

    @pl.when(step == pl.num_programs(0) - 1)
    def _():
        for n in range(3 * heads):
            wide = jnp.concatenate([grid_ref[n], jnp.zeros((NB, NB), f32)], axis=1)
            skew = pltpu.roll(wide, 0, 1, stride=1, stride_axis=0)
            ext_ref[n : n + 1, :] = jnp.sum(skew, axis=0, keepdims=True)


def spec(shape):
    n = len(shape)
    return pl.BlockSpec((1,) + tuple(shape[1:]), lambda d: (d,) + (0,) * (n - 1))


def whole(shape):
    return pl.BlockSpec(tuple(shape), lambda d: (0,) * len(shape))


def call(kernel, docs, ins, in_whole, outs, out_whole, scratch=(), flops=0):
    in_specs = [whole(a.shape) if w else spec(a.shape) for a, w in zip(ins, in_whole)]
    out_specs = [whole(s.shape) if w else spec(s.shape) for s, w in zip(outs, out_whole)]
    moved = sum(a.size * a.dtype.itemsize for a in list(ins) + list(outs))
    return pl.pallas_call(
        kernel,
        grid=(docs,),
        in_specs=in_specs,
        out_specs=out_specs,
        out_shape=outs,
        scratch_shapes=list(scratch),
        cost_estimate=pl.CostEstimate(flops=flops, bytes_accessed=moved, transcendentals=0),
        compiler_params=pltpu.CompilerParams(
            dimension_semantics=("arbitrary",), vmem_limit_bytes=40 * 2**20
        ),
    )(*ins)


def norm_parts(values):
    average = jnp.mean(values, axis=-1, keepdims=True)
    centred = values - average
    spread = jnp.mean(centred * centred, axis=-1, keepdims=True)
    scale = lax.rsqrt(spread + EPSILON)
    return centred * scale, scale


def norm_back(grad, gain, hat, scale):
    scaled = grad * gain
    first = jnp.mean(scaled, axis=-1, keepdims=True)
    second = jnp.mean(scaled * hat, axis=-1, keepdims=True)
    return (scaled - first - hat * second) * scale


def pad_rows(x):
    return jnp.pad(x, ((0, ROWS - SLOTS), (0, 0)))


def local(
    tokens,
    out_grad,
    text_len,
    x_bucket,
    y_bucket,
    patch_mask,
    qkv_weight,
    qv_bias,
    proj_weight,
    proj_bias,
    first_gain,
    first_shift,
    rel_tables,
    up_weight,
    up_bias,
    down_weight,
    down_bias,
    second_gain,
    second_shift,
):
    inner = axis_bits("fsdp")
    outer = axis_bits("dp")
    every = outer + inner
    tp = lax.axis_size("fsdp")
    dpn = lax.axis_size("dp")
    n_dev = tp * dpn
    rows = D // n_dev
    heads = H // tp
    width = heads * HD
    hidden = FF // tp
    me = lax.axis_index("fsdp")

    smalls = [
        qv_bias, proj_bias, first_gain, first_shift, rel_tables, up_bias, down_bias,
        second_gain, second_shift,
    ]
    counts = [s.shape[0] for s in smalls]
    total = sum(counts)
    packed = jnp.concatenate(smalls)
    packed = jnp.pad(packed, (0, -total % 128))
    small_all = gather_over(packed[None, :], every[::-1], every).reshape(n_dev, -1)
    small_full, start = [], 0
    for c in counts:
        small_full.append(small_all[:, start : start + c].reshape(-1).astype(f32))
        start += c
    qv_full, projb, gain_one, shift_one, tables, upb, downb, gain_two, shift_two = small_full

    def columns_of(shard, groups):
        c = shard.shape[1] // (groups * tp)
        blocks = shard.reshape(rows, groups, tp, c).transpose(2, 0, 1, 3)
        blocks = exchange(blocks.reshape(tp, rows, groups * c), inner)
        return gather_over(blocks.reshape(tp * rows, groups * c), outer, outer).reshape(
            D, groups * c
        )

    def columns_back(partial_sum, groups):
        cols = partial_sum.shape[1]
        mine = scatter_sum(
            partial_sum.astype(bf16).reshape(dpn, tp * rows, cols), outer[::-1], outer
        )
        back = exchange(mine.astype(bf16).reshape(tp, rows, cols), inner)
        back = back.reshape(tp, rows, groups, cols // groups).transpose(1, 2, 0, 3)
        return back.reshape(rows, tp * cols).astype(f32)

    qkv_mine = columns_of(qkv_weight, 3)

    places = jnp.arange(TEXT, dtype=jnp.int32)
    live_own = jnp.concatenate(
        [places[None, :] < text_len[:, None], patch_mask > 0], axis=1
    ).astype(f32)
    pad_cols = ((0, 0), (0, D - SLOTS))
    doc_rows = jnp.concatenate(
        [
            tokens[0],
            jnp.pad(x_bucket.astype(bf16), pad_cols),
            jnp.pad(y_bucket.astype(bf16), pad_cols),
            jnp.pad(live_own.astype(bf16), pad_cols),
            jnp.zeros((ROWS - SLOTS - 3, D), bf16),
        ],
        axis=0,
    )
    docs = gather_over(doc_rows, inner, inner)
    notes = docs[:, SLOTS : SLOTS + 3, :ROWS].astype(f32)
    positions = jnp.minimum(jnp.arange(ROWS, dtype=jnp.int32), SLOTS - 1) * NB // SLOTS
    position_col = jnp.broadcast_to(positions[None, :, None], (tp, ROWS, 1))
    ids = jnp.concatenate(
        [position_col, notes[:, :2].transpose(0, 2, 1).astype(jnp.int32)], axis=2
    )
    ids = jnp.pad(ids, ((0, 0), (0, 0), (0, 5)))
    live_group = notes[:, 2:3]

    reach = jnp.clip(jnp.arange(2 * NB) - (NB // 2 - 1), 0, NB - 1)
    my_tables = lax.dynamic_slice_in_dim(tables.reshape(3, H, NB), me * heads, heads, 1)
    ext = my_tables.reshape(3 * heads, NB)
    ext = jnp.concatenate(
        [
            jnp.broadcast_to(ext[:, :1], (3 * heads, NB // 2 - 1)),
            ext,
            jnp.broadcast_to(ext[:, NB - 1 :], (3 * heads, NB // 2 + 1)),
        ],
        axis=1,
    )
    (bias,) = call(
        partial(bias_kernel, heads),
        tp,
        [ids, live_group, ext],
        [False, False, True],
        [jax.ShapeDtypeStruct((tp, heads, ROWS, ROWS), f32)],
        [False],
        flops=tp * heads * 3 * 2 * ROWS * NB * (NB + ROWS),
    )

    q_bias = lax.dynamic_slice_in_dim(qv_full[:D], me * width, width)
    v_bias = lax.dynamic_slice_in_dim(qv_full[D:], me * width, width)
    qkv_bias = jnp.concatenate([q_bias, jnp.zeros((width,), f32), v_bias])
    group = docs.reshape(tp * ROWS, D)
    qkv = (jnp.dot(group, qkv_mine, preferred_element_type=f32) + qkv_bias).astype(bf16)
    qkv = qkv.reshape(tp, ROWS, 3 * width)
    (mixed,) = call(
        partial(attend_kernel, heads),
        tp,
        [qkv, bias],
        [False, False],
        [jax.ShapeDtypeStruct((tp, ROWS, width), bf16)],
        [False],
        flops=tp * heads * 4 * ROWS * ROWS * HD,
    )
    attended = exchange(mixed, inner).transpose(1, 0, 2).reshape(ROWS, D)

    proj_full = gather_over(proj_weight, outer + inner, every).reshape(D, D)
    up_mine = columns_of(up_weight, 1)
    down_mine = columns_of(down_weight, 1)

    rows_in = pad_rows(tokens[0]).astype(f32)
    row_keep = jnp.pad(live_own[0], (0, ROWS - SLOTS))[:, None]
    branch = jnp.dot(attended, proj_full, preferred_element_type=f32) + projb
    resid_one = rows_in + branch
    hat_one, scale_one = norm_parts(resid_one)
    normed_one = hat_one * gain_one + shift_one
    normed_low = normed_one.astype(bf16)

    normed_group = gather_over(normed_low, inner, inner).reshape(tp * ROWS, D)
    my_upb = lax.dynamic_slice_in_dim(upb, me * hidden, hidden)
    pre_act = jnp.dot(normed_group, up_mine, preferred_element_type=f32) + my_upb
    act_low = jax.nn.gelu(pre_act, approximate=False).astype(bf16)
    ffn_part = dot_nt(act_low, down_mine).reshape(tp, ROWS, D)
    ffn_out = scatter_sum(ffn_part, inner[::-1], inner) + downb
    resid_two = normed_one + ffn_out
    hat_two, scale_two = norm_parts(resid_two)
    encoded = ((hat_two * gain_two + shift_two) * row_keep)[:SLOTS].astype(bf16)[None]

    grad_rows = pad_rows(out_grad[0]).astype(f32) * row_keep
    d_gain_two = jnp.sum(grad_rows * hat_two, axis=0)
    d_shift_two = jnp.sum(grad_rows, axis=0)
    d_resid_two = norm_back(grad_rows, gain_two, hat_two, scale_two)
    d_ffn = d_resid_two.astype(bf16)
    d_down_bias = jnp.sum(d_ffn.astype(f32), axis=0)
    d_ffn_group = gather_over(d_ffn, inner, inner).reshape(tp * ROWS, D)
    grad_down = columns_back(dot_tn(d_ffn_group, act_low), 1)
    d_act = jnp.dot(d_ffn_group, down_mine, preferred_element_type=f32)
    unused, gelu_back = jax.vjp(partial(jax.nn.gelu, approximate=False), pre_act)
    d_pre = gelu_back(d_act)[0].astype(bf16)
    d_up_bias = jnp.sum(d_pre.astype(f32), axis=0)
    grad_up = columns_back(dot_tn(normed_group, d_pre), 1)
    d_normed_part = dot_nt(d_pre, up_mine).reshape(tp, ROWS, D)
    d_normed = d_resid_two + scatter_sum(d_normed_part, inner[::-1], inner)
    d_gain_one = jnp.sum(d_normed * hat_one, axis=0)
    d_shift_one = jnp.sum(d_normed, axis=0)
    d_resid_one = norm_back(d_normed, gain_one, hat_one, scale_one)
    d_branch = d_resid_one.astype(bf16)
    d_proj_bias = jnp.sum(d_branch.astype(f32), axis=0)
    d_attended = dot_nt(d_branch, proj_full).astype(bf16)
    d_mixed = exchange(d_attended.reshape(ROWS, tp, width).transpose(1, 0, 2), inner)
    grad_proj = scatter_sum(
        dot_tn(attended, d_branch).astype(bf16).reshape(n_dev, rows, D), (inner[::-1] + outer[::-1]), every
    )
    d_qkv, d_sums, d_ext = call(
        partial(attend_back_kernel, heads),
        tp,
        [qkv, bias, d_mixed, ids],
        [False, False, False, False],
        [
            jax.ShapeDtypeStruct((tp, ROWS, 3 * width), bf16),
            jax.ShapeDtypeStruct((1, 3 * width), f32),
            jax.ShapeDtypeStruct((3 * heads, 2 * NB), f32),
        ],
        [False, True, True],
        scratch=[pltpu.VMEM((3 * heads, NB, NB), f32)],
        flops=tp * heads * (14 * ROWS * ROWS * HD + 6 * ROWS * NB * (ROWS + NB)),
    )
    d_qkv_rows = d_qkv.reshape(tp * ROWS, 3 * width)
    grad_qkv = columns_back(dot_tn(group, d_qkv_rows), 3)
    d_tokens_part = dot_nt(d_qkv_rows, qkv_mine).reshape(tp, ROWS, D)
    grad_tokens = d_resid_one + scatter_sum(d_tokens_part, inner[::-1], inner)

    half = NB // 2
    low = jnp.sum(d_ext[:, :half], axis=1, keepdims=True)
    high = jnp.sum(d_ext[:, NB + half - 2 :], axis=1, keepdims=True)
    d_tables = jnp.concatenate([low, d_ext[:, half : NB + half - 2], high], axis=1)

    def spread(part, size):
        return lax.dynamic_update_slice_in_dim(jnp.zeros((size,), f32), part, me * part.shape[0], 0)

    tables_wide = lax.dynamic_update_slice_in_dim(
        jnp.zeros((3, H, NB), f32), d_tables.reshape(3, heads, NB), me * heads, 1
    ).reshape(-1)
    qv_wide = jnp.concatenate(
        [spread(d_sums[0, :width], D), spread(d_sums[0, 2 * width :], D)]
    )
    grads = [
        qv_wide, d_proj_bias, d_gain_one, d_shift_one, tables_wide, spread(d_up_bias, FF),
        d_down_bias, d_gain_two, d_shift_two,
    ]
    block = jnp.concatenate([g.reshape(n_dev, -1) for g in grads], axis=1)
    block = jnp.pad(block, ((0, 0), (0, -total % 128)))
    arrived = lax.all_to_all(block, ("dp", "fsdp"), split_axis=0, concat_axis=0, tiled=True)
    summed = jnp.sum(arrived, axis=0)
    out, start = [], 0
    for c in counts:
        out.append(summed[start : start + c])
        start += c
    return (
        encoded,
        grad_tokens[:SLOTS][None],
        grad_qkv,
        out[0],
        grad_proj,
        out[1],
        out[2],
        out[3],
        out[4],
        grad_up,
        out[5],
        grad_down,
        out[6],
        out[7],
        out[8],
    )


def solution(mesh):
    split = ("dp", "fsdp")
    one, two, three = P(split), P(split, None), P(split, None, None)
    return jax.shard_map(
        local,
        mesh=mesh,
        in_specs=(
            three, three, one, two, two, two, two, one, two, one, one, one, one, two, one, two,
            one, one, one,
        ),
        out_specs=(
            three, three, two, one, two, one, one, one, one, two, one, two, one, one, one,
        ),
        check_vma=False,
    )
```

```python
from functools import partial

import jax
import jax.numpy as jnp
from jax import lax
from jax.experimental import pallas as pl
from jax.experimental.pallas import tpu as pltpu
from jax.sharding import PartitionSpec as P

D = 1024
H = 16
HD = 64
FF = 4096
NB = 128
TEXT = 120
SLOTS = 169
ROWS = 176
NEGATIVE = -1e30
EPSILON = 1e-05

f32 = jnp.float32
bf16 = jnp.bfloat16


def axis_bits(axis):
    bits, b = [], lax.axis_size(axis) // 2
    while b >= 1:
        bits.append((axis, b))
        b //= 2
    return bits


def swap(x, bit):
    axis, b = bit
    return lax.ppermute(x, axis, [(i, i ^ b) for i in range(lax.axis_size(axis))])


def side(bit):
    axis, b = bit
    return (lax.axis_index(axis) // b) % 2


def pair_up(mine, other, bit, pos):
    one = side(bit) == 1
    return jnp.stack([jnp.where(one, other, mine), jnp.where(one, mine, other)], axis=pos)


class Order:
    def __init__(self):
        self.last = None

    def tie(self, args, extra=()):
        extra = tuple(extra) + (() if self.last is None else (self.last,))
        if not extra:
            return args
        return lax.optimization_barrier(tuple(args) + extra)[: len(args)]

    def __call__(self, fn, *args):
        out = fn(*self.tie(args))
        self.last = jax.tree.leaves(out)[0]
        return out


class Gather:
    def __init__(self, run, x, axis):
        self.run, self.x, self.bits = run, x, axis_bits(axis)[3:][::-1] + axis_bits(axis)[:3]
        while len(self.bits) > 3:
            self.send().join()

    def send(self, after=()):
        x = self.x
        if after:
            x = lax.optimization_barrier((x,) + tuple(after))[0]
        self.other = swap(x, self.bits[0])
        return self

    def join(self):
        bit = self.bits.pop(0)
        if len(self.bits) >= 3:
            self.x = self.run(
                lambda m, o: pair_up(m, o, bit, 0).reshape(-1, m.shape[1]), self.x, self.other
            )
        else:
            self.x = self.run(lambda m, o: jnp.concatenate([m, o], axis=0), self.x, self.other)
        return self


class Scatter:
    def __init__(self, run, keep, give, axis, order):
        self.run = run
        bits = axis_bits(axis)
        self.high, self.rest = bits[:3], bits[3:]
        shape = (2, 2) + (2,) * len(self.rest) + (-1, keep.shape[1])
        self.have = [self.high[2], self.high[1], self.high[0]] + self.rest
        self.order = [self.high[i] for i in order] + self.rest
        if give is None:
            self.terms = [keep.reshape((2,) + shape)]
        else:
            self.terms = [keep.reshape(shape)]
            self.have.pop(0)
            self.first = give.reshape(shape)
        self.whole = give is None

    def part(self, t, bit, mine):
        pos = self.have.index(bit)
        if bit in self.high:
            return lax.index_in_dim(t, 0 if mine else 1, pos, keepdims=False)
        me = side(bit)
        return lax.dynamic_index_in_dim(t, me if mine else 1 - me, pos, keepdims=False)

    def send(self, after=()):
        bit = self.order[0]
        if not self.whole:
            out = self.first
        else:
            out = self.run(
                lambda *t: sum(self.part(x, bit, False).astype(f32) for x in t).astype(bf16),
                *self.terms,
            )
        if after:
            out = lax.optimization_barrier((out,) + tuple(after))[0]
        self.other = swap(out, bit)
        return self

    def take(self):
        bit = self.order.pop(0)
        if self.whole:
            self.terms = [self.part(t, bit, True) for t in self.terms]
            self.have.remove(bit)
        self.whole = True
        self.terms.append(self.other)
        while 0 < len(self.order) <= len(self.rest):
            self.send().take()
        return self


class Exchange:
    def __init__(self, run, x, canon):
        self.run, self.shape, self.canon = run, x.shape, list(canon)
        self.x = x.reshape((2,) * len(canon) + x.shape[1:])
        self.left = list(range(len(canon)))

    def send(self):
        pos = self.left[-1]
        bit = self.canon[pos]
        me = side(bit)
        give = self.run(
            lambda x: lax.dynamic_index_in_dim(x, 1 - me, pos, keepdims=False), self.x
        )
        self.other = swap(give, bit)
        return self

    def join(self):
        pos = self.left.pop()
        bit = self.canon[pos]
        me = side(bit)

        def both(x, other):
            return pair_up(lax.dynamic_index_in_dim(x, me, pos, keepdims=False), other, bit, pos)

        self.x = self.run(both, self.x, self.other)
        return self

    def done(self):
        return self.x.reshape(self.shape)


def dot_nn(a, b):
    return jnp.dot(a, b, preferred_element_type=f32)


def dot_nt(a, b):
    return lax.dot_general(a, b, (((1,), (1,)), ((), ())), preferred_element_type=f32)


def dot_tn(a, b):
    return lax.dot_general(a, b, (((0,), (0,)), ((), ())), preferred_element_type=f32)


def shape_of(shape, kind):
    return jax.ShapeDtypeStruct(tuple(shape), kind)


def call(kernel, steps, ins, in_maps, outs, out_maps, scratch=(), vmem=16):
    def spec(a, m):
        if m == "scalar":
            return pl.BlockSpec(memory_space=pltpu.SMEM)
        if steps == 1:
            return pl.BlockSpec(memory_space=pltpu.VMEM)
        if m is None:
            n = len(a.shape)
            return pl.BlockSpec(tuple(a.shape), lambda d: (0,) * n, pipeline_mode=pl.Buffered(1))
        return pl.BlockSpec(*m)

    return pl.pallas_call(
        kernel,
        grid=(steps,) if steps > 1 else (),
        in_specs=[spec(a, m) for a, m in zip(ins, in_maps)],
        out_specs=[spec(s, m) for s, m in zip(outs, out_maps)],
        out_shape=list(outs),
        scratch_shapes=list(scratch),
        cost_estimate=pl.CostEstimate(flops=0, bytes_accessed=0, transcendentals=0),
        compiler_params=pltpu.CompilerParams(
            dimension_semantics=("arbitrary",) if steps > 1 else None, vmem_limit_bytes=vmem * 2**20
        ),
    )(*ins)


def by_doc(a):
    n = len(a.shape)
    return ((1,) + tuple(a.shape[1:]), lambda d: (d,) + (0,) * (n - 1))


def at_block(ref, me, j, size):
    return pl.ds(pl.multiple_of((me ^ j) * size, size), size)


FLIPS = (0, 4, 2, 6, 1, 5, 3, 7)
BLOCK = D // 8


def far_block(place, q):
    return pl.ds(pl.multiple_of((place ^ FLIPS[q]) * BLOCK, BLOCK), BLOCK)


def relative(src, dst, place, rows):
    for q in range(8):
        dst[rows, q * BLOCK : (q + 1) * BLOCK] = src[:, far_block(place, q)]


def hot_rows(notes, flip=False):
    buckets = lax.broadcasted_iota(jnp.int32, (NB, ROWS), 0).astype(f32)
    if flip:
        buckets = (NB - 1) - buckets
    return [(notes[r : r + 1, :ROWS] == buckets).astype(f32).astype(bf16) for r in (12, 9, 10)]


def bias_kernel(heads, notes_ref, ext_ref, out_ref):
    notes = notes_ref[0].astype(f32)
    hots = hot_rows(notes)
    every_hot = jnp.concatenate(hots, axis=0)
    live = notes[11:12, :ROWS] > 0.5
    for h in range(heads):
        codes = []
        for k in range(3):
            row = ext_ref[k * heads + h : k * heads + h + 1, :]
            spread = jnp.broadcast_to(row, (NB, 2 * NB))
            skew = pltpu.roll(spread, NB + 1, 1, stride=1, stride_axis=0)
            codes.append(dot_tn(hots[k], skew[:, :NB].astype(bf16)).astype(bf16))
        total = dot_nn(jnp.concatenate(codes, axis=1), every_hot)
        out_ref[0, h] = jnp.where(live, total, NEGATIVE)


def softmax_rows(q, k, bias):
    s = dot_nt(q, k) * 0.125 + bias
    e = jnp.exp(s - jnp.max(s, axis=-1, keepdims=True))
    return e / jnp.sum(e, axis=-1, keepdims=True)


def attend_kernel(
    heads, at_ref, d0, d1, d2, d3, near_ref, far_ref, add_ref, bias_ref,
    group_ref, qkv_ref, probs_ref, m0_ref, m1_ref, m2_ref,
):
    step = pl.program_id(0)
    width = heads * HD

    @pl.when(step == 0)
    def _():
        for j, piece in enumerate((d0, d1, d2, d3)):
            relative(piece, group_ref, at_ref[1], slice(j * ROWS, (j + 1) * ROWS))

    here = pl.ds(pl.multiple_of(step * ROWS, ROWS), ROWS)
    qkv = dot_nn(group_ref[here, : D // 2], near_ref[:, : 3 * width])
    qkv = qkv + dot_nn(group_ref[here, D // 2 :], far_ref[:, : 3 * width])
    qkv_ref[0] = (qkv + add_ref[...]).astype(bf16)
    outs = []
    for h in range(heads):
        q = qkv_ref[0, :, h * HD : (h + 1) * HD]
        k = qkv_ref[0, :, width + h * HD : width + (h + 1) * HD]
        v = qkv_ref[0, :, 2 * width + h * HD : 2 * width + (h + 1) * HD]
        probs = softmax_rows(q, k, bias_ref[0, h])
        probs_ref[0, h] = probs
        outs.append(dot_nn(probs.astype(bf16), v).astype(bf16))
    mixed = jnp.concatenate(outs, axis=1)

    @pl.when(step == 0)
    def _():
        m0_ref[...] = mixed

    @pl.when(step == 1)
    def _():
        m1_ref[...] = mixed

    @pl.when(step == 2)
    def _():
        m2_ref[0] = mixed

    @pl.when(step == 3)
    def _():
        m2_ref[1] = mixed


def norm_parts(values):
    average = jnp.mean(values, axis=-1, keepdims=True)
    centred = values - average
    spread = jnp.mean(centred * centred, axis=-1, keepdims=True)
    scale = lax.rsqrt(spread + EPSILON)
    return centred * scale, scale


def norm_back(grad, gain, hat, scale):
    scaled = grad * gain
    first = jnp.mean(scaled, axis=-1, keepdims=True)
    second = jnp.mean(scaled * hat, axis=-1, keepdims=True)
    return (scaled - first - hat * second) * scale


def first_norm_kernel(
    width, at_ref, a0, a1, a2, a3, *rest
):
    near, far = rest[:4], rest[4:8]
    tokens_ref, vec_ref, att_ref, low_ref, normed_ref, hat_ref, scale_ref, branch_ref, plain_ref = rest[8:]
    me = at_ref[0]
    for j, piece in enumerate((a0[...], a1[...], a2[0], a3[...])):
        plain_ref[:, at_block(plain_ref, me, j, width)] = piece
    relative(plain_ref, att_ref, at_ref[1], slice(None))
    left, right = att_ref[:, : D // 2], att_ref[:, D // 2 :]
    for j in range(4):
        branch_ref[:, at_block(branch_ref, me, j, width)] = dot_nn(left, near[j][...]) + dot_nn(
            right, far[j][...]
        )
    resid = tokens_ref[...].astype(f32) + branch_ref[...] + vec_ref[0:1, :]
    hat, scale = norm_parts(resid)
    normed = hat * vec_ref[1:2, :] + vec_ref[2:3, :]
    low_ref[...] = normed.astype(bf16)
    normed_ref[...] = normed
    hat_ref[...] = hat
    scale_ref[...] = scale


def split_parts(total, keep_ref, give_ref, place):
    for q in range(8):
        at = slice(q * BLOCK, (q + 1) * BLOCK)
        for n, j in enumerate((0, 2)):
            keep_ref[n, :, far_block(place, q)] = total[j * ROWS : (j + 1) * ROWS, at]
        for n, j in enumerate((1, 3)):
            give_ref[n, :, far_block(place, q)] = total[j * ROWS : (j + 1) * ROWS, at].astype(bf16)


def stack_once(pieces, group_ref, place):
    @pl.when(pl.program_id(0) == 0)
    def _():
        for j, piece in enumerate(pieces):
            relative(piece, group_ref, place, slice(j * ROWS, (j + 1) * ROWS))


def add_part(acc_ref, left, near_ref, far_ref):
    step = pl.program_id(0)
    for n, ref in enumerate((near_ref, far_ref)):
        part = dot_nt(left, ref[...])
        at = slice(n * (D // 2), (n + 1) * (D // 2))

        @pl.when(step == 0)
        def _():
            acc_ref[:, at] = part

        @pl.when(step > 0)
        def _():
            acc_ref[:, at] += part


def normal_parts(u):
    density = jnp.exp(-0.5 * u * u)
    return 0.5 + 0.5 * lax.erf(u * (0.5**0.5)), u * density * ((2 * jnp.pi) ** -0.5)


def up_kernel(
    at_ref, x0, x1, x2, x3, up_near, up_far, down_near, down_far, add_ref,
    group_ref, slope_ref, act_ref, keep_ref, give_ref, acc_ref,
):
    stack_once((x0, x1, x2, x3), group_ref, at_ref[1])
    pre = dot_nn(group_ref[:, : D // 2], up_near[...])
    pre = pre + dot_nn(group_ref[:, D // 2 :], up_far[...]) + add_ref[...]
    below, tilt = normal_parts(pre)
    slope_ref[...] = below + tilt
    act = (pre * below).astype(bf16)
    act_ref[...] = act
    add_part(acc_ref, act, down_near, down_far)

    @pl.when(pl.program_id(0) == pl.num_programs(0) - 1)
    def _():
        split_parts(acc_ref, keep_ref, give_ref, at_ref[1])


def down_back_kernel(
    at_ref, g0, g1, g2, g3, down_near, down_far, up_near, up_far, slope_ref,
    group_ref, dpre_ref, sums_ref, keep_ref, give_ref, acc_ref,
):
    stack_once((g0, g1, g2, g3), group_ref, at_ref[1])
    d_act = dot_nn(group_ref[:, : D // 2], down_near[...])
    d_act = d_act + dot_nn(group_ref[:, D // 2 :], down_far[...])
    d_pre = (d_act * slope_ref[...]).astype(bf16)
    dpre_ref[...] = d_pre
    sums_ref[...] = jnp.sum(d_pre.astype(f32), axis=0, keepdims=True)
    add_part(acc_ref, d_pre, up_near, up_far)

    @pl.when(pl.program_id(0) == pl.num_programs(0) - 1)
    def _():
        split_parts(acc_ref, keep_ref, give_ref, at_ref[1])


def second_norm_kernel(
    keep_ref, got_c, got_y, normed_ref, grad_ref, live_ref, vec_ref,
    enc_ref, dffn_ref, dres_ref, sums_ref,
):
    ffn = keep_ref[0] + got_c[0].astype(f32) + got_y[...].astype(f32) + vec_ref[0:1, :]
    hat, scale = norm_parts(normed_ref[...] + ffn)
    live = live_ref[...]
    gain = vec_ref[1:2, :]
    enc = ((hat * gain + vec_ref[2:3, :]) * live).astype(bf16)
    enc_ref[0] = enc[:SLOTS]
    grad = grad_ref[...].astype(f32) * live
    d_resid = norm_back(grad, gain, hat, scale)
    dres_ref[...] = d_resid
    low = d_resid.astype(bf16)
    dffn_ref[...] = low
    sums_ref[0:1, :] = jnp.sum(low.astype(f32), axis=0, keepdims=True)
    sums_ref[1:2, :] = jnp.sum(grad * hat, axis=0, keepdims=True)
    sums_ref[2:3, :] = jnp.sum(grad, axis=0, keepdims=True)


def first_back_kernel(width, at_ref, keep_ref, got_c, got_y, dres_ref, hat_ref, scale_ref, vec_ref, *rest):
    near, far = rest[:4], rest[4:8]
    branch_ref, done_ref, sums_ref, a0_ref, a1_ref, a2_ref, plain_ref = rest[8:]
    me = at_ref[0]
    hat = hat_ref[...]
    grad = dres_ref[...] + keep_ref[0] + got_c[0].astype(f32) + got_y[...].astype(f32)
    d_one = norm_back(grad, vec_ref[1:2, :], hat, scale_ref[...])
    done_ref[...] = d_one
    low = d_one.astype(bf16)
    branch_ref[...] = low
    sums_ref[0:1, :] = jnp.sum(low.astype(f32), axis=0, keepdims=True)
    sums_ref[1:2, :] = jnp.sum(grad * hat, axis=0, keepdims=True)
    sums_ref[2:3, :] = jnp.sum(grad, axis=0, keepdims=True)
    for n, proj in enumerate((near, far)):
        total = None
        for j in range(4):
            part = dot_nt(branch_ref[:, at_block(branch_ref, me, j, width)], proj[j][...])
            total = part if total is None else total + part
        for q in range(4):
            plain_ref[:, far_block(at_ref[1], 4 * n + q)] = total[
                :, q * BLOCK : (q + 1) * BLOCK
            ].astype(bf16)
    for i, out in enumerate((a0_ref, a1_ref, a2_ref.at[0], a2_ref.at[1])):
        out[...] = plain_ref[:, at_block(plain_ref, me, i, width)]


def proj_grad_kernel(width, at_ref, att_ref, branch_ref, keep_ref, give_ref):
    me = at_ref[0]
    att = att_ref[...]
    for n, j in enumerate((0, 2)):
        keep_ref[n] = dot_tn(att, branch_ref[:, at_block(branch_ref, me, j, width)]).astype(bf16)
    for n, j in enumerate((1, 3)):
        give_ref[n] = dot_tn(att, branch_ref[:, at_block(branch_ref, me, j, width)]).astype(bf16)


def attend_back_kernel(
    heads, qkv_ref, probs_ref, g0, g1, g2, g3, notes_ref, dqkv_ref, sums_ref, ext_ref, grid_ref, grad_ref
):
    step = pl.program_id(0)
    width = heads * HD
    notes = notes_ref[0].astype(f32)
    hots = jnp.concatenate(hot_rows(notes), axis=0)
    flipped = hot_rows(notes, flip=True)

    @pl.when(step == 0)
    def _():
        grid_ref[...] = jnp.zeros_like(grid_ref)
        sums_ref[...] = jnp.zeros_like(sums_ref)

    for j, piece in enumerate((g0, g1, g2.at[0], g3)):

        @pl.when(step == j)
        def _():
            grad_ref[...] = piece[...]

    for h in range(heads):
        q = qkv_ref[0, :, h * HD : (h + 1) * HD]
        k = qkv_ref[0, :, width + h * HD : width + (h + 1) * HD]
        v = qkv_ref[0, :, 2 * width + h * HD : 2 * width + (h + 1) * HD]
        g = grad_ref[:, h * HD : (h + 1) * HD]
        p = probs_ref[0, h]
        dp = dot_nt(g, v)
        ds = (p * (dp - jnp.sum(p * dp, axis=-1, keepdims=True))).astype(bf16)
        dqkv_ref[0, :, h * HD : (h + 1) * HD] = (dot_nn(ds, k) * 0.125).astype(bf16)
        dqkv_ref[0, :, width + h * HD : width + (h + 1) * HD] = (dot_tn(ds, q) * 0.125).astype(bf16)
        dqkv_ref[0, :, 2 * width + h * HD : 2 * width + (h + 1) * HD] = dot_tn(
            p.astype(bf16), g
        ).astype(bf16)
        part = dot_nt(ds, hots).astype(bf16)
        for n in range(3):
            grid_ref[n * heads + h] += dot_nn(flipped[n], part[:, n * NB : (n + 1) * NB])
    sums_ref[...] += jnp.sum(dqkv_ref[0].astype(f32), axis=0, keepdims=True)

    @pl.when(step == pl.num_programs(0) - 1)
    def _():
        for n in range(3 * heads):
            wide = jnp.concatenate([grid_ref[n], jnp.zeros((NB, NB), f32)], axis=1)
            skew = pltpu.roll(wide, 0, 1, stride=1, stride_axis=0)
            ext_ref[n : n + 1, :] = jnp.sum(skew, axis=0, keepdims=True)


def tokens_back_kernel(width, at_ref, d_ref, near_ref, far_ref, keep_ref, give_ref):
    step = pl.program_id(0)
    parts = [dot_nt(d_ref[0], ref[:, : 3 * width]) for ref in (near_ref, far_ref)]
    for n, part in enumerate(parts):
        for q in range(4):
            block = part[:, q * BLOCK : (q + 1) * BLOCK]

            @pl.when(step % 2 == 0)
            def _():
                keep_ref[step // 2, :, far_block(at_ref[1], 4 * n + q)] = block

            @pl.when(step % 2 == 1)
            def _():
                give_ref[step // 2, :, far_block(at_ref[1], 4 * n + q)] = block.astype(bf16)


def pad_rows(x):
    return jnp.pad(x, ((0, ROWS - SLOTS), (0, 0)))


def local(
    tokens,
    out_grad,
    text_len,
    x_bucket,
    y_bucket,
    patch_mask,
    qkv_weight,
    qv_bias,
    proj_weight,
    proj_bias,
    first_gain,
    first_shift,
    rel_tables,
    up_weight,
    up_bias,
    down_weight,
    down_bias,
    second_gain,
    second_shift,
):
    inner = axis_bits("fsdp")
    outer = axis_bits("dp")
    tp = 4
    by_y, by_c = inner
    dpn = lax.axis_size("dp")
    n_dev = tp * dpn
    rows = D // n_dev
    heads = H // tp
    width = heads * HD
    hidden = FF // tp
    me = lax.axis_index("fsdp")
    place = lax.axis_index("dp") // (dpn // 8)
    at = jnp.stack([me, place]).astype(jnp.int32)
    run = Order()

    def group_of(own):
        far = swap(own, by_y)
        return own, swap(own, by_c), far, swap(far, by_c)

    def trade(p0, p1, p2):
        far = swap(p2, by_y)
        return p0, swap(p1, by_c), far, swap(far[1], by_c)

    class Meet:
        def __init__(self, keep, give):
            self.keep, self.near = keep, swap(give, by_c)

        def send(self):
            both = run(lambda k, g: (k[1].astype(f32) + g[1].astype(f32)).astype(bf16), self.keep, self.near)
            self.far = swap(both, by_y)
            return self

    def blocks_of(shard, groups):
        c = shard.shape[1] // (groups * tp)
        blocks = shard.reshape(rows, groups, tp, c).transpose(2, 0, 1, 3)
        return blocks.reshape(tp, rows, groups * c)

    ex_first = Exchange(
        run,
        run(
            lambda a, b: jnp.concatenate([blocks_of(a, 3), blocks_of(b, 1)], axis=2),
            qkv_weight, proj_weight,
        ),
        inner,
    ).send()

    smalls = [
        proj_bias, first_gain, first_shift, down_bias, second_gain, second_shift,
        qv_bias, rel_tables, up_bias,
    ]
    counts = [s.shape[0] for s in smalls]
    total = sum(counts)

    def pack(*smalls):
        packed = jnp.concatenate([s[None, :] for s in smalls], axis=1)
        packed = jnp.pad(packed, ((0, 0), (0, -total % 128)))
        return jnp.broadcast_to(packed[None].astype(f32), (n_dev, 1, packed.shape[1]))

    places = jnp.arange(TEXT, dtype=jnp.int32)
    live_own = jnp.concatenate(
        [places[None, :] < text_len[:, None], patch_mask > 0], axis=1
    ).astype(f32)

    def document(tokens, x_bucket, y_bucket, live):
        pad_cols = ((0, 0), (0, D - SLOTS))
        positions = (jnp.arange(SLOTS, dtype=jnp.int32) * NB // SLOTS)[None]
        return jnp.concatenate(
            [
                tokens[0],
                jnp.pad(x_bucket.astype(bf16), pad_cols),
                jnp.pad(y_bucket.astype(bf16), pad_cols),
                jnp.pad(live.astype(bf16), pad_cols),
                jnp.pad(positions.astype(bf16), pad_cols),
                jnp.zeros((ROWS - SLOTS - 4, D), bf16),
            ],
            axis=0,
        )

    doc_rows = run(document, tokens, x_bucket, y_bucket, live_own)
    ex_first.join().send()
    packed = run(pack, *smalls)
    ex_ffn = Exchange(
        run,
        run(
            lambda a, b: jnp.concatenate([blocks_of(a, 1), blocks_of(b, 1)], axis=2),
            up_weight, down_weight,
        ),
        inner,
    ).send()
    ex_first.join()
    g_first = Gather(run, ex_first.done().reshape(tp * rows, D), "dp").send()
    ex_ffn.join().send()
    doc_pieces = group_of(doc_rows)
    small_all = lax.all_to_all(packed, ("dp", "fsdp"), split_axis=0, concat_axis=0, tiled=True)
    grad_in = run(pad_rows, out_grad[0])
    live_col = run(lambda l: jnp.pad(l[0], (0, ROWS - SLOTS))[:, None], live_own)
    ex_ffn.join()
    ffn_blocks = ex_ffn.done().reshape(tp * rows, 2 * hidden)
    g_up = Gather(run, run(lambda b: b[:, :hidden], ffn_blocks), "dp").send()
    g_first.join().send()

    def unpack(small_all):
        flat = small_all[:, 0]
        vecs = flat[:, : 6 * rows].reshape(n_dev, 6, rows).transpose(1, 0, 2).reshape(6, D)
        parts, start = [], 6 * rows
        for c in counts[6:]:
            parts.append(flat[:, start : start + c].reshape(-1))
            start += c
        qv, tables, upb = parts
        q_bias = lax.dynamic_slice_in_dim(qv[:D], me * width, width)
        v_bias = lax.dynamic_slice_in_dim(qv[D:], me * width, width)
        qkv_bias = jnp.concatenate([q_bias, jnp.zeros((width,), f32), v_bias])[None]
        ext = lax.dynamic_slice_in_dim(tables.reshape(3, H, NB), me * heads, heads, 1)
        ext = ext.reshape(3 * heads, NB)
        ext = jnp.concatenate(
            [
                jnp.broadcast_to(ext[:, :1], (3 * heads, NB // 2 - 1)),
                ext,
                jnp.broadcast_to(ext[:, NB - 1 :], (3 * heads, NB // 2 + 1)),
            ],
            axis=1,
        )
        my_upb = lax.dynamic_slice_in_dim(upb, me * hidden, hidden)[None]
        return ext, qkv_bias, my_upb, vecs

    notes = run(
        lambda *d: jnp.stack([x[ROWS - 16 :, : 2 * NB] for x in d]), *doc_pieces
    )
    ext, qkv_bias, my_upb, vecs = run(unpack, small_all)
    vec_one, vec_two = run(lambda v: (v[:3], v[3:]), vecs)
    g_down = Gather(run, run(lambda b: b[:, hidden:], ffn_blocks), "dp")
    g_first.join().send()

    (bias,) = run(
        lambda *ins: call(
            partial(bias_kernel, heads),
            tp, ins, [by_doc(notes), None],
            [shape_of((tp, heads, ROWS, ROWS), f32)],
            [by_doc(shape_of((tp, heads, ROWS, ROWS), f32))],
        ),
        notes, ext,
    )
    proj_near = group_of(run(lambda w: w[:, 3 * width :], g_first.x))
    g_up.join().send()
    g_down.send()
    g_up.join()
    g_down.join().send()

    g_up.send(after=(g_first.other,))
    proj_far = group_of(run(lambda w: w[:, 3 * width :], g_first.other))
    doc_out = shape_of((ROWS, width), bf16)
    qkv_out = shape_of((tp, ROWS, 3 * width), bf16)
    pair_out = shape_of((2, ROWS, width), bf16)
    probs_out = shape_of((tp, heads, ROWS, ROWS), f32)
    group_out = shape_of((tp * ROWS, D), bf16)
    group, qkv, probs, m0, m1, m2 = run(
        lambda *ins: call(
            partial(attend_kernel, heads),
            tp, ins, ["scalar"] + [None] * 7 + [by_doc(bias)],
            [group_out, qkv_out, probs_out, doc_out, doc_out, pair_out],
            [None, by_doc(qkv_out), by_doc(probs_out), None, None, None],
        ),
        at, *doc_pieces, g_first.x, g_first.other, qkv_bias, bias,
    )
    att_pieces = trade(m0, m1, m2)
    g_down.join()

    wide_f = shape_of((ROWS, D), f32)
    wide_b = shape_of((ROWS, D), bf16)
    attended, normed_low, normed_one, hat_one, scale_one = run(
        lambda *ins: call(
            partial(first_norm_kernel, width),
            1, ins, ["scalar"] + [None] * 14,
            [wide_b, wide_b, wide_f, wide_f, shape_of((ROWS, 1), f32)],
            [None] * 5,
            [pltpu.VMEM((ROWS, D), f32), pltpu.VMEM((ROWS, D), bf16)],
        ),
        at, *att_pieces, *proj_near, *proj_far, doc_rows, vec_one,
    )

    normed_pieces = group_of(normed_low)
    g_down.send(after=(g_up.other,))
    tile = 256
    steps = hidden // tile
    col_w = ((D // 2, tile), lambda d: (0, d))
    col_x = ((tp * ROWS, tile), lambda d: (0, d))
    col_b = ((1, tile), lambda d: (0, d))
    hid_f = shape_of((tp * ROWS, hidden), f32)
    hid_b = shape_of((tp * ROWS, hidden), bf16)
    two_f, two_b = shape_of((2, ROWS, D), f32), shape_of((2, ROWS, D), bf16)
    acc = pltpu.VMEM((tp * ROWS, D), f32)
    normed_group, slope, act_low, keep, give = run(
        lambda *ins: call(
            up_kernel,
            steps, ins, ["scalar"] + [None] * 4 + [col_w] * 4 + [col_b],
            [group_out, hid_f, hid_b, two_f, two_b],
            [None, col_x, col_x, None, None],
            [acc], vmem=24,
        ),
        at, *normed_pieces, g_up.x, g_up.other, g_down.x, g_down.other, my_upb,
    )
    meet = Meet(keep, give).send()
    encoded, d_ffn, d_resid_two, sums_two = run(
        lambda *ins: call(
            second_norm_kernel,
            1, ins, [None] * 7,
            [shape_of((1, SLOTS, D), bf16), wide_b, wide_f, shape_of((3, D), f32)],
            [None] * 4,
        ),
        meet.keep, meet.near, meet.far, normed_one, grad_in, live_col, vec_two,
    )

    d_ffn_pieces = group_of(d_ffn)
    d_ffn_group, d_pre, d_up_bias, keep, give = run(
        lambda *ins: call(
            down_back_kernel,
            steps, ins, ["scalar"] + [None] * 4 + [col_w] * 4 + [col_x],
            [group_out, hid_b, shape_of((1, hidden), f32), two_f, two_b],
            [None, col_x, col_b, None, None],
            [acc], vmem=24,
        ),
        at, *d_ffn_pieces, g_down.x, g_down.other, g_up.x, g_up.other, slope,
    )
    meet = Meet(keep, give)

    def half_grad(left, right, near):
        left = left[:, : D // 2] if near else left[:, D // 2 :]
        return dot_tn(left, right).astype(bf16)

    give = run(partial(half_grad, near=False), d_ffn_group, act_low)
    keep = run(partial(half_grad, near=True), d_ffn_group, act_low)
    s_down = Scatter(run, keep, give, "dp", (2, 1, 0)).send()
    meet.send()
    grad = run(lambda a, b: dot_tn(a, b).astype(bf16), normed_group, d_pre)
    s_up = Scatter(run, grad, None, "dp", (1, 0, 2)).send()

    d_branch, d_resid_one, sums_one, a0, a1, a2 = run(
        lambda *ins: call(
            partial(first_back_kernel, width),
            1, ins, ["scalar"] + [None] * 15,
            [wide_b, wide_f, shape_of((3, D), f32), doc_out, doc_out, pair_out],
            [None] * 6,
            [pltpu.VMEM((ROWS, D), bf16)],
        ),
        at, meet.keep, meet.near, meet.far, d_resid_two, hat_one, scale_one, vec_one,
        *proj_near, *proj_far,
    )
    grad_pieces = trade(a0, a1, a2)
    two_p = shape_of((2, D, width), bf16)
    keep, give = run(
        lambda *ins: call(
            partial(proj_grad_kernel, width),
            1, ins, ["scalar", None, None], [two_p, two_p], [None, None],
        ),
        at, attended, d_branch,
    )
    meet_proj = Meet(keep, give)
    s_down.take().send()
    d_qkv, d_sums, d_ext = run(
        lambda *ins: call(
            partial(attend_back_kernel, heads),
            tp, ins, [by_doc(qkv), by_doc(probs), None, None, None, None, by_doc(notes)],
            [qkv_out, shape_of((1, 3 * width), f32), shape_of((3 * heads, 2 * NB), f32)],
            [by_doc(qkv_out), None, None],
            [pltpu.VMEM((3 * heads, NB, NB), f32), pltpu.VMEM((ROWS, width), bf16)],
        ),
        qkv, probs, *grad_pieces, notes,
    )
    d_qkv_rows = d_qkv.reshape(tp * ROWS, 3 * width)
    meet_proj.send()
    s_up.take().send()
    s_down.take().send()

    def first_half(group, d_qkv, k, c, y, near):
        rows_at = slice(0, D // 2) if near else slice(D // 2, D)
        q = half_grad(group, d_qkv, near)
        p = (k[0, rows_at].astype(f32) + c[0, rows_at].astype(f32) + y[rows_at].astype(f32)).astype(bf16)
        return jnp.concatenate([q, p], axis=1)

    proj_terms = (meet_proj.keep, meet_proj.near, meet_proj.far)
    give = run(partial(first_half, near=False), group, d_qkv_rows, *proj_terms)
    keep = run(partial(first_half, near=True), group, d_qkv_rows, *proj_terms)
    s_first = Scatter(run, keep, give, "dp", (2, 1, 0)).send()
    keep, give = run(
        lambda *ins: call(
            partial(tokens_back_kernel, width),
            tp, ins, ["scalar", by_doc(d_qkv), None, None], [two_f, two_b], [None, None],
        ),
        at, d_qkv, g_first.x, g_first.other,
    )
    meet_tok = Meet(keep, give)

    half = NB // 2

    def spread(part, size):
        return lax.dynamic_update_slice_in_dim(jnp.zeros((size,), f32), part, me * part.shape[0], 0)

    def small_blocks(d_ext, d_sums, d_up_bias, sums_one, sums_two):
        low = jnp.sum(d_ext[:, :half], axis=1, keepdims=True)
        high = jnp.sum(d_ext[:, NB + half - 2 :], axis=1, keepdims=True)
        d_tables = jnp.concatenate([low, d_ext[:, half : NB + half - 2], high], axis=1)
        tables_wide = lax.dynamic_update_slice_in_dim(
            jnp.zeros((3, H, NB), f32), d_tables.reshape(3, heads, NB), me * heads, 1
        ).reshape(-1)
        qv_wide = jnp.concatenate(
            [spread(d_sums[0, :width], D), spread(d_sums[0, 2 * width :], D)]
        )
        vecs = jnp.concatenate([sums_one, sums_two]).reshape(6, n_dev, rows)
        grads = [qv_wide, tables_wide, spread(d_up_bias[0], FF)]
        block = jnp.concatenate(
            [vecs.transpose(1, 0, 2).reshape(n_dev, 6 * rows)]
            + [g.reshape(n_dev, -1) for g in grads],
            axis=1,
        )
        return jnp.pad(block, ((0, 0), (0, -total % 128)))[:, None]

    block = run(small_blocks, d_ext, d_sums, d_up_bias, sums_one, sums_two)
    arrived = lax.all_to_all(block, ("dp", "fsdp"), split_axis=0, concat_axis=0, tiled=True)
    meet_tok.send()
    s_up.take().send()
    s_down.take()
    s_first.take().send()
    s_up.take()

    def low_sums(*t):
        n = len(s_up.terms)
        return jnp.concatenate(
            [sum(x.astype(f32) for x in part).astype(bf16) for part in (t[:n], t[n:])], axis=1
        )

    both = run(low_sums, *s_up.terms, *s_down.terms)
    x_ffn = Exchange(run, both.reshape(tp, rows, 2 * hidden), inner).send()
    grad_tokens = run(
        lambda d, k, c, y: (d + k[0] + c[0].astype(f32) + y.astype(f32))[:SLOTS][None],
        d_resid_one, meet_tok.keep, meet_tok.near, meet_tok.far,
    )
    x_ffn.join().send()
    s_first.take().send()

    def small_outs(arrived):
        summed = jnp.sum(arrived[:, 0], axis=0)
        out, start = [], 0
        for c in counts:
            out.append(summed[start : start + c])
            start += c
        return out

    out = run(small_outs, arrived)
    x_ffn.join()

    def columns(back, groups):
        cols = back.shape[-1]
        back = back.reshape(tp, rows, groups, cols // groups).transpose(1, 2, 0, 3)
        return back.reshape(rows, tp * cols).astype(f32)

    back = x_ffn.done()
    grad_up, grad_down = run(
        lambda b: (columns(b[:, :, :hidden], 1), columns(b[:, :, hidden:], 1)), back
    )
    s_first.take()
    mine = run(lambda *t: sum(x.astype(f32) for x in t).astype(bf16), *s_first.terms)
    x_first = Exchange(run, mine.reshape(tp, rows, D), inner).send().join().send().join()
    back = x_first.done()
    grad_qkv = columns(back[:, :, : 3 * width], 3)
    grad_proj = columns(back[:, :, 3 * width :], 1)
    return (
        encoded,
        grad_tokens,
        grad_qkv,
        out[6],
        grad_proj,
        out[0],
        out[1],
        out[2],
        out[7],
        grad_up,
        out[8],
        grad_down,
        out[3],
        out[4],
        out[5],
    )


def solution(mesh):
    split = ("dp", "fsdp")
    one, two, three = P(split), P(split, None), P(split, None, None)
    return jax.shard_map(
        local,
        mesh=mesh,
        in_specs=(
            three, three, one, two, two, two, two, one, two, one, one, one, one, two, one, two,
            one, one, one,
        ),
        out_specs=(
            three, three, two, one, two, one, one, one, one, two, one, two, one, one, one,
        ),
        check_vma=False,
    )
```

```python
from functools import partial

import jax
import jax.numpy as jnp
from jax import lax
from jax.experimental import pallas as pl
from jax.experimental.pallas import tpu as pltpu
from jax.sharding import PartitionSpec as P

D = 1024
H = 16
HD = 64
FF = 4096
NB = 128
TEXT = 120
SLOTS = 169
ROWS = 176
NEGATIVE = -1e30
EPSILON = 1e-05

f32 = jnp.float32
bf16 = jnp.bfloat16


def axis_bits(axis):
    bits, b = [], lax.axis_size(axis) // 2
    while b >= 1:
        bits.append((axis, b))
        b //= 2
    return bits


def swap(x, bit):
    axis, b = bit
    return lax.ppermute(x, axis, [(i, i ^ b) for i in range(lax.axis_size(axis))])


def side(bit):
    axis, b = bit
    return (lax.axis_index(axis) // b) % 2


def pair_up(mine, other, bit, pos):
    one = side(bit) == 1
    return jnp.stack([jnp.where(one, other, mine), jnp.where(one, mine, other)], axis=pos)


class Order:
    def __init__(self):
        self.last = ()

    def tie(self, args):
        if not self.last:
            return args
        return lax.optimization_barrier(tuple(args) + self.last)[: len(args)]

    def wait(self, *arrays):
        self.last = self.last + arrays

    def __call__(self, fn, *args):
        out = fn(*self.tie(args))
        self.last = tuple(jax.tree.leaves(out))
        return out


def after(x, *earlier):
    return lax.optimization_barrier((x,) + earlier)[0]


def high_bits(axis, order):
    bits = axis_bits(axis)
    return [bits[i] for i in order]


class Gather:
    def __init__(self, run, x, axis, order):
        self.run, self.x = run, x
        self.bits = axis_bits(axis)[3:][::-1] + high_bits(axis, order)
        while len(self.bits) > 3:
            self.send().join()

    def send(self, *earlier):
        self.other = swap(after(self.x, *earlier), self.bits[0])
        return self

    def join(self):
        bit = self.bits.pop(0)
        if len(self.bits) >= 3:
            self.x = self.run(
                lambda m, o: pair_up(m, o, bit, 0).reshape(-1, m.shape[1]), self.x, self.other
            )
        else:
            self.x = self.run(lambda m, o: jnp.concatenate([m, o], axis=0), self.x, self.other)
        return self


class Scatter:
    def __init__(self, run, keep, give, axis, order, walk=None):
        self.run = run
        self.high, self.rest = high_bits(axis, order), axis_bits(axis)[3:]
        shape = (2, 2) + (2,) * len(self.rest) + (-1, keep.shape[1])
        self.have = self.high[::-1] + self.rest
        self.order = (high_bits(axis, walk) if walk else self.high[::-1]) + self.rest
        self.whole = give is None
        if self.whole:
            self.terms = [keep.reshape((2,) + shape)]
        else:
            self.terms, self.first = [keep.reshape(shape)], give.reshape(shape)
            self.have.pop(0)

    def part(self, t, bit, mine):
        pos = self.have.index(bit)
        if bit in self.high:
            return lax.index_in_dim(t, 0 if mine else 1, pos, keepdims=False)
        me = side(bit)
        return lax.dynamic_index_in_dim(t, me if mine else 1 - me, pos, keepdims=False)

    def send(self, *earlier):
        bit = self.order[0]
        out = self.first if not self.whole else self.run(
            lambda *t: sum(self.part(x, bit, False).astype(f32) for x in t).astype(bf16),
            *self.terms,
        )
        self.other = swap(after(out, *earlier), bit)
        return self

    def take(self):
        bit = self.order.pop(0)
        if self.whole:
            self.terms = [self.part(t, bit, True) for t in self.terms]
            self.have.remove(bit)
        self.whole = True
        self.terms.append(self.other)
        while 0 < len(self.order) <= len(self.rest):
            self.send().take()
        return self


class Exchange:
    def __init__(self, run, x, canon):
        self.run, self.shape, self.canon = run, x.shape, list(canon)
        self.x = x.reshape((2,) * len(canon) + x.shape[1:])
        self.left = list(range(len(canon)))

    def send(self, *earlier):
        pos = self.left[-1]
        bit = self.canon[pos]
        me = side(bit)
        give = self.run(
            lambda x: lax.dynamic_index_in_dim(x, 1 - me, pos, keepdims=False), self.x
        )
        self.other = swap(after(give, *earlier), bit)
        return self

    def join(self):
        pos = self.left.pop()
        bit = self.canon[pos]
        me = side(bit)

        def both(x, other):
            return pair_up(lax.dynamic_index_in_dim(x, me, pos, keepdims=False), other, bit, pos)

        self.x = self.run(both, self.x, self.other)
        return self

    def done(self):
        return self.x.reshape(self.shape)


def dot_nn(a, b):
    return jnp.dot(a, b, preferred_element_type=f32)


def dot_nt(a, b):
    return lax.dot_general(a, b, (((1,), (1,)), ((), ())), preferred_element_type=f32)


def dot_tn(a, b):
    return lax.dot_general(a, b, (((0,), (0,)), ((), ())), preferred_element_type=f32)


def shape_of(shape, kind):
    return jax.ShapeDtypeStruct(tuple(shape), kind)


def call(kernel, ins, outs, scratch=(), scalars=0, alias=None, vmem=16):
    spaces = [pltpu.SMEM] * scalars + [pltpu.VMEM] * (len(ins) - scalars)
    return pl.pallas_call(
        kernel,
        in_specs=[pl.BlockSpec(memory_space=m) for m in spaces],
        out_specs=[pl.BlockSpec(memory_space=pltpu.VMEM) for _ in outs],
        out_shape=list(outs),
        scratch_shapes=list(scratch),
        input_output_aliases=alias or {},
        cost_estimate=pl.CostEstimate(flops=0, bytes_accessed=0, transcendentals=0),
        compiler_params=pltpu.CompilerParams(vmem_limit_bytes=vmem * 2**20),
    )(*ins)


def call_docs(kernel, docs, ins, in_whole, outs):
    def spec(a, whole):
        n = len(a.shape)
        if whole:
            return pl.BlockSpec(tuple(a.shape), lambda d: (0,) * n)
        return pl.BlockSpec((1,) + tuple(a.shape[1:]), lambda d: (d,) + (0,) * (n - 1))

    return pl.pallas_call(
        kernel,
        grid=(docs,),
        in_specs=[spec(a, w) for a, w in zip(ins, in_whole)],
        out_specs=[spec(a, False) for a in outs],
        out_shape=list(outs),
        cost_estimate=pl.CostEstimate(flops=0, bytes_accessed=0, transcendentals=0),
        compiler_params=pltpu.CompilerParams(vmem_limit_bytes=16 * 2**20),
    )(*ins)


def at_block(ref, me, j, size):
    return pl.ds(pl.multiple_of((me ^ j) * size, size), size)


BLOCK = D // 8
Z_X = (0, 1, 2)
X_Z = (0, 2, 1)


def far_block(place, q, order):
    away = sum(((q >> n) & 1) * (4 >> bit) for n, bit in enumerate(order))
    return pl.ds(pl.multiple_of((place ^ away) * BLOCK, BLOCK), BLOCK)


def relative(src, dst, place, order, rows):
    for q in range(8):
        dst[rows, q * BLOCK : (q + 1) * BLOCK] = src[:, far_block(place, q, order)]


def doc_at(j):
    return slice(j * ROWS, (j + 1) * ROWS)


def hot_rows(notes, flip=False):
    buckets = lax.broadcasted_iota(jnp.int32, (NB, ROWS), 0).astype(f32)
    if flip:
        buckets = (NB - 1) - buckets
    return [(notes[r : r + 1, :ROWS] == buckets).astype(f32).astype(bf16) for r in (12, 9, 10)]


def bias_kernel(heads, notes_ref, ext_ref, out_ref):
    notes = notes_ref[0].astype(f32)
    hots = hot_rows(notes)
    every_hot = jnp.concatenate(hots, axis=0)
    live = notes[11:12, :ROWS] > 0.5
    for h in range(heads):
        codes = []
        for k in range(3):
            row = ext_ref[k * heads + h : k * heads + h + 1, :]
            spread = jnp.broadcast_to(row, (NB, 2 * NB))
            skew = pltpu.roll(spread, NB + 1, 1, stride=1, stride_axis=0)
            codes.append(dot_tn(hots[k], skew[:, :NB].astype(bf16)).astype(bf16))
        total = dot_nn(jnp.concatenate(codes, axis=1), every_hot)
        out_ref[0, h] = jnp.where(live, total, NEGATIVE)


def softmax_rows(q, k, bias):
    s = dot_nt(q, k) * 0.125 + bias
    e = jnp.exp(s - jnp.max(s, axis=-1, keepdims=True))
    return e / jnp.sum(e, axis=-1, keepdims=True)


def attend_kernel(heads, pair, at_ref, d0, d1, near_ref, far_ref, add_ref, bias_ref, *rest):
    group_ref, qkv_ref, probs_ref, m0_ref, m1_ref = rest[-5:]
    width = heads * HD
    for j, piece, out in zip(pair, (d0, d1), (m0_ref, m1_ref)):
        relative(piece, group_ref, at_ref[1], Z_X, doc_at(j))
    both = slice(pair[0] * ROWS, (pair[1] + 1) * ROWS)
    for n in range(3):
        at = slice(n * width, (n + 1) * width)
        qkv = dot_nn(group_ref[both, : D // 2], near_ref[:, at])
        qkv = qkv + dot_nn(group_ref[both, D // 2 :], far_ref[:, at])
        qkv_ref[both, at] = (qkv + add_ref[:, at]).astype(bf16)
    for j, out in zip(pair, (m0_ref, m1_ref)):
        outs = []
        for h in range(heads):
            q = qkv_ref[doc_at(j), h * HD : (h + 1) * HD]
            k = qkv_ref[doc_at(j), width + h * HD : width + (h + 1) * HD]
            v = qkv_ref[doc_at(j), 2 * width + h * HD : 2 * width + (h + 1) * HD]
            probs = softmax_rows(q, k, bias_ref[j, h])
            probs_ref[j, h] = probs
            outs.append(dot_nn(probs.astype(bf16), v).astype(bf16))
        out[...] = jnp.concatenate(outs, axis=1)


def norm_parts(values):
    average = jnp.mean(values, axis=-1, keepdims=True)
    centred = values - average
    spread = jnp.mean(centred * centred, axis=-1, keepdims=True)
    scale = lax.rsqrt(spread + EPSILON)
    return centred * scale, scale


def norm_back(grad, gain, hat, scale):
    scaled = grad * gain
    first = jnp.mean(scaled, axis=-1, keepdims=True)
    second = jnp.mean(scaled * hat, axis=-1, keepdims=True)
    return (scaled - first - hat * second) * scale


def first_norm_kernel(
    width, at_ref, a0, a1, a2, a3, *rest
):
    near, far = rest[:4], rest[4:8]
    tokens_ref, vec_ref, att_ref, low_ref, normed_ref, hat_ref, scale_ref, branch_ref, plain_ref = rest[8:]
    me = at_ref[0]
    for j, piece in enumerate((a0[...], a1[...], a2[0], a3[...])):
        plain_ref[:, at_block(plain_ref, me, j, width)] = piece
    relative(plain_ref, att_ref, at_ref[1], Z_X, slice(None))
    left, right = att_ref[:, : D // 2], att_ref[:, D // 2 :]
    for j in range(4):
        branch_ref[:, at_block(branch_ref, me, j, width)] = dot_nn(left, near[j][...]) + dot_nn(
            right, far[j][...]
        )
    resid = tokens_ref[...].astype(f32) + branch_ref[...] + vec_ref[0:1, :]
    hat, scale = norm_parts(resid)
    normed = hat * vec_ref[1:2, :] + vec_ref[2:3, :]
    low_ref[...] = normed.astype(bf16)
    normed_ref[...] = normed
    hat_ref[...] = hat
    scale_ref[...] = scale


def parts_back(left, near_ref, far_ref, outs, place, order):
    for q in range(0, 8, 2):
        ref = near_ref if q < 4 else far_ref
        at = slice((q % 4) * BLOCK, (q % 4 + 2) * BLOCK)
        part = dot_nt(left, ref[at, :])
        for n, out in enumerate(outs):
            for half in range(2):
                block = part[doc_at(n), half * BLOCK : (half + 1) * BLOCK]
                out[:, far_block(place, q + half, order)] = block.astype(out.dtype)


def normal_parts(u):
    density = jnp.exp(-0.5 * u * u)
    return 0.5 + 0.5 * lax.erf(u * (0.5**0.5)), u * density * ((2 * jnp.pi) ** -0.5)


TILE = 256


def up_kernel(pair, at_ref, x0, x1, up_near, up_far, down_near, down_far, add_ref, *rest):
    group_ref, slope_ref, act_ref, keep_ref, give_ref = rest[-5:]
    for j, piece in zip(pair, (x0, x1)):
        relative(piece, group_ref, at_ref[1], Z_X, doc_at(j))
    both = slice(pair[0] * ROWS, (pair[1] + 1) * ROWS)
    for n in range(act_ref.shape[1] // TILE):
        at = slice(n * TILE, (n + 1) * TILE)
        pre = dot_nn(group_ref[both, : D // 2], up_near[:, at])
        pre = pre + dot_nn(group_ref[both, D // 2 :], up_far[:, at]) + add_ref[:, at]
        below, tilt = normal_parts(pre)
        slope_ref[both, at] = below + tilt
        act_ref[both, at] = (pre * below).astype(bf16)
    parts_back(act_ref[both, :], down_near, down_far, (keep_ref, give_ref), at_ref[1], X_Z)


def down_back_kernel(pair, at_ref, g0, g1, down_near, down_far, up_near, up_far, slope_ref, *rest):
    group_ref, dpre_ref, sums_ref, keep_ref, give_ref = rest[-5:]
    for j, piece in zip(pair, (g0, g1)):
        relative(piece, group_ref, at_ref[1], X_Z, doc_at(j))
    both = slice(pair[0] * ROWS, (pair[1] + 1) * ROWS)
    for n in range(dpre_ref.shape[1] // TILE):
        at = slice(n * TILE, (n + 1) * TILE)
        d_act = dot_nn(group_ref[both, : D // 2], down_near[:, at])
        d_act = d_act + dot_nn(group_ref[both, D // 2 :], down_far[:, at])
        d_pre = (d_act * slope_ref[both, at]).astype(bf16)
        dpre_ref[both, at] = d_pre
        sums_ref[pair[0] // 2 : pair[0] // 2 + 1, at] = jnp.sum(d_pre.astype(f32), axis=0, keepdims=True)
    parts_back(dpre_ref[both, :], up_near, up_far, (keep_ref, give_ref), at_ref[1], Z_X)


def second_norm_kernel(
    keep_ref, got_c, got_y, normed_ref, grad_ref, live_ref, vec_ref,
    enc_ref, dffn_ref, dres_ref, sums_ref,
):
    ffn = keep_ref[...] + got_c[...].astype(f32) + got_y[...].astype(f32) + vec_ref[0:1, :]
    hat, scale = norm_parts(normed_ref[...] + ffn)
    live = live_ref[...]
    gain = vec_ref[1:2, :]
    enc = ((hat * gain + vec_ref[2:3, :]) * live).astype(bf16)
    enc_ref[0] = enc[:SLOTS]
    grad = grad_ref[...].astype(f32) * live
    d_resid = norm_back(grad, gain, hat, scale)
    dres_ref[...] = d_resid
    low = d_resid.astype(bf16)
    dffn_ref[...] = low
    sums_ref[0:1, :] = jnp.sum(low.astype(f32), axis=0, keepdims=True)
    sums_ref[1:2, :] = jnp.sum(grad * hat, axis=0, keepdims=True)
    sums_ref[2:3, :] = jnp.sum(grad, axis=0, keepdims=True)


def first_back_kernel(width, at_ref, keep_ref, got_c, got_y, dres_ref, hat_ref, scale_ref, vec_ref, *rest):
    near, far = rest[:4], rest[4:8]
    branch_ref, done_ref, sums_ref, a0_ref, a1_ref, a2_ref, plain_ref = rest[8:]
    me = at_ref[0]
    hat = hat_ref[...]
    grad = dres_ref[...] + keep_ref[...] + got_c[...].astype(f32) + got_y[...].astype(f32)
    d_one = norm_back(grad, vec_ref[1:2, :], hat, scale_ref[...])
    done_ref[...] = d_one
    low = d_one.astype(bf16)
    branch_ref[...] = low
    sums_ref[0:1, :] = jnp.sum(low.astype(f32), axis=0, keepdims=True)
    sums_ref[1:2, :] = jnp.sum(grad * hat, axis=0, keepdims=True)
    sums_ref[2:3, :] = jnp.sum(grad, axis=0, keepdims=True)
    for n, proj in enumerate((near, far)):
        total = None
        for j in range(4):
            part = dot_nt(branch_ref[:, at_block(branch_ref, me, j, width)], proj[j][...])
            total = part if total is None else total + part
        for q in range(4):
            plain_ref[:, far_block(at_ref[1], 4 * n + q, Z_X)] = total[
                :, q * BLOCK : (q + 1) * BLOCK
            ].astype(bf16)
    for i, out in enumerate((a0_ref, a1_ref, a2_ref.at[0], a2_ref.at[1])):
        out[...] = plain_ref[:, at_block(plain_ref, me, i, width)]


def proj_grad_kernel(width, at_ref, att_ref, branch_ref, *outs):
    me = at_ref[0]
    att = att_ref[...]
    for j, out in enumerate(outs):
        out[...] = dot_tn(att, branch_ref[:, at_block(branch_ref, me, j, width)]).astype(bf16)


def attend_back_kernel(heads, pair, last, qkv_ref, probs_ref, g0, g1, notes_ref, *rest):
    dqkv_ref, sums_ref, grid_ref = rest[-4:-1] if last else rest[-3:]
    width = heads * HD
    for j, grad_ref in zip(pair, (g0, g1)):
        notes = notes_ref[j].astype(f32)
        hots = jnp.concatenate(hot_rows(notes), axis=0)
        flipped = hot_rows(notes, flip=True)
        for h in range(heads):
            q = qkv_ref[doc_at(j), h * HD : (h + 1) * HD]
            k = qkv_ref[doc_at(j), width + h * HD : width + (h + 1) * HD]
            v = qkv_ref[doc_at(j), 2 * width + h * HD : 2 * width + (h + 1) * HD]
            g = grad_ref[:, h * HD : (h + 1) * HD]
            p = probs_ref[j, h]
            dp = dot_nt(g, v)
            ds = (p * (dp - jnp.sum(p * dp, axis=-1, keepdims=True))).astype(bf16)
            dq = (dot_nn(ds, k) * 0.125).astype(bf16)
            dk = (dot_tn(ds, q) * 0.125).astype(bf16)
            dv = dot_tn(p.astype(bf16), g).astype(bf16)
            for c, d in enumerate((dq, dk, dv)):
                at = slice(c * width + h * HD, c * width + (h + 1) * HD)
                dqkv_ref[doc_at(j), at] = d
            part = dot_nt(ds, hots).astype(bf16)
            for n in range(3):
                term = dot_nn(flipped[n], part[:, n * NB : (n + 1) * NB])
                if j == 0:
                    grid_ref[n * heads + h] = term
                else:
                    grid_ref[n * heads + h] += term
        sums_ref[j : j + 1, :] = jnp.sum(dqkv_ref[doc_at(j), :].astype(f32), axis=0, keepdims=True)
    if last:
        ext_ref = rest[-1]
        for n in range(3 * heads):
            wide = jnp.concatenate([grid_ref[n], jnp.zeros((NB, NB), f32)], axis=1)
            skew = pltpu.roll(wide, 0, 1, stride=1, stride_axis=0)
            ext_ref[n : n + 1, :] = jnp.sum(skew, axis=0, keepdims=True)


def tokens_back_kernel(width, at_ref, d_ref, near_ref, far_ref, *outs):
    for q in range(0, 8, 2):
        ref = near_ref if q < 4 else far_ref
        at = slice((q % 4) * BLOCK, (q % 4 + 2) * BLOCK)
        part = dot_nt(d_ref[...], ref[at, : 3 * width])
        for n, out in enumerate(outs):
            for half in range(2):
                block = part[doc_at(n), half * BLOCK : (half + 1) * BLOCK]
                out[:, far_block(at_ref[1], q + half, Z_X)] = block.astype(out.dtype)


def pad_rows(x):
    return jnp.pad(x, ((0, ROWS - SLOTS), (0, 0)))


def local(
    tokens,
    out_grad,
    text_len,
    x_bucket,
    y_bucket,
    patch_mask,
    qkv_weight,
    qv_bias,
    proj_weight,
    proj_bias,
    first_gain,
    first_shift,
    rel_tables,
    up_weight,
    up_bias,
    down_weight,
    down_bias,
    second_gain,
    second_shift,
):
    inner = axis_bits("fsdp")
    outer = axis_bits("dp")
    tp = 4
    by_y, by_c = inner
    dpn = lax.axis_size("dp")
    n_dev = tp * dpn
    rows = D // n_dev
    heads = H // tp
    width = heads * HD
    hidden = FF // tp
    me = lax.axis_index("fsdp")
    place = lax.axis_index("dp") // (dpn // 8)
    at = jnp.stack([me, place]).astype(jnp.int32)
    run = Order()
    run.wait(at)

    def group_of(own, *earlier):
        far = swap(after(own, *earlier), by_y)
        return own, swap(own, by_c), far, swap(far, by_c)

    def trade(p0, p1, p2, far):
        return p0, swap(p1, by_c), far, swap(far[1], by_c)

    class Meet:
        def near_pair(self, keep, give):
            self.keep, self.near = keep, swap(give, by_c)
            return self

        def far_pair(self, keep, give):
            self.held, self.both = keep, swap(give, by_c)
            return self

        def send(self):
            both = run(
                lambda k, g: (k.astype(f32) + g.astype(f32)).astype(bf16), self.held, self.both
            )
            self.far = swap(both, by_y)
            return self

        def terms(self):
            return self.keep, self.near, self.far

    def blocks_of(shard, groups):
        c = shard.shape[1] // (groups * tp)
        blocks = shard.reshape(rows, groups, tp, c).transpose(2, 0, 1, 3)
        return blocks.reshape(tp, rows, groups * c)

    ex_first = Exchange(
        run,
        run(
            lambda a, b: jnp.concatenate([blocks_of(a, 3), blocks_of(b, 1)], axis=2),
            qkv_weight, proj_weight,
        ),
        inner,
    ).send()

    smalls = [
        proj_bias, first_gain, first_shift, down_bias, second_gain, second_shift,
        qv_bias, rel_tables, up_bias,
    ]
    counts = [s.shape[0] for s in smalls]
    total = sum(counts)

    def pack(*smalls):
        packed = jnp.concatenate([s[None, :] for s in smalls], axis=1)
        packed = jnp.pad(packed, ((0, 0), (0, -total % 128)))
        return jnp.broadcast_to(packed[None].astype(f32), (n_dev, 1, packed.shape[1]))

    places = jnp.arange(TEXT, dtype=jnp.int32)
    live_own = jnp.concatenate(
        [places[None, :] < text_len[:, None], patch_mask > 0], axis=1
    ).astype(f32)

    def document(tokens, x_bucket, y_bucket, live):
        pad_cols = ((0, 0), (0, D - SLOTS))
        positions = (jnp.arange(SLOTS, dtype=jnp.int32) * NB // SLOTS)[None]
        return jnp.concatenate(
            [
                tokens[0],
                jnp.pad(x_bucket.astype(bf16), pad_cols),
                jnp.pad(y_bucket.astype(bf16), pad_cols),
                jnp.pad(live.astype(bf16), pad_cols),
                jnp.pad(positions.astype(bf16), pad_cols),
                jnp.zeros((ROWS - SLOTS - 4, D), bf16),
            ],
            axis=0,
        )

    doc_rows = run(document, tokens, x_bucket, y_bucket, live_own)
    packed = run(pack, *smalls)
    ex_first.join().send()
    ex_ffn = Exchange(
        run,
        run(
            lambda a, b: jnp.concatenate([blocks_of(a, 1), blocks_of(b, 1)], axis=2),
            up_weight, down_weight,
        ),
        inner,
    ).send()
    grad_in, live_col = run(
        lambda g, l: (pad_rows(g[0]), jnp.pad(l[0], (0, ROWS - SLOTS))[:, None]), out_grad, live_own
    )
    ex_first.join()
    g_first = Gather(run, ex_first.done().reshape(tp * rows, D), "dp", Z_X).send()
    ex_ffn.join().send()
    doc_pieces = group_of(doc_rows, ex_ffn.other)
    ex_ffn.join()
    ffn_blocks = ex_ffn.done().reshape(tp * rows, 2 * hidden)
    up_own, down_own = run(lambda b: (b[:, :hidden], b[:, hidden:]), ffn_blocks)
    g_up = Gather(run, up_own, "dp", Z_X).send(g_first.other)
    g_first.join().send()
    small_all = lax.all_to_all(
        after(packed, g_first.x), ("dp", "fsdp"), split_axis=0, concat_axis=0, tiled=True
    )

    def unpack(small_all, me):
        flat = small_all[:, 0]
        vecs = flat[:, : 6 * rows].reshape(n_dev, 6, rows).transpose(1, 0, 2).reshape(6, D)
        parts, start = [], 6 * rows
        for c in counts[6:]:
            parts.append(flat[:, start : start + c].reshape(-1))
            start += c
        qv, tables, upb = parts
        q_bias = lax.dynamic_slice_in_dim(qv[:D], me * width, width)
        v_bias = lax.dynamic_slice_in_dim(qv[D:], me * width, width)
        qkv_bias = jnp.concatenate([q_bias, jnp.zeros((width,), f32), v_bias])[None]
        ext = lax.dynamic_slice_in_dim(tables.reshape(3, H, NB), me * heads, heads, 1)
        ext = ext.reshape(3 * heads, NB)
        ext = jnp.concatenate(
            [
                jnp.broadcast_to(ext[:, :1], (3 * heads, NB // 2 - 1)),
                ext,
                jnp.broadcast_to(ext[:, NB - 1 :], (3 * heads, NB // 2 + 1)),
            ],
            axis=1,
        )
        my_upb = lax.dynamic_slice_in_dim(upb, me * hidden, hidden)[None]
        return ext, qkv_bias, my_upb, vecs[:3], vecs[3:]

    notes = run(
        lambda *d: jnp.stack([x[ROWS - 16 :, : 2 * NB] for x in d]), *doc_pieces
    )
    ext, qkv_bias, my_upb, vec_one, vec_two = run(unpack, small_all, me)
    g_first.join().send()
    g_down = Gather(run, down_own, "dp", X_Z).send(g_up.other)
    g_up.join().send()

    (bias,) = run(
        lambda *ins: call_docs(
            partial(bias_kernel, heads), tp, ins, [False, True],
            [shape_of((tp, heads, ROWS, ROWS), f32)],
        ),
        notes, ext,
    )
    proj_near = group_of(run(lambda w: w[:, 3 * width :], g_first.x))
    g_down.join()
    g_up.join()
    run.wait(*proj_near)

    g_down.send(g_first.other)
    proj_far = group_of(run(lambda w: w[:, 3 * width :], g_first.other))
    g_up.send(g_down.other)
    doc_out = shape_of((ROWS, width), bf16)
    pair_out = shape_of((2, ROWS, width), bf16)
    group_out = shape_of((tp * ROWS, D), bf16)
    qkv_out = shape_of((tp * ROWS, 3 * width), bf16)
    probs_out = shape_of((tp, heads, ROWS, ROWS), f32)
    group, qkv, probs, m2, m3 = run(
        lambda *ins: call(
            partial(attend_kernel, heads, (2, 3)), ins,
            [group_out, qkv_out, probs_out, doc_out, doc_out], scalars=1,
        ),
        at, *doc_pieces[2:], g_first.x, g_first.other, qkv_bias, bias,
    )
    mixed_far = swap(jnp.stack([m2, m3]), by_y)
    group, qkv, probs, m0, m1 = run(
        lambda *ins: call(
            partial(attend_kernel, heads, (0, 1)), ins,
            [group_out, qkv_out, probs_out, doc_out, doc_out], scalars=1,
            alias={7: 0, 8: 1, 9: 2},
        ),
        at, *doc_pieces[:2], g_first.x, g_first.other, qkv_bias, bias, group, qkv, probs,
    )
    att_pieces = trade(m0, m1, None, mixed_far)

    wide_f = shape_of((ROWS, D), f32)
    wide_b = shape_of((ROWS, D), bf16)
    attended, normed_low, normed_one, hat_one, scale_one = run(
        lambda *ins: call(
            partial(first_norm_kernel, width), ins,
            [wide_b, wide_b, wide_f, wide_f, shape_of((ROWS, 1), f32)],
            [pltpu.VMEM((ROWS, D), f32), pltpu.VMEM((ROWS, D), bf16)], scalars=1,
        ),
        at, *att_pieces, *proj_near, *proj_far, doc_rows, vec_one,
    )

    normed_pieces = group_of(normed_low)
    g_down.join().send()
    hid_f = shape_of((tp * ROWS, hidden), f32)
    hid_b = shape_of((tp * ROWS, hidden), bf16)
    ffn_weights = (g_up.x, g_up.other, g_down.x, g_down.other)
    normed_group, slope, act_low, keep, give = run(
        lambda *ins: call(
            partial(up_kernel, (0, 1)), ins, [group_out, hid_f, hid_b, wide_f, wide_b], scalars=1,
        ),
        at, *normed_pieces[:2], *ffn_weights, my_upb,
    )
    meet = Meet().near_pair(keep, give)
    normed_group, slope, act_low, keep, give = run(
        lambda *ins: call(
            partial(up_kernel, (2, 3)), ins, [group_out, hid_f, hid_b, wide_f, wide_b], scalars=1,
            alias={8: 0, 9: 1, 10: 2},
        ),
        at, *normed_pieces[2:], *ffn_weights, my_upb, normed_group, slope, act_low,
    )
    meet.far_pair(keep, give).send()
    encoded, d_ffn, d_resid_two, sums_two = run(
        lambda *ins: call(
            second_norm_kernel, ins,
            [shape_of((1, SLOTS, D), bf16), wide_b, wide_f, shape_of((3, D), f32)],
        ),
        *meet.terms(), normed_one, grad_in, live_col, vec_two,
    )

    d_ffn_pieces = group_of(d_ffn)
    ffn_weights = (g_down.x, g_down.other, g_up.x, g_up.other)
    sums_out = shape_of((2, hidden), f32)
    d_ffn_group, d_pre, d_up_bias, keep, give = run(
        lambda *ins: call(
            partial(down_back_kernel, (0, 1)), ins,
            [group_out, hid_b, sums_out, wide_f, wide_b], scalars=1,
        ),
        at, *d_ffn_pieces[:2], *ffn_weights, slope,
    )
    meet = Meet().near_pair(keep, give)
    d_ffn_group, d_pre, d_up_bias, keep, give = run(
        lambda *ins: call(
            partial(down_back_kernel, (2, 3)), ins,
            [group_out, hid_b, sums_out, wide_f, wide_b], scalars=1,
            alias={8: 0, 9: 1, 10: 2},
        ),
        at, *d_ffn_pieces[2:], *ffn_weights, slope, d_ffn_group, d_pre, d_up_bias,
    )
    meet.far_pair(keep, give)

    def half_grad(left, right, near):
        left = left[:, : D // 2] if near else left[:, D // 2 :]
        return dot_tn(left, right).astype(bf16)

    give = run(partial(half_grad, near=False), d_ffn_group, act_low)
    meet.send()
    keep = run(partial(half_grad, near=True), d_ffn_group, act_low)
    s_down = Scatter(run, keep, give, "dp", X_Z).send()
    give = run(partial(half_grad, near=False), normed_group, d_pre)
    keep = run(partial(half_grad, near=True), normed_group, d_pre)
    s_up = Scatter(run, keep, give, "dp", Z_X).send()

    d_branch, d_resid_one, sums_one, a0, a1, a2 = run(
        lambda *ins: call(
            partial(first_back_kernel, width), ins,
            [wide_b, wide_f, shape_of((3, D), f32), doc_out, doc_out, pair_out],
            [pltpu.VMEM((ROWS, D), bf16)], scalars=1,
        ),
        at, *meet.terms(), d_resid_two, hat_one, scale_one, vec_one, *proj_near, *proj_far,
    )
    grad_pieces = trade(a0, a1, None, swap(a2, by_y))
    col_out = shape_of((D, width), bf16)
    parts = run(
        lambda *ins: call(partial(proj_grad_kernel, width), ins, [col_out] * 4, scalars=1),
        at, attended, d_branch,
    )
    meet_proj = Meet().near_pair(parts[0], parts[1]).far_pair(parts[2], parts[3])
    grids = shape_of((3 * heads, NB, NB), f32)
    d_qkv, d_sums, d_grid = run(
        lambda *ins: call(
            partial(attend_back_kernel, heads, (0, 1), False), ins,
            [qkv_out, shape_of((tp, 3 * width), f32), grids],
        ),
        qkv, probs, *grad_pieces[:2], notes,
    )
    meet_proj.send()
    s_down.take().send()
    s_up.take().send()
    d_qkv, d_sums, d_grid, d_ext = run(
        lambda *ins: call(
            partial(attend_back_kernel, heads, (2, 3), True), ins,
            [qkv_out, shape_of((tp, 3 * width), f32), grids, shape_of((3 * heads, 2 * NB), f32)],
            alias={5: 0, 6: 1, 7: 2},
        ),
        qkv, probs, run(lambda p: p[0], grad_pieces[2]), grad_pieces[3], notes, d_qkv, d_sums, d_grid,
    )

    def first_grad(group, d_qkv, k, c, y):
        q = dot_tn(group, d_qkv).astype(bf16)
        p = (k.astype(f32) + c.astype(f32) + y.astype(f32)).astype(bf16)
        return q[:, : D // 2], jnp.concatenate([q[:, D // 2 :], p], axis=1)

    grad_a, grad_b = run(first_grad, group, d_qkv, *meet_proj.terms())
    s_first = Scatter(run, grad_a, None, "dp", Z_X).send()
    s_second = Scatter(run, grad_b, None, "dp", Z_X, (1, 2, 0)).send()
    parts = run(
        lambda *ins: call(
            partial(tokens_back_kernel, width), ins, [wide_f, wide_b, wide_f, wide_b], scalars=1
        ),
        at, d_qkv, g_first.x, g_first.other,
    )
    meet_tok = Meet().near_pair(parts[0], parts[1]).far_pair(parts[2], parts[3]).send()
    s_down.take().send()
    s_up.take().send()

    half = NB // 2

    def spread(part, size):
        return lax.dynamic_update_slice_in_dim(jnp.zeros((size,), f32), part, me * part.shape[0], 0)

    def small_blocks(d_ext, d_sums, d_up_bias, sums_one, sums_two):
        low = jnp.sum(d_ext[:, :half], axis=1, keepdims=True)
        high = jnp.sum(d_ext[:, NB + half - 2 :], axis=1, keepdims=True)
        d_tables = jnp.concatenate([low, d_ext[:, half : NB + half - 2], high], axis=1)
        tables_wide = lax.dynamic_update_slice_in_dim(
            jnp.zeros((3, H, NB), f32), d_tables.reshape(3, heads, NB), me * heads, 1
        ).reshape(-1)
        d_sums = jnp.sum(d_sums, axis=0)
        qv_wide = jnp.concatenate([spread(d_sums[:width], D), spread(d_sums[2 * width :], D)])
        vecs = jnp.concatenate([sums_one, sums_two]).reshape(6, n_dev, rows)
        grads = [qv_wide, tables_wide, spread(jnp.sum(d_up_bias, axis=0), FF)]
        block = jnp.concatenate(
            [vecs.transpose(1, 0, 2).reshape(n_dev, 6 * rows)]
            + [g.reshape(n_dev, -1) for g in grads],
            axis=1,
        )
        return jnp.pad(block, ((0, 0), (0, -total % 128)))[:, None]

    block = run(small_blocks, d_ext, d_sums, d_up_bias, sums_one, sums_two)
    arrived = lax.all_to_all(block, ("dp", "fsdp"), split_axis=0, concat_axis=0, tiled=True)
    s_first.take().send()
    s_second.take().send()
    s_down.take()
    s_up.take()

    def low_sums(*t):
        n = len(s_up.terms)
        return jnp.concatenate(
            [sum(x.astype(f32) for x in part).astype(bf16) for part in (t[:n], t[n:])], axis=1
        )

    both = run(low_sums, *s_up.terms, *s_down.terms)
    x_ffn = Exchange(run, both.reshape(tp, rows, 2 * hidden), inner).send()
    grad_tokens = run(
        lambda d, k, c, y: (d + k + c.astype(f32) + y.astype(f32))[:SLOTS][None],
        d_resid_one, *meet_tok.terms(),
    )
    x_ffn.join().send()
    s_first.take().send()
    s_second.take().send()

    def small_outs(arrived):
        summed = jnp.sum(arrived[:, 0], axis=0)
        out, start = [], 0
        for c in counts:
            out.append(summed[start : start + c])
            start += c
        return out

    out = run(small_outs, arrived)
    x_ffn.join()

    def columns(back, groups):
        cols = back.shape[-1]
        back = back.reshape(tp, rows, groups, cols // groups).transpose(1, 2, 0, 3)
        return back.reshape(rows, tp * cols).astype(f32)

    back = x_ffn.done()
    grad_up, grad_down = run(
        lambda b: (columns(b[:, :, :hidden], 1), columns(b[:, :, hidden:], 1)), back
    )
    s_first.take()
    s_second.take()
    n = len(s_first.terms)
    mine = run(
        lambda *t: jnp.concatenate(
            [sum(x.astype(f32) for x in part).astype(bf16) for part in (t[:n], t[n:])], axis=1
        ),
        *s_first.terms, *s_second.terms,
    )
    x_first = Exchange(run, mine.reshape(tp, rows, D), inner).send().join().send().join()
    back = x_first.done()
    grad_qkv = columns(back[:, :, : 3 * width], 3)
    grad_proj = columns(back[:, :, 3 * width :], 1)
    return (
        encoded,
        grad_tokens,
        grad_qkv,
        out[6],
        grad_proj,
        out[0],
        out[1],
        out[2],
        out[7],
        grad_up,
        out[8],
        grad_down,
        out[3],
        out[4],
        out[5],
    )


def solution(mesh):
    split = ("dp", "fsdp")
    one, two, three = P(split), P(split, None), P(split, None, None)
    return jax.shard_map(
        local,
        mesh=mesh,
        in_specs=(
            three, three, one, two, two, two, two, one, two, one, one, one, one, two, one, two,
            one, one, one,
        ),
        out_specs=(
            three, three, two, one, two, one, one, one, one, two, one, two, one, one, one,
        ),
        check_vma=False,
    )
```

```python
from functools import partial

import jax
import jax.numpy as jnp
from jax import lax
from jax.experimental import pallas as pl
from jax.experimental.pallas import tpu as pltpu
from jax.sharding import PartitionSpec as P

D = 1024
H = 16
HD = 64
FF = 4096
NB = 128
TEXT = 120
SLOTS = 169
ROWS = 176
NEGATIVE = -1e30
EPSILON = 1e-05

f32 = jnp.float32
bf16 = jnp.bfloat16


def shape_of(shape, kind):
    return jax.ShapeDtypeStruct(tuple(shape), kind)


def call(kernel, ins, outs, scratch=(), scalars=0, alias=None, vmem=16):
    spaces = [pltpu.SMEM] * scalars + [pltpu.VMEM] * (len(ins) - scalars)
    return pl.pallas_call(
        kernel,
        in_specs=[pl.BlockSpec(memory_space=m) for m in spaces],
        out_specs=[pl.BlockSpec(memory_space=pltpu.VMEM) for _ in outs],
        out_shape=list(outs),
        scratch_shapes=list(scratch),
        input_output_aliases=alias or {},
        cost_estimate=pl.CostEstimate(flops=0, bytes_accessed=0, transcendentals=0),
        compiler_params=pltpu.CompilerParams(vmem_limit_bytes=vmem * 2**20),
    )(*ins)


def glue(fn, outs, *ins, scalars=0):
    def kernel(*refs):
        made = fn(*refs[: len(ins)])
        for out, value in zip(refs[len(ins) :], made if isinstance(made, tuple) else (made,)):
            out[...] = value

    made = call(kernel, ins, outs, scalars=scalars)
    return made[0] if len(outs) == 1 else made


def axis_bits(axis):
    bits, b = [], lax.axis_size(axis) // 2
    while b >= 1:
        bits.append((axis, b))
        b //= 2
    return bits


def swap(x, bit):
    axis, b = bit
    return lax.ppermute(x, axis, [(i, i ^ b) for i in range(lax.axis_size(axis))])


def side(bit):
    axis, b = bit
    return (lax.axis_index(axis) // b) % 2


def pair_up(mine, other, bit, pos):
    one = side(bit) == 1
    return jnp.stack([jnp.where(one, other, mine), jnp.where(one, mine, other)], axis=pos)


class Order:
    def __init__(self):
        self.last = ()

    def tie(self, args):
        if not self.last:
            return args
        return lax.optimization_barrier(tuple(args) + self.last)[: len(args)]

    def wait(self, *arrays):
        self.last = self.last + arrays

    def __call__(self, fn, *args):
        out = fn(*self.tie(args))
        self.last = tuple(jax.tree.leaves(out))
        return out


def after(x, *earlier):
    return lax.optimization_barrier((x,) + earlier)[0]


def high_bits(axis, order):
    bits = axis_bits(axis)
    return [bits[i] for i in order]


class Gather:
    def __init__(self, run, x, axis, order):
        self.run, self.x = run, x
        self.bits = axis_bits(axis)[3:][::-1] + high_bits(axis, order)
        while len(self.bits) > 3:
            self.send().join()

    def send(self, *earlier):
        self.other = swap(after(self.x, *earlier), self.bits[0])
        return self

    def join(self):
        bit = self.bits.pop(0)
        if len(self.bits) >= 3:
            self.x = self.run(
                lambda m, o: pair_up(m, o, bit, 0).reshape(-1, m.shape[1]), self.x, self.other
            )
        else:
            r, c = self.x.shape

            def join(m, o, out):
                out[:r], out[r:] = m[...], o[...]

            (self.x,) = self.run(
                lambda *ins: call(join, ins, [shape_of((2 * r, c), bf16)]), self.x, self.other
            )
        return self


class Scatter:
    def __init__(self, run, arrays, axis, order, walk=None, base=None, given=None):
        self.run = run
        self.high, rest = high_bits(axis, order), axis_bits(axis)[3:]
        have = self.high[::-1] + rest
        self.order = (high_bits(axis, walk) if walk else self.high[::-1]) + rest
        self.low = len(rest)
        if given is not None:
            have = [bit for bit in have if bit != self.order[0]]
            given = given.reshape((2,) * len(have) + (-1, given.shape[-1]))
        self.given = given
        arrays = tuple(a.reshape((2,) * len(have) + (-1, a.shape[-1])) for a in arrays)
        self.terms = [(arrays, have, [], base or (lambda x: x.astype(f32)))]

    def own(self, array):
        arrays, *rest = self.terms[0]
        self.terms[0] = ((array.reshape(arrays[0].shape),), *rest)

    def flat(self):
        return [a for arrays, *unused in self.terms for a in arrays]

    def value(self, flat, extra=()):
        flat, total = list(flat), None
        for arrays, have, cuts, base in self.terms:
            chosen = dict(list(cuts) + list(extra))
            at = tuple(
                slice(None) if bit not in chosen
                else (0 if chosen[bit] else 1) if bit in self.high
                else side(bit) if chosen[bit] else 1 - side(bit)
                for bit in have
            )
            part = base(*[flat.pop(0)[at] for unused in arrays])
            total = part if total is None else total + part
        return total

    def sum(self, extra=()):
        flat = self.flat()
        fn = lambda *f: self.value(f, extra).astype(bf16)
        if self.low:
            return self.run(fn, *flat)
        out = jax.eval_shape(fn, *flat)
        return self.run(lambda *f: glue(fn, [out], *f), *flat)

    def send(self, *earlier):
        bit = self.order[0]
        out = self.given if self.given is not None else self.sum([(bit, False)])
        self.other = swap(after(out, *earlier), bit)
        return self

    def take(self):
        bit = self.order.pop(0)
        for arrays, have, cuts, base in self.terms:
            if self.given is None:
                cuts.append((bit, True))
        self.given = None
        self.terms.append(((self.other,), list(self.order_left()), [], lambda x: x.astype(f32)))
        while 0 < len(self.order) <= self.low:
            self.send().take()
        return self

    def order_left(self):
        arrays, have, cuts, base = self.terms[0]
        gone = [bit for bit, keep in cuts]
        return [bit for bit in have if bit not in gone]


class Exchange:
    def __init__(self, run, at, give, keep):
        self.run, self.at, self.keep = run, at, keep
        self.other = swap(give, axis_bits("fsdp")[1])

    def turn(self, *earlier):
        def fn(at, keep, got, give, mine):
            y, c = at[0] // 2, at[0] % 2
            give[c], give[1 - c] = keep[1 - y], got[1 - y]
            mine[c], mine[1 - c] = keep[y], got[y]

        out = shape_of(self.keep.shape, self.keep.dtype)
        give, self.mine = self.run(
            lambda *ins: call(fn, ins, [out, out], scalars=1), self.at, self.keep, self.other
        )
        self.other = swap(after(give, *earlier), axis_bits("fsdp")[0])
        return self


def source_of(at, near, n):
    y = at[0] // 2
    return (y if near else 1 - y) * 2 + n


def dot_nn(a, b):
    return jnp.dot(a, b, preferred_element_type=f32)


def dot_nt(a, b):
    return lax.dot_general(a, b, (((1,), (1,)), ((), ())), preferred_element_type=f32)


def dot_tn(a, b):
    return lax.dot_general(a, b, (((0,), (0,)), ((), ())), preferred_element_type=f32)


def call_docs(kernel, docs, ins, in_whole, outs):
    def spec(a, whole):
        n = len(a.shape)
        if whole:
            return pl.BlockSpec(tuple(a.shape), lambda d: (0,) * n)
        return pl.BlockSpec((1,) + tuple(a.shape[1:]), lambda d: (d,) + (0,) * (n - 1))

    return pl.pallas_call(
        kernel,
        grid=(docs,),
        in_specs=[spec(a, w) for a, w in zip(ins, in_whole)],
        out_specs=[spec(a, False) for a in outs],
        out_shape=list(outs),
        cost_estimate=pl.CostEstimate(flops=0, bytes_accessed=0, transcendentals=0),
        compiler_params=pltpu.CompilerParams(vmem_limit_bytes=16 * 2**20),
    )(*ins)


def at_block(ref, me, j, size):
    return pl.ds(pl.multiple_of((me ^ j) * size, size), size)


BLOCK = D // 8
Z_X = (0, 1, 2)
X_Z = (0, 2, 1)
X_FIRST = (2, 1, 0)


def far_block(place, q, order):
    away = sum(((q >> n) & 1) * (4 >> bit) for n, bit in enumerate(order))
    return pl.ds(pl.multiple_of((place ^ away) * BLOCK, BLOCK), BLOCK)


def relative(src, dst, place, order, rows):
    for q in range(8):
        dst[rows, q * BLOCK : (q + 1) * BLOCK] = src[:, far_block(place, q, order)]


def doc_at(j):
    return slice(j * ROWS, (j + 1) * ROWS)


def hot_rows(notes, flip=False):
    buckets = lax.broadcasted_iota(jnp.int32, (NB, ROWS), 0).astype(f32)
    if flip:
        buckets = (NB - 1) - buckets
    return [(notes[r : r + 1, :ROWS] == buckets).astype(f32).astype(bf16) for r in (12, 9, 10)]


ROW_QV, ROW_TABLES, ROW_UP = 6, 7, 9
TILE_ROWS = 16


def pack_kernel(*refs):
    *smalls, out_ref = refs
    rows = smalls[0].shape[1]
    tile = jnp.zeros(out_ref.shape, f32)
    row = lax.broadcasted_iota(jnp.int32, out_ref.shape, 0)
    qv, tables, up = smalls[6:]
    parts = list(smalls[:6]) + [qv] + [tables.at[:, 3 * n * rows : 3 * (n + 1) * rows] for n in range(2)]
    for n, ref in enumerate(parts + [up]):
        value = ref[...].astype(f32)
        wide = jnp.concatenate(
            [value, jnp.zeros((1, 128 - value.shape[1]), f32)], axis=1
        ) if value.shape[1] < 128 else value
        tile = jnp.where(row == n, jnp.broadcast_to(wide, out_ref.shape), tile)
    out_ref[...] = tile.astype(bf16)


def unpack_kernel(heads, count, at_ref, all_ref, ext_ref, add_ref, up_ref, one_ref, two_ref, qv_ref, tab_ref, upb_ref):
    me, place = at_ref[0], at_ref[1]
    rows, width, low = D // count, heads * HD, count // 32
    for d in range(count):
        q = place ^ (d // (4 * low))
        block = (q * low + (d // 4) % low) * 4 + (me ^ (d % 4))
        place_of = pl.ds(pl.multiple_of(block * TILE_ROWS, TILE_ROWS), TILE_ROWS)
        tile = all_ref[place_of, :].astype(f32)
        at = slice(d * rows, (d + 1) * rows)
        one_ref[:, at] = tile[0:3, :rows]
        two_ref[:, at] = tile[3:6, :rows]
        qv_ref[:, 2 * d * rows : 2 * (d + 1) * rows] = tile[ROW_QV : ROW_QV + 1, : 2 * rows]
        for n in range(2):
            start = (2 * d + n) * 3 * rows
            row = tile[ROW_TABLES + n : ROW_TABLES + n + 1, : 3 * rows]
            tab_ref[:, start : start + 3 * rows] = row
        upb_ref[:, 4 * d * rows : 4 * (d + 1) * rows] = tile[ROW_UP : ROW_UP + 1, : 4 * rows]
    start = pl.multiple_of(me * width, width)
    add_ref[:, :width] = qv_ref[:, pl.ds(start, width)]
    add_ref[:, width : 2 * width] = jnp.zeros((1, width), f32)
    add_ref[:, 2 * width :] = qv_ref[:, pl.ds(D + start, width)]
    hidden = up_ref.shape[1]
    up_ref[...] = upb_ref[:, pl.ds(pl.multiple_of(me * hidden, hidden), hidden)]
    half = NB // 2
    for k in range(3):
        for h in range(heads):
            n = k * heads + h
            row = tab_ref[:, pl.ds(pl.multiple_of((k * H + me * heads + h) * NB, NB), NB)]
            ext_ref[n : n + 1, :half] = jnp.broadcast_to(row[:, :1], (1, half))
            ext_ref[n : n + 1, half : half + NB] = row
            ext_ref[n : n + 1, half + NB :] = jnp.broadcast_to(row[:, NB - 1 :], (1, half))


PIECES = 18


def small_grads_kernel(
    heads, count, at_ref, ext_ref, sums_ref, up_ref, one_ref, two_ref, out_ref,
    qv_ref, tab_ref, upb_ref, plain_ref, order_ref,
):
    me = at_ref[0]
    rows, width = D // count, heads * HD
    for ref in (qv_ref, tab_ref, upb_ref, plain_ref):
        ref[...] = jnp.zeros_like(ref)
    start = pl.multiple_of(me * width, width)
    sums = jnp.sum(sums_ref[...], axis=0, keepdims=True)
    qv_ref[:, pl.ds(start, width)] = sums[:, :width]
    qv_ref[:, pl.ds(D + start, width)] = sums[:, 2 * width :]
    hidden = up_ref.shape[1]
    upb_ref[:, pl.ds(pl.multiple_of(me * hidden, hidden), hidden)] = jnp.sum(
        up_ref[...], axis=0, keepdims=True
    )
    half = NB // 2
    lane = lax.broadcasted_iota(jnp.int32, (1, NB), 1)
    for k in range(3):
        for h in range(heads):
            row = ext_ref[k * heads + h : k * heads + h + 1, :]
            low = jnp.sum(row[:, :half], axis=1, keepdims=True)
            high = jnp.sum(row[:, half + NB :], axis=1, keepdims=True)
            grad = row[:, half : half + NB] + jnp.where(lane == 0, low, 0.0)
            grad = grad + jnp.where(lane == NB - 1, high, 0.0)
            tab_ref[:, pl.ds(pl.multiple_of((k * H + me * heads + h) * NB, NB), NB)] = grad
    plain_ref[0:3, :] = one_ref[...]
    plain_ref[3:6, :] = two_ref[...]
    for d in range(count):
        at = slice(d * rows, (d + 1) * rows)
        row = 6
        for ref, times in ((qv_ref, 2), (tab_ref, 6), (upb_ref, 4)):
            for n in range(times):
                begin = (d * times + n) * rows
                plain_ref[row : row + 1, at] = ref[:, begin : begin + rows]
                row += 1
    relative(plain_ref, order_ref, at_ref[1], Z_X, slice(None))
    shape = (plain_ref.shape[0], 128)
    same = lax.broadcasted_iota(jnp.int32, shape, 0) == lax.broadcasted_iota(jnp.int32, shape, 1)
    out_ref[...] = dot_tn(order_ref[...].astype(bf16), same.astype(f32).astype(bf16)).astype(bf16)


def small_outs(total, outs):
    rows = total.shape[0]
    shape = (rows, rows)
    same = lax.broadcasted_iota(jnp.int32, shape, 0) == lax.broadcasted_iota(jnp.int32, shape, 1)
    turned = lax.dot_general(
        total, same.astype(f32), (((0,), (0,)), ((), ())),
        precision=lax.Precision.HIGHEST, preferred_element_type=f32,
    )
    row = 0
    for out in outs:
        for n in range(out.shape[1] // rows):
            out[:, n * rows : (n + 1) * rows] = turned[row : row + 1, :]
            row += 1


def bias_kernel(heads, notes_ref, ext_ref, out_ref):
    notes = notes_ref[0].astype(f32)
    hots = hot_rows(notes)
    every_hot = jnp.concatenate(hots, axis=0)
    live = notes[11:12, :ROWS] > 0.5
    for h in range(heads):
        codes = []
        for k in range(3):
            row = ext_ref[k * heads + h : k * heads + h + 1, :]
            spread = jnp.broadcast_to(row, (NB, 2 * NB))
            skew = pltpu.roll(spread, NB, 1, stride=1, stride_axis=0)
            codes.append(dot_tn(hots[k], skew[:, :NB].astype(bf16)).astype(bf16))
        total = dot_nn(jnp.concatenate(codes, axis=1), every_hot)
        out_ref[0, h] = jnp.where(live, total, NEGATIVE)


def softmax_rows(q, k, bias):
    s = dot_nt(q, k) * 0.125 + bias
    e = jnp.exp(s - jnp.max(s, axis=-1, keepdims=True))
    return e / jnp.sum(e, axis=-1, keepdims=True)


def attend_kernel(heads, pair, at_ref, d0, d1, near_ref, far_ref, add_ref, bias_ref, *rest):
    group_ref, qkv_ref, probs_ref, mixed_ref = rest[-4:]
    width = heads * HD
    for j, piece in zip(pair, (d0, d1)):
        relative(piece, group_ref, at_ref[1], Z_X, doc_at(j))
    both = slice(pair[0] * ROWS, (pair[1] + 1) * ROWS)
    for n in range(3):
        at = slice(n * width, (n + 1) * width)
        qkv = dot_nn(group_ref[both, : D // 2], near_ref[:, at])
        qkv = qkv + dot_nn(group_ref[both, D // 2 :], far_ref[:, at])
        qkv_ref[both, at] = (qkv + add_ref[:, at]).astype(bf16)
    for n, j in enumerate(pair):
        outs = []
        for h in range(heads):
            q = qkv_ref[doc_at(j), h * HD : (h + 1) * HD]
            k = qkv_ref[doc_at(j), width + h * HD : width + (h + 1) * HD]
            v = qkv_ref[doc_at(j), 2 * width + h * HD : 2 * width + (h + 1) * HD]
            probs = softmax_rows(q, k, bias_ref[j, h])
            probs_ref[j, h] = probs
            outs.append(dot_nn(probs.astype(bf16), v).astype(bf16))
        mixed_ref[n] = jnp.concatenate(outs, axis=1)


def norm_parts(values):
    average = jnp.mean(values, axis=-1, keepdims=True)
    centred = values - average
    spread = jnp.mean(centred * centred, axis=-1, keepdims=True)
    scale = lax.rsqrt(spread + EPSILON)
    return centred * scale, scale


def norm_back(grad, gain, hat, scale):
    scaled = grad * gain
    first = jnp.mean(scaled, axis=-1, keepdims=True)
    second = jnp.mean(scaled * hat, axis=-1, keepdims=True)
    return (scaled - first - hat * second) * scale


def first_norm_kernel(
    width, at_ref, a0, a1, a2, a3, *rest
):
    near, far = rest[:4], rest[4:8]
    tokens_ref, vec_ref, att_ref, low_ref, normed_ref, hat_ref, scale_ref, branch_ref, plain_ref = rest[8:]
    me = at_ref[0]
    for j, piece in enumerate((a0[0], a1[...], a2[0], a3[...])):
        plain_ref[:, at_block(plain_ref, me, j, width)] = piece
    relative(plain_ref, att_ref, at_ref[1], Z_X, slice(None))
    left, right = att_ref[:, : D // 2], att_ref[:, D // 2 :]
    for j in range(4):
        branch_ref[:, at_block(branch_ref, me, j, width)] = dot_nn(left, near[j][...]) + dot_nn(
            right, far[j][...]
        )
    resid = tokens_ref[...].astype(f32) + branch_ref[...] + vec_ref[0:1, :]
    hat, scale = norm_parts(resid)
    normed = hat * vec_ref[1:2, :] + vec_ref[2:3, :]
    low_ref[...] = normed.astype(bf16)
    normed_ref[...] = normed
    hat_ref[...] = hat
    scale_ref[...] = scale


def parts_back(left, near_ref, far_ref, outs, place, order):
    for q in range(0, 8, 2):
        ref = near_ref if q < 4 else far_ref
        at = slice((q % 4) * BLOCK, (q % 4 + 2) * BLOCK)
        part = dot_nt(left, ref[at, :])
        for n, out in enumerate(outs):
            for half in range(2):
                block = part[doc_at(n), half * BLOCK : (half + 1) * BLOCK]
                out[:, far_block(place, q + half, order)] = block.astype(out.dtype)


def normal_parts(u):
    density = jnp.exp(-0.5 * u * u)
    return 0.5 + 0.5 * lax.erf(u * (0.5**0.5)), u * density * ((2 * jnp.pi) ** -0.5)


TILE = 256


def up_kernel(pair, at_ref, x0, x1, up_near, up_far, down_near, down_far, add_ref, *rest):
    group_ref, slope_ref, act_ref, keep_ref, give_ref = rest[-5:]
    for j, piece in zip(pair, (x0, x1)):
        relative(piece, group_ref, at_ref[1], Z_X, doc_at(j))
    both = slice(pair[0] * ROWS, (pair[1] + 1) * ROWS)
    for n in range(act_ref.shape[1] // TILE):
        at = slice(n * TILE, (n + 1) * TILE)
        pre = dot_nn(group_ref[both, : D // 2], up_near[:, at])
        pre = pre + dot_nn(group_ref[both, D // 2 :], up_far[:, at]) + add_ref[:, at]
        below, tilt = normal_parts(pre)
        slope_ref[both, at] = below + tilt
        act_ref[both, at] = (pre * below).astype(bf16)
    parts_back(act_ref[both, :], down_near, down_far, (keep_ref, give_ref), at_ref[1], X_Z)


def down_back_kernel(pair, at_ref, g0, g1, down_near, down_far, up_near, up_far, slope_ref, *rest):
    group_ref, dpre_ref, sums_ref, keep_ref, give_ref = rest[-5:]
    for j, piece in zip(pair, (g0, g1)):
        relative(piece, group_ref, at_ref[1], X_Z, doc_at(j))
    both = slice(pair[0] * ROWS, (pair[1] + 1) * ROWS)
    for n in range(dpre_ref.shape[1] // TILE):
        at = slice(n * TILE, (n + 1) * TILE)
        d_act = dot_nn(group_ref[both, : D // 2], down_near[:, at])
        d_act = d_act + dot_nn(group_ref[both, D // 2 :], down_far[:, at])
        d_pre = (d_act * slope_ref[both, at]).astype(bf16)
        dpre_ref[both, at] = d_pre
        sums_ref[pair[0] // 2 : pair[0] // 2 + 1, at] = jnp.sum(d_pre.astype(f32), axis=0, keepdims=True)
    parts_back(dpre_ref[both, :], up_near, up_far, (keep_ref, give_ref), at_ref[1], Z_X)


def second_norm_kernel(
    keep_ref, got_c, got_y, normed_ref, grad_ref, live_ref, vec_ref,
    enc_ref, dffn_ref, dres_ref, sums_ref,
):
    ffn = keep_ref[...] + got_c[...].astype(f32) + got_y[...].astype(f32) + vec_ref[0:1, :]
    hat, scale = norm_parts(normed_ref[...] + ffn)
    ones = jnp.ones((8, 128), bf16)
    live = dot_tn(live_ref[...].astype(bf16), ones)[:, :1]
    gain = vec_ref[1:2, :]
    enc = ((hat * gain + vec_ref[2:3, :]) * live).astype(bf16)
    enc_ref[0] = enc[:SLOTS]
    grad = grad_ref[...].astype(f32) * live
    d_resid = norm_back(grad, gain, hat, scale)
    dres_ref[...] = d_resid
    low = d_resid.astype(bf16)
    dffn_ref[...] = low
    sums_ref[0:1, :] = jnp.sum(low.astype(f32), axis=0, keepdims=True)
    sums_ref[1:2, :] = jnp.sum(grad * hat, axis=0, keepdims=True)
    sums_ref[2:3, :] = jnp.sum(grad, axis=0, keepdims=True)


def first_back_kernel(width, at_ref, keep_ref, got_c, got_y, dres_ref, hat_ref, scale_ref, vec_ref, *rest):
    near, far = rest[:4], rest[4:8]
    branch_ref, done_ref, sums_ref, a0_ref, a1_ref, a2_ref, plain_ref = rest[8:]
    me = at_ref[0]
    hat = hat_ref[...]
    grad = dres_ref[...] + keep_ref[...] + got_c[...].astype(f32) + got_y[...].astype(f32)
    d_one = norm_back(grad, vec_ref[1:2, :], hat, scale_ref[...])
    done_ref[...] = d_one
    low = d_one.astype(bf16)
    branch_ref[...] = low
    sums_ref[0:1, :] = jnp.sum(low.astype(f32), axis=0, keepdims=True)
    sums_ref[1:2, :] = jnp.sum(grad * hat, axis=0, keepdims=True)
    sums_ref[2:3, :] = jnp.sum(grad, axis=0, keepdims=True)
    for n, proj in enumerate((near, far)):
        total = None
        for j in range(4):
            part = dot_nt(branch_ref[:, at_block(branch_ref, me, j, width)], proj[j][...])
            total = part if total is None else total + part
        for q in range(4):
            plain_ref[:, far_block(at_ref[1], 4 * n + q, Z_X)] = total[
                :, q * BLOCK : (q + 1) * BLOCK
            ].astype(bf16)
    for i, out in enumerate((a0_ref, a1_ref, a2_ref.at[0], a2_ref.at[1])):
        out[...] = plain_ref[:, at_block(plain_ref, me, i, width)]


def proj_grad_kernel(width, at_ref, att_ref, branch_ref, *outs):
    me = at_ref[0]
    att = att_ref[...]
    for j, out in enumerate(outs):
        out[...] = dot_tn(att, branch_ref[:, at_block(branch_ref, me, j, width)]).astype(bf16)


def attend_back_kernel(heads, pair, last, qkv_ref, probs_ref, g0, g1, notes_ref, *rest):
    dqkv_ref, sums_ref, grid_ref = rest[-4:-1] if last else rest[-3:]
    width = heads * HD
    for j, grad_ref in zip(pair, (g0.at[0] if last else g0, g1)):
        notes = notes_ref[j].astype(f32)
        hots = jnp.concatenate(hot_rows(notes), axis=0)
        flipped = hot_rows(notes, flip=True)
        for h in range(heads):
            q = qkv_ref[doc_at(j), h * HD : (h + 1) * HD]
            k = qkv_ref[doc_at(j), width + h * HD : width + (h + 1) * HD]
            v = qkv_ref[doc_at(j), 2 * width + h * HD : 2 * width + (h + 1) * HD]
            g = grad_ref[:, h * HD : (h + 1) * HD]
            p = probs_ref[j, h]
            dp = dot_nt(g, v)
            ds = (p * (dp - jnp.sum(p * dp, axis=-1, keepdims=True))).astype(bf16)
            dq = (dot_nn(ds, k) * 0.125).astype(bf16)
            dk = (dot_tn(ds, q) * 0.125).astype(bf16)
            dv = dot_tn(p.astype(bf16), g).astype(bf16)
            for c, d in enumerate((dq, dk, dv)):
                at = slice(c * width + h * HD, c * width + (h + 1) * HD)
                dqkv_ref[doc_at(j), at] = d
            part = dot_nt(ds, hots).astype(bf16)
            for n in range(3):
                term = dot_nn(flipped[n], part[:, n * NB : (n + 1) * NB])
                if j == 0:
                    grid_ref[n * heads + h] = term
                else:
                    grid_ref[n * heads + h] += term
        sums_ref[j : j + 1, :] = jnp.sum(dqkv_ref[doc_at(j), :].astype(f32), axis=0, keepdims=True)
    if last:
        ext_ref = rest[-1]
        for n in range(3 * heads):
            wide = jnp.concatenate([grid_ref[n], jnp.zeros((NB, NB), f32)], axis=1)
            skew = pltpu.roll(wide, 1, 1, stride=1, stride_axis=0)
            ext_ref[n : n + 1, :] = jnp.sum(skew, axis=0, keepdims=True)


def tokens_back_kernel(width, at_ref, d_ref, near_ref, far_ref, *outs):
    for q in range(0, 8, 2):
        ref = near_ref if q < 4 else far_ref
        at = slice((q % 4) * BLOCK, (q % 4 + 2) * BLOCK)
        part = dot_nt(d_ref[...], ref[at, : 3 * width])
        for n, out in enumerate(outs):
            for half in range(2):
                block = part[doc_at(n), half * BLOCK : (half + 1) * BLOCK]
                out[:, far_block(at_ref[1], q + half, Z_X)] = block.astype(out.dtype)


def pad_rows(x):
    return jnp.pad(x, ((0, ROWS - SLOTS), (0, 0)))


def local(
    tokens,
    out_grad,
    text_len,
    x_bucket,
    y_bucket,
    patch_mask,
    qkv_weight,
    qv_bias,
    proj_weight,
    proj_bias,
    first_gain,
    first_shift,
    rel_tables,
    up_weight,
    up_bias,
    down_weight,
    down_bias,
    second_gain,
    second_shift,
):
    inner = axis_bits("fsdp")
    outer = axis_bits("dp")
    tp = 4
    by_y, by_c = inner
    dpn = lax.axis_size("dp")
    n_dev = tp * dpn
    rows = D // n_dev
    heads = H // tp
    width = heads * HD
    hidden = FF // tp
    me = lax.axis_index("fsdp")
    place = lax.axis_index("dp") // (dpn // 8)
    at = jnp.stack([me, place]).astype(jnp.int32)
    run = Order()
    run.wait(at)
    doc_out = shape_of((ROWS, width), bf16)

    def group_of(own):
        far = swap(own, by_y)
        return own, swap(own, by_c), far, swap(far, by_c)

    def second(pair):
        return run(lambda p: glue(lambda ref: ref[1], [doc_out], p), pair)

    def trade(p1, far):
        return swap(p1, by_c), far, swap(second(far), by_c)

    class Meet:
        def near_pair(self, keep, give):
            self.keep, self.near = keep, swap(give, by_c)
            return self

        def far_pair(self, keep, give):
            self.held, self.both = keep, swap(give, by_c)
            return self

        def send(self):
            out = shape_of(self.held.shape, bf16)
            fn = lambda k, g: (k[...].astype(f32) + g[...].astype(f32)).astype(bf16)
            both = run(lambda *ins: glue(fn, [out], *ins), self.held, self.both)
            self.far = swap(both, by_y)
            return self

        def terms(self):
            return self.keep, self.near, self.far

    def column_blocks(shards, groups):
        widths = [a.shape[1] // (g * tp) for a, g in zip(shards, groups)]
        out = shape_of((2, rows, sum(w * g for w, g in zip(widths, groups))), bf16)

        def fn(at, *refs):
            for target, c in ((refs[-2], 1 - at[0] % 2), (refs[-1], at[0] % 2)):
                for y in range(2):
                    start = 0
                    for ref, w, g in zip(refs, widths, groups):
                        for n in range(g):
                            place = pl.multiple_of((n * tp + 2 * y + c) * w, w)
                            target[y, :, start : start + w] = ref[:, pl.ds(place, w)]
                            start += w

        return Exchange(
            run, at,
            *run(lambda *ins: call(fn, ins, [out, out], scalars=1), at, *shards),
        )

    def block_rows(exchanged, parts):
        cols = exchanged.mine.shape[2] // parts

        def fn(at, mine, other, *outs):
            for near, ref in ((True, mine), (False, other)):
                for n in range(2):
                    for p, out in enumerate(outs):
                        out[source_of(at, near, n)] = ref[n, :, p * cols : (p + 1) * cols]

        outs = run(
            lambda *ins: call(fn, ins, [shape_of((tp, rows, cols), bf16)] * parts, scalars=1),
            at, exchanged.mine, exchanged.other,
        )
        return [o.reshape(tp * rows, cols) for o in outs]

    ex_first = column_blocks((qkv_weight, proj_weight), (3, 1))

    smalls = [
        proj_bias, first_gain, first_shift, down_bias, second_gain, second_shift,
        qv_bias, rel_tables, up_bias,
    ]
    flats = [pltpu.VMEM((1, n), f32) for n in (2 * D, 3 * H * NB, FF)]

    places = jnp.arange(TEXT, dtype=jnp.int32)
    live_own = jnp.concatenate(
        [places[None, :] < text_len[:, None], patch_mask > 0], axis=1
    ).astype(f32)

    def document(tokens, x_bucket, y_bucket, live):
        pad_cols = ((0, 0), (0, D - SLOTS))
        positions = (jnp.arange(SLOTS, dtype=jnp.int32) * NB // SLOTS)[None]
        return jnp.concatenate(
            [
                tokens[0],
                jnp.pad(x_bucket.astype(bf16), pad_cols),
                jnp.pad(y_bucket.astype(bf16), pad_cols),
                jnp.pad(live.astype(bf16), pad_cols),
                jnp.pad(positions.astype(bf16), pad_cols),
                jnp.zeros((ROWS - SLOTS - 4, D), bf16),
            ],
            axis=0,
        )

    ex_ffn = column_blocks((up_weight, down_weight), (1, 1))
    ex_first.turn()
    ex_ffn.turn(ex_first.other)
    doc_rows = run(document, tokens, x_bucket, y_bucket, live_own)
    (packed,) = run(
        lambda *ins: call(pack_kernel, [x[None] for x in ins], [shape_of((TILE_ROWS, 128), bf16)]),
        *smalls,
    )

    def beside(m, o):
        r = m.shape[0]

        def join(m, o, out):
            out[:r], out[r:] = m[...], o[...]

        return run(lambda *ins: call(join, ins, [shape_of((2 * r, 128), bf16)]), m, o)[0]

    small_near = swap(packed, by_c)
    grad_in, live_row = run(
        lambda g, l: (pad_rows(g[0]), jnp.pad(l, ((0, 7), (0, ROWS - SLOTS)))), out_grad, live_own
    )
    pair = beside(packed, small_near)
    small_far = swap(pair, by_y)
    g_first = Gather(run, *block_rows(ex_first, 1), "dp", Z_X).send()
    g_small = Gather(run, beside(pair, small_far), "dp", X_FIRST).send()
    doc_far = swap(after(doc_rows, ex_ffn.other, small_far), by_y)
    doc_near = swap(doc_rows, by_c)
    up_own, down_own = block_rows(ex_ffn, 2)
    g_small.join().send()
    g_small.join().send()
    g_down = Gather(run, down_own, "dp", X_Z)
    g_first.join().send()
    g_down.send(g_first.x)
    doc_pieces = (doc_rows, doc_near, doc_far, swap(after(doc_far, g_first.x), by_c))

    def take_notes(*refs):
        for n in range(4):
            refs[4][n] = refs[n][ROWS - 16 :, : 2 * NB]

    (notes,) = run(
        lambda *ins: call(take_notes, ins, [shape_of((tp, 16, 2 * NB), bf16)]), *doc_pieces
    )
    run.wait(g_small.other)
    g_down.join()
    g_first.join().send()
    g_down.send()
    g_up = Gather(run, up_own, "dp", Z_X).send(g_down.x)
    ext, qkv_bias, my_upb, vec_one, vec_two = run(
        lambda *ins: call(
            partial(unpack_kernel, heads, n_dev), ins,
            [
                shape_of((3 * heads, 2 * NB), f32), shape_of((1, 3 * width), f32),
                shape_of((1, hidden), f32), shape_of((3, D), f32), shape_of((3, D), f32),
            ],
            flats, scalars=1,
        ),
        at, beside(g_small.x, g_small.other),
    )

    (bias,) = run(
        lambda *ins: call_docs(
            partial(bias_kernel, heads), tp, ins, [False, True],
            [shape_of((tp, heads, ROWS, ROWS), f32)],
        ),
        notes, ext,
    )
    g_up.join().send()
    col_out = shape_of((D, width), bf16)
    half_out = shape_of((D // 2, width), bf16)

    def proj_part(rows_of):
        return group_of(
            run(lambda w: glue(lambda ref: ref[:, 3 * width :], [half_out], w), rows_of)
        )

    proj_near = proj_part(g_first.x)
    g_up.join()
    run.wait(*proj_near)

    proj_far = proj_part(g_first.other)
    pair_out = shape_of((2, ROWS, width), bf16)
    group_out = shape_of((tp * ROWS, D), bf16)
    qkv_out = shape_of((tp * ROWS, 3 * width), bf16)
    probs_out = shape_of((tp, heads, ROWS, ROWS), f32)
    group, qkv, probs, far = run(
        lambda *ins: call(
            partial(attend_kernel, heads, (2, 3)), ins,
            [group_out, qkv_out, probs_out, pair_out], scalars=1,
        ),
        at, *doc_pieces[2:], g_first.x, g_first.other, qkv_bias, bias,
    )
    mixed_far = swap(far, by_y)
    g_up.send(g_first.other)
    g_down.join().send()
    group, qkv, probs, near = run(
        lambda *ins: call(
            partial(attend_kernel, heads, (0, 1)), ins,
            [group_out, qkv_out, probs_out, pair_out], scalars=1,
            alias={7: 0, 8: 1, 9: 2},
        ),
        at, *doc_pieces[:2], g_first.x, g_first.other, qkv_bias, bias, group, qkv, probs,
    )
    att_pieces = (near, *trade(second(near), mixed_far))

    wide_f = shape_of((ROWS, D), f32)
    wide_b = shape_of((ROWS, D), bf16)
    attended, normed_low, normed_one, hat_one, scale_one = run(
        lambda *ins: call(
            partial(first_norm_kernel, width), ins,
            [wide_b, wide_b, wide_f, wide_f, shape_of((ROWS, 1), f32)],
            [pltpu.VMEM((ROWS, D), f32), pltpu.VMEM((ROWS, D), bf16)], scalars=1,
        ),
        at, *att_pieces, *proj_near, *proj_far, doc_rows, vec_one,
    )

    normed_pieces = group_of(normed_low)
    hid_f = shape_of((tp * ROWS, hidden), f32)
    hid_b = shape_of((tp * ROWS, hidden), bf16)
    ffn_weights = (g_up.x, g_up.other, g_down.x, g_down.other)
    normed_group, slope, act_low, keep, give = run(
        lambda *ins: call(
            partial(up_kernel, (0, 1)), ins, [group_out, hid_f, hid_b, wide_f, wide_b], scalars=1,
        ),
        at, *normed_pieces[:2], *ffn_weights, my_upb,
    )
    meet = Meet().near_pair(keep, give)
    normed_group, slope, act_low, keep, give = run(
        lambda *ins: call(
            partial(up_kernel, (2, 3)), ins, [group_out, hid_f, hid_b, wide_f, wide_b], scalars=1,
            alias={8: 0, 9: 1, 10: 2},
        ),
        at, *normed_pieces[2:], *ffn_weights, my_upb, normed_group, slope, act_low,
    )
    meet.far_pair(keep, give).send()
    encoded, d_ffn, d_resid_two, sums_two = run(
        lambda *ins: call(
            second_norm_kernel, ins,
            [shape_of((1, SLOTS, D), bf16), wide_b, wide_f, shape_of((3, D), f32)],
        ),
        *meet.terms(), normed_one, grad_in, live_row, vec_two,
    )

    d_ffn_pieces = group_of(d_ffn)
    ffn_weights = (g_down.x, g_down.other, g_up.x, g_up.other)
    sums_out = shape_of((2, hidden), f32)
    d_ffn_group, d_pre, d_up_bias, keep, give = run(
        lambda *ins: call(
            partial(down_back_kernel, (0, 1)), ins,
            [group_out, hid_b, sums_out, wide_f, wide_b], scalars=1,
        ),
        at, *d_ffn_pieces[:2], *ffn_weights, slope,
    )
    meet = Meet().near_pair(keep, give)
    d_ffn_group, d_pre, d_up_bias, keep, give = run(
        lambda *ins: call(
            partial(down_back_kernel, (2, 3)), ins,
            [group_out, hid_b, sums_out, wide_f, wide_b], scalars=1,
            alias={8: 0, 9: 1, 10: 2},
        ),
        at, *d_ffn_pieces[2:], *ffn_weights, slope, d_ffn_group, d_pre, d_up_bias,
    )
    meet.far_pair(keep, give)

    def half_grad(left, right, near):
        left = left[:, : D // 2] if near else left[:, D // 2 :]
        return dot_tn(left, right).astype(bf16)

    give = run(partial(half_grad, near=False), d_ffn_group, act_low)
    s_down = Scatter(run, (give,), "dp", X_Z, given=give)
    s_down.send()
    meet.send()
    keep = run(partial(half_grad, near=True), d_ffn_group, act_low)
    s_down.own(keep)
    keep = run(partial(half_grad, near=True), normed_group, d_pre)
    give = run(partial(half_grad, near=False), normed_group, d_pre)
    s_up = Scatter(run, (keep,), "dp", Z_X, given=give).send()

    d_branch, d_resid_one, sums_one, a0, a1, a2 = run(
        lambda *ins: call(
            partial(first_back_kernel, width), ins,
            [wide_b, wide_f, shape_of((3, D), f32), doc_out, doc_out, pair_out],
            [pltpu.VMEM((ROWS, D), bf16)], scalars=1,
        ),
        at, *meet.terms(), d_resid_two, hat_one, scale_one, vec_one, *proj_near, *proj_far,
    )
    far = swap(a2, by_y)
    got_c = swap(a1, by_c)
    parts = run(
        lambda *ins: call(partial(proj_grad_kernel, width), ins, [col_out] * 4, scalars=1),
        at, attended, d_branch,
    )
    meet_proj = Meet().near_pair(parts[0], parts[1]).far_pair(parts[2], parts[3])
    grids = shape_of((3 * heads, NB, NB), f32)
    d_qkv, d_sums, d_grid = run(
        lambda *ins: call(
            partial(attend_back_kernel, heads, (0, 1), False), ins,
            [qkv_out, shape_of((tp, 3 * width), f32), grids],
        ),
        qkv, probs, a0, got_c, notes,
    )
    got_far = swap(second(far), by_c)
    meet_proj.send()
    run.wait(s_up.other, s_down.other)
    s_up.take().send()
    d_qkv, d_sums, d_grid, d_ext = run(
        lambda *ins: call(
            partial(attend_back_kernel, heads, (2, 3), True), ins,
            [qkv_out, shape_of((tp, 3 * width), f32), grids, shape_of((3 * heads, 2 * NB), f32)],
            alias={5: 0, 6: 1, 7: 2},
        ),
        qkv, probs, far, got_far, notes, d_qkv, d_sums, d_grid,
    )

    def columns_grad(group, d_qkv, near):
        left = group[:, : D // 2] if near else group[:, D // 2 :]
        return dot_tn(left, d_qkv[:, : D // 2]).astype(bf16)

    def with_proj(q, k, c, y, small):
        p = (k.astype(f32) + c.astype(f32) + y.astype(f32)).astype(bf16)
        return jnp.concatenate([q, p, small], axis=-1).astype(f32)

    keep = run(partial(columns_grad, near=True), group, d_qkv)
    grad_b = run(lambda g, d: dot_tn(g, d[:, D // 2 :]).astype(bf16), group, d_qkv)
    give = run(partial(columns_grad, near=False), group, d_qkv)
    s_first = Scatter(run, (keep,), "dp", Z_X, given=give).send()
    plains = [pltpu.VMEM((24, D), f32)] * 2
    (small_grads,) = run(
        lambda *ins: call(
            partial(small_grads_kernel, heads, n_dev), ins, [shape_of((D, 128), bf16)],
            flats + plains, scalars=1,
        ),
        at, d_ext, d_sums, d_up_bias, sums_one, sums_two,
    )
    s_second = Scatter(
        run, (grad_b, *meet_proj.terms(), small_grads), "dp", Z_X, walk=(1, 2, 0), base=with_proj
    ).send()
    parts = run(
        lambda *ins: call(
            partial(tokens_back_kernel, width), ins, [wide_f, wide_b, wide_f, wide_b], scalars=1
        ),
        at, d_qkv, g_first.x, g_first.other,
    )
    meet_tok = Meet().near_pair(parts[0], parts[1]).far_pair(parts[2], parts[3])
    s_up.take().send()
    meet_tok.send()
    s_first.take().send()
    s_down.take().send()
    run.wait(s_second.other, s_first.other, s_up.other)
    s_second.take().send()
    s_first.take().send()
    run.wait(s_down.other, s_second.other)
    s_down.take().send()
    s_second.take().send()

    def columns_back(scatters):
        sums = [x.sum().reshape(tp, rows, -1) for x in scatters]
        out = shape_of((2, rows, sum(x.shape[2] for x in sums)), bf16)

        def fn(at, *refs):
            for target, c in ((refs[-2], 1 - at[0] % 2), (refs[-1], at[0] % 2)):
                for y in range(2):
                    target[y] = jnp.concatenate([ref[2 * y + c] for ref in refs[:-2]], axis=1)

        return Exchange(run, at, *run(lambda *ins: call(fn, ins, [out, out], scalars=1), at, *sums))

    def whole_rows(exchanged, groups, widths, smalls):
        outs = [shape_of((rows, tp * g * w), f32) for g, w in zip(groups, widths)]
        ends = [shape_of((1, n * rows), f32) for n in smalls]

        def fn(at, mine, other, *refs):
            outs, ends = refs[: len(groups)], refs[len(groups) :]
            total = None
            for near, ref in ((True, mine), (False, other)):
                for n in range(2):
                    start, f = 0, source_of(at, near, n)
                    for out, g, w in zip(outs, groups, widths):
                        for i in range(g):
                            place = pl.multiple_of((i * tp + f) * w, w)
                            out[:, pl.ds(place, w)] = ref[n, :, start : start + w].astype(f32)
                            start += w
                    part = ref[n, :, start:].astype(f32)
                    total = part if total is None else total + part
            small_outs(total, ends)

        return run(
            lambda *ins: call(fn, ins, outs + ends, scalars=1), at, exchanged.mine, exchanged.other
        )

    out_f = shape_of((1, SLOTS, D), f32)
    grad_tokens = run(
        lambda *ins: glue(
            lambda d, k, c, y: (
                d[...] + k[...] + c[...].astype(f32) + y[...].astype(f32)
            )[:SLOTS][None],
            [out_f], *ins,
        ),
        d_resid_one, *meet_tok.terms(),
    )
    run.wait(s_down.other, s_first.other, s_second.other)
    s_down.take()
    s_up.take()
    s_first.take()
    s_second.take()
    back = columns_back([s_up, s_down, s_first, s_second]).turn()

    grad_up, grad_down, grad_qkv, grad_proj, *out = whole_rows(
        back, (1, 1, 3, 1), (hidden, hidden, width, width), (1,) * 6 + (2, 6, 4)
    )
    out = [x.reshape(-1) for x in out]
    return (
        encoded,
        grad_tokens,
        grad_qkv,
        out[6],
        grad_proj,
        out[0],
        out[1],
        out[2],
        out[7],
        grad_up,
        out[8],
        grad_down,
        out[3],
        out[4],
        out[5],
    )


def solution(mesh):
    split = ("dp", "fsdp")
    one, two, three = P(split), P(split, None), P(split, None, None)
    return jax.shard_map(
        local,
        mesh=mesh,
        in_specs=(
            three, three, one, two, two, two, two, one, two, one, one, one, one, two, one, two,
            one, one, one,
        ),
        out_specs=(
            three, three, two, one, two, one, one, one, one, two, one, two, one, one, one,
        ),
        check_vma=False,
    )
```

```python
from functools import partial

import jax
import jax.numpy as jnp
from jax import lax
from jax.experimental import pallas as pl
from jax.experimental.pallas import tpu as pltpu
from jax.sharding import PartitionSpec as P

D = 1024
H = 16
HD = 64
FF = 4096
NB = 128
TEXT = 120
SLOTS = 169
ROWS = 176
NEGATIVE = -1e30
EPSILON = 1e-05

f32 = jnp.float32
bf16 = jnp.bfloat16


def shape_of(shape, kind):
    return jax.ShapeDtypeStruct(tuple(shape), kind)


def call(kernel, ins, outs, scratch=(), scalars=0, alias=None, vmem=16, cost=0):
    spaces = [pltpu.SMEM] * scalars + [pltpu.VMEM] * (len(ins) - scalars)
    return pl.pallas_call(
        kernel,
        in_specs=[pl.BlockSpec(memory_space=m) for m in spaces],
        out_specs=[pl.BlockSpec(memory_space=pltpu.VMEM) for _ in outs],
        out_shape=list(outs),
        scratch_shapes=list(scratch),
        input_output_aliases=alias or {},
        cost_estimate=pl.CostEstimate(
            flops=int(cost * 1e9), bytes_accessed=0, transcendentals=0
        ),
        compiler_params=pltpu.CompilerParams(vmem_limit_bytes=vmem * 2**20),
    )(*ins)


def glue(fn, outs, *ins, scalars=0):
    def kernel(*refs):
        made = fn(*refs[: len(ins)])
        for out, value in zip(refs[len(ins) :], made if isinstance(made, tuple) else (made,)):
            out[...] = value

    made = call(kernel, ins, outs, scalars=scalars)
    return made[0] if len(outs) == 1 else made


def axis_bits(axis):
    bits, b = [], lax.axis_size(axis) // 2
    while b >= 1:
        bits.append((axis, b))
        b //= 2
    return bits


def swap(x, bit):
    axis, b = bit
    return lax.ppermute(x, axis, [(i, i ^ b) for i in range(lax.axis_size(axis))])


def side(bit):
    axis, b = bit
    return (lax.axis_index(axis) // b) % 2


def pair_up(mine, other, bit, pos):
    one = side(bit) == 1
    return jnp.stack([jnp.where(one, other, mine), jnp.where(one, mine, other)], axis=pos)


class Order:
    def __init__(self):
        self.last = ()

    def tie(self, args):
        if not self.last:
            return args
        return lax.optimization_barrier(tuple(args) + self.last)[: len(args)]

    def wait(self, *arrays):
        self.last = self.last + arrays

    def __call__(self, fn, *args):
        out = fn(*self.tie(args))
        self.last = tuple(jax.tree.leaves(out))
        return out


def after(x, *earlier):
    return lax.optimization_barrier((x,) + earlier)[0]


def high_bits(axis, order):
    bits = axis_bits(axis)
    return [bits[i] for i in order]


class Gather:
    def __init__(self, run, x, axis, order):
        self.run, self.x = run, x
        self.bits = axis_bits(axis)[3:][::-1] + high_bits(axis, order)
        while len(self.bits) > 3:
            self.send().join()

    def send(self, *earlier):
        self.other = swap(after(self.x, *earlier), self.bits[0])
        return self

    def join(self):
        bit = self.bits.pop(0)
        if len(self.bits) >= 3:
            self.x = self.run(
                lambda m, o: pair_up(m, o, bit, 0).reshape(-1, m.shape[1]), self.x, self.other
            )
        else:
            r, c = self.x.shape

            def join(m, o, out):
                out[:r], out[r:] = m[...], o[...]

            (self.x,) = self.run(
                lambda *ins: call(join, ins, [shape_of((2 * r, c), bf16)]), self.x, self.other
            )
        return self


class Scatter:
    def __init__(self, run, arrays, axis, order, walk=None, base=None, given=None):
        self.run = run
        self.high, rest = high_bits(axis, order), axis_bits(axis)[3:]
        have = self.high[::-1] + rest
        self.order = (high_bits(axis, walk) if walk else self.high[::-1]) + rest
        self.low = len(rest)
        if given is not None:
            have = [bit for bit in have if bit != self.order[0]]
            given = given.reshape((2,) * len(have) + (-1, given.shape[-1]))
        self.given = given
        arrays = tuple(a.reshape((2,) * len(have) + (-1, a.shape[-1])) for a in arrays)
        self.terms = [(arrays, have, [], base or (lambda x: x.astype(f32)))]

    def own(self, array):
        arrays, *rest = self.terms[0]
        self.terms[0] = ((array.reshape(arrays[0].shape),), *rest)

    def flat(self):
        return [a for arrays, *unused in self.terms for a in arrays]

    def value(self, flat, extra=()):
        flat, total = list(flat), None
        for arrays, have, cuts, base in self.terms:
            chosen = dict(list(cuts) + list(extra))
            at = tuple(
                slice(None) if bit not in chosen
                else (0 if chosen[bit] else 1) if bit in self.high
                else side(bit) if chosen[bit] else 1 - side(bit)
                for bit in have
            )
            part = base(*[flat.pop(0)[at] for unused in arrays])
            total = part if total is None else total + part
        return total

    def sum(self, extra=()):
        flat = self.flat()
        fn = lambda *f: self.value(f, extra).astype(bf16)
        if self.low:
            return self.run(fn, *flat)
        out = jax.eval_shape(fn, *flat)
        return self.run(lambda *f: glue(fn, [out], *f), *flat)

    def send(self, *earlier):
        bit = self.order[0]
        out = self.given if self.given is not None else self.sum([(bit, False)])
        self.other = swap(after(out, *earlier), bit)
        return self

    def take(self):
        bit = self.order.pop(0)
        for arrays, have, cuts, base in self.terms:
            if self.given is None:
                cuts.append((bit, True))
        self.given = None
        self.terms.append(((self.other,), list(self.order_left()), [], lambda x: x.astype(f32)))
        while 0 < len(self.order) <= self.low:
            self.send().take()
        return self

    def order_left(self):
        arrays, have, cuts, base = self.terms[0]
        gone = [bit for bit, keep in cuts]
        return [bit for bit in have if bit not in gone]


class Exchange:
    def __init__(self, run, at, give, keep):
        self.run, self.at, self.keep = run, at, keep
        self.other = swap(give, axis_bits("fsdp")[1])

    def turn(self, *earlier):
        def fn(at, keep, got, give, mine):
            y, c = at[0] // 2, at[0] % 2
            give[c], give[1 - c] = keep[1 - y], got[1 - y]
            mine[c], mine[1 - c] = keep[y], got[y]

        out = shape_of(self.keep.shape, self.keep.dtype)
        give, self.mine = self.run(
            lambda *ins: call(fn, ins, [out, out], scalars=1), self.at, self.keep, self.other
        )
        self.other = swap(after(give, *earlier), axis_bits("fsdp")[0])
        return self


def source_of(at, near, n):
    y = at[0] // 2
    return (y if near else 1 - y) * 2 + n


def dot_nn(a, b):
    return jnp.dot(a, b, preferred_element_type=f32)


def dot_nt(a, b):
    return lax.dot_general(a, b, (((1,), (1,)), ((), ())), preferred_element_type=f32)


def dot_tn(a, b):
    return lax.dot_general(a, b, (((0,), (0,)), ((), ())), preferred_element_type=f32)


def call_docs(kernel, docs, ins, in_whole, outs):
    def spec(a, whole):
        n = len(a.shape)
        if whole:
            return pl.BlockSpec(tuple(a.shape), lambda d: (0,) * n)
        return pl.BlockSpec((1,) + tuple(a.shape[1:]), lambda d: (d,) + (0,) * (n - 1))

    return pl.pallas_call(
        kernel,
        grid=(docs,),
        in_specs=[spec(a, w) for a, w in zip(ins, in_whole)],
        out_specs=[spec(a, False) for a in outs],
        out_shape=list(outs),
        cost_estimate=pl.CostEstimate(flops=0, bytes_accessed=0, transcendentals=0),
        compiler_params=pltpu.CompilerParams(vmem_limit_bytes=16 * 2**20),
    )(*ins)


def at_block(ref, me, j, size):
    return pl.ds(pl.multiple_of((me ^ j) * size, size), size)


BLOCK = D // 8
Z_X = (0, 1, 2)
X_Z = (0, 2, 1)
X_FIRST = (2, 1, 0)


def far_block(place, q, order):
    away = sum(((q >> n) & 1) * (4 >> bit) for n, bit in enumerate(order))
    return pl.ds(pl.multiple_of((place ^ away) * BLOCK, BLOCK), BLOCK)


def relative(src, dst, place, order, rows):
    for q in range(8):
        dst[rows, q * BLOCK : (q + 1) * BLOCK] = src[:, far_block(place, q, order)]


def doc_at(j):
    return slice(j * ROWS, (j + 1) * ROWS)


def hot_rows(notes, flip=False):
    buckets = lax.broadcasted_iota(jnp.int32, (NB, ROWS), 0).astype(f32)
    if flip:
        buckets = (NB - 1) - buckets
    return [(notes[r : r + 1, :ROWS] == buckets).astype(f32).astype(bf16) for r in (12, 9, 10)]


ROW_QV, ROW_TABLES, ROW_UP = 6, 7, 9
TILE_ROWS = 16


def pack_kernel(*refs):
    *smalls, out_ref = refs
    rows = smalls[0].shape[1]
    tile = jnp.zeros(out_ref.shape, f32)
    row = lax.broadcasted_iota(jnp.int32, out_ref.shape, 0)
    qv, tables, up = smalls[6:]
    parts = list(smalls[:6]) + [qv] + [tables.at[:, 3 * n * rows : 3 * (n + 1) * rows] for n in range(2)]
    for n, ref in enumerate(parts + [up]):
        value = ref[...].astype(f32)
        wide = jnp.concatenate(
            [value, jnp.zeros((1, 128 - value.shape[1]), f32)], axis=1
        ) if value.shape[1] < 128 else value
        tile = jnp.where(row == n, jnp.broadcast_to(wide, out_ref.shape), tile)
    out_ref[...] = tile.astype(bf16)


def unpack_kernel(heads, count, at_ref, all_ref, ext_ref, add_ref, up_ref, one_ref, two_ref, qv_ref, tab_ref, upb_ref):
    me, place = at_ref[0], at_ref[1]
    rows, width, low = D // count, heads * HD, count // 32
    for d in range(count):
        q = place ^ (d // (4 * low))
        block = (q * low + (d // 4) % low) * 4 + (me ^ (d % 4))
        place_of = pl.ds(pl.multiple_of(block * TILE_ROWS, TILE_ROWS), TILE_ROWS)
        tile = all_ref[place_of, :].astype(f32)
        at = slice(d * rows, (d + 1) * rows)
        one_ref[:, at] = tile[0:3, :rows]
        two_ref[:, at] = tile[3:6, :rows]
        qv_ref[:, 2 * d * rows : 2 * (d + 1) * rows] = tile[ROW_QV : ROW_QV + 1, : 2 * rows]
        for n in range(2):
            start = (2 * d + n) * 3 * rows
            row = tile[ROW_TABLES + n : ROW_TABLES + n + 1, : 3 * rows]
            tab_ref[:, start : start + 3 * rows] = row
        upb_ref[:, 4 * d * rows : 4 * (d + 1) * rows] = tile[ROW_UP : ROW_UP + 1, : 4 * rows]
    start = pl.multiple_of(me * width, width)
    add_ref[:, :width] = qv_ref[:, pl.ds(start, width)]
    add_ref[:, width : 2 * width] = jnp.zeros((1, width), f32)
    add_ref[:, 2 * width :] = qv_ref[:, pl.ds(D + start, width)]
    hidden = up_ref.shape[1]
    up_ref[...] = upb_ref[:, pl.ds(pl.multiple_of(me * hidden, hidden), hidden)]
    half = NB // 2
    for k in range(3):
        for h in range(heads):
            n = k * heads + h
            row = tab_ref[:, pl.ds(pl.multiple_of((k * H + me * heads + h) * NB, NB), NB)]
            ext_ref[n : n + 1, :half] = jnp.broadcast_to(row[:, :1], (1, half))
            ext_ref[n : n + 1, half : half + NB] = row
            ext_ref[n : n + 1, half + NB :] = jnp.broadcast_to(row[:, NB - 1 :], (1, half))


PIECES = 18


def small_grads_kernel(
    heads, count, at_ref, ext_ref, sums_ref, up_ref, one_ref, two_ref, out_ref,
    qv_ref, tab_ref, upb_ref, plain_ref, order_ref,
):
    me = at_ref[0]
    rows, width = D // count, heads * HD
    for ref in (qv_ref, tab_ref, upb_ref, plain_ref):
        ref[...] = jnp.zeros_like(ref)
    start = pl.multiple_of(me * width, width)
    sums = jnp.sum(sums_ref[...], axis=0, keepdims=True)
    qv_ref[:, pl.ds(start, width)] = sums[:, :width]
    qv_ref[:, pl.ds(D + start, width)] = sums[:, 2 * width :]
    hidden = up_ref.shape[1]
    upb_ref[:, pl.ds(pl.multiple_of(me * hidden, hidden), hidden)] = jnp.sum(
        up_ref[...], axis=0, keepdims=True
    )
    half = NB // 2
    lane = lax.broadcasted_iota(jnp.int32, (1, NB), 1)
    for k in range(3):
        for h in range(heads):
            row = ext_ref[k * heads + h : k * heads + h + 1, :]
            low = jnp.sum(row[:, :half], axis=1, keepdims=True)
            high = jnp.sum(row[:, half + NB :], axis=1, keepdims=True)
            grad = row[:, half : half + NB] + jnp.where(lane == 0, low, 0.0)
            grad = grad + jnp.where(lane == NB - 1, high, 0.0)
            tab_ref[:, pl.ds(pl.multiple_of((k * H + me * heads + h) * NB, NB), NB)] = grad
    plain_ref[0:3, :] = one_ref[...]
    plain_ref[3:6, :] = two_ref[...]
    for d in range(count):
        at = slice(d * rows, (d + 1) * rows)
        row = 6
        for ref, times in ((qv_ref, 2), (tab_ref, 6), (upb_ref, 4)):
            for n in range(times):
                begin = (d * times + n) * rows
                plain_ref[row : row + 1, at] = ref[:, begin : begin + rows]
                row += 1
    relative(plain_ref, order_ref, at_ref[1], Z_X, slice(None))
    shape = (plain_ref.shape[0], 128)
    same = lax.broadcasted_iota(jnp.int32, shape, 0) == lax.broadcasted_iota(jnp.int32, shape, 1)
    out_ref[...] = dot_tn(order_ref[...].astype(bf16), same.astype(f32).astype(bf16)).astype(bf16)


def small_outs(total, outs):
    rows = total.shape[0]
    shape = (rows, rows)
    same = lax.broadcasted_iota(jnp.int32, shape, 0) == lax.broadcasted_iota(jnp.int32, shape, 1)
    turned = lax.dot_general(
        total, same.astype(f32), (((0,), (0,)), ((), ())),
        precision=lax.Precision.HIGHEST, preferred_element_type=f32,
    )
    row = 0
    for out in outs:
        for n in range(out.shape[1] // rows):
            out[:, n * rows : (n + 1) * rows] = turned[row : row + 1, :]
            row += 1


def bias_kernel(heads, notes_ref, ext_ref, out_ref):
    notes = notes_ref[0].astype(f32)
    hots = hot_rows(notes)
    every_hot = jnp.concatenate(hots, axis=0)
    live = notes[11:12, :ROWS] > 0.5
    for h in range(heads):
        codes = []
        for k in range(3):
            row = ext_ref[k * heads + h : k * heads + h + 1, :]
            spread = jnp.broadcast_to(row, (NB, 2 * NB))
            skew = pltpu.roll(spread, NB, 1, stride=1, stride_axis=0)
            codes.append(dot_tn(hots[k], skew[:, :NB].astype(bf16)).astype(bf16))
        total = dot_nn(jnp.concatenate(codes, axis=1), every_hot)
        out_ref[0, h] = jnp.where(live, total, NEGATIVE)


def softmax_rows(q, k, bias):
    s = dot_nt(q, k) * 0.125 + bias
    e = jnp.exp(s - jnp.max(s, axis=-1, keepdims=True))
    return e / jnp.sum(e, axis=-1, keepdims=True)


def attend_kernel(heads, pair, at_ref, d0, d1, near_ref, far_ref, add_ref, bias_ref, *rest):
    group_ref, qkv_ref, probs_ref, mixed_ref = rest[-4:]
    width = heads * HD
    for j, piece in zip(pair, (d0, d1)):
        relative(piece, group_ref, at_ref[1], Z_X, doc_at(j))
    both = slice(pair[0] * ROWS, (pair[1] + 1) * ROWS)
    for n in range(3):
        at = slice(n * width, (n + 1) * width)
        qkv = dot_nn(group_ref[both, : D // 2], near_ref[:, at])
        qkv = qkv + dot_nn(group_ref[both, D // 2 :], far_ref[:, at])
        qkv_ref[both, at] = (qkv + add_ref[:, at]).astype(bf16)
    for n, j in enumerate(pair):
        outs = []
        for h in range(heads):
            q = qkv_ref[doc_at(j), h * HD : (h + 1) * HD]
            k = qkv_ref[doc_at(j), width + h * HD : width + (h + 1) * HD]
            v = qkv_ref[doc_at(j), 2 * width + h * HD : 2 * width + (h + 1) * HD]
            probs = softmax_rows(q, k, bias_ref[j, h])
            probs_ref[j, h] = probs
            outs.append(dot_nn(probs.astype(bf16), v).astype(bf16))
        mixed_ref[n] = jnp.concatenate(outs, axis=1)


def norm_parts(values):
    average = jnp.mean(values, axis=-1, keepdims=True)
    centred = values - average
    spread = jnp.mean(centred * centred, axis=-1, keepdims=True)
    scale = lax.rsqrt(spread + EPSILON)
    return centred * scale, scale


def norm_back(grad, gain, hat, scale):
    scaled = grad * gain
    first = jnp.mean(scaled, axis=-1, keepdims=True)
    second = jnp.mean(scaled * hat, axis=-1, keepdims=True)
    return (scaled - first - hat * second) * scale


def first_norm_kernel(
    width, at_ref, a0, a1, a2, a3, *rest
):
    near, far = rest[:4], rest[4:8]
    tokens_ref, vec_ref, att_ref, low_ref, normed_ref, hat_ref, scale_ref, branch_ref, plain_ref = rest[8:]
    me = at_ref[0]
    for j, piece in enumerate((a0[0], a1[...], a2[0], a3[...])):
        plain_ref[:, at_block(plain_ref, me, j, width)] = piece
    relative(plain_ref, att_ref, at_ref[1], Z_X, slice(None))
    left, right = att_ref[:, : D // 2], att_ref[:, D // 2 :]
    for j in range(4):
        branch_ref[:, at_block(branch_ref, me, j, width)] = dot_nn(left, near[j][...]) + dot_nn(
            right, far[j][...]
        )
    resid = tokens_ref[...].astype(f32) + branch_ref[...] + vec_ref[0:1, :]
    hat, scale = norm_parts(resid)
    normed = hat * vec_ref[1:2, :] + vec_ref[2:3, :]
    low_ref[...] = normed.astype(bf16)
    normed_ref[...] = normed
    hat_ref[...] = hat
    scale_ref[...] = scale


def parts_back(left, near_ref, far_ref, outs, place, order):
    for q in range(0, 8, 2):
        ref = near_ref if q < 4 else far_ref
        at = slice((q % 4) * BLOCK, (q % 4 + 2) * BLOCK)
        part = dot_nt(left, ref[at, :])
        for n, out in enumerate(outs):
            for half in range(2):
                block = part[doc_at(n), half * BLOCK : (half + 1) * BLOCK]
                out[:, far_block(place, q + half, order)] = block.astype(out.dtype)


def half_grad_kernel(near, start, left_ref, right_ref, out_ref):
    left = left_ref[...]
    if near is not None:
        left = left_ref[:, : D // 2] if near else left_ref[:, D // 2 :]
    for n in range(out_ref.shape[1] // TILE):
        at = slice(start + n * TILE, start + (n + 1) * TILE)
        out_ref[:, n * TILE : (n + 1) * TILE] = dot_tn(left, right_ref[:, at]).astype(bf16)


def normal_parts(u):
    density = jnp.exp(-0.5 * u * u)
    return 0.5 + 0.5 * lax.erf(u * (0.5**0.5)), u * density * ((2 * jnp.pi) ** -0.5)


TILE = 256


def up_kernel(pair, at_ref, x0, x1, up_near, up_far, down_near, down_far, add_ref, *rest):
    group_ref, slope_ref, act_ref, keep_ref, give_ref = rest[-5:]
    for j, piece in zip(pair, (x0, x1)):
        relative(piece, group_ref, at_ref[1], Z_X, doc_at(j))
    both = slice(pair[0] * ROWS, (pair[1] + 1) * ROWS)
    for n in range(act_ref.shape[1] // TILE):
        at = slice(n * TILE, (n + 1) * TILE)
        pre = dot_nn(group_ref[both, : D // 2], up_near[:, at])
        pre = pre + dot_nn(group_ref[both, D // 2 :], up_far[:, at]) + add_ref[:, at]
        below, tilt = normal_parts(pre)
        slope_ref[both, at] = below + tilt
        act_ref[both, at] = (pre * below).astype(bf16)
    parts_back(act_ref[both, :], down_near, down_far, (keep_ref, give_ref), at_ref[1], X_Z)


def down_back_kernel(pair, at_ref, g0, g1, down_near, down_far, up_near, up_far, slope_ref, *rest):
    group_ref, dpre_ref, sums_ref, keep_ref, give_ref = rest[-5:]
    for j, piece in zip(pair, (g0, g1)):
        relative(piece, group_ref, at_ref[1], X_Z, doc_at(j))
    both = slice(pair[0] * ROWS, (pair[1] + 1) * ROWS)
    for n in range(dpre_ref.shape[1] // TILE):
        at = slice(n * TILE, (n + 1) * TILE)
        d_act = dot_nn(group_ref[both, : D // 2], down_near[:, at])
        d_act = d_act + dot_nn(group_ref[both, D // 2 :], down_far[:, at])
        d_pre = (d_act * slope_ref[both, at]).astype(bf16)
        dpre_ref[both, at] = d_pre
        sums_ref[pair[0] // 2 : pair[0] // 2 + 1, at] = jnp.sum(d_pre.astype(f32), axis=0, keepdims=True)
    parts_back(dpre_ref[both, :], up_near, up_far, (keep_ref, give_ref), at_ref[1], Z_X)


def second_norm_kernel(
    keep_ref, got_c, got_y, normed_ref, grad_ref, live_ref, vec_ref,
    enc_ref, dffn_ref, dres_ref, sums_ref,
):
    ffn = keep_ref[...] + got_c[...].astype(f32) + got_y[...].astype(f32) + vec_ref[0:1, :]
    hat, scale = norm_parts(normed_ref[...] + ffn)
    ones = jnp.ones((8, 128), bf16)
    live = dot_tn(live_ref[...].astype(bf16), ones)[:, :1]
    gain = vec_ref[1:2, :]
    enc = ((hat * gain + vec_ref[2:3, :]) * live).astype(bf16)
    enc_ref[0] = enc[:SLOTS]
    grad = grad_ref[...].astype(f32) * live
    d_resid = norm_back(grad, gain, hat, scale)
    dres_ref[...] = d_resid
    low = d_resid.astype(bf16)
    dffn_ref[...] = low
    sums_ref[0:1, :] = jnp.sum(low.astype(f32), axis=0, keepdims=True)
    sums_ref[1:2, :] = jnp.sum(grad * hat, axis=0, keepdims=True)
    sums_ref[2:3, :] = jnp.sum(grad, axis=0, keepdims=True)


def first_back_kernel(width, at_ref, keep_ref, got_c, got_y, dres_ref, hat_ref, scale_ref, vec_ref, *rest):
    near, far = rest[:4], rest[4:8]
    branch_ref, done_ref, sums_ref, a0_ref, a1_ref, a2_ref, plain_ref = rest[8:]
    me = at_ref[0]
    hat = hat_ref[...]
    grad = dres_ref[...] + keep_ref[...] + got_c[...].astype(f32) + got_y[...].astype(f32)
    d_one = norm_back(grad, vec_ref[1:2, :], hat, scale_ref[...])
    done_ref[...] = d_one
    low = d_one.astype(bf16)
    branch_ref[...] = low
    sums_ref[0:1, :] = jnp.sum(low.astype(f32), axis=0, keepdims=True)
    sums_ref[1:2, :] = jnp.sum(grad * hat, axis=0, keepdims=True)
    sums_ref[2:3, :] = jnp.sum(grad, axis=0, keepdims=True)
    for n, proj in enumerate((near, far)):
        total = None
        for j in range(4):
            part = dot_nt(branch_ref[:, at_block(branch_ref, me, j, width)], proj[j][...])
            total = part if total is None else total + part
        for q in range(4):
            plain_ref[:, far_block(at_ref[1], 4 * n + q, Z_X)] = total[
                :, q * BLOCK : (q + 1) * BLOCK
            ].astype(bf16)
    for i, out in enumerate((a0_ref, a1_ref, a2_ref.at[0], a2_ref.at[1])):
        out[...] = plain_ref[:, at_block(plain_ref, me, i, width)]


def proj_grad_kernel(width, at_ref, att_ref, branch_ref, *outs):
    me = at_ref[0]
    att = att_ref[...]
    for j, out in enumerate(outs):
        out[...] = dot_tn(att, branch_ref[:, at_block(branch_ref, me, j, width)]).astype(bf16)


def attend_back_kernel(heads, pair, last, qkv_ref, probs_ref, g0, g1, notes_ref, *rest):
    dqkv_ref, sums_ref, grid_ref = rest[-4:-1] if last else rest[-3:]
    width = heads * HD
    for j, grad_ref in zip(pair, (g0.at[0] if last else g0, g1)):
        notes = notes_ref[j].astype(f32)
        hots = jnp.concatenate(hot_rows(notes), axis=0)
        flipped = hot_rows(notes, flip=True)
        for h in range(heads):
            q = qkv_ref[doc_at(j), h * HD : (h + 1) * HD]
            k = qkv_ref[doc_at(j), width + h * HD : width + (h + 1) * HD]
            v = qkv_ref[doc_at(j), 2 * width + h * HD : 2 * width + (h + 1) * HD]
            g = grad_ref[:, h * HD : (h + 1) * HD]
            p = probs_ref[j, h]
            dp = dot_nt(g, v)
            ds = (p * (dp - jnp.sum(p * dp, axis=-1, keepdims=True))).astype(bf16)
            dq = (dot_nn(ds, k) * 0.125).astype(bf16)
            dk = (dot_tn(ds, q) * 0.125).astype(bf16)
            dv = dot_tn(p.astype(bf16), g).astype(bf16)
            for c, d in enumerate((dq, dk, dv)):
                at = slice(c * width + h * HD, c * width + (h + 1) * HD)
                dqkv_ref[doc_at(j), at] = d
            part = dot_nt(ds, hots).astype(bf16)
            for n in range(3):
                term = dot_nn(flipped[n], part[:, n * NB : (n + 1) * NB])
                if j == 0:
                    grid_ref[n * heads + h] = term
                else:
                    grid_ref[n * heads + h] += term
        sums_ref[j : j + 1, :] = jnp.sum(dqkv_ref[doc_at(j), :].astype(f32), axis=0, keepdims=True)
    if last:
        ext_ref = rest[-1]
        for n in range(3 * heads):
            wide = jnp.concatenate([grid_ref[n], jnp.zeros((NB, NB), f32)], axis=1)
            skew = pltpu.roll(wide, 1, 1, stride=1, stride_axis=0)
            ext_ref[n : n + 1, :] = jnp.sum(skew, axis=0, keepdims=True)


def tokens_back_kernel(width, at_ref, d_ref, near_ref, far_ref, *outs):
    for q in range(0, 8, 2):
        ref = near_ref if q < 4 else far_ref
        at = slice((q % 4) * BLOCK, (q % 4 + 2) * BLOCK)
        part = dot_nt(d_ref[...], ref[at, : 3 * width])
        for n, out in enumerate(outs):
            for half in range(2):
                block = part[doc_at(n), half * BLOCK : (half + 1) * BLOCK]
                out[:, far_block(at_ref[1], q + half, Z_X)] = block.astype(out.dtype)


def pad_rows(x):
    return jnp.pad(x, ((0, ROWS - SLOTS), (0, 0)))


def local(
    tokens,
    out_grad,
    text_len,
    x_bucket,
    y_bucket,
    patch_mask,
    qkv_weight,
    qv_bias,
    proj_weight,
    proj_bias,
    first_gain,
    first_shift,
    rel_tables,
    up_weight,
    up_bias,
    down_weight,
    down_bias,
    second_gain,
    second_shift,
):
    inner = axis_bits("fsdp")
    outer = axis_bits("dp")
    tp = 4
    by_y, by_c = inner
    dpn = lax.axis_size("dp")
    n_dev = tp * dpn
    rows = D // n_dev
    heads = H // tp
    width = heads * HD
    hidden = FF // tp
    me = lax.axis_index("fsdp")
    place = lax.axis_index("dp") // (dpn // 8)
    at = jnp.stack([me, place]).astype(jnp.int32)
    run = Order()
    run.wait(at)
    doc_out = shape_of((ROWS, width), bf16)

    def group_of(own):
        far = swap(own, by_y)
        return own, swap(own, by_c), far, swap(far, by_c)

    def second(pair):
        return run(lambda p: glue(lambda ref: ref[1], [doc_out], p), pair)

    def trade(p1, far):
        return swap(p1, by_c), far, swap(second(far), by_c)

    class Meet:
        def near_pair(self, keep, give):
            self.keep, self.near = keep, swap(give, by_c)
            return self

        def far_pair(self, keep, give):
            self.held, self.both = keep, swap(give, by_c)
            return self

        def send(self):
            out = shape_of(self.held.shape, bf16)
            fn = lambda k, g: (k[...].astype(f32) + g[...].astype(f32)).astype(bf16)
            both = run(lambda *ins: glue(fn, [out], *ins), self.held, self.both)
            self.far = swap(both, by_y)
            return self

        def terms(self):
            return self.keep, self.near, self.far

    def column_blocks(shards, groups):
        widths = [a.shape[1] // (g * tp) for a, g in zip(shards, groups)]
        out = shape_of((2, rows, sum(w * g for w, g in zip(widths, groups))), bf16)

        def fn(at, *refs):
            for target, c in ((refs[-2], 1 - at[0] % 2), (refs[-1], at[0] % 2)):
                for y in range(2):
                    start = 0
                    for ref, w, g in zip(refs, widths, groups):
                        for n in range(g):
                            place = pl.multiple_of((n * tp + 2 * y + c) * w, w)
                            target[y, :, start : start + w] = ref[:, pl.ds(place, w)]
                            start += w

        return Exchange(
            run, at,
            *run(lambda *ins: call(fn, ins, [out, out], scalars=1), at, *shards),
        )

    def block_rows(exchanged, parts):
        cols = exchanged.mine.shape[2] // parts

        def fn(at, mine, other, *outs):
            for near, ref in ((True, mine), (False, other)):
                for n in range(2):
                    for p, out in enumerate(outs):
                        out[source_of(at, near, n)] = ref[n, :, p * cols : (p + 1) * cols]

        outs = run(
            lambda *ins: call(fn, ins, [shape_of((tp, rows, cols), bf16)] * parts, scalars=1),
            at, exchanged.mine, exchanged.other,
        )
        return [o.reshape(tp * rows, cols) for o in outs]

    ex_first = column_blocks((qkv_weight, proj_weight), (3, 1))

    smalls = [
        proj_bias, first_gain, first_shift, down_bias, second_gain, second_shift,
        qv_bias, rel_tables, up_bias,
    ]
    flats = [pltpu.VMEM((1, n), f32) for n in (2 * D, 3 * H * NB, FF)]

    places = jnp.arange(TEXT, dtype=jnp.int32)
    live_own = jnp.concatenate(
        [places[None, :] < text_len[:, None], patch_mask > 0], axis=1
    ).astype(f32)

    def document(tokens, x_bucket, y_bucket, live):
        pad_cols = ((0, 0), (0, D - SLOTS))
        positions = (jnp.arange(SLOTS, dtype=jnp.int32) * NB // SLOTS)[None]
        return jnp.concatenate(
            [
                tokens[0],
                jnp.pad(x_bucket.astype(bf16), pad_cols),
                jnp.pad(y_bucket.astype(bf16), pad_cols),
                jnp.pad(live.astype(bf16), pad_cols),
                jnp.pad(positions.astype(bf16), pad_cols),
                jnp.zeros((ROWS - SLOTS - 4, D), bf16),
            ],
            axis=0,
        )

    ex_ffn = column_blocks((up_weight, down_weight), (1, 1))
    ex_first.turn()
    ex_ffn.turn(ex_first.other)
    doc_rows = run(document, tokens, x_bucket, y_bucket, live_own)
    (packed,) = run(
        lambda *ins: call(pack_kernel, [x[None] for x in ins], [shape_of((TILE_ROWS, 128), bf16)]),
        *smalls,
    )

    def beside(m, o):
        r = m.shape[0]

        def join(m, o, out):
            out[:r], out[r:] = m[...], o[...]

        return run(lambda *ins: call(join, ins, [shape_of((2 * r, 128), bf16)]), m, o)[0]

    small_near = swap(packed, by_c)
    grad_in, live_row = run(
        lambda g, l: (pad_rows(g[0]), jnp.pad(l, ((0, 7), (0, ROWS - SLOTS)))), out_grad, live_own
    )
    pair = beside(packed, small_near)
    small_far = swap(pair, by_y)
    g_first = Gather(run, *block_rows(ex_first, 1), "dp", Z_X).send()
    g_small = Gather(run, beside(pair, small_far), "dp", X_FIRST).send()
    doc_far = swap(after(doc_rows, ex_ffn.other, small_far), by_y)
    doc_near = swap(doc_rows, by_c)
    up_own, down_own = block_rows(ex_ffn, 2)
    g_small.join().send()
    g_small.join().send()
    g_down = Gather(run, down_own, "dp", X_Z)
    g_first.join().send()
    g_down.send(g_first.x)
    doc_pieces = (doc_rows, doc_near, doc_far, swap(after(doc_far, g_first.x), by_c))

    def take_notes(*refs):
        for n in range(4):
            refs[4][n] = refs[n][ROWS - 16 :, : 2 * NB]

    (notes,) = run(
        lambda *ins: call(take_notes, ins, [shape_of((tp, 16, 2 * NB), bf16)]), *doc_pieces
    )
    run.wait(g_small.other)
    g_down.join()
    g_first.join().send()
    g_down.send()
    g_up = Gather(run, up_own, "dp", Z_X).send(g_down.x)
    ext, qkv_bias, my_upb, vec_one, vec_two = run(
        lambda *ins: call(
            partial(unpack_kernel, heads, n_dev), ins,
            [
                shape_of((3 * heads, 2 * NB), f32), shape_of((1, 3 * width), f32),
                shape_of((1, hidden), f32), shape_of((3, D), f32), shape_of((3, D), f32),
            ],
            flats, scalars=1,
        ),
        at, beside(g_small.x, g_small.other),
    )

    (bias,) = run(
        lambda *ins: call_docs(
            partial(bias_kernel, heads), tp, ins, [False, True],
            [shape_of((tp, heads, ROWS, ROWS), f32)],
        ),
        notes, ext,
    )
    g_up.join().send()
    col_out = shape_of((D, width), bf16)
    half_out = shape_of((D // 2, width), bf16)

    def proj_part(rows_of):
        return group_of(
            run(lambda w: glue(lambda ref: ref[:, 3 * width :], [half_out], w), rows_of)
        )

    proj_near = proj_part(g_first.x)
    g_up.join()
    run.wait(*proj_near)

    proj_far = proj_part(g_first.other)
    pair_out = shape_of((2, ROWS, width), bf16)
    group_out = shape_of((tp * ROWS, D), bf16)
    qkv_out = shape_of((tp * ROWS, 3 * width), bf16)
    probs_out = shape_of((tp, heads, ROWS, ROWS), f32)
    group, qkv, probs, far = run(
        lambda *ins: call(
            partial(attend_kernel, heads, (2, 3)), ins,
            [group_out, qkv_out, probs_out, pair_out], scalars=1,
        ),
        at, *doc_pieces[2:], g_first.x, g_first.other, qkv_bias, bias,
    )
    mixed_far = swap(far, by_y)
    g_up.send(g_first.other)
    g_down.join().send()
    group, qkv, probs, near = run(
        lambda *ins: call(
            partial(attend_kernel, heads, (0, 1)), ins,
            [group_out, qkv_out, probs_out, pair_out], scalars=1,
            alias={7: 0, 8: 1, 9: 2},
        ),
        at, *doc_pieces[:2], g_first.x, g_first.other, qkv_bias, bias, group, qkv, probs,
    )
    att_pieces = (near, *trade(second(near), mixed_far))

    wide_f = shape_of((ROWS, D), f32)
    wide_b = shape_of((ROWS, D), bf16)
    attended, normed_low, normed_one, hat_one, scale_one = run(
        lambda *ins: call(
            partial(first_norm_kernel, width), ins,
            [wide_b, wide_b, wide_f, wide_f, shape_of((ROWS, 1), f32)],
            [pltpu.VMEM((ROWS, D), f32), pltpu.VMEM((ROWS, D), bf16)], scalars=1,
        ),
        at, *att_pieces, *proj_near, *proj_far, doc_rows, vec_one,
    )

    normed_pieces = group_of(normed_low)
    hid_f = shape_of((tp * ROWS, hidden), f32)
    hid_b = shape_of((tp * ROWS, hidden), bf16)
    ffn_weights = (g_up.x, g_up.other, g_down.x, g_down.other)
    normed_group, slope, act_low, keep, give = run(
        lambda *ins: call(
            partial(up_kernel, (0, 1)), ins, [group_out, hid_f, hid_b, wide_f, wide_b], scalars=1,
        ),
        at, *normed_pieces[:2], *ffn_weights, my_upb,
    )
    meet = Meet().near_pair(keep, give)
    normed_group, slope, act_low, keep, give = run(
        lambda *ins: call(
            partial(up_kernel, (2, 3)), ins, [group_out, hid_f, hid_b, wide_f, wide_b], scalars=1,
            alias={8: 0, 9: 1, 10: 2},
        ),
        at, *normed_pieces[2:], *ffn_weights, my_upb, normed_group, slope, act_low,
    )
    meet.far_pair(keep, give).send()
    encoded, d_ffn, d_resid_two, sums_two = run(
        lambda *ins: call(
            second_norm_kernel, ins,
            [shape_of((1, SLOTS, D), bf16), wide_b, wide_f, shape_of((3, D), f32)],
        ),
        *meet.terms(), normed_one, grad_in, live_row, vec_two,
    )

    d_ffn_pieces = group_of(d_ffn)
    ffn_weights = (g_down.x, g_down.other, g_up.x, g_up.other)
    sums_out = shape_of((2, hidden), f32)
    d_ffn_group, d_pre, d_up_bias, keep, give = run(
        lambda *ins: call(
            partial(down_back_kernel, (0, 1)), ins,
            [group_out, hid_b, sums_out, wide_f, wide_b], scalars=1,
        ),
        at, *d_ffn_pieces[:2], *ffn_weights, slope,
    )
    meet = Meet().near_pair(keep, give)
    d_ffn_group, d_pre, d_up_bias, keep, give = run(
        lambda *ins: call(
            partial(down_back_kernel, (2, 3)), ins,
            [group_out, hid_b, sums_out, wide_f, wide_b], scalars=1,
            alias={8: 0, 9: 1, 10: 2},
        ),
        at, *d_ffn_pieces[2:], *ffn_weights, slope, d_ffn_group, d_pre, d_up_bias,
    )
    meet.far_pair(keep, give)

    def half_grad(left, right, near, start=0, columns=None):
        out = shape_of((D if near is None else D // 2, columns or right.shape[1]), bf16)
        (made,) = run(
            lambda *ins: call(partial(half_grad_kernel, near, start), ins, [out]), left, right
        )
        return made

    meet.send()
    give = half_grad(d_ffn_group, act_low, False)
    s_down = Scatter(run, (give,), "dp", X_Z, given=give).send()
    give = half_grad(normed_group, d_pre, False)
    s_up = Scatter(run, (give,), "dp", Z_X, given=give).send()
    s_down.own(half_grad(d_ffn_group, act_low, True))
    s_up.own(half_grad(normed_group, d_pre, True))

    d_branch, d_resid_one, sums_one, a0, a1, a2 = run(
        lambda *ins: call(
            partial(first_back_kernel, width), ins,
            [wide_b, wide_f, shape_of((3, D), f32), doc_out, doc_out, pair_out],
            [pltpu.VMEM((ROWS, D), bf16)], scalars=1,
        ),
        at, *meet.terms(), d_resid_two, hat_one, scale_one, vec_one, *proj_near, *proj_far,
    )
    far = swap(a2, by_y)
    got_c = swap(a1, by_c)
    parts = run(
        lambda *ins: call(
            partial(proj_grad_kernel, width), ins, [col_out] * 4, scalars=1, cost=1.3
        ),
        at, attended, d_branch,
    )
    meet_proj = Meet().near_pair(parts[0], parts[1]).far_pair(parts[2], parts[3])
    grids = shape_of((3 * heads, NB, NB), f32)
    d_qkv, d_sums, d_grid = run(
        lambda *ins: call(
            partial(attend_back_kernel, heads, (0, 1), False), ins,
            [qkv_out, shape_of((tp, 3 * width), f32), grids], cost=10,
        ),
        qkv, probs, a0, got_c, notes,
    )
    got_far = swap(second(far), by_c)
    meet_proj.send()
    d_qkv, d_sums, d_grid, d_ext = run(
        lambda *ins: call(
            partial(attend_back_kernel, heads, (2, 3), True), ins,
            [qkv_out, shape_of((tp, 3 * width), f32), grids, shape_of((3 * heads, 2 * NB), f32)],
            alias={5: 0, 6: 1, 7: 2},
        ),
        qkv, probs, far, got_far, notes, d_qkv, d_sums, d_grid,
    )

    def with_proj(q, k, c, y, small):
        p = (k.astype(f32) + c.astype(f32) + y.astype(f32)).astype(bf16)
        return jnp.concatenate([q, p, small], axis=-1).astype(f32)

    give = half_grad(group, d_qkv, False, 0, D // 2)
    s_first = Scatter(run, (give,), "dp", Z_X, given=give).send()
    across = s_first.other
    run.wait(s_up.other, s_down.other)
    s_up.take().send()
    s_first.own(half_grad(group, d_qkv, True, 0, D // 2))
    grad_b = half_grad(group, d_qkv, None, D // 2, 3 * width - D // 2)
    plains = [pltpu.VMEM((24, D), f32)] * 2
    (small_grads,) = run(
        lambda *ins: call(
            partial(small_grads_kernel, heads, n_dev), ins, [shape_of((D, 128), bf16)],
            flats + plains, scalars=1,
        ),
        at, d_ext, d_sums, d_up_bias, sums_one, sums_two,
    )
    parts = run(
        lambda *ins: call(
            partial(tokens_back_kernel, width), ins, [wide_f, wide_b, wide_f, wide_b], scalars=1
        ),
        at, d_qkv, g_first.x, g_first.other,
    )
    meet_tok = Meet().near_pair(parts[0], parts[1]).far_pair(parts[2], parts[3])
    s_second = Scatter(
        run, (grad_b, *meet_proj.terms(), small_grads), "dp", Z_X, walk=(1, 2, 0), base=with_proj
    ).send()
    s_up.take().send()
    s_first.take().send()
    s_down.take().send(across)
    meet_tok.send()
    run.wait(s_down.other, s_second.other, s_first.other, s_up.other)
    s_down.take().send()
    s_second.take().send()
    s_first.take().send()

    def columns_back(scatters):
        sums = [x.sum().reshape(tp, rows, -1) for x in scatters]
        out = shape_of((2, rows, sum(x.shape[2] for x in sums)), bf16)

        def fn(at, *refs):
            for target, c in ((refs[-2], 1 - at[0] % 2), (refs[-1], at[0] % 2)):
                for y in range(2):
                    target[y] = jnp.concatenate([ref[2 * y + c] for ref in refs[:-2]], axis=1)

        return Exchange(run, at, *run(lambda *ins: call(fn, ins, [out, out], scalars=1), at, *sums))

    def whole_rows(exchanged, groups, widths, smalls):
        outs = [shape_of((rows, tp * g * w), f32) for g, w in zip(groups, widths)]
        ends = [shape_of((1, n * rows), f32) for n in smalls]

        def fn(at, mine, other, *refs):
            outs, ends = refs[: len(groups)], refs[len(groups) :]
            total = None
            for near, ref in ((True, mine), (False, other)):
                for n in range(2):
                    start, f = 0, source_of(at, near, n)
                    for out, g, w in zip(outs, groups, widths):
                        for i in range(g):
                            place = pl.multiple_of((i * tp + f) * w, w)
                            out[:, pl.ds(place, w)] = ref[n, :, start : start + w].astype(f32)
                            start += w
                    if ends:
                        part = ref[n, :, start:].astype(f32)
                        total = part if total is None else total + part
            if ends:
                small_outs(total, ends)

        return run(
            lambda *ins: call(fn, ins, outs + ends, scalars=1), at, exchanged.mine, exchanged.other
        )

    s_up.take()
    x_up = columns_back([s_up]).turn()
    s_second.take().send()
    run.wait(x_up.other, s_down.other, s_first.other, s_second.other)
    s_down.take()
    s_first.take()
    s_second.take()
    x_rest = columns_back([s_down, s_first, s_second])
    out_f = shape_of((1, SLOTS, D), f32)
    grad_tokens = run(
        lambda *ins: glue(
            lambda d, k, c, y: (
                d[...] + k[...] + c[...].astype(f32) + y[...].astype(f32)
            )[:SLOTS][None],
            [out_f], *ins,
        ),
        d_resid_one, *meet_tok.terms(),
    )
    x_rest.turn()
    (grad_up,) = whole_rows(x_up, (1,), (hidden,), ())
    grad_down, grad_qkv, grad_proj, *out = whole_rows(
        x_rest, (1, 3, 1), (hidden, width, width), (1,) * 6 + (2, 6, 4)
    )
    out = [x.reshape(-1) for x in out]
    return (
        encoded,
        grad_tokens,
        grad_qkv,
        out[6],
        grad_proj,
        out[0],
        out[1],
        out[2],
        out[7],
        grad_up,
        out[8],
        grad_down,
        out[3],
        out[4],
        out[5],
    )


def solution(mesh):
    split = ("dp", "fsdp")
    one, two, three = P(split), P(split, None), P(split, None, None)
    return jax.shard_map(
        local,
        mesh=mesh,
        in_specs=(
            three, three, one, two, two, two, two, one, two, one, one, one, one, two, one, two,
            one, one, one,
        ),
        out_specs=(
            three, three, two, one, two, one, one, one, one, two, one, two, one, one, one,
        ),
        check_vma=False,
    )
```

```python
from functools import partial

import jax
import jax.numpy as jnp
from jax import lax
from jax.experimental import pallas as pl
from jax.experimental.pallas import tpu as pltpu
from jax.sharding import PartitionSpec as P

D = 1024
H = 16
HD = 64
FF = 4096
NB = 128
TEXT = 120
SLOTS = 169
ROWS = 176
NEGATIVE = -1e30
EPSILON = 1e-05

f32 = jnp.float32
bf16 = jnp.bfloat16


def shape_of(shape, kind):
    return jax.ShapeDtypeStruct(tuple(shape), kind)


def call(kernel, ins, outs, scratch=(), scalars=0, alias=None, vmem=16, cost=0):
    spaces = [pltpu.SMEM] * scalars + [pltpu.VMEM] * (len(ins) - scalars)
    return pl.pallas_call(
        kernel,
        in_specs=[pl.BlockSpec(memory_space=m) for m in spaces],
        out_specs=[pl.BlockSpec(memory_space=pltpu.VMEM) for _ in outs],
        out_shape=list(outs),
        scratch_shapes=list(scratch),
        input_output_aliases=alias or {},
        cost_estimate=pl.CostEstimate(
            flops=int(cost * 1e9), bytes_accessed=0, transcendentals=0
        ),
        compiler_params=pltpu.CompilerParams(vmem_limit_bytes=vmem * 2**20),
    )(*ins)


def glue(fn, outs, *ins, scalars=0):
    def kernel(*refs):
        made = fn(*refs[: len(ins)])
        for out, value in zip(refs[len(ins) :], made if isinstance(made, tuple) else (made,)):
            out[...] = value

    made = call(kernel, ins, outs, scalars=scalars)
    return made[0] if len(outs) == 1 else made


def axis_bits(axis):
    bits, b = [], lax.axis_size(axis) // 2
    while b >= 1:
        bits.append((axis, b))
        b //= 2
    return bits


def swap(x, bit):
    axis, b = bit
    return lax.ppermute(x, axis, [(i, i ^ b) for i in range(lax.axis_size(axis))])


def side(bit):
    axis, b = bit
    return (lax.axis_index(axis) // b) % 2


def pair_up(mine, other, bit, pos):
    one = side(bit) == 1
    return jnp.stack([jnp.where(one, other, mine), jnp.where(one, mine, other)], axis=pos)


class Order:
    def __init__(self):
        self.last = ()

    def tie(self, args):
        if not self.last:
            return args
        return lax.optimization_barrier(tuple(args) + self.last)[: len(args)]

    def wait(self, *arrays):
        self.last = self.last + arrays

    def __call__(self, fn, *args):
        out = fn(*self.tie(args))
        self.last = tuple(jax.tree.leaves(out))
        return out


def after(x, *earlier):
    return lax.optimization_barrier((x,) + earlier)[0]


def high_bits(axis, order):
    bits = axis_bits(axis)
    return [bits[i] for i in order]


class Gather:
    def __init__(self, run, x, axis, order):
        self.run, self.x = run, x
        self.bits = axis_bits(axis)[3:][::-1] + high_bits(axis, order)
        while len(self.bits) > 3:
            self.send().join()

    def send(self, *earlier):
        self.other = swap(after(self.x, *earlier), self.bits[0])
        return self

    def join(self):
        bit = self.bits.pop(0)
        if len(self.bits) >= 3:
            self.x = self.run(
                lambda m, o: pair_up(m, o, bit, 0).reshape(-1, m.shape[1]), self.x, self.other
            )
        else:
            r, c = self.x.shape

            def join(m, o, out):
                out[:r], out[r:] = m[...], o[...]

            (self.x,) = self.run(
                lambda *ins: call(join, ins, [shape_of((2 * r, c), bf16)]), self.x, self.other
            )
        return self


class Scatter:
    def __init__(self, run, arrays, axis, order, walk=None, base=None, given=None):
        self.run = run
        self.high, rest = high_bits(axis, order), axis_bits(axis)[3:]
        have = self.high[::-1] + rest
        self.order = (high_bits(axis, walk) if walk else self.high[::-1]) + rest
        self.low = len(rest)
        if given is not None:
            have = [bit for bit in have if bit != self.order[0]]
            given = given.reshape((2,) * len(have) + (-1, given.shape[-1]))
        self.given = given
        arrays = tuple(a.reshape((2,) * len(have) + (-1, a.shape[-1])) for a in arrays)
        self.terms = [(arrays, have, [], base or (lambda x: x.astype(f32)))]

    def own(self, array):
        arrays, *rest = self.terms[0]
        self.terms[0] = ((array.reshape(arrays[0].shape),), *rest)

    def flat(self):
        return [a for arrays, *unused in self.terms for a in arrays]

    def value(self, flat, extra=()):
        flat, total = list(flat), None
        for arrays, have, cuts, base in self.terms:
            chosen = dict(list(cuts) + list(extra))
            at = tuple(
                slice(None) if bit not in chosen
                else (0 if chosen[bit] else 1) if bit in self.high
                else side(bit) if chosen[bit] else 1 - side(bit)
                for bit in have
            )
            part = base(*[flat.pop(0)[at] for unused in arrays])
            total = part if total is None else total + part
        return total

    def sum(self, extra=()):
        flat = self.flat()
        fn = lambda *f: self.value(f, extra).astype(bf16)
        if self.low:
            return self.run(fn, *flat)
        out = jax.eval_shape(fn, *flat)
        return self.run(lambda *f: glue(fn, [out], *f), *flat)

    def send(self, *earlier):
        bit = self.order[0]
        out = self.given if self.given is not None else self.sum([(bit, False)])
        self.other = swap(after(out, *earlier), bit)
        return self

    def take(self):
        bit = self.order.pop(0)
        for arrays, have, cuts, base in self.terms:
            if self.given is None:
                cuts.append((bit, True))
        self.given = None
        self.terms.append(((self.other,), list(self.order_left()), [], lambda x: x.astype(f32)))
        while 0 < len(self.order) <= self.low:
            self.send().take()
        return self

    def order_left(self):
        arrays, have, cuts, base = self.terms[0]
        gone = [bit for bit, keep in cuts]
        return [bit for bit in have if bit not in gone]


class Exchange:
    def __init__(self, run, at, give, keep):
        self.run, self.at, self.keep = run, at, keep
        self.other = swap(give, axis_bits("fsdp")[1])

    def turn(self, *earlier):
        def fn(at, keep, got, give, mine):
            y, c = at[0] // 2, at[0] % 2
            give[c], give[1 - c] = keep[1 - y], got[1 - y]
            mine[c], mine[1 - c] = keep[y], got[y]

        out = shape_of(self.keep.shape, self.keep.dtype)
        give, self.mine = self.run(
            lambda *ins: call(fn, ins, [out, out], scalars=1), self.at, self.keep, self.other
        )
        self.other = swap(after(give, *earlier), axis_bits("fsdp")[0])
        return self


def source_of(at, near, n):
    y = at[0] // 2
    return (y if near else 1 - y) * 2 + n


def dot_nn(a, b):
    return jnp.dot(a, b, preferred_element_type=f32)


def dot_nt(a, b):
    return lax.dot_general(a, b, (((1,), (1,)), ((), ())), preferred_element_type=f32)


def dot_tn(a, b):
    return lax.dot_general(a, b, (((0,), (0,)), ((), ())), preferred_element_type=f32)


def call_docs(kernel, docs, ins, in_whole, outs):
    def spec(a, whole):
        n = len(a.shape)
        if whole:
            return pl.BlockSpec(tuple(a.shape), lambda d: (0,) * n)
        return pl.BlockSpec((1,) + tuple(a.shape[1:]), lambda d: (d,) + (0,) * (n - 1))

    return pl.pallas_call(
        kernel,
        grid=(docs,),
        in_specs=[spec(a, w) for a, w in zip(ins, in_whole)],
        out_specs=[spec(a, False) for a in outs],
        out_shape=list(outs),
        cost_estimate=pl.CostEstimate(flops=0, bytes_accessed=0, transcendentals=0),
        compiler_params=pltpu.CompilerParams(vmem_limit_bytes=16 * 2**20),
    )(*ins)


def at_block(ref, me, j, size):
    return pl.ds(pl.multiple_of((me ^ j) * size, size), size)


BLOCK = D // 8
Z_X = (0, 1, 2)
X_Z = (0, 2, 1)
X_FIRST = (2, 1, 0)


def far_block(place, q, order):
    away = sum(((q >> n) & 1) * (4 >> bit) for n, bit in enumerate(order))
    return pl.ds(pl.multiple_of((place ^ away) * BLOCK, BLOCK), BLOCK)


def relative(src, dst, place, order, rows):
    for q in range(8):
        dst[rows, q * BLOCK : (q + 1) * BLOCK] = src[:, far_block(place, q, order)]


def doc_at(j):
    return slice(j * ROWS, (j + 1) * ROWS)


def hot_rows(notes, flip=False):
    buckets = lax.broadcasted_iota(jnp.int32, (NB, ROWS), 0).astype(f32)
    if flip:
        buckets = (NB - 1) - buckets
    return [(notes[r : r + 1, :ROWS] == buckets).astype(f32).astype(bf16) for r in (12, 9, 10)]


ROW_QV, ROW_TABLES, ROW_UP = 6, 7, 9
TILE_ROWS = 16


def pack_kernel(*refs):
    *smalls, out_ref = refs
    rows = smalls[0].shape[1]
    tile = jnp.zeros(out_ref.shape, f32)
    row = lax.broadcasted_iota(jnp.int32, out_ref.shape, 0)
    qv, tables, up = smalls[6:]
    parts = list(smalls[:6]) + [qv] + [tables.at[:, 3 * n * rows : 3 * (n + 1) * rows] for n in range(2)]
    for n, ref in enumerate(parts + [up]):
        value = ref[...].astype(f32)
        wide = jnp.concatenate(
            [value, jnp.zeros((1, 128 - value.shape[1]), f32)], axis=1
        ) if value.shape[1] < 128 else value
        tile = jnp.where(row == n, jnp.broadcast_to(wide, out_ref.shape), tile)
    out_ref[...] = tile.astype(bf16)


def unpack_kernel(heads, count, at_ref, all_ref, ext_ref, add_ref, up_ref, one_ref, two_ref, qv_ref, tab_ref, upb_ref):
    me, place = at_ref[0], at_ref[1]
    rows, width, low = D // count, heads * HD, count // 32
    for d in range(count):
        q = place ^ (d // (4 * low))
        block = (q * low + (d // 4) % low) * 4 + (me ^ (d % 4))
        place_of = pl.ds(pl.multiple_of(block * TILE_ROWS, TILE_ROWS), TILE_ROWS)
        tile = all_ref[place_of, :].astype(f32)
        at = slice(d * rows, (d + 1) * rows)
        one_ref[:, at] = tile[0:3, :rows]
        two_ref[:, at] = tile[3:6, :rows]
        qv_ref[:, 2 * d * rows : 2 * (d + 1) * rows] = tile[ROW_QV : ROW_QV + 1, : 2 * rows]
        for n in range(2):
            start = (2 * d + n) * 3 * rows
            row = tile[ROW_TABLES + n : ROW_TABLES + n + 1, : 3 * rows]
            tab_ref[:, start : start + 3 * rows] = row
        upb_ref[:, 4 * d * rows : 4 * (d + 1) * rows] = tile[ROW_UP : ROW_UP + 1, : 4 * rows]
    start = pl.multiple_of(me * width, width)
    add_ref[:, :width] = qv_ref[:, pl.ds(start, width)]
    add_ref[:, width : 2 * width] = jnp.zeros((1, width), f32)
    add_ref[:, 2 * width :] = qv_ref[:, pl.ds(D + start, width)]
    hidden = up_ref.shape[1]
    up_ref[...] = upb_ref[:, pl.ds(pl.multiple_of(me * hidden, hidden), hidden)]
    half = NB // 2
    for k in range(3):
        for h in range(heads):
            n = k * heads + h
            row = tab_ref[:, pl.ds(pl.multiple_of((k * H + me * heads + h) * NB, NB), NB)]
            ext_ref[n : n + 1, :half] = jnp.broadcast_to(row[:, :1], (1, half))
            ext_ref[n : n + 1, half : half + NB] = row
            ext_ref[n : n + 1, half + NB :] = jnp.broadcast_to(row[:, NB - 1 :], (1, half))


PIECES = 18


def small_grads_kernel(
    heads, count, at_ref, ext_ref, sums_ref, up_ref, one_ref, two_ref, out_ref,
    qv_ref, tab_ref, upb_ref, plain_ref, order_ref,
):
    me = at_ref[0]
    rows, width = D // count, heads * HD
    for ref in (qv_ref, tab_ref, upb_ref, plain_ref):
        ref[...] = jnp.zeros_like(ref)
    start = pl.multiple_of(me * width, width)
    sums = jnp.sum(sums_ref[...], axis=0, keepdims=True)
    qv_ref[:, pl.ds(start, width)] = sums[:, :width]
    qv_ref[:, pl.ds(D + start, width)] = sums[:, 2 * width :]
    hidden = up_ref.shape[1]
    upb_ref[:, pl.ds(pl.multiple_of(me * hidden, hidden), hidden)] = jnp.sum(
        up_ref[...], axis=0, keepdims=True
    )
    half = NB // 2
    lane = lax.broadcasted_iota(jnp.int32, (1, NB), 1)
    for k in range(3):
        for h in range(heads):
            row = ext_ref[k * heads + h : k * heads + h + 1, :]
            low = jnp.sum(row[:, :half], axis=1, keepdims=True)
            high = jnp.sum(row[:, half + NB :], axis=1, keepdims=True)
            grad = row[:, half : half + NB] + jnp.where(lane == 0, low, 0.0)
            grad = grad + jnp.where(lane == NB - 1, high, 0.0)
            tab_ref[:, pl.ds(pl.multiple_of((k * H + me * heads + h) * NB, NB), NB)] = grad
    plain_ref[0:3, :] = one_ref[...]
    plain_ref[3:6, :] = two_ref[...]
    for d in range(count):
        at = slice(d * rows, (d + 1) * rows)
        row = 6
        for ref, times in ((qv_ref, 2), (tab_ref, 6), (upb_ref, 4)):
            for n in range(times):
                begin = (d * times + n) * rows
                plain_ref[row : row + 1, at] = ref[:, begin : begin + rows]
                row += 1
    relative(plain_ref, order_ref, at_ref[1], Z_X, slice(None))
    shape = (plain_ref.shape[0], 128)
    same = lax.broadcasted_iota(jnp.int32, shape, 0) == lax.broadcasted_iota(jnp.int32, shape, 1)
    out_ref[...] = dot_tn(order_ref[...].astype(bf16), same.astype(f32).astype(bf16)).astype(bf16)


def small_outs(total, outs):
    rows = total.shape[0]
    shape = (rows, rows)
    same = lax.broadcasted_iota(jnp.int32, shape, 0) == lax.broadcasted_iota(jnp.int32, shape, 1)
    turned = lax.dot_general(
        total, same.astype(f32), (((0,), (0,)), ((), ())),
        precision=lax.Precision.HIGHEST, preferred_element_type=f32,
    )
    row = 0
    for out in outs:
        for n in range(out.shape[1] // rows):
            out[:, n * rows : (n + 1) * rows] = turned[row : row + 1, :]
            row += 1


def bias_kernel(heads, notes_ref, ext_ref, out_ref):
    notes = notes_ref[0].astype(f32)
    hots = hot_rows(notes)
    every_hot = jnp.concatenate(hots, axis=0)
    live = notes[11:12, :ROWS] > 0.5
    for h in range(heads):
        codes = []
        for k in range(3):
            row = ext_ref[k * heads + h : k * heads + h + 1, :]
            spread = jnp.broadcast_to(row, (NB, 2 * NB))
            skew = pltpu.roll(spread, NB, 1, stride=1, stride_axis=0)
            codes.append(dot_tn(hots[k], skew[:, :NB].astype(bf16)).astype(bf16))
        total = dot_nn(jnp.concatenate(codes, axis=1), every_hot)
        out_ref[0, h] = jnp.where(live, total, NEGATIVE)


def softmax_rows(q, k, bias):
    s = dot_nt(q, k) * 0.125 + bias
    e = jnp.exp(s - jnp.max(s, axis=-1, keepdims=True))
    return e / jnp.sum(e, axis=-1, keepdims=True)


def attend_kernel(heads, pair, at_ref, d0, d1, near_ref, far_ref, add_ref, bias_ref, *rest):
    group_ref, qkv_ref, probs_ref, mixed_ref = rest[-4:]
    width = heads * HD
    for j, piece in zip(pair, (d0, d1)):
        relative(piece, group_ref, at_ref[1], Z_X, doc_at(j))
    both = slice(pair[0] * ROWS, (pair[1] + 1) * ROWS)
    for n in range(3):
        at = slice(n * width, (n + 1) * width)
        qkv = dot_nn(group_ref[both, : D // 2], near_ref[:, at])
        qkv = qkv + dot_nn(group_ref[both, D // 2 :], far_ref[:, at])
        qkv_ref[both, at] = (qkv + add_ref[:, at]).astype(bf16)
    for n, j in enumerate(pair):
        outs = []
        for h in range(heads):
            q = qkv_ref[doc_at(j), h * HD : (h + 1) * HD]
            k = qkv_ref[doc_at(j), width + h * HD : width + (h + 1) * HD]
            v = qkv_ref[doc_at(j), 2 * width + h * HD : 2 * width + (h + 1) * HD]
            probs = softmax_rows(q, k, bias_ref[j, h])
            probs_ref[j, h] = probs
            outs.append(dot_nn(probs.astype(bf16), v).astype(bf16))
        mixed_ref[n] = jnp.concatenate(outs, axis=1)


def norm_parts(values):
    average = jnp.mean(values, axis=-1, keepdims=True)
    centred = values - average
    spread = jnp.mean(centred * centred, axis=-1, keepdims=True)
    scale = lax.rsqrt(spread + EPSILON)
    return centred * scale, scale


def norm_back(grad, gain, hat, scale):
    scaled = grad * gain
    first = jnp.mean(scaled, axis=-1, keepdims=True)
    second = jnp.mean(scaled * hat, axis=-1, keepdims=True)
    return (scaled - first - hat * second) * scale


def first_norm_kernel(
    width, at_ref, a0, a1, a2, a3, *rest
):
    near, far = rest[:4], rest[4:8]
    tokens_ref, vec_ref, att_ref, low_ref, normed_ref, hat_ref, scale_ref, branch_ref, plain_ref = rest[8:]
    me = at_ref[0]
    for j, piece in enumerate((a0[0], a1[...], a2[0], a3[...])):
        plain_ref[:, at_block(plain_ref, me, j, width)] = piece
    relative(plain_ref, att_ref, at_ref[1], Z_X, slice(None))
    left, right = att_ref[:, : D // 2], att_ref[:, D // 2 :]
    for j in range(4):
        branch_ref[:, at_block(branch_ref, me, j, width)] = dot_nn(left, near[j][...]) + dot_nn(
            right, far[j][...]
        )
    resid = tokens_ref[...].astype(f32) + branch_ref[...] + vec_ref[0:1, :]
    hat, scale = norm_parts(resid)
    normed = hat * vec_ref[1:2, :] + vec_ref[2:3, :]
    low_ref[...] = normed.astype(bf16)
    normed_ref[...] = normed
    hat_ref[...] = hat
    scale_ref[...] = scale


def parts_back(left, near_ref, far_ref, outs, place, order):
    for q in range(0, 8, 2):
        ref = near_ref if q < 4 else far_ref
        at = slice((q % 4) * BLOCK, (q % 4 + 2) * BLOCK)
        part = dot_nt(left, ref[at, :])
        for n, out in enumerate(outs):
            for half in range(2):
                block = part[doc_at(n), half * BLOCK : (half + 1) * BLOCK]
                out[:, far_block(place, q + half, order)] = block.astype(out.dtype)


def half_grad_kernel(near, left_ref, right_ref, out_ref):
    left = left_ref[:, : D // 2] if near else left_ref[:, D // 2 :]
    for n in range(right_ref.shape[1] // TILE):
        at = slice(n * TILE, (n + 1) * TILE)
        out_ref[:, at] = dot_tn(left, right_ref[:, at]).astype(bf16)


def normal_parts(u):
    density = jnp.exp(-0.5 * u * u)
    return 0.5 + 0.5 * lax.erf(u * (0.5**0.5)), u * density * ((2 * jnp.pi) ** -0.5)


TILE = 256


def up_kernel(pair, at_ref, x0, x1, up_near, up_far, down_near, down_far, add_ref, *rest):
    group_ref, slope_ref, act_ref, keep_ref, give_ref = rest[-5:]
    for j, piece in zip(pair, (x0, x1)):
        relative(piece, group_ref, at_ref[1], Z_X, doc_at(j))
    both = slice(pair[0] * ROWS, (pair[1] + 1) * ROWS)
    for n in range(act_ref.shape[1] // TILE):
        at = slice(n * TILE, (n + 1) * TILE)
        pre = dot_nn(group_ref[both, : D // 2], up_near[:, at])
        pre = pre + dot_nn(group_ref[both, D // 2 :], up_far[:, at]) + add_ref[:, at]
        below, tilt = normal_parts(pre)
        slope_ref[both, at] = below + tilt
        act_ref[both, at] = (pre * below).astype(bf16)
    parts_back(act_ref[both, :], down_near, down_far, (keep_ref, give_ref), at_ref[1], X_Z)


def down_back_kernel(pair, at_ref, g0, g1, down_near, down_far, up_near, up_far, slope_ref, *rest):
    group_ref, dpre_ref, sums_ref, keep_ref, give_ref = rest[-5:]
    for j, piece in zip(pair, (g0, g1)):
        relative(piece, group_ref, at_ref[1], X_Z, doc_at(j))
    both = slice(pair[0] * ROWS, (pair[1] + 1) * ROWS)
    for n in range(dpre_ref.shape[1] // TILE):
        at = slice(n * TILE, (n + 1) * TILE)
        d_act = dot_nn(group_ref[both, : D // 2], down_near[:, at])
        d_act = d_act + dot_nn(group_ref[both, D // 2 :], down_far[:, at])
        d_pre = (d_act * slope_ref[both, at]).astype(bf16)
        dpre_ref[both, at] = d_pre
        sums_ref[pair[0] // 2 : pair[0] // 2 + 1, at] = jnp.sum(d_pre.astype(f32), axis=0, keepdims=True)
    parts_back(dpre_ref[both, :], up_near, up_far, (keep_ref, give_ref), at_ref[1], Z_X)


def second_norm_kernel(
    keep_ref, got_c, got_y, normed_ref, grad_ref, live_ref, vec_ref,
    enc_ref, dffn_ref, dres_ref, sums_ref,
):
    ffn = keep_ref[...] + got_c[...].astype(f32) + got_y[...].astype(f32) + vec_ref[0:1, :]
    hat, scale = norm_parts(normed_ref[...] + ffn)
    ones = jnp.ones((8, 128), bf16)
    live = dot_tn(live_ref[...].astype(bf16), ones)[:, :1]
    gain = vec_ref[1:2, :]
    enc = ((hat * gain + vec_ref[2:3, :]) * live).astype(bf16)
    enc_ref[0] = enc[:SLOTS]
    grad = grad_ref[...].astype(f32) * live
    d_resid = norm_back(grad, gain, hat, scale)
    dres_ref[...] = d_resid
    low = d_resid.astype(bf16)
    dffn_ref[...] = low
    sums_ref[0:1, :] = jnp.sum(low.astype(f32), axis=0, keepdims=True)
    sums_ref[1:2, :] = jnp.sum(grad * hat, axis=0, keepdims=True)
    sums_ref[2:3, :] = jnp.sum(grad, axis=0, keepdims=True)


def first_back_kernel(width, at_ref, keep_ref, got_c, got_y, dres_ref, hat_ref, scale_ref, vec_ref, *rest):
    near, far = rest[:4], rest[4:8]
    branch_ref, done_ref, sums_ref, a0_ref, a1_ref, a2_ref, plain_ref = rest[8:]
    me = at_ref[0]
    hat = hat_ref[...]
    grad = dres_ref[...] + keep_ref[...] + got_c[...].astype(f32) + got_y[...].astype(f32)
    d_one = norm_back(grad, vec_ref[1:2, :], hat, scale_ref[...])
    done_ref[...] = d_one
    low = d_one.astype(bf16)
    branch_ref[...] = low
    sums_ref[0:1, :] = jnp.sum(low.astype(f32), axis=0, keepdims=True)
    sums_ref[1:2, :] = jnp.sum(grad * hat, axis=0, keepdims=True)
    sums_ref[2:3, :] = jnp.sum(grad, axis=0, keepdims=True)
    for n, proj in enumerate((near, far)):
        total = None
        for j in range(4):
            part = dot_nt(branch_ref[:, at_block(branch_ref, me, j, width)], proj[j][...])
            total = part if total is None else total + part
        for q in range(4):
            plain_ref[:, far_block(at_ref[1], 4 * n + q, Z_X)] = total[
                :, q * BLOCK : (q + 1) * BLOCK
            ].astype(bf16)
    for i, out in enumerate((a0_ref, a1_ref, a2_ref.at[0], a2_ref.at[1])):
        out[...] = plain_ref[:, at_block(plain_ref, me, i, width)]


def proj_grad_kernel(width, at_ref, att_ref, branch_ref, *outs):
    me = at_ref[0]
    att = att_ref[...]
    for j, out in enumerate(outs):
        out[...] = dot_tn(att, branch_ref[:, at_block(branch_ref, me, j, width)]).astype(bf16)


def attend_back_kernel(heads, pair, last, qkv_ref, probs_ref, g0, g1, notes_ref, *rest):
    dqkv_ref, sums_ref, grid_ref = rest[-4:-1] if last else rest[-3:]
    width = heads * HD
    for j, grad_ref in zip(pair, (g0.at[0] if last else g0, g1)):
        notes = notes_ref[j].astype(f32)
        hots = jnp.concatenate(hot_rows(notes), axis=0)
        flipped = hot_rows(notes, flip=True)
        for h in range(heads):
            q = qkv_ref[doc_at(j), h * HD : (h + 1) * HD]
            k = qkv_ref[doc_at(j), width + h * HD : width + (h + 1) * HD]
            v = qkv_ref[doc_at(j), 2 * width + h * HD : 2 * width + (h + 1) * HD]
            g = grad_ref[:, h * HD : (h + 1) * HD]
            p = probs_ref[j, h]
            dp = dot_nt(g, v)
            ds = (p * (dp - jnp.sum(p * dp, axis=-1, keepdims=True))).astype(bf16)
            dq = (dot_nn(ds, k) * 0.125).astype(bf16)
            dk = (dot_tn(ds, q) * 0.125).astype(bf16)
            dv = dot_tn(p.astype(bf16), g).astype(bf16)
            for c, d in enumerate((dq, dk, dv)):
                at = slice(c * width + h * HD, c * width + (h + 1) * HD)
                dqkv_ref[doc_at(j), at] = d
            part = dot_nt(ds, hots).astype(bf16)
            for n in range(3):
                term = dot_nn(flipped[n], part[:, n * NB : (n + 1) * NB])
                if j == 0:
                    grid_ref[n * heads + h] = term
                else:
                    grid_ref[n * heads + h] += term
        sums_ref[j : j + 1, :] = jnp.sum(dqkv_ref[doc_at(j), :].astype(f32), axis=0, keepdims=True)
    if last:
        ext_ref = rest[-1]
        for n in range(3 * heads):
            wide = jnp.concatenate([grid_ref[n], jnp.zeros((NB, NB), f32)], axis=1)
            skew = pltpu.roll(wide, 1, 1, stride=1, stride_axis=0)
            ext_ref[n : n + 1, :] = jnp.sum(skew, axis=0, keepdims=True)


def tokens_back_kernel(width, at_ref, d_ref, near_ref, far_ref, *outs):
    for q in range(0, 8, 2):
        ref = near_ref if q < 4 else far_ref
        at = slice((q % 4) * BLOCK, (q % 4 + 2) * BLOCK)
        part = dot_nt(d_ref[...], ref[at, : 3 * width])
        for n, out in enumerate(outs):
            for half in range(2):
                block = part[doc_at(n), half * BLOCK : (half + 1) * BLOCK]
                out[:, far_block(at_ref[1], q + half, Z_X)] = block.astype(out.dtype)


def pad_rows(x):
    return jnp.pad(x, ((0, ROWS - SLOTS), (0, 0)))


def local(
    tokens,
    out_grad,
    text_len,
    x_bucket,
    y_bucket,
    patch_mask,
    qkv_weight,
    qv_bias,
    proj_weight,
    proj_bias,
    first_gain,
    first_shift,
    rel_tables,
    up_weight,
    up_bias,
    down_weight,
    down_bias,
    second_gain,
    second_shift,
):
    inner = axis_bits("fsdp")
    outer = axis_bits("dp")
    tp = 4
    by_y, by_c = inner
    dpn = lax.axis_size("dp")
    n_dev = tp * dpn
    rows = D // n_dev
    heads = H // tp
    width = heads * HD
    hidden = FF // tp
    me = lax.axis_index("fsdp")
    place = lax.axis_index("dp") // (dpn // 8)
    at = jnp.stack([me, place]).astype(jnp.int32)
    run = Order()
    run.wait(at)
    doc_out = shape_of((ROWS, width), bf16)

    def group_of(own):
        far = swap(own, by_y)
        return own, swap(own, by_c), far, swap(far, by_c)

    def second(pair):
        return run(lambda p: glue(lambda ref: ref[1], [doc_out], p), pair)

    def trade(p1, far):
        return swap(p1, by_c), far, swap(second(far), by_c)

    class Meet:
        def near_pair(self, keep, give):
            self.keep, self.near = keep, swap(give, by_c)
            return self

        def far_pair(self, keep, give):
            self.held, self.both = keep, swap(give, by_c)
            return self

        def send(self):
            out = shape_of(self.held.shape, bf16)
            fn = lambda k, g: (k[...].astype(f32) + g[...].astype(f32)).astype(bf16)
            both = run(lambda *ins: glue(fn, [out], *ins), self.held, self.both)
            self.far = swap(both, by_y)
            return self

        def terms(self):
            return self.keep, self.near, self.far

    def column_blocks(shards, groups):
        widths = [a.shape[1] // (g * tp) for a, g in zip(shards, groups)]
        out = shape_of((2, rows, sum(w * g for w, g in zip(widths, groups))), bf16)

        def fn(at, *refs):
            for target, c in ((refs[-2], 1 - at[0] % 2), (refs[-1], at[0] % 2)):
                for y in range(2):
                    start = 0
                    for ref, w, g in zip(refs, widths, groups):
                        for n in range(g):
                            place = pl.multiple_of((n * tp + 2 * y + c) * w, w)
                            target[y, :, start : start + w] = ref[:, pl.ds(place, w)]
                            start += w

        return Exchange(
            run, at,
            *run(lambda *ins: call(fn, ins, [out, out], scalars=1), at, *shards),
        )

    def block_rows(exchanged, parts):
        cols = exchanged.mine.shape[2] // parts

        def fn(at, mine, other, *outs):
            for near, ref in ((True, mine), (False, other)):
                for n in range(2):
                    for p, out in enumerate(outs):
                        out[source_of(at, near, n)] = ref[n, :, p * cols : (p + 1) * cols]

        outs = run(
            lambda *ins: call(fn, ins, [shape_of((tp, rows, cols), bf16)] * parts, scalars=1),
            at, exchanged.mine, exchanged.other,
        )
        return [o.reshape(tp * rows, cols) for o in outs]

    ex_first = column_blocks((qkv_weight, proj_weight), (3, 1))

    smalls = [
        proj_bias, first_gain, first_shift, down_bias, second_gain, second_shift,
        qv_bias, rel_tables, up_bias,
    ]
    flats = [pltpu.VMEM((1, n), f32) for n in (2 * D, 3 * H * NB, FF)]

    places = jnp.arange(TEXT, dtype=jnp.int32)
    live_own = jnp.concatenate(
        [places[None, :] < text_len[:, None], patch_mask > 0], axis=1
    ).astype(f32)

    def document(tokens, x_bucket, y_bucket, live):
        pad_cols = ((0, 0), (0, D - SLOTS))
        positions = (jnp.arange(SLOTS, dtype=jnp.int32) * NB // SLOTS)[None]
        return jnp.concatenate(
            [
                tokens[0],
                jnp.pad(x_bucket.astype(bf16), pad_cols),
                jnp.pad(y_bucket.astype(bf16), pad_cols),
                jnp.pad(live.astype(bf16), pad_cols),
                jnp.pad(positions.astype(bf16), pad_cols),
                jnp.zeros((ROWS - SLOTS - 4, D), bf16),
            ],
            axis=0,
        )

    ex_ffn = column_blocks((up_weight, down_weight), (1, 1))
    ex_first.turn()
    ex_ffn.turn(ex_first.other)
    doc_rows = run(document, tokens, x_bucket, y_bucket, live_own)
    (packed,) = run(
        lambda *ins: call(pack_kernel, [x[None] for x in ins], [shape_of((TILE_ROWS, 128), bf16)]),
        *smalls,
    )

    def beside(m, o):
        r = m.shape[0]

        def join(m, o, out):
            out[:r], out[r:] = m[...], o[...]

        return run(lambda *ins: call(join, ins, [shape_of((2 * r, 128), bf16)]), m, o)[0]

    small_near = swap(packed, by_c)
    grad_in, live_row = run(
        lambda g, l: (pad_rows(g[0]), jnp.pad(l, ((0, 7), (0, ROWS - SLOTS)))), out_grad, live_own
    )
    pair = beside(packed, small_near)
    small_far = swap(pair, by_y)
    g_first = Gather(run, *block_rows(ex_first, 1), "dp", Z_X).send()
    g_small = Gather(run, beside(pair, small_far), "dp", X_FIRST).send()
    doc_far = swap(after(doc_rows, ex_ffn.other, small_far), by_y)
    doc_near = swap(doc_rows, by_c)
    up_own, down_own = block_rows(ex_ffn, 2)
    g_small.join().send()
    g_small.join().send()
    g_down = Gather(run, down_own, "dp", X_Z)
    g_first.join().send()
    g_down.send(g_first.x)
    doc_pieces = (doc_rows, doc_near, doc_far, swap(after(doc_far, g_first.x), by_c))

    def take_notes(*refs):
        for n in range(4):
            refs[4][n] = refs[n][ROWS - 16 :, : 2 * NB]

    (notes,) = run(
        lambda *ins: call(take_notes, ins, [shape_of((tp, 16, 2 * NB), bf16)]), *doc_pieces
    )
    run.wait(g_small.other)
    g_down.join()
    g_first.join().send()
    g_down.send()
    g_up = Gather(run, up_own, "dp", Z_X).send(g_down.x)
    ext, qkv_bias, my_upb, vec_one, vec_two = run(
        lambda *ins: call(
            partial(unpack_kernel, heads, n_dev), ins,
            [
                shape_of((3 * heads, 2 * NB), f32), shape_of((1, 3 * width), f32),
                shape_of((1, hidden), f32), shape_of((3, D), f32), shape_of((3, D), f32),
            ],
            flats, scalars=1,
        ),
        at, beside(g_small.x, g_small.other),
    )

    (bias,) = run(
        lambda *ins: call_docs(
            partial(bias_kernel, heads), tp, ins, [False, True],
            [shape_of((tp, heads, ROWS, ROWS), f32)],
        ),
        notes, ext,
    )
    g_up.join().send()
    col_out = shape_of((D, width), bf16)
    half_out = shape_of((D // 2, width), bf16)

    def proj_part(rows_of):
        return group_of(
            run(lambda w: glue(lambda ref: ref[:, 3 * width :], [half_out], w), rows_of)
        )

    proj_near = proj_part(g_first.x)
    g_up.join()
    run.wait(*proj_near)

    proj_far = proj_part(g_first.other)
    pair_out = shape_of((2, ROWS, width), bf16)
    group_out = shape_of((tp * ROWS, D), bf16)
    qkv_out = shape_of((tp * ROWS, 3 * width), bf16)
    probs_out = shape_of((tp, heads, ROWS, ROWS), f32)
    group, qkv, probs, far = run(
        lambda *ins: call(
            partial(attend_kernel, heads, (2, 3)), ins,
            [group_out, qkv_out, probs_out, pair_out], scalars=1,
        ),
        at, *doc_pieces[2:], g_first.x, g_first.other, qkv_bias, bias,
    )
    mixed_far = swap(far, by_y)
    g_up.send(g_first.other)
    g_down.join().send()
    group, qkv, probs, near = run(
        lambda *ins: call(
            partial(attend_kernel, heads, (0, 1)), ins,
            [group_out, qkv_out, probs_out, pair_out], scalars=1,
            alias={7: 0, 8: 1, 9: 2},
        ),
        at, *doc_pieces[:2], g_first.x, g_first.other, qkv_bias, bias, group, qkv, probs,
    )
    att_pieces = (near, *trade(second(near), mixed_far))

    wide_f = shape_of((ROWS, D), f32)
    wide_b = shape_of((ROWS, D), bf16)
    attended, normed_low, normed_one, hat_one, scale_one = run(
        lambda *ins: call(
            partial(first_norm_kernel, width), ins,
            [wide_b, wide_b, wide_f, wide_f, shape_of((ROWS, 1), f32)],
            [pltpu.VMEM((ROWS, D), f32), pltpu.VMEM((ROWS, D), bf16)], scalars=1,
        ),
        at, *att_pieces, *proj_near, *proj_far, doc_rows, vec_one,
    )

    normed_pieces = group_of(normed_low)
    hid_f = shape_of((tp * ROWS, hidden), f32)
    hid_b = shape_of((tp * ROWS, hidden), bf16)
    ffn_weights = (g_up.x, g_up.other, g_down.x, g_down.other)
    normed_group, slope, act_low, keep, give = run(
        lambda *ins: call(
            partial(up_kernel, (0, 1)), ins, [group_out, hid_f, hid_b, wide_f, wide_b], scalars=1,
        ),
        at, *normed_pieces[:2], *ffn_weights, my_upb,
    )
    meet = Meet().near_pair(keep, give)
    normed_group, slope, act_low, keep, give = run(
        lambda *ins: call(
            partial(up_kernel, (2, 3)), ins, [group_out, hid_f, hid_b, wide_f, wide_b], scalars=1,
            alias={8: 0, 9: 1, 10: 2},
        ),
        at, *normed_pieces[2:], *ffn_weights, my_upb, normed_group, slope, act_low,
    )
    meet.far_pair(keep, give).send()
    encoded, d_ffn, d_resid_two, sums_two = run(
        lambda *ins: call(
            second_norm_kernel, ins,
            [shape_of((1, SLOTS, D), bf16), wide_b, wide_f, shape_of((3, D), f32)],
        ),
        *meet.terms(), normed_one, grad_in, live_row, vec_two,
    )

    d_ffn_pieces = group_of(d_ffn)
    ffn_weights = (g_down.x, g_down.other, g_up.x, g_up.other)
    sums_out = shape_of((2, hidden), f32)
    d_ffn_group, d_pre, d_up_bias, keep, give = run(
        lambda *ins: call(
            partial(down_back_kernel, (0, 1)), ins,
            [group_out, hid_b, sums_out, wide_f, wide_b], scalars=1,
        ),
        at, *d_ffn_pieces[:2], *ffn_weights, slope,
    )
    meet = Meet().near_pair(keep, give)
    d_ffn_group, d_pre, d_up_bias, keep, give = run(
        lambda *ins: call(
            partial(down_back_kernel, (2, 3)), ins,
            [group_out, hid_b, sums_out, wide_f, wide_b], scalars=1,
            alias={8: 0, 9: 1, 10: 2},
        ),
        at, *d_ffn_pieces[2:], *ffn_weights, slope, d_ffn_group, d_pre, d_up_bias,
    )
    meet.far_pair(keep, give)

    def half_grad(left, right, near):
        out = shape_of((D // 2, right.shape[1]), bf16)
        (made,) = run(lambda *ins: call(partial(half_grad_kernel, near), ins, [out]), left, right)
        return made

    meet.send()
    give = half_grad(d_ffn_group, act_low, False)
    s_down = Scatter(run, (give,), "dp", X_Z, given=give).send()
    give = half_grad(normed_group, d_pre, False)
    s_up = Scatter(run, (give,), "dp", Z_X, given=give).send()
    s_down.own(half_grad(d_ffn_group, act_low, True))
    s_up.own(half_grad(normed_group, d_pre, True))

    d_branch, d_resid_one, sums_one, a0, a1, a2 = run(
        lambda *ins: call(
            partial(first_back_kernel, width), ins,
            [wide_b, wide_f, shape_of((3, D), f32), doc_out, doc_out, pair_out],
            [pltpu.VMEM((ROWS, D), bf16)], scalars=1,
        ),
        at, *meet.terms(), d_resid_two, hat_one, scale_one, vec_one, *proj_near, *proj_far,
    )
    far = swap(a2, by_y)
    got_c = swap(a1, by_c)
    parts = run(
        lambda *ins: call(
            partial(proj_grad_kernel, width), ins, [col_out] * 4, scalars=1, cost=1.3
        ),
        at, attended, d_branch,
    )
    meet_proj = Meet().near_pair(parts[0], parts[1]).far_pair(parts[2], parts[3])
    grids = shape_of((3 * heads, NB, NB), f32)
    d_qkv, d_sums, d_grid = run(
        lambda *ins: call(
            partial(attend_back_kernel, heads, (0, 1), False), ins,
            [qkv_out, shape_of((tp, 3 * width), f32), grids], cost=10,
        ),
        qkv, probs, a0, got_c, notes,
    )
    got_far = swap(second(far), by_c)
    meet_proj.send()
    d_qkv, d_sums, d_grid, d_ext = run(
        lambda *ins: call(
            partial(attend_back_kernel, heads, (2, 3), True), ins,
            [qkv_out, shape_of((tp, 3 * width), f32), grids, shape_of((3 * heads, 2 * NB), f32)],
            alias={5: 0, 6: 1, 7: 2},
        ),
        qkv, probs, far, got_far, notes, d_qkv, d_sums, d_grid,
    )

    def with_proj(k, c, y, small):
        p = (k.astype(f32) + c.astype(f32) + y.astype(f32)).astype(bf16)
        return jnp.concatenate([p, small], axis=-1).astype(f32)

    give = half_grad(group, d_qkv, False)
    s_first = Scatter(run, (give,), "dp", Z_X, given=give).send()
    run.wait(s_up.other, s_down.other)
    s_up.take().send()
    s_down.take().send()
    s_first.own(half_grad(group, d_qkv, True))
    plains = [pltpu.VMEM((24, D), f32)] * 2
    (small_grads,) = run(
        lambda *ins: call(
            partial(small_grads_kernel, heads, n_dev), ins, [shape_of((D, 128), bf16)],
            flats + plains, scalars=1,
        ),
        at, d_ext, d_sums, d_up_bias, sums_one, sums_two,
    )
    parts = run(
        lambda *ins: call(
            partial(tokens_back_kernel, width), ins, [wide_f, wide_b, wide_f, wide_b], scalars=1
        ),
        at, d_qkv, g_first.x, g_first.other,
    )
    meet_tok = Meet().near_pair(parts[0], parts[1]).far_pair(parts[2], parts[3])
    s_second = Scatter(
        run, (*meet_proj.terms(), small_grads), "dp", Z_X, base=with_proj
    ).send()
    s_up.take().send()
    s_first.take().send()
    run.wait(s_first.other)
    s_first.take().send()
    meet_tok.send()
    run.wait(s_up.other, s_down.other, s_second.other, s_first.other)
    s_second.take().send()
    s_down.take().send()

    def columns_back(scatters):
        sums = [x.sum().reshape(tp, rows, -1) for x in scatters]
        out = shape_of((2, rows, sum(x.shape[2] for x in sums)), bf16)

        def fn(at, *refs):
            for target, c in ((refs[-2], 1 - at[0] % 2), (refs[-1], at[0] % 2)):
                for y in range(2):
                    target[y] = jnp.concatenate([ref[2 * y + c] for ref in refs[:-2]], axis=1)

        return Exchange(run, at, *run(lambda *ins: call(fn, ins, [out, out], scalars=1), at, *sums))

    def whole_rows(exchanged, groups, widths, smalls):
        outs = [shape_of((rows, tp * g * w), f32) for g, w in zip(groups, widths)]
        ends = [shape_of((1, n * rows), f32) for n in smalls]

        def fn(at, mine, other, *refs):
            outs, ends = refs[: len(groups)], refs[len(groups) :]
            total = None
            for near, ref in ((True, mine), (False, other)):
                for n in range(2):
                    start, f = 0, source_of(at, near, n)
                    for out, g, w in zip(outs, groups, widths):
                        for i in range(g):
                            place = pl.multiple_of((i * tp + f) * w, w)
                            out[:, pl.ds(place, w)] = ref[n, :, start : start + w].astype(f32)
                            start += w
                    if ends:
                        part = ref[n, :, start:].astype(f32)
                        total = part if total is None else total + part
            if ends:
                small_outs(total, ends)

        return run(
            lambda *ins: call(fn, ins, outs + ends, scalars=1), at, exchanged.mine, exchanged.other
        )

    s_up.take()
    x_up = columns_back([s_up]).turn()
    out_f = shape_of((1, SLOTS, D), f32)
    grad_tokens = run(
        lambda *ins: glue(
            lambda d, k, c, y: (
                d[...] + k[...] + c[...].astype(f32) + y[...].astype(f32)
            )[:SLOTS][None],
            [out_f], *ins,
        ),
        d_resid_one, *meet_tok.terms(),
    )
    run.wait(s_second.other, x_up.other)
    s_second.take().send()
    run.wait(s_down.other, s_second.other)
    s_down.take()
    s_first.take()
    s_second.take()
    x_rest = columns_back([s_down, s_first, s_second])
    x_rest.turn()
    (grad_up,) = whole_rows(x_up, (1,), (hidden,), ())
    grad_down, grad_qkv, grad_proj, *out = whole_rows(
        x_rest, (1, 3, 1), (hidden, width, width), (1,) * 6 + (2, 6, 4)
    )
    out = [x.reshape(-1) for x in out]
    return (
        encoded,
        grad_tokens,
        grad_qkv,
        out[6],
        grad_proj,
        out[0],
        out[1],
        out[2],
        out[7],
        grad_up,
        out[8],
        grad_down,
        out[3],
        out[4],
        out[5],
    )


def solution(mesh):
    split = ("dp", "fsdp")
    one, two, three = P(split), P(split, None), P(split, None, None)
    return jax.shard_map(
        local,
        mesh=mesh,
        in_specs=(
            three, three, one, two, two, two, two, one, two, one, one, one, one, two, one, two,
            one, one, one,
        ),
        out_specs=(
            three, three, two, one, two, one, one, one, one, two, one, two, one, one, one,
        ),
        check_vma=False,
    )
```

```python
from functools import partial

import jax
import jax.numpy as jnp
from jax import lax
from jax.experimental import pallas as pl
from jax.experimental.pallas import tpu as pltpu
from jax.sharding import PartitionSpec as P

D = 1024
H = 16
HD = 64
FF = 4096
NB = 128
TEXT = 120
SLOTS = 169
ROWS = 176
NEGATIVE = -1e30
EPSILON = 1e-05

f32 = jnp.float32
bf16 = jnp.bfloat16


def shape_of(shape, kind):
    return jax.ShapeDtypeStruct(tuple(shape), kind)


def call(kernel, ins, outs, scratch=(), scalars=0, alias=None, vmem=16, cost=0):
    spaces = [pltpu.SMEM] * scalars + [pltpu.VMEM] * (len(ins) - scalars)
    return pl.pallas_call(
        kernel,
        in_specs=[pl.BlockSpec(memory_space=m) for m in spaces],
        out_specs=[pl.BlockSpec(memory_space=pltpu.VMEM) for _ in outs],
        out_shape=list(outs),
        scratch_shapes=list(scratch),
        input_output_aliases=alias or {},
        cost_estimate=pl.CostEstimate(
            flops=int(cost * 1e9), bytes_accessed=0, transcendentals=0
        ),
        compiler_params=pltpu.CompilerParams(vmem_limit_bytes=vmem * 2**20),
    )(*ins)


def glue(fn, outs, *ins, scalars=0):
    def kernel(*refs):
        made = fn(*refs[: len(ins)])
        for out, value in zip(refs[len(ins) :], made if isinstance(made, tuple) else (made,)):
            out[...] = value

    made = call(kernel, ins, outs, scalars=scalars)
    return made[0] if len(outs) == 1 else made


def axis_bits(axis):
    bits, b = [], lax.axis_size(axis) // 2
    while b >= 1:
        bits.append((axis, b))
        b //= 2
    return bits


def swap(x, bit):
    axis, b = bit
    return lax.ppermute(x, axis, [(i, i ^ b) for i in range(lax.axis_size(axis))])


def side(bit):
    axis, b = bit
    return (lax.axis_index(axis) // b) % 2


def pair_up(mine, other, bit, pos):
    one = side(bit) == 1
    return jnp.stack([jnp.where(one, other, mine), jnp.where(one, mine, other)], axis=pos)


class Order:
    def __init__(self):
        self.last = ()

    def tie(self, args):
        if not self.last:
            return args
        return lax.optimization_barrier(tuple(args) + self.last)[: len(args)]

    def wait(self, *arrays):
        self.last = self.last + arrays

    def __call__(self, fn, *args):
        out = fn(*self.tie(args))
        self.last = tuple(jax.tree.leaves(out))
        return out


def after(x, *earlier):
    return lax.optimization_barrier((x,) + earlier)[0]


def high_bits(axis, order):
    bits = axis_bits(axis)
    return [bits[i] for i in order]


class Gather:
    def __init__(self, run, x, axis, order):
        self.run, self.x = run, x
        self.bits = axis_bits(axis)[3:][::-1] + high_bits(axis, order)
        while len(self.bits) > 3:
            self.send().join()

    def send(self, *earlier):
        self.other = swap(after(self.x, *earlier), self.bits[0])
        return self

    def join(self):
        bit = self.bits.pop(0)
        if len(self.bits) >= 3:
            self.x = self.run(
                lambda m, o: pair_up(m, o, bit, 0).reshape(-1, m.shape[1]), self.x, self.other
            )
        else:
            r, c = self.x.shape

            def join(m, o, out):
                out[:r], out[r:] = m[...], o[...]

            (self.x,) = self.run(
                lambda *ins: call(join, ins, [shape_of((2 * r, c), bf16)]), self.x, self.other
            )
        return self


class Scatter:
    def __init__(self, run, arrays, axis, order, walk=None, base=None, given=None):
        self.run = run
        self.high, rest = high_bits(axis, order), axis_bits(axis)[3:]
        have = self.high[::-1] + rest
        self.order = (high_bits(axis, walk) if walk else self.high[::-1]) + rest
        self.low = len(rest)
        if given is not None:
            have = [bit for bit in have if bit != self.order[0]]
            given = given.reshape((2,) * len(have) + (-1, given.shape[-1]))
        self.given = given
        arrays = tuple(a.reshape((2,) * len(have) + (-1, a.shape[-1])) for a in arrays)
        self.terms = [(arrays, have, [], base or (lambda x: x.astype(f32)))]

    def own(self, array):
        arrays, *rest = self.terms[0]
        self.terms[0] = ((array.reshape(arrays[0].shape),), *rest)

    def flat(self):
        return [a for arrays, *unused in self.terms for a in arrays]

    def value(self, flat, extra=()):
        flat, total = list(flat), None
        for arrays, have, cuts, base in self.terms:
            chosen = dict(list(cuts) + list(extra))
            at = tuple(
                slice(None) if bit not in chosen
                else (0 if chosen[bit] else 1) if bit in self.high
                else side(bit) if chosen[bit] else 1 - side(bit)
                for bit in have
            )
            part = base(*[flat.pop(0)[at] for unused in arrays])
            total = part if total is None else total + part
        return total

    def sum(self, extra=()):
        flat = self.flat()
        fn = lambda *f: self.value(f, extra).astype(bf16)
        if self.low:
            return self.run(fn, *flat)
        out = jax.eval_shape(fn, *flat)
        return self.run(lambda *f: glue(fn, [out], *f), *flat)

    def send(self, *earlier):
        bit = self.order[0]
        out = self.given if self.given is not None else self.sum([(bit, False)])
        self.other = swap(after(out, *earlier), bit)
        return self

    def take(self):
        bit = self.order.pop(0)
        for arrays, have, cuts, base in self.terms:
            if self.given is None:
                cuts.append((bit, True))
        self.given = None
        self.terms.append(((self.other,), list(self.order_left()), [], lambda x: x.astype(f32)))
        while 0 < len(self.order) <= self.low:
            self.send().take()
        return self

    def order_left(self):
        arrays, have, cuts, base = self.terms[0]
        gone = [bit for bit, keep in cuts]
        return [bit for bit in have if bit not in gone]


class Exchange:
    def __init__(self, run, at, give, keep):
        self.run, self.at, self.keep = run, at, keep
        self.other = swap(give, axis_bits("fsdp")[1])

    def turn(self, *earlier):
        def fn(at, keep, got, give, mine):
            y, c = at[0] // 2, at[0] % 2
            give[c], give[1 - c] = keep[1 - y], got[1 - y]
            mine[c], mine[1 - c] = keep[y], got[y]

        out = shape_of(self.keep.shape, self.keep.dtype)
        give, self.mine = self.run(
            lambda *ins: call(fn, ins, [out, out], scalars=1), self.at, self.keep, self.other
        )
        self.other = swap(after(give, *earlier), axis_bits("fsdp")[0])
        return self


def source_of(at, near, n):
    y = at[0] // 2
    return (y if near else 1 - y) * 2 + n


def dot_nn(a, b):
    return jnp.dot(a, b, preferred_element_type=f32)


def dot_nt(a, b):
    return lax.dot_general(a, b, (((1,), (1,)), ((), ())), preferred_element_type=f32)


def dot_tn(a, b):
    return lax.dot_general(a, b, (((0,), (0,)), ((), ())), preferred_element_type=f32)


def call_docs(kernel, docs, ins, in_whole, outs):
    def spec(a, whole):
        n = len(a.shape)
        if whole:
            return pl.BlockSpec(tuple(a.shape), lambda d: (0,) * n)
        return pl.BlockSpec((1,) + tuple(a.shape[1:]), lambda d: (d,) + (0,) * (n - 1))

    return pl.pallas_call(
        kernel,
        grid=(docs,),
        in_specs=[spec(a, w) for a, w in zip(ins, in_whole)],
        out_specs=[spec(a, False) for a in outs],
        out_shape=list(outs),
        cost_estimate=pl.CostEstimate(flops=0, bytes_accessed=0, transcendentals=0),
        compiler_params=pltpu.CompilerParams(vmem_limit_bytes=16 * 2**20),
    )(*ins)


def at_block(ref, me, j, size):
    return pl.ds(pl.multiple_of((me ^ j) * size, size), size)


BLOCK = D // 8
Z_X = (0, 1, 2)
X_Z = (0, 2, 1)
X_FIRST = (2, 1, 0)


def far_block(place, q, order):
    away = sum(((q >> n) & 1) * (4 >> bit) for n, bit in enumerate(order))
    return pl.ds(pl.multiple_of((place ^ away) * BLOCK, BLOCK), BLOCK)


def relative(src, dst, place, order, rows):
    for q in range(8):
        dst[rows, q * BLOCK : (q + 1) * BLOCK] = src[:, far_block(place, q, order)]


def doc_at(j):
    return slice(j * ROWS, (j + 1) * ROWS)


def hot_rows(notes, flip=False):
    buckets = lax.broadcasted_iota(jnp.int32, (NB, ROWS), 0).astype(f32)
    if flip:
        buckets = (NB - 1) - buckets
    return [(notes[r : r + 1, :ROWS] == buckets).astype(f32).astype(bf16) for r in (12, 9, 10)]


ROW_QV, ROW_TABLES, ROW_UP = 6, 7, 9
TILE_ROWS = 16


def pack_kernel(*refs):
    *smalls, out_ref = refs
    rows = smalls[0].shape[1]
    tile = jnp.zeros(out_ref.shape, f32)
    row = lax.broadcasted_iota(jnp.int32, out_ref.shape, 0)
    qv, tables, up = smalls[6:]
    parts = list(smalls[:6]) + [qv] + [tables.at[:, 3 * n * rows : 3 * (n + 1) * rows] for n in range(2)]
    for n, ref in enumerate(parts + [up]):
        value = ref[...].astype(f32)
        wide = jnp.concatenate(
            [value, jnp.zeros((1, 128 - value.shape[1]), f32)], axis=1
        ) if value.shape[1] < 128 else value
        tile = jnp.where(row == n, jnp.broadcast_to(wide, out_ref.shape), tile)
    out_ref[...] = tile.astype(bf16)


def unpack_kernel(heads, count, at_ref, all_ref, ext_ref, add_ref, up_ref, one_ref, two_ref, qv_ref, tab_ref, upb_ref):
    me, place = at_ref[0], at_ref[1]
    rows, width, low = D // count, heads * HD, count // 32
    for d in range(count):
        q = place ^ (d // (4 * low))
        block = (q * low + (d // 4) % low) * 4 + (me ^ (d % 4))
        place_of = pl.ds(pl.multiple_of(block * TILE_ROWS, TILE_ROWS), TILE_ROWS)
        tile = all_ref[place_of, :].astype(f32)
        at = slice(d * rows, (d + 1) * rows)
        one_ref[:, at] = tile[0:3, :rows]
        two_ref[:, at] = tile[3:6, :rows]
        qv_ref[:, 2 * d * rows : 2 * (d + 1) * rows] = tile[ROW_QV : ROW_QV + 1, : 2 * rows]
        for n in range(2):
            start = (2 * d + n) * 3 * rows
            row = tile[ROW_TABLES + n : ROW_TABLES + n + 1, : 3 * rows]
            tab_ref[:, start : start + 3 * rows] = row
        upb_ref[:, 4 * d * rows : 4 * (d + 1) * rows] = tile[ROW_UP : ROW_UP + 1, : 4 * rows]
    start = pl.multiple_of(me * width, width)
    add_ref[:, :width] = qv_ref[:, pl.ds(start, width)]
    add_ref[:, width : 2 * width] = jnp.zeros((1, width), f32)
    add_ref[:, 2 * width :] = qv_ref[:, pl.ds(D + start, width)]
    hidden = up_ref.shape[1]
    up_ref[...] = upb_ref[:, pl.ds(pl.multiple_of(me * hidden, hidden), hidden)]
    half = NB // 2
    for k in range(3):
        for h in range(heads):
            n = k * heads + h
            row = tab_ref[:, pl.ds(pl.multiple_of((k * H + me * heads + h) * NB, NB), NB)]
            ext_ref[n : n + 1, :half] = jnp.broadcast_to(row[:, :1], (1, half))
            ext_ref[n : n + 1, half : half + NB] = row
            ext_ref[n : n + 1, half + NB :] = jnp.broadcast_to(row[:, NB - 1 :], (1, half))


PIECES = 18


def small_grads_kernel(
    heads, count, at_ref, ext_ref, sums_ref, up_ref, one_ref, two_ref, out_ref,
    qv_ref, tab_ref, upb_ref, plain_ref, order_ref,
):
    me = at_ref[0]
    rows, width = D // count, heads * HD
    for ref in (qv_ref, tab_ref, upb_ref, plain_ref):
        ref[...] = jnp.zeros_like(ref)
    start = pl.multiple_of(me * width, width)
    sums = jnp.sum(sums_ref[...], axis=0, keepdims=True)
    qv_ref[:, pl.ds(start, width)] = sums[:, :width]
    qv_ref[:, pl.ds(D + start, width)] = sums[:, 2 * width :]
    hidden = up_ref.shape[1]
    upb_ref[:, pl.ds(pl.multiple_of(me * hidden, hidden), hidden)] = jnp.sum(
        up_ref[...], axis=0, keepdims=True
    )
    half = NB // 2
    lane = lax.broadcasted_iota(jnp.int32, (1, NB), 1)
    for k in range(3):
        for h in range(heads):
            row = ext_ref[k * heads + h : k * heads + h + 1, :]
            low = jnp.sum(row[:, :half], axis=1, keepdims=True)
            high = jnp.sum(row[:, half + NB :], axis=1, keepdims=True)
            grad = row[:, half : half + NB] + jnp.where(lane == 0, low, 0.0)
            grad = grad + jnp.where(lane == NB - 1, high, 0.0)
            tab_ref[:, pl.ds(pl.multiple_of((k * H + me * heads + h) * NB, NB), NB)] = grad
    plain_ref[0:3, :] = one_ref[...]
    plain_ref[3:6, :] = two_ref[...]
    for d in range(count):
        at = slice(d * rows, (d + 1) * rows)
        row = 6
        for ref, times in ((qv_ref, 2), (tab_ref, 6), (upb_ref, 4)):
            for n in range(times):
                begin = (d * times + n) * rows
                plain_ref[row : row + 1, at] = ref[:, begin : begin + rows]
                row += 1
    relative(plain_ref, order_ref, at_ref[1], Z_X, slice(None))
    shape = (plain_ref.shape[0], 128)
    same = lax.broadcasted_iota(jnp.int32, shape, 0) == lax.broadcasted_iota(jnp.int32, shape, 1)
    out_ref[...] = dot_tn(order_ref[...].astype(bf16), same.astype(f32).astype(bf16)).astype(bf16)


def small_outs(total, outs):
    rows = total.shape[0]
    shape = (rows, rows)
    same = lax.broadcasted_iota(jnp.int32, shape, 0) == lax.broadcasted_iota(jnp.int32, shape, 1)
    turned = lax.dot_general(
        total, same.astype(f32), (((0,), (0,)), ((), ())),
        precision=lax.Precision.HIGHEST, preferred_element_type=f32,
    )
    row = 0
    for out in outs:
        for n in range(out.shape[1] // rows):
            out[:, n * rows : (n + 1) * rows] = turned[row : row + 1, :]
            row += 1


def bias_kernel(heads, notes_ref, ext_ref, out_ref):
    notes = notes_ref[0].astype(f32)
    hots = hot_rows(notes)
    every_hot = jnp.concatenate(hots, axis=0)
    live = notes[11:12, :ROWS] > 0.5
    for h in range(heads):
        codes = []
        for k in range(3):
            row = ext_ref[k * heads + h : k * heads + h + 1, :]
            spread = jnp.broadcast_to(row, (NB, 2 * NB))
            skew = pltpu.roll(spread, NB, 1, stride=1, stride_axis=0)
            codes.append(dot_tn(hots[k], skew[:, :NB].astype(bf16)).astype(bf16))
        total = dot_nn(jnp.concatenate(codes, axis=1), every_hot)
        out_ref[0, h] = jnp.where(live, total, NEGATIVE)


def softmax_rows(q, k, bias):
    s = dot_nt(q, k) * 0.125 + bias
    e = jnp.exp(s - jnp.max(s, axis=-1, keepdims=True))
    return e * (1.0 / jnp.sum(e, axis=-1, keepdims=True))


def attend_kernel(heads, pair, at_ref, d0, d1, near_ref, far_ref, add_ref, bias_ref, *rest):
    group_ref, qkv_ref, probs_ref, mixed_ref = rest[-4:]
    width = heads * HD
    for j, piece in zip(pair, (d0, d1)):
        relative(piece, group_ref, at_ref[1], Z_X, doc_at(j))
    both = slice(pair[0] * ROWS, (pair[1] + 1) * ROWS)
    for n in range(3):
        at = slice(n * width, (n + 1) * width)
        qkv = dot_nn(group_ref[both, : D // 2], near_ref[:, at])
        qkv = qkv + dot_nn(group_ref[both, D // 2 :], far_ref[:, at])
        qkv_ref[both, at] = (qkv + add_ref[:, at]).astype(bf16)
    for n, j in enumerate(pair):
        outs = []
        for h in range(heads):
            q = qkv_ref[doc_at(j), h * HD : (h + 1) * HD]
            k = qkv_ref[doc_at(j), width + h * HD : width + (h + 1) * HD]
            v = qkv_ref[doc_at(j), 2 * width + h * HD : 2 * width + (h + 1) * HD]
            probs = softmax_rows(q, k, bias_ref[j, h])
            probs_ref[j, h] = probs
            outs.append(dot_nn(probs.astype(bf16), v).astype(bf16))
        mixed_ref[n] = jnp.concatenate(outs, axis=1)


def norm_parts(values):
    average = jnp.mean(values, axis=-1, keepdims=True)
    centred = values - average
    spread = jnp.mean(centred * centred, axis=-1, keepdims=True)
    scale = lax.rsqrt(spread + EPSILON)
    return centred * scale, scale


def norm_back(grad, gain, hat, scale):
    scaled = grad * gain
    first = jnp.mean(scaled, axis=-1, keepdims=True)
    second = jnp.mean(scaled * hat, axis=-1, keepdims=True)
    return (scaled - first - hat * second) * scale


def first_norm_kernel(
    width, at_ref, a0, a1, a2, a3, *rest
):
    near, far = rest[:4], rest[4:8]
    tokens_ref, vec_ref, att_ref, low_ref, normed_ref, hat_ref, scale_ref, branch_ref, plain_ref = rest[8:]
    me = at_ref[0]
    for j, piece in enumerate((a0[0], a1[...], a2[0], a3[...])):
        plain_ref[:, at_block(plain_ref, me, j, width)] = piece
    relative(plain_ref, att_ref, at_ref[1], Z_X, slice(None))
    left, right = att_ref[:, : D // 2], att_ref[:, D // 2 :]
    for j in range(4):
        branch_ref[:, at_block(branch_ref, me, j, width)] = dot_nn(left, near[j][...]) + dot_nn(
            right, far[j][...]
        )
    resid = tokens_ref[...].astype(f32) + branch_ref[...] + vec_ref[0:1, :]
    hat, scale = norm_parts(resid)
    normed = hat * vec_ref[1:2, :] + vec_ref[2:3, :]
    low_ref[...] = normed.astype(bf16)
    normed_ref[...] = normed
    hat_ref[...] = hat
    scale_ref[...] = scale


def parts_back(left, near_ref, far_ref, outs, place, order):
    for q in range(0, 8, 2):
        ref = near_ref if q < 4 else far_ref
        at = slice((q % 4) * BLOCK, (q % 4 + 2) * BLOCK)
        part = dot_nt(left, ref[at, :])
        for n, out in enumerate(outs):
            for half in range(2):
                block = part[doc_at(n), half * BLOCK : (half + 1) * BLOCK]
                out[:, far_block(place, q + half, order)] = block.astype(out.dtype)


def half_grad_kernel(near, left_ref, right_ref, out_ref):
    left = left_ref[:, : D // 2] if near else left_ref[:, D // 2 :]
    for n in range(right_ref.shape[1] // TILE):
        at = slice(n * TILE, (n + 1) * TILE)
        out_ref[:, at] = dot_tn(left, right_ref[:, at]).astype(bf16)


def normal_below(u):
    return 0.5 + 0.5 * lax.erf(u * (0.5**0.5))


def slope_kernel(pre_ref, slope_ref):
    for n in range(pre_ref.shape[1] // TILE):
        at = slice(n * TILE, (n + 1) * TILE)
        u = pre_ref[:, at]
        density = jnp.exp(-0.5 * u * u) * ((2 * jnp.pi) ** -0.5)
        slope_ref[:, at] = normal_below(u) + u * density


TILE = 256


def up_kernel(pair, at_ref, x0, x1, up_near, up_far, down_near, down_far, add_ref, *rest):
    group_ref, slope_ref, act_ref, keep_ref, give_ref = rest[-5:]
    for j, piece in zip(pair, (x0, x1)):
        relative(piece, group_ref, at_ref[1], Z_X, doc_at(j))
    both = slice(pair[0] * ROWS, (pair[1] + 1) * ROWS)
    for n in range(act_ref.shape[1] // TILE):
        at = slice(n * TILE, (n + 1) * TILE)
        pre = dot_nn(group_ref[both, : D // 2], up_near[:, at])
        pre = pre + dot_nn(group_ref[both, D // 2 :], up_far[:, at]) + add_ref[:, at]
        slope_ref[both, at] = pre
        act_ref[both, at] = (pre * normal_below(pre)).astype(bf16)
    parts_back(act_ref[both, :], down_near, down_far, (keep_ref, give_ref), at_ref[1], X_Z)


def down_back_kernel(pair, at_ref, g0, g1, down_near, down_far, up_near, up_far, slope_ref, *rest):
    group_ref, dpre_ref, sums_ref, keep_ref, give_ref = rest[-5:]
    for j, piece in zip(pair, (g0, g1)):
        relative(piece, group_ref, at_ref[1], X_Z, doc_at(j))
    both = slice(pair[0] * ROWS, (pair[1] + 1) * ROWS)
    for n in range(dpre_ref.shape[1] // TILE):
        at = slice(n * TILE, (n + 1) * TILE)
        d_act = dot_nn(group_ref[both, : D // 2], down_near[:, at])
        d_act = d_act + dot_nn(group_ref[both, D // 2 :], down_far[:, at])
        d_pre = (d_act * slope_ref[both, at]).astype(bf16)
        dpre_ref[both, at] = d_pre
        sums_ref[pair[0] // 2 : pair[0] // 2 + 1, at] = jnp.sum(d_pre.astype(f32), axis=0, keepdims=True)
    parts_back(dpre_ref[both, :], up_near, up_far, (keep_ref, give_ref), at_ref[1], Z_X)


def second_norm_kernel(
    keep_ref, got_c, got_y, normed_ref, grad_ref, live_ref, vec_ref,
    enc_ref, dffn_ref, dres_ref, sums_ref,
):
    ffn = keep_ref[...] + got_c[...].astype(f32) + got_y[...].astype(f32) + vec_ref[0:1, :]
    hat, scale = norm_parts(normed_ref[...] + ffn)
    ones = jnp.ones((8, 128), bf16)
    live = dot_tn(live_ref[...].astype(bf16), ones)[:, :1]
    gain = vec_ref[1:2, :]
    enc = ((hat * gain + vec_ref[2:3, :]) * live).astype(bf16)
    enc_ref[0] = enc[:SLOTS]
    grad = grad_ref[...].astype(f32) * live
    d_resid = norm_back(grad, gain, hat, scale)
    dres_ref[...] = d_resid
    low = d_resid.astype(bf16)
    dffn_ref[...] = low
    sums_ref[0:1, :] = jnp.sum(low.astype(f32), axis=0, keepdims=True)
    sums_ref[1:2, :] = jnp.sum(grad * hat, axis=0, keepdims=True)
    sums_ref[2:3, :] = jnp.sum(grad, axis=0, keepdims=True)


def first_back_kernel(width, at_ref, keep_ref, got_c, got_y, dres_ref, hat_ref, scale_ref, vec_ref, *rest):
    near, far = rest[:4], rest[4:8]
    branch_ref, done_ref, sums_ref, a0_ref, a1_ref, a2_ref, plain_ref = rest[8:]
    me = at_ref[0]
    hat = hat_ref[...]
    grad = dres_ref[...] + keep_ref[...] + got_c[...].astype(f32) + got_y[...].astype(f32)
    d_one = norm_back(grad, vec_ref[1:2, :], hat, scale_ref[...])
    done_ref[...] = d_one
    low = d_one.astype(bf16)
    branch_ref[...] = low
    sums_ref[0:1, :] = jnp.sum(low.astype(f32), axis=0, keepdims=True)
    sums_ref[1:2, :] = jnp.sum(grad * hat, axis=0, keepdims=True)
    sums_ref[2:3, :] = jnp.sum(grad, axis=0, keepdims=True)
    for n, proj in enumerate((near, far)):
        total = None
        for j in range(4):
            part = dot_nt(branch_ref[:, at_block(branch_ref, me, j, width)], proj[j][...])
            total = part if total is None else total + part
        for q in range(4):
            plain_ref[:, far_block(at_ref[1], 4 * n + q, Z_X)] = total[
                :, q * BLOCK : (q + 1) * BLOCK
            ].astype(bf16)
    for i, out in enumerate((a0_ref, a1_ref, a2_ref.at[0], a2_ref.at[1])):
        out[...] = plain_ref[:, at_block(plain_ref, me, i, width)]


def proj_grad_kernel(width, at_ref, att_ref, branch_ref, *outs):
    me = at_ref[0]
    att = att_ref[...]
    for j, out in enumerate(outs):
        out[...] = dot_tn(att, branch_ref[:, at_block(branch_ref, me, j, width)]).astype(bf16)


def attend_back_kernel(heads, pair, last, qkv_ref, probs_ref, g0, g1, notes_ref, *rest):
    ds_ref, wide_ref = rest[-2:]
    dqkv_ref, sums_ref, grid_ref = rest[-6:-3] if last else rest[-5:-2]
    width = heads * HD
    for j, grad_ref in zip(pair, (g0.at[0] if last else g0, g1)):
        notes = notes_ref[j].astype(f32)
        hots = jnp.concatenate(hot_rows(notes), axis=0)
        flipped = hot_rows(notes, flip=True)
        for h in range(heads):
            q = qkv_ref[doc_at(j), h * HD : (h + 1) * HD]
            k = qkv_ref[doc_at(j), width + h * HD : width + (h + 1) * HD]
            v = qkv_ref[doc_at(j), 2 * width + h * HD : 2 * width + (h + 1) * HD]
            g = grad_ref[:, h * HD : (h + 1) * HD]
            p = probs_ref[j, h]
            dp = dot_nt(g, v)
            ds = (p * (dp - jnp.sum(p * dp, axis=-1, keepdims=True))).astype(bf16)
            ds_ref[doc_at(h), :] = ds
            dq = (dot_nn(ds, k) * 0.125).astype(bf16)
            dk = (dot_tn(ds, q) * 0.125).astype(bf16)
            dv = dot_tn(p.astype(bf16), g).astype(bf16)
            for c, d in enumerate((dq, dk, dv)):
                at = slice(c * width + h * HD, c * width + (h + 1) * HD)
                dqkv_ref[doc_at(j), at] = d
        part = dot_nt(ds_ref[...], hots).astype(bf16)
        for n in range(3):
            for h in range(heads):
                wide_ref[:, h * NB : (h + 1) * NB] = part[doc_at(h), n * NB : (n + 1) * NB]
            term = dot_nn(flipped[n], wide_ref[...])
            if j == 0:
                grid_ref[n] = term
            else:
                grid_ref[n] += term
        sums_ref[j : j + 1, :] = jnp.sum(dqkv_ref[doc_at(j), :].astype(f32), axis=0, keepdims=True)
    if last:
        ext_ref = rest[-3]
        for n in range(3 * heads):
            block = grid_ref[n // heads, :, (n % heads) * NB : (n % heads + 1) * NB]
            wide = jnp.concatenate([block, jnp.zeros((NB, NB), f32)], axis=1)
            skew = pltpu.roll(wide, 1, 1, stride=1, stride_axis=0)
            ext_ref[n : n + 1, :] = jnp.sum(skew, axis=0, keepdims=True)


def tokens_back_kernel(width, at_ref, d_ref, near_ref, far_ref, *outs):
    for q in range(0, 8, 2):
        ref = near_ref if q < 4 else far_ref
        at = slice((q % 4) * BLOCK, (q % 4 + 2) * BLOCK)
        part = dot_nt(d_ref[...], ref[at, : 3 * width])
        for n, out in enumerate(outs):
            for half in range(2):
                block = part[doc_at(n), half * BLOCK : (half + 1) * BLOCK]
                out[:, far_block(at_ref[1], q + half, Z_X)] = block.astype(out.dtype)


def pad_rows(x):
    return jnp.pad(x, ((0, ROWS - SLOTS), (0, 0)))


def local(
    tokens,
    out_grad,
    text_len,
    x_bucket,
    y_bucket,
    patch_mask,
    qkv_weight,
    qv_bias,
    proj_weight,
    proj_bias,
    first_gain,
    first_shift,
    rel_tables,
    up_weight,
    up_bias,
    down_weight,
    down_bias,
    second_gain,
    second_shift,
):
    inner = axis_bits("fsdp")
    outer = axis_bits("dp")
    tp = 4
    by_y, by_c = inner
    dpn = lax.axis_size("dp")
    n_dev = tp * dpn
    rows = D // n_dev
    heads = H // tp
    width = heads * HD
    hidden = FF // tp
    me = lax.axis_index("fsdp")
    place = lax.axis_index("dp") // (dpn // 8)
    at = jnp.stack([me, place]).astype(jnp.int32)
    run = Order()
    run.wait(at)
    doc_out = shape_of((ROWS, width), bf16)

    def group_of(own):
        far = swap(own, by_y)
        return own, swap(own, by_c), far, swap(far, by_c)

    def second(pair):
        return run(lambda p: glue(lambda ref: ref[1], [doc_out], p), pair)

    def trade(p1, far):
        return swap(p1, by_c), far, swap(second(far), by_c)

    class Meet:
        def near_pair(self, keep, give):
            self.keep, self.near = keep, swap(give, by_c)
            return self

        def far_pair(self, keep, give):
            self.held, self.both = keep, swap(give, by_c)
            return self

        def send(self):
            out = shape_of(self.held.shape, bf16)
            fn = lambda k, g: (k[...].astype(f32) + g[...].astype(f32)).astype(bf16)
            both = run(lambda *ins: glue(fn, [out], *ins), self.held, self.both)
            self.far = swap(both, by_y)
            return self

        def terms(self):
            return self.keep, self.near, self.far

    def column_blocks(shards, groups):
        widths = [a.shape[1] // (g * tp) for a, g in zip(shards, groups)]
        out = shape_of((2, rows, sum(w * g for w, g in zip(widths, groups))), bf16)

        def fn(at, *refs):
            for target, c in ((refs[-2], 1 - at[0] % 2), (refs[-1], at[0] % 2)):
                for y in range(2):
                    start = 0
                    for ref, w, g in zip(refs, widths, groups):
                        for n in range(g):
                            place = pl.multiple_of((n * tp + 2 * y + c) * w, w)
                            target[y, :, start : start + w] = ref[:, pl.ds(place, w)]
                            start += w

        return Exchange(
            run, at,
            *run(lambda *ins: call(fn, ins, [out, out], scalars=1), at, *shards),
        )

    def block_rows(exchanged, parts):
        cols = exchanged.mine.shape[2] // parts

        def fn(at, mine, other, *outs):
            for near, ref in ((True, mine), (False, other)):
                for n in range(2):
                    for p, out in enumerate(outs):
                        out[source_of(at, near, n)] = ref[n, :, p * cols : (p + 1) * cols]

        outs = run(
            lambda *ins: call(fn, ins, [shape_of((tp, rows, cols), bf16)] * parts, scalars=1),
            at, exchanged.mine, exchanged.other,
        )
        return [o.reshape(tp * rows, cols) for o in outs]

    ex_first = column_blocks((qkv_weight, proj_weight), (3, 1))

    smalls = [
        proj_bias, first_gain, first_shift, down_bias, second_gain, second_shift,
        qv_bias, rel_tables, up_bias,
    ]
    flats = [pltpu.VMEM((1, n), f32) for n in (2 * D, 3 * H * NB, FF)]

    places = jnp.arange(TEXT, dtype=jnp.int32)
    live_own = jnp.concatenate(
        [places[None, :] < text_len[:, None], patch_mask > 0], axis=1
    ).astype(f32)

    def document(tokens, x_bucket, y_bucket, live):
        pad_cols = ((0, 0), (0, D - SLOTS))
        positions = (jnp.arange(SLOTS, dtype=jnp.int32) * NB // SLOTS)[None]
        return jnp.concatenate(
            [
                tokens[0],
                jnp.pad(x_bucket.astype(bf16), pad_cols),
                jnp.pad(y_bucket.astype(bf16), pad_cols),
                jnp.pad(live.astype(bf16), pad_cols),
                jnp.pad(positions.astype(bf16), pad_cols),
                jnp.zeros((ROWS - SLOTS - 4, D), bf16),
            ],
            axis=0,
        )

    ex_ffn = column_blocks((up_weight, down_weight), (1, 1))
    ex_first.turn()
    ex_ffn.turn(ex_first.other)
    doc_rows = run(document, tokens, x_bucket, y_bucket, live_own)
    (packed,) = run(
        lambda *ins: call(pack_kernel, [x[None] for x in ins], [shape_of((TILE_ROWS, 128), bf16)]),
        *smalls,
    )

    def beside(m, o):
        r = m.shape[0]

        def join(m, o, out):
            out[:r], out[r:] = m[...], o[...]

        return run(lambda *ins: call(join, ins, [shape_of((2 * r, 128), bf16)]), m, o)[0]

    small_near = swap(packed, by_c)
    grad_in, live_row = run(
        lambda g, l: (pad_rows(g[0]), jnp.pad(l, ((0, 7), (0, ROWS - SLOTS)))), out_grad, live_own
    )
    pair = beside(packed, small_near)
    small_far = swap(pair, by_y)
    g_first = Gather(run, *block_rows(ex_first, 1), "dp", Z_X).send()
    g_small = Gather(run, beside(pair, small_far), "dp", X_FIRST).send()
    doc_far = swap(after(doc_rows, ex_ffn.other, small_far), by_y)
    doc_near = swap(doc_rows, by_c)
    up_own, down_own = block_rows(ex_ffn, 2)
    g_small.join().send()
    g_small.join().send()
    g_down = Gather(run, down_own, "dp", X_Z)
    g_first.join().send()
    g_down.send(g_first.x)
    doc_pieces = (doc_rows, doc_near, doc_far, swap(after(doc_far, g_first.x), by_c))

    def take_notes(*refs):
        for n in range(4):
            refs[4][n] = refs[n][ROWS - 16 :, : 2 * NB]

    (notes,) = run(
        lambda *ins: call(take_notes, ins, [shape_of((tp, 16, 2 * NB), bf16)]), *doc_pieces
    )
    run.wait(g_small.other)
    g_down.join()
    g_first.join().send()
    g_down.send()
    g_up = Gather(run, up_own, "dp", Z_X).send(g_down.x)
    ext, qkv_bias, my_upb, vec_one, vec_two = run(
        lambda *ins: call(
            partial(unpack_kernel, heads, n_dev), ins,
            [
                shape_of((3 * heads, 2 * NB), f32), shape_of((1, 3 * width), f32),
                shape_of((1, hidden), f32), shape_of((3, D), f32), shape_of((3, D), f32),
            ],
            flats, scalars=1,
        ),
        at, beside(g_small.x, g_small.other),
    )

    (bias,) = run(
        lambda *ins: call_docs(
            partial(bias_kernel, heads), tp, ins, [False, True],
            [shape_of((tp, heads, ROWS, ROWS), f32)],
        ),
        notes, ext,
    )
    g_up.join().send()
    col_out = shape_of((D, width), bf16)
    half_out = shape_of((D // 2, width), bf16)

    def proj_part(rows_of):
        return group_of(
            run(lambda w: glue(lambda ref: ref[:, 3 * width :], [half_out], w), rows_of)
        )

    proj_near = proj_part(g_first.x)
    g_up.join()
    run.wait(*proj_near)

    proj_far = proj_part(g_first.other)
    pair_out = shape_of((2, ROWS, width), bf16)
    group_out = shape_of((tp * ROWS, D), bf16)
    qkv_out = shape_of((tp * ROWS, 3 * width), bf16)
    probs_out = shape_of((tp, heads, ROWS, ROWS), f32)
    group, qkv, probs, far = run(
        lambda *ins: call(
            partial(attend_kernel, heads, (2, 3)), ins,
            [group_out, qkv_out, probs_out, pair_out], scalars=1,
        ),
        at, *doc_pieces[2:], g_first.x, g_first.other, qkv_bias, bias,
    )
    mixed_far = swap(far, by_y)
    g_up.send(g_first.other)
    g_down.join().send()
    group, qkv, probs, near = run(
        lambda *ins: call(
            partial(attend_kernel, heads, (0, 1)), ins,
            [group_out, qkv_out, probs_out, pair_out], scalars=1,
            alias={7: 0, 8: 1, 9: 2},
        ),
        at, *doc_pieces[:2], g_first.x, g_first.other, qkv_bias, bias, group, qkv, probs,
    )
    att_pieces = (near, *trade(second(near), mixed_far))

    wide_f = shape_of((ROWS, D), f32)
    wide_b = shape_of((ROWS, D), bf16)
    attended, normed_low, normed_one, hat_one, scale_one = run(
        lambda *ins: call(
            partial(first_norm_kernel, width), ins,
            [wide_b, wide_b, wide_f, wide_f, shape_of((ROWS, 1), f32)],
            [pltpu.VMEM((ROWS, D), f32), pltpu.VMEM((ROWS, D), bf16)], scalars=1,
        ),
        at, *att_pieces, *proj_near, *proj_far, doc_rows, vec_one,
    )

    normed_pieces = group_of(normed_low)
    hid_f = shape_of((tp * ROWS, hidden), f32)
    hid_b = shape_of((tp * ROWS, hidden), bf16)
    ffn_weights = (g_up.x, g_up.other, g_down.x, g_down.other)
    normed_group, slope, act_low, keep, give = run(
        lambda *ins: call(
            partial(up_kernel, (0, 1)), ins, [group_out, hid_f, hid_b, wide_f, wide_b], scalars=1,
        ),
        at, *normed_pieces[:2], *ffn_weights, my_upb,
    )
    meet = Meet().near_pair(keep, give)
    normed_group, slope, act_low, keep, give = run(
        lambda *ins: call(
            partial(up_kernel, (2, 3)), ins, [group_out, hid_f, hid_b, wide_f, wide_b], scalars=1,
            alias={8: 0, 9: 1, 10: 2},
        ),
        at, *normed_pieces[2:], *ffn_weights, my_upb, normed_group, slope, act_low,
    )
    meet.far_pair(keep, give).send()
    (slope,) = run(lambda *ins: call(slope_kernel, ins, [hid_f]), slope)
    encoded, d_ffn, d_resid_two, sums_two = run(
        lambda *ins: call(
            second_norm_kernel, ins,
            [shape_of((1, SLOTS, D), bf16), wide_b, wide_f, shape_of((3, D), f32)],
        ),
        *meet.terms(), normed_one, grad_in, live_row, vec_two,
    )

    d_ffn_pieces = group_of(d_ffn)
    ffn_weights = (g_down.x, g_down.other, g_up.x, g_up.other)
    sums_out = shape_of((2, hidden), f32)
    d_ffn_group, d_pre, d_up_bias, keep, give = run(
        lambda *ins: call(
            partial(down_back_kernel, (0, 1)), ins,
            [group_out, hid_b, sums_out, wide_f, wide_b], scalars=1,
        ),
        at, *d_ffn_pieces[:2], *ffn_weights, slope,
    )
    meet = Meet().near_pair(keep, give)
    d_ffn_group, d_pre, d_up_bias, keep, give = run(
        lambda *ins: call(
            partial(down_back_kernel, (2, 3)), ins,
            [group_out, hid_b, sums_out, wide_f, wide_b], scalars=1,
            alias={8: 0, 9: 1, 10: 2},
        ),
        at, *d_ffn_pieces[2:], *ffn_weights, slope, d_ffn_group, d_pre, d_up_bias,
    )
    meet.far_pair(keep, give)

    def half_grad(left, right, near):
        out = shape_of((D // 2, right.shape[1]), bf16)
        (made,) = run(lambda *ins: call(partial(half_grad_kernel, near), ins, [out]), left, right)
        return made

    meet.send()
    give = half_grad(d_ffn_group, act_low, False)
    s_down = Scatter(run, (give,), "dp", X_Z, given=give).send()
    give = half_grad(normed_group, d_pre, False)
    s_up = Scatter(run, (give,), "dp", Z_X, given=give).send()
    s_down.own(half_grad(d_ffn_group, act_low, True))
    s_up.own(half_grad(normed_group, d_pre, True))

    d_branch, d_resid_one, sums_one, a0, a1, a2 = run(
        lambda *ins: call(
            partial(first_back_kernel, width), ins,
            [wide_b, wide_f, shape_of((3, D), f32), doc_out, doc_out, pair_out],
            [pltpu.VMEM((ROWS, D), bf16)], scalars=1,
        ),
        at, *meet.terms(), d_resid_two, hat_one, scale_one, vec_one, *proj_near, *proj_far,
    )
    far = swap(a2, by_y)
    got_c = swap(a1, by_c)
    parts = run(
        lambda *ins: call(
            partial(proj_grad_kernel, width), ins, [col_out] * 4, scalars=1, cost=1.3
        ),
        at, attended, d_branch,
    )
    meet_proj = Meet().near_pair(parts[0], parts[1]).far_pair(parts[2], parts[3])
    grids = shape_of((3, NB, heads * NB), f32)
    room = [pltpu.VMEM((heads * ROWS, ROWS), bf16), pltpu.VMEM((ROWS, heads * NB), bf16)]
    d_qkv, d_sums, d_grid = run(
        lambda *ins: call(
            partial(attend_back_kernel, heads, (0, 1), False), ins,
            [qkv_out, shape_of((tp, 3 * width), f32), grids], room, cost=10,
        ),
        qkv, probs, a0, got_c, notes,
    )
    got_far = swap(second(far), by_c)
    meet_proj.send()
    d_qkv, d_sums, d_grid, d_ext = run(
        lambda *ins: call(
            partial(attend_back_kernel, heads, (2, 3), True), ins,
            [qkv_out, shape_of((tp, 3 * width), f32), grids, shape_of((3 * heads, 2 * NB), f32)],
            room,
            alias={5: 0, 6: 1, 7: 2},
        ),
        qkv, probs, far, got_far, notes, d_qkv, d_sums, d_grid,
    )

    def with_proj(k, c, y, small):
        p = (k.astype(f32) + c.astype(f32) + y.astype(f32)).astype(bf16)
        return jnp.concatenate([p, small], axis=-1).astype(f32)

    give = half_grad(group, d_qkv, False)
    s_first = Scatter(run, (give,), "dp", Z_X, given=give).send()
    run.wait(s_up.other, s_down.other)
    s_up.take().send()
    s_down.take().send()
    s_first.own(half_grad(group, d_qkv, True))
    plains = [pltpu.VMEM((24, D), f32)] * 2
    (small_grads,) = run(
        lambda *ins: call(
            partial(small_grads_kernel, heads, n_dev), ins, [shape_of((D, 128), bf16)],
            flats + plains, scalars=1,
        ),
        at, d_ext, d_sums, d_up_bias, sums_one, sums_two,
    )
    parts = run(
        lambda *ins: call(
            partial(tokens_back_kernel, width), ins, [wide_f, wide_b, wide_f, wide_b], scalars=1
        ),
        at, d_qkv, g_first.x, g_first.other,
    )
    meet_tok = Meet().near_pair(parts[0], parts[1]).far_pair(parts[2], parts[3])
    s_second = Scatter(
        run, (*meet_proj.terms(), small_grads), "dp", Z_X, base=with_proj
    ).send()
    s_up.take().send()
    s_first.take().send()
    run.wait(s_first.other)
    s_first.take().send()
    meet_tok.send()
    run.wait(s_up.other, s_down.other, s_second.other, s_first.other)
    s_second.take().send()
    s_down.take().send()

    def columns_back(scatters):
        sums = [x.sum().reshape(tp, rows, -1) for x in scatters]
        out = shape_of((2, rows, sum(x.shape[2] for x in sums)), bf16)

        def fn(at, *refs):
            for target, c in ((refs[-2], 1 - at[0] % 2), (refs[-1], at[0] % 2)):
                for y in range(2):
                    target[y] = jnp.concatenate([ref[2 * y + c] for ref in refs[:-2]], axis=1)

        return Exchange(run, at, *run(lambda *ins: call(fn, ins, [out, out], scalars=1), at, *sums))

    def whole_rows(exchanged, groups, widths, smalls):
        outs = [shape_of((rows, tp * g * w), f32) for g, w in zip(groups, widths)]
        ends = [shape_of((1, n * rows), f32) for n in smalls]

        def fn(at, mine, other, *refs):
            outs, ends = refs[: len(groups)], refs[len(groups) :]
            total = None
            for near, ref in ((True, mine), (False, other)):
                for n in range(2):
                    start, f = 0, source_of(at, near, n)
                    for out, g, w in zip(outs, groups, widths):
                        for i in range(g):
                            place = pl.multiple_of((i * tp + f) * w, w)
                            out[:, pl.ds(place, w)] = ref[n, :, start : start + w].astype(f32)
                            start += w
                    if ends:
                        part = ref[n, :, start:].astype(f32)
                        total = part if total is None else total + part
            if ends:
                small_outs(total, ends)

        return run(
            lambda *ins: call(fn, ins, outs + ends, scalars=1), at, exchanged.mine, exchanged.other
        )

    s_up.take()
    x_up = columns_back([s_up]).turn()
    out_f = shape_of((1, SLOTS, D), f32)
    grad_tokens = run(
        lambda *ins: glue(
            lambda d, k, c, y: (
                d[...] + k[...] + c[...].astype(f32) + y[...].astype(f32)
            )[:SLOTS][None],
            [out_f], *ins,
        ),
        d_resid_one, *meet_tok.terms(),
    )
    run.wait(s_second.other, x_up.other)
    s_second.take().send()
    run.wait(s_down.other, s_second.other)
    s_down.take()
    s_first.take()
    s_second.take()
    x_rest = columns_back([s_down, s_first, s_second])
    x_rest.turn()
    (grad_up,) = whole_rows(x_up, (1,), (hidden,), ())
    grad_down, grad_qkv, grad_proj, *out = whole_rows(
        x_rest, (1, 3, 1), (hidden, width, width), (1,) * 6 + (2, 6, 4)
    )
    out = [x.reshape(-1) for x in out]
    return (
        encoded,
        grad_tokens,
        grad_qkv,
        out[6],
        grad_proj,
        out[0],
        out[1],
        out[2],
        out[7],
        grad_up,
        out[8],
        grad_down,
        out[3],
        out[4],
        out[5],
    )


def solution(mesh):
    split = ("dp", "fsdp")
    one, two, three = P(split), P(split, None), P(split, None, None)
    return jax.shard_map(
        local,
        mesh=mesh,
        in_specs=(
            three, three, one, two, two, two, two, one, two, one, one, one, one, two, one, two,
            one, one, one,
        ),
        out_specs=(
            three, three, two, one, two, one, one, one, one, two, one, two, one, one, one,
        ),
        check_vma=False,
    )
```

```python
from functools import partial

import jax
import jax.numpy as jnp
from jax import lax
from jax.experimental import pallas as pl
from jax.experimental.pallas import tpu as pltpu
from jax.sharding import PartitionSpec as P

D = 1024
H = 16
HD = 64
FF = 4096
NB = 128
TEXT = 120
SLOTS = 169
ROWS = 176
NEGATIVE = -1e30
EPSILON = 1e-05

f32 = jnp.float32
bf16 = jnp.bfloat16


def shape_of(shape, kind):
    return jax.ShapeDtypeStruct(tuple(shape), kind)


def call(kernel, ins, outs, scratch=(), scalars=0, alias=None, vmem=16, cost=0):
    spaces = [pltpu.SMEM] * scalars + [pltpu.VMEM] * (len(ins) - scalars)
    return pl.pallas_call(
        kernel,
        in_specs=[pl.BlockSpec(memory_space=m) for m in spaces],
        out_specs=[pl.BlockSpec(memory_space=pltpu.VMEM) for _ in outs],
        out_shape=list(outs),
        scratch_shapes=list(scratch),
        input_output_aliases=alias or {},
        cost_estimate=pl.CostEstimate(
            flops=int(cost * 1e9), bytes_accessed=0, transcendentals=0
        ),
        compiler_params=pltpu.CompilerParams(vmem_limit_bytes=vmem * 2**20),
    )(*ins)


def glue(fn, outs, *ins, scalars=0):
    def kernel(*refs):
        made = fn(*refs[: len(ins)])
        for out, value in zip(refs[len(ins) :], made if isinstance(made, tuple) else (made,)):
            out[...] = value

    made = call(kernel, ins, outs, scalars=scalars)
    return made[0] if len(outs) == 1 else made


def axis_bits(axis):
    bits, b = [], lax.axis_size(axis) // 2
    while b >= 1:
        bits.append((axis, b))
        b //= 2
    return bits


def swap(x, bit):
    axis, b = bit
    return lax.ppermute(x, axis, [(i, i ^ b) for i in range(lax.axis_size(axis))])


def side(bit):
    axis, b = bit
    return (lax.axis_index(axis) // b) % 2


def pair_up(mine, other, bit, pos):
    one = side(bit) == 1
    return jnp.stack([jnp.where(one, other, mine), jnp.where(one, mine, other)], axis=pos)


class Order:
    def __init__(self):
        self.last = ()

    def tie(self, args):
        if not self.last:
            return args
        return lax.optimization_barrier(tuple(args) + self.last)[: len(args)]

    def wait(self, *arrays):
        self.last = self.last + arrays

    def __call__(self, fn, *args):
        out = fn(*self.tie(args))
        self.last = tuple(jax.tree.leaves(out))
        return out


def after(x, *earlier):
    return lax.optimization_barrier((x,) + earlier)[0]


def high_bits(axis, order):
    bits = axis_bits(axis)
    return [bits[i] for i in order]


class Gather:
    def __init__(self, run, x, axis, order):
        self.run, self.x = run, x
        self.bits = axis_bits(axis)[3:][::-1] + high_bits(axis, order)
        while len(self.bits) > 3:
            self.send().join()

    def send(self, *earlier):
        self.other = swap(after(self.x, *earlier), self.bits[0])
        return self

    def join(self):
        bit = self.bits.pop(0)
        if len(self.bits) >= 3:
            self.x = self.run(
                lambda m, o: pair_up(m, o, bit, 0).reshape(-1, m.shape[1]), self.x, self.other
            )
        else:
            r, c = self.x.shape

            def join(m, o, out):
                out[:r], out[r:] = m[...], o[...]

            (self.x,) = self.run(
                lambda *ins: call(join, ins, [shape_of((2 * r, c), bf16)]), self.x, self.other
            )
        return self


class Scatter:
    def __init__(self, run, arrays, axis, order, walk=None, base=None, given=None):
        self.run = run
        self.high, rest = high_bits(axis, order), axis_bits(axis)[3:]
        have = self.high[::-1] + rest
        self.order = (high_bits(axis, walk) if walk else self.high[::-1]) + rest
        self.low = len(rest)
        if given is not None:
            have = [bit for bit in have if bit != self.order[0]]
            given = given.reshape((2,) * len(have) + (-1, given.shape[-1]))
        self.given = given
        arrays = tuple(a.reshape((2,) * len(have) + (-1, a.shape[-1])) for a in arrays)
        self.terms = [(arrays, have, [], base or (lambda x: x.astype(f32)))]

    def own(self, array):
        arrays, *rest = self.terms[0]
        self.terms[0] = ((array.reshape(arrays[0].shape),), *rest)

    def flat(self):
        return [a for arrays, *unused in self.terms for a in arrays]

    def value(self, flat, extra=()):
        flat, total = list(flat), None
        for arrays, have, cuts, base in self.terms:
            chosen = dict(list(cuts) + list(extra))
            at = tuple(
                slice(None) if bit not in chosen
                else (0 if chosen[bit] else 1) if bit in self.high
                else side(bit) if chosen[bit] else 1 - side(bit)
                for bit in have
            )
            part = base(*[flat.pop(0)[at] for unused in arrays])
            total = part if total is None else total + part
        return total

    def sum(self, extra=()):
        flat = self.flat()
        fn = lambda *f: self.value(f, extra).astype(bf16)
        if self.low:
            return self.run(fn, *flat)
        out = jax.eval_shape(fn, *flat)
        return self.run(lambda *f: glue(fn, [out], *f), *flat)

    def send(self, *earlier):
        bit = self.order[0]
        out = self.given if self.given is not None else self.sum([(bit, False)])
        self.other = swap(after(out, *earlier), bit)
        return self

    def take(self):
        bit = self.order.pop(0)
        for arrays, have, cuts, base in self.terms:
            if self.given is None:
                cuts.append((bit, True))
        self.given = None
        self.terms.append(((self.other,), list(self.order_left()), [], lambda x: x.astype(f32)))
        while 0 < len(self.order) <= self.low:
            self.send().take()
        return self

    def order_left(self):
        arrays, have, cuts, base = self.terms[0]
        gone = [bit for bit, keep in cuts]
        return [bit for bit in have if bit not in gone]


class Exchange:
    def __init__(self, run, at, give, keep):
        self.run, self.at, self.keep = run, at, keep
        self.other = swap(give, axis_bits("fsdp")[1])

    def turn(self, *earlier):
        def fn(at, keep, got, give, mine):
            y, c = at[0] // 2, at[0] % 2
            give[c], give[1 - c] = keep[1 - y], got[1 - y]
            mine[c], mine[1 - c] = keep[y], got[y]

        out = shape_of(self.keep.shape, self.keep.dtype)
        give, self.mine = self.run(
            lambda *ins: call(fn, ins, [out, out], scalars=1), self.at, self.keep, self.other
        )
        self.other = swap(after(give, *earlier), axis_bits("fsdp")[0])
        return self


def source_of(at, near, n):
    y = at[0] // 2
    return (y if near else 1 - y) * 2 + n


def dot_nn(a, b):
    return jnp.dot(a, b, preferred_element_type=f32)


def dot_nt(a, b):
    return lax.dot_general(a, b, (((1,), (1,)), ((), ())), preferred_element_type=f32)


def dot_tn(a, b):
    return lax.dot_general(a, b, (((0,), (0,)), ((), ())), preferred_element_type=f32)


def call_docs(kernel, docs, ins, in_whole, outs):
    def spec(a, whole):
        n = len(a.shape)
        if whole:
            return pl.BlockSpec(tuple(a.shape), lambda d: (0,) * n)
        return pl.BlockSpec((1,) + tuple(a.shape[1:]), lambda d: (d,) + (0,) * (n - 1))

    return pl.pallas_call(
        kernel,
        grid=(docs,),
        in_specs=[spec(a, w) for a, w in zip(ins, in_whole)],
        out_specs=[spec(a, False) for a in outs],
        out_shape=list(outs),
        cost_estimate=pl.CostEstimate(flops=0, bytes_accessed=0, transcendentals=0),
        compiler_params=pltpu.CompilerParams(vmem_limit_bytes=16 * 2**20),
    )(*ins)


def at_block(ref, me, j, size):
    return pl.ds(pl.multiple_of((me ^ j) * size, size), size)


BLOCK = D // 8
Z_X = (0, 1, 2)
X_Z = (0, 2, 1)
X_FIRST = (2, 1, 0)


def far_block(place, q, order):
    away = sum(((q >> n) & 1) * (4 >> bit) for n, bit in enumerate(order))
    return pl.ds(pl.multiple_of((place ^ away) * BLOCK, BLOCK), BLOCK)


def relative(src, dst, place, order, rows):
    for q in range(8):
        dst[rows, q * BLOCK : (q + 1) * BLOCK] = src[:, far_block(place, q, order)]


def doc_at(j):
    return slice(j * ROWS, (j + 1) * ROWS)


def hot_rows(notes, flip=False):
    buckets = lax.broadcasted_iota(jnp.int32, (NB, ROWS), 0).astype(f32)
    if flip:
        buckets = (NB - 1) - buckets
    return [(notes[r : r + 1, :ROWS] == buckets).astype(f32).astype(bf16) for r in (12, 9, 10)]


ROW_QV, ROW_TABLES, ROW_UP = 6, 7, 9
TILE_ROWS = 16


def pack_kernel(*refs):
    *smalls, out_ref = refs
    rows = smalls[0].shape[1]
    tile = jnp.zeros(out_ref.shape, f32)
    row = lax.broadcasted_iota(jnp.int32, out_ref.shape, 0)
    qv, tables, up = smalls[6:]
    parts = list(smalls[:6]) + [qv] + [tables.at[:, 3 * n * rows : 3 * (n + 1) * rows] for n in range(2)]
    for n, ref in enumerate(parts + [up]):
        value = ref[...].astype(f32)
        wide = jnp.concatenate(
            [value, jnp.zeros((1, 128 - value.shape[1]), f32)], axis=1
        ) if value.shape[1] < 128 else value
        tile = jnp.where(row == n, jnp.broadcast_to(wide, out_ref.shape), tile)
    out_ref[...] = tile.astype(bf16)


def unpack_kernel(heads, count, at_ref, all_ref, ext_ref, add_ref, up_ref, one_ref, two_ref, qv_ref, tab_ref, upb_ref):
    me, place = at_ref[0], at_ref[1]
    rows, width, low = D // count, heads * HD, count // 32
    for d in range(count):
        q = place ^ (d // (4 * low))
        block = (q * low + (d // 4) % low) * 4 + (me ^ (d % 4))
        place_of = pl.ds(pl.multiple_of(block * TILE_ROWS, TILE_ROWS), TILE_ROWS)
        tile = all_ref[place_of, :].astype(f32)
        at = slice(d * rows, (d + 1) * rows)
        one_ref[:, at] = tile[0:3, :rows]
        two_ref[:, at] = tile[3:6, :rows]
        qv_ref[:, 2 * d * rows : 2 * (d + 1) * rows] = tile[ROW_QV : ROW_QV + 1, : 2 * rows]
        for n in range(2):
            start = (2 * d + n) * 3 * rows
            row = tile[ROW_TABLES + n : ROW_TABLES + n + 1, : 3 * rows]
            tab_ref[:, start : start + 3 * rows] = row
        upb_ref[:, 4 * d * rows : 4 * (d + 1) * rows] = tile[ROW_UP : ROW_UP + 1, : 4 * rows]
    start = pl.multiple_of(me * width, width)
    add_ref[:, :width] = qv_ref[:, pl.ds(start, width)]
    add_ref[:, width : 2 * width] = jnp.zeros((1, width), f32)
    add_ref[:, 2 * width :] = qv_ref[:, pl.ds(D + start, width)]
    hidden = up_ref.shape[1]
    up_ref[...] = upb_ref[:, pl.ds(pl.multiple_of(me * hidden, hidden), hidden)]
    half = NB // 2
    for k in range(3):
        for h in range(heads):
            n = k * heads + h
            row = tab_ref[:, pl.ds(pl.multiple_of((k * H + me * heads + h) * NB, NB), NB)]
            ext_ref[n : n + 1, :half] = jnp.broadcast_to(row[:, :1], (1, half))
            ext_ref[n : n + 1, half : half + NB] = row
            ext_ref[n : n + 1, half + NB :] = jnp.broadcast_to(row[:, NB - 1 :], (1, half))


PIECES = 18


def small_grads_kernel(
    heads, count, at_ref, ext_ref, sums_ref, up_ref, one_ref, two_ref, out_ref,
    qv_ref, tab_ref, upb_ref, plain_ref, order_ref,
):
    me = at_ref[0]
    rows, width = D // count, heads * HD
    for ref in (qv_ref, tab_ref, upb_ref, plain_ref):
        ref[...] = jnp.zeros_like(ref)
    start = pl.multiple_of(me * width, width)
    sums = jnp.sum(sums_ref[...], axis=0, keepdims=True)
    qv_ref[:, pl.ds(start, width)] = sums[:, :width]
    qv_ref[:, pl.ds(D + start, width)] = sums[:, 2 * width :]
    hidden = up_ref.shape[1]
    upb_ref[:, pl.ds(pl.multiple_of(me * hidden, hidden), hidden)] = jnp.sum(
        up_ref[...], axis=0, keepdims=True
    )
    half = NB // 2
    lane = lax.broadcasted_iota(jnp.int32, (1, NB), 1)
    for k in range(3):
        for h in range(heads):
            row = ext_ref[k * heads + h : k * heads + h + 1, :]
            low = jnp.sum(row[:, :half], axis=1, keepdims=True)
            high = jnp.sum(row[:, half + NB :], axis=1, keepdims=True)
            grad = row[:, half : half + NB] + jnp.where(lane == 0, low, 0.0)
            grad = grad + jnp.where(lane == NB - 1, high, 0.0)
            tab_ref[:, pl.ds(pl.multiple_of((k * H + me * heads + h) * NB, NB), NB)] = grad
    plain_ref[0:3, :] = one_ref[...]
    plain_ref[3:6, :] = two_ref[...]
    for d in range(count):
        at = slice(d * rows, (d + 1) * rows)
        row = 6
        for ref, times in ((qv_ref, 2), (tab_ref, 6), (upb_ref, 4)):
            for n in range(times):
                begin = (d * times + n) * rows
                plain_ref[row : row + 1, at] = ref[:, begin : begin + rows]
                row += 1
    relative(plain_ref, order_ref, at_ref[1], Z_X, slice(None))
    shape = (plain_ref.shape[0], 128)
    same = lax.broadcasted_iota(jnp.int32, shape, 0) == lax.broadcasted_iota(jnp.int32, shape, 1)
    out_ref[...] = dot_tn(order_ref[...].astype(bf16), same.astype(f32).astype(bf16)).astype(bf16)


def small_outs(total, outs):
    rows = total.shape[0]
    shape = (rows, rows)
    same = lax.broadcasted_iota(jnp.int32, shape, 0) == lax.broadcasted_iota(jnp.int32, shape, 1)
    turned = lax.dot_general(
        total, same.astype(f32), (((0,), (0,)), ((), ())),
        precision=lax.Precision.HIGHEST, preferred_element_type=f32,
    )
    row = 0
    for out in outs:
        for n in range(out.shape[1] // rows):
            out[:, n * rows : (n + 1) * rows] = turned[row : row + 1, :]
            row += 1


def bias_kernel(heads, notes_ref, ext_ref, out_ref):
    notes = notes_ref[0].astype(f32)
    hots = hot_rows(notes)
    every_hot = jnp.concatenate(hots, axis=0)
    live = notes[11:12, :ROWS] > 0.5
    for h in range(heads):
        codes = []
        for k in range(3):
            row = ext_ref[k * heads + h : k * heads + h + 1, :]
            spread = jnp.broadcast_to(row, (NB, 2 * NB))
            skew = pltpu.roll(spread, NB, 1, stride=1, stride_axis=0)
            codes.append(dot_tn(hots[k], skew[:, :NB].astype(bf16)).astype(bf16))
        total = dot_nn(jnp.concatenate(codes, axis=1), every_hot)
        out_ref[0, h] = jnp.where(live, total, NEGATIVE)


def softmax_rows(q, k, bias):
    s = dot_nt(q, k) * 0.125 + bias
    e = jnp.exp(s - jnp.max(s, axis=-1, keepdims=True))
    return e * (1.0 / jnp.sum(e, axis=-1, keepdims=True))


def attend_kernel(heads, pair, at_ref, d0, d1, near_ref, far_ref, add_ref, bias_ref, *rest):
    group_ref, qkv_ref, probs_ref, mixed_ref = rest[-4:]
    width = heads * HD
    for j, piece in zip(pair, (d0, d1)):
        relative(piece, group_ref, at_ref[1], Z_X, doc_at(j))
    both = slice(pair[0] * ROWS, (pair[1] + 1) * ROWS)
    for n in range(3):
        at = slice(n * width, (n + 1) * width)
        qkv = dot_nn(group_ref[both, : D // 2], near_ref[:, at])
        qkv = qkv + dot_nn(group_ref[both, D // 2 :], far_ref[:, at])
        qkv_ref[both, at] = (qkv + add_ref[:, at]).astype(bf16)
    for n, j in enumerate(pair):
        outs = []
        for h in range(heads):
            q = qkv_ref[doc_at(j), h * HD : (h + 1) * HD]
            k = qkv_ref[doc_at(j), width + h * HD : width + (h + 1) * HD]
            v = qkv_ref[doc_at(j), 2 * width + h * HD : 2 * width + (h + 1) * HD]
            probs = softmax_rows(q, k, bias_ref[j, h])
            probs_ref[j, h] = probs
            outs.append(dot_nn(probs.astype(bf16), v).astype(bf16))
        mixed_ref[n] = jnp.concatenate(outs, axis=1)


def norm_parts(values):
    average = jnp.mean(values, axis=-1, keepdims=True)
    centred = values - average
    spread = jnp.mean(centred * centred, axis=-1, keepdims=True)
    scale = lax.rsqrt(spread + EPSILON)
    return centred * scale, scale


def norm_back(grad, gain, hat, scale):
    scaled = grad * gain
    first = jnp.mean(scaled, axis=-1, keepdims=True)
    second = jnp.mean(scaled * hat, axis=-1, keepdims=True)
    return (scaled - first - hat * second) * scale


def first_norm_kernel(
    width, at_ref, a0, a1, a2, a3, *rest
):
    near, far = rest[:4], rest[4:8]
    tokens_ref, vec_ref, att_ref, low_ref, normed_ref, hat_ref, scale_ref, branch_ref, plain_ref = rest[8:]
    me = at_ref[0]
    for j, piece in enumerate((a0[0], a1[...], a2[0], a3[...])):
        plain_ref[:, at_block(plain_ref, me, j, width)] = piece
    relative(plain_ref, att_ref, at_ref[1], Z_X, slice(None))
    left, right = att_ref[:, : D // 2], att_ref[:, D // 2 :]
    for j in range(4):
        branch_ref[:, at_block(branch_ref, me, j, width)] = dot_nn(left, near[j][...]) + dot_nn(
            right, far[j][...]
        )
    resid = tokens_ref[...].astype(f32) + branch_ref[...] + vec_ref[0:1, :]
    hat, scale = norm_parts(resid)
    normed = hat * vec_ref[1:2, :] + vec_ref[2:3, :]
    low_ref[...] = normed.astype(bf16)
    normed_ref[...] = normed
    hat_ref[...] = hat
    scale_ref[...] = scale


def parts_back(left, near_ref, far_ref, outs, place, order):
    for q in range(0, 8, 2):
        ref = near_ref if q < 4 else far_ref
        at = slice((q % 4) * BLOCK, (q % 4 + 2) * BLOCK)
        part = dot_nt(left, ref[at, :])
        for n, out in enumerate(outs):
            for half in range(2):
                block = part[doc_at(n), half * BLOCK : (half + 1) * BLOCK]
                out[:, far_block(place, q + half, order)] = block.astype(out.dtype)


def half_grad_kernel(near, left_ref, right_ref, out_ref):
    left = left_ref[:, : D // 2] if near else left_ref[:, D // 2 :]

    def tile(n):
        at = pl.ds(pl.multiple_of(n * TILE, TILE), TILE)
        out_ref[:, at] = dot_tn(left, right_ref[:, at]).astype(bf16)

    steps = right_ref.shape[1] // TILE
    if near:
        pl.loop(0, steps)(tile)
    else:
        for n in range(steps):
            tile(n)


def normal_below(u):
    return 0.5 + 0.5 * lax.erf(u * (0.5**0.5))


def slope_kernel(pre_ref, slope_ref):
    for n in range(pre_ref.shape[1] // TILE):
        at = slice(n * TILE, (n + 1) * TILE)
        u = pre_ref[:, at]
        density = jnp.exp(-0.5 * u * u) * ((2 * jnp.pi) ** -0.5)
        slope_ref[:, at] = normal_below(u) + u * density


TILE = 256


def up_kernel(pair, at_ref, x0, x1, up_near, up_far, down_near, down_far, add_ref, *rest):
    group_ref, slope_ref, act_ref, keep_ref, give_ref = rest[-5:]
    for j, piece in zip(pair, (x0, x1)):
        relative(piece, group_ref, at_ref[1], Z_X, doc_at(j))
    both = slice(pair[0] * ROWS, (pair[1] + 1) * ROWS)
    for n in range(act_ref.shape[1] // TILE):
        at = slice(n * TILE, (n + 1) * TILE)
        pre = dot_nn(group_ref[both, : D // 2], up_near[:, at])
        pre = pre + dot_nn(group_ref[both, D // 2 :], up_far[:, at]) + add_ref[:, at]
        slope_ref[both, at] = pre
        act_ref[both, at] = (pre * normal_below(pre)).astype(bf16)
    parts_back(act_ref[both, :], down_near, down_far, (keep_ref, give_ref), at_ref[1], X_Z)


def down_back_kernel(pair, at_ref, g0, g1, down_near, down_far, up_near, up_far, slope_ref, *rest):
    group_ref, dpre_ref, sums_ref, keep_ref, give_ref = rest[-5:]
    for j, piece in zip(pair, (g0, g1)):
        relative(piece, group_ref, at_ref[1], X_Z, doc_at(j))
    both = slice(pair[0] * ROWS, (pair[1] + 1) * ROWS)
    for n in range(dpre_ref.shape[1] // TILE):
        at = slice(n * TILE, (n + 1) * TILE)
        d_act = dot_nn(group_ref[both, : D // 2], down_near[:, at])
        d_act = d_act + dot_nn(group_ref[both, D // 2 :], down_far[:, at])
        d_pre = (d_act * slope_ref[both, at]).astype(bf16)
        dpre_ref[both, at] = d_pre
        sums_ref[pair[0] // 2 : pair[0] // 2 + 1, at] = jnp.sum(d_pre.astype(f32), axis=0, keepdims=True)
    parts_back(dpre_ref[both, :], up_near, up_far, (keep_ref, give_ref), at_ref[1], Z_X)


def second_norm_kernel(
    keep_ref, got_c, got_y, normed_ref, grad_ref, live_ref, vec_ref,
    enc_ref, dffn_ref, dres_ref, sums_ref,
):
    ffn = keep_ref[...] + got_c[...].astype(f32) + got_y[...].astype(f32) + vec_ref[0:1, :]
    hat, scale = norm_parts(normed_ref[...] + ffn)
    ones = jnp.ones((8, 128), bf16)
    live = dot_tn(live_ref[...].astype(bf16), ones)[:, :1]
    gain = vec_ref[1:2, :]
    enc = ((hat * gain + vec_ref[2:3, :]) * live).astype(bf16)
    enc_ref[0] = enc[:SLOTS]
    grad = grad_ref[...].astype(f32) * live
    d_resid = norm_back(grad, gain, hat, scale)
    dres_ref[...] = d_resid
    low = d_resid.astype(bf16)
    dffn_ref[...] = low
    sums_ref[0:1, :] = jnp.sum(low.astype(f32), axis=0, keepdims=True)
    sums_ref[1:2, :] = jnp.sum(grad * hat, axis=0, keepdims=True)
    sums_ref[2:3, :] = jnp.sum(grad, axis=0, keepdims=True)


def first_back_kernel(width, at_ref, keep_ref, got_c, got_y, dres_ref, hat_ref, scale_ref, vec_ref, *rest):
    near, far = rest[:4], rest[4:8]
    branch_ref, done_ref, sums_ref, a0_ref, a1_ref, a2_ref, plain_ref = rest[8:]
    me = at_ref[0]
    hat = hat_ref[...]
    grad = dres_ref[...] + keep_ref[...] + got_c[...].astype(f32) + got_y[...].astype(f32)
    d_one = norm_back(grad, vec_ref[1:2, :], hat, scale_ref[...])
    done_ref[...] = d_one
    low = d_one.astype(bf16)
    branch_ref[...] = low
    sums_ref[0:1, :] = jnp.sum(low.astype(f32), axis=0, keepdims=True)
    sums_ref[1:2, :] = jnp.sum(grad * hat, axis=0, keepdims=True)
    sums_ref[2:3, :] = jnp.sum(grad, axis=0, keepdims=True)
    for n, proj in enumerate((near, far)):
        total = None
        for j in range(4):
            part = dot_nt(branch_ref[:, at_block(branch_ref, me, j, width)], proj[j][...])
            total = part if total is None else total + part
        for q in range(4):
            plain_ref[:, far_block(at_ref[1], 4 * n + q, Z_X)] = total[
                :, q * BLOCK : (q + 1) * BLOCK
            ].astype(bf16)
    for i, out in enumerate((a0_ref, a1_ref, a2_ref.at[0], a2_ref.at[1])):
        out[...] = plain_ref[:, at_block(plain_ref, me, i, width)]


def proj_grad_kernel(width, at_ref, att_ref, branch_ref, *outs):
    me = at_ref[0]
    att = att_ref[...]
    for j, out in enumerate(outs):
        out[...] = dot_tn(att, branch_ref[:, at_block(branch_ref, me, j, width)]).astype(bf16)


def attend_back_kernel(heads, pair, last, qkv_ref, probs_ref, g0, g1, notes_ref, *rest):
    ds_ref, wide_ref = rest[-2:]
    dqkv_ref, sums_ref, grid_ref = rest[-6:-3] if last else rest[-5:-2]
    width = heads * HD
    for j, grad_ref in zip(pair, (g0.at[0] if last else g0, g1)):
        notes = notes_ref[j].astype(f32)
        hots = jnp.concatenate(hot_rows(notes), axis=0)
        flipped = hot_rows(notes, flip=True)
        for h in range(heads):
            q = qkv_ref[doc_at(j), h * HD : (h + 1) * HD]
            k = qkv_ref[doc_at(j), width + h * HD : width + (h + 1) * HD]
            v = qkv_ref[doc_at(j), 2 * width + h * HD : 2 * width + (h + 1) * HD]
            g = grad_ref[:, h * HD : (h + 1) * HD]
            p = probs_ref[j, h]
            dp = dot_nt(g, v)
            ds = (p * (dp - jnp.sum(p * dp, axis=-1, keepdims=True))).astype(bf16)
            ds_ref[doc_at(h), :] = ds
            dq = (dot_nn(ds, k) * 0.125).astype(bf16)
            dk = (dot_tn(ds, q) * 0.125).astype(bf16)
            dv = dot_tn(p.astype(bf16), g).astype(bf16)
            for c, d in enumerate((dq, dk, dv)):
                at = slice(c * width + h * HD, c * width + (h + 1) * HD)
                dqkv_ref[doc_at(j), at] = d
        part = dot_nt(ds_ref[...], hots).astype(bf16)
        for n in range(3):
            for h in range(heads):
                wide_ref[:, h * NB : (h + 1) * NB] = part[doc_at(h), n * NB : (n + 1) * NB]
            term = dot_nn(flipped[n], wide_ref[...])
            if j == 0:
                grid_ref[n] = term
            else:
                grid_ref[n] += term
        sums_ref[j : j + 1, :] = jnp.sum(dqkv_ref[doc_at(j), :].astype(f32), axis=0, keepdims=True)
    if last:
        ext_ref = rest[-3]
        for n in range(3 * heads):
            block = grid_ref[n // heads, :, (n % heads) * NB : (n % heads + 1) * NB]
            wide = jnp.concatenate([block, jnp.zeros((NB, NB), f32)], axis=1)
            skew = pltpu.roll(wide, 1, 1, stride=1, stride_axis=0)
            ext_ref[n : n + 1, :] = jnp.sum(skew, axis=0, keepdims=True)


def tokens_back_kernel(width, at_ref, d_ref, near_ref, far_ref, *outs):
    for q in range(0, 8, 2):
        ref = near_ref if q < 4 else far_ref
        at = slice((q % 4) * BLOCK, (q % 4 + 2) * BLOCK)
        part = dot_nt(d_ref[...], ref[at, : 3 * width])
        for n, out in enumerate(outs):
            for half in range(2):
                block = part[doc_at(n), half * BLOCK : (half + 1) * BLOCK]
                out[:, far_block(at_ref[1], q + half, Z_X)] = block.astype(out.dtype)


def pad_rows(x):
    return jnp.pad(x, ((0, ROWS - SLOTS), (0, 0)))


def local(
    tokens,
    out_grad,
    text_len,
    x_bucket,
    y_bucket,
    patch_mask,
    qkv_weight,
    qv_bias,
    proj_weight,
    proj_bias,
    first_gain,
    first_shift,
    rel_tables,
    up_weight,
    up_bias,
    down_weight,
    down_bias,
    second_gain,
    second_shift,
):
    inner = axis_bits("fsdp")
    outer = axis_bits("dp")
    tp = 4
    by_y, by_c = inner
    dpn = lax.axis_size("dp")
    n_dev = tp * dpn
    rows = D // n_dev
    heads = H // tp
    width = heads * HD
    hidden = FF // tp
    me = lax.axis_index("fsdp")
    place = lax.axis_index("dp") // (dpn // 8)
    at = jnp.stack([me, place]).astype(jnp.int32)
    run = Order()
    run.wait(at)
    doc_out = shape_of((ROWS, width), bf16)

    def group_of(own):
        far = swap(own, by_y)
        return own, swap(own, by_c), far, swap(far, by_c)

    def second(pair):
        return run(lambda p: glue(lambda ref: ref[1], [doc_out], p), pair)

    def trade(p1, far):
        return swap(p1, by_c), far, swap(second(far), by_c)

    class Meet:
        def near_pair(self, keep, give):
            self.keep, self.near = keep, swap(give, by_c)
            return self

        def far_pair(self, keep, give):
            self.held, self.both = keep, swap(give, by_c)
            return self

        def send(self):
            out = shape_of(self.held.shape, bf16)
            fn = lambda k, g: (k[...].astype(f32) + g[...].astype(f32)).astype(bf16)
            both = run(lambda *ins: glue(fn, [out], *ins), self.held, self.both)
            self.far = swap(both, by_y)
            return self

        def terms(self):
            return self.keep, self.near, self.far

    def column_blocks(shards, groups):
        widths = [a.shape[1] // (g * tp) for a, g in zip(shards, groups)]
        out = shape_of((2, rows, sum(w * g for w, g in zip(widths, groups))), bf16)

        def fn(at, *refs):
            for target, c in ((refs[-2], 1 - at[0] % 2), (refs[-1], at[0] % 2)):
                for y in range(2):
                    start = 0
                    for ref, w, g in zip(refs, widths, groups):
                        for n in range(g):
                            place = pl.multiple_of((n * tp + 2 * y + c) * w, w)
                            target[y, :, start : start + w] = ref[:, pl.ds(place, w)]
                            start += w

        return Exchange(
            run, at,
            *run(lambda *ins: call(fn, ins, [out, out], scalars=1), at, *shards),
        )

    def block_rows(exchanged, parts):
        cols = exchanged.mine.shape[2] // parts

        def fn(at, mine, other, *outs):
            for near, ref in ((True, mine), (False, other)):
                for n in range(2):
                    for p, out in enumerate(outs):
                        out[source_of(at, near, n)] = ref[n, :, p * cols : (p + 1) * cols]

        outs = run(
            lambda *ins: call(fn, ins, [shape_of((tp, rows, cols), bf16)] * parts, scalars=1),
            at, exchanged.mine, exchanged.other,
        )
        return [o.reshape(tp * rows, cols) for o in outs]

    ex_first = column_blocks((qkv_weight, proj_weight), (3, 1))

    smalls = [
        proj_bias, first_gain, first_shift, down_bias, second_gain, second_shift,
        qv_bias, rel_tables, up_bias,
    ]
    flats = [pltpu.VMEM((1, n), f32) for n in (2 * D, 3 * H * NB, FF)]

    places = jnp.arange(TEXT, dtype=jnp.int32)
    live_own = jnp.concatenate(
        [places[None, :] < text_len[:, None], patch_mask > 0], axis=1
    ).astype(f32)

    def document(tokens, x_bucket, y_bucket, live):
        pad_cols = ((0, 0), (0, D - SLOTS))
        positions = (jnp.arange(SLOTS, dtype=jnp.int32) * NB // SLOTS)[None]
        return jnp.concatenate(
            [
                tokens[0],
                jnp.pad(x_bucket.astype(bf16), pad_cols),
                jnp.pad(y_bucket.astype(bf16), pad_cols),
                jnp.pad(live.astype(bf16), pad_cols),
                jnp.pad(positions.astype(bf16), pad_cols),
                jnp.zeros((ROWS - SLOTS - 4, D), bf16),
            ],
            axis=0,
        )

    ex_ffn = column_blocks((up_weight, down_weight), (1, 1))
    ex_first.turn()
    ex_ffn.turn(ex_first.other)
    doc_rows = run(document, tokens, x_bucket, y_bucket, live_own)
    (packed,) = run(
        lambda *ins: call(pack_kernel, [x[None] for x in ins], [shape_of((TILE_ROWS, 128), bf16)]),
        *smalls,
    )

    def beside(m, o):
        r = m.shape[0]

        def join(m, o, out):
            out[:r], out[r:] = m[...], o[...]

        return run(lambda *ins: call(join, ins, [shape_of((2 * r, 128), bf16)]), m, o)[0]

    small_near = swap(packed, by_c)
    grad_in, live_row = run(
        lambda g, l: (pad_rows(g[0]), jnp.pad(l, ((0, 7), (0, ROWS - SLOTS)))), out_grad, live_own
    )
    pair = beside(packed, small_near)
    small_far = swap(pair, by_y)
    g_first = Gather(run, *block_rows(ex_first, 1), "dp", Z_X).send()
    g_small = Gather(run, beside(pair, small_far), "dp", X_FIRST).send()
    doc_far = swap(after(doc_rows, ex_ffn.other, small_far), by_y)
    doc_near = swap(doc_rows, by_c)
    up_own, down_own = block_rows(ex_ffn, 2)
    g_small.join().send()
    g_small.join().send()
    g_down = Gather(run, down_own, "dp", X_Z)
    g_first.join().send()
    g_down.send(g_first.x)
    doc_pieces = (doc_rows, doc_near, doc_far, swap(after(doc_far, g_first.x), by_c))

    def take_notes(*refs):
        for n in range(4):
            refs[4][n] = refs[n][ROWS - 16 :, : 2 * NB]

    (notes,) = run(
        lambda *ins: call(take_notes, ins, [shape_of((tp, 16, 2 * NB), bf16)]), *doc_pieces
    )
    run.wait(g_small.other)
    g_down.join()
    g_first.join().send()
    g_down.send()
    g_up = Gather(run, up_own, "dp", Z_X).send(g_down.x)
    ext, qkv_bias, my_upb, vec_one, vec_two = run(
        lambda *ins: call(
            partial(unpack_kernel, heads, n_dev), ins,
            [
                shape_of((3 * heads, 2 * NB), f32), shape_of((1, 3 * width), f32),
                shape_of((1, hidden), f32), shape_of((3, D), f32), shape_of((3, D), f32),
            ],
            flats, scalars=1,
        ),
        at, beside(g_small.x, g_small.other),
    )

    (bias,) = run(
        lambda *ins: call_docs(
            partial(bias_kernel, heads), tp, ins, [False, True],
            [shape_of((tp, heads, ROWS, ROWS), f32)],
        ),
        notes, ext,
    )
    g_up.join().send()
    col_out = shape_of((D, width), bf16)
    half_out = shape_of((D // 2, width), bf16)

    def proj_part(rows_of):
        return group_of(
            run(lambda w: glue(lambda ref: ref[:, 3 * width :], [half_out], w), rows_of)
        )

    proj_near = proj_part(g_first.x)
    g_up.join()
    run.wait(*proj_near)

    proj_far = proj_part(g_first.other)
    pair_out = shape_of((2, ROWS, width), bf16)
    group_out = shape_of((tp * ROWS, D), bf16)
    qkv_out = shape_of((tp * ROWS, 3 * width), bf16)
    probs_out = shape_of((tp, heads, ROWS, ROWS), f32)
    group, qkv, probs, far = run(
        lambda *ins: call(
            partial(attend_kernel, heads, (2, 3)), ins,
            [group_out, qkv_out, probs_out, pair_out], scalars=1,
        ),
        at, *doc_pieces[2:], g_first.x, g_first.other, qkv_bias, bias,
    )
    mixed_far = swap(far, by_y)
    g_up.send(g_first.other)
    g_down.join().send()
    group, qkv, probs, near = run(
        lambda *ins: call(
            partial(attend_kernel, heads, (0, 1)), ins,
            [group_out, qkv_out, probs_out, pair_out], scalars=1,
            alias={7: 0, 8: 1, 9: 2},
        ),
        at, *doc_pieces[:2], g_first.x, g_first.other, qkv_bias, bias, group, qkv, probs,
    )
    att_pieces = (near, *trade(second(near), mixed_far))

    wide_f = shape_of((ROWS, D), f32)
    wide_b = shape_of((ROWS, D), bf16)
    attended, normed_low, normed_one, hat_one, scale_one = run(
        lambda *ins: call(
            partial(first_norm_kernel, width), ins,
            [wide_b, wide_b, wide_f, wide_f, shape_of((ROWS, 1), f32)],
            [pltpu.VMEM((ROWS, D), f32), pltpu.VMEM((ROWS, D), bf16)], scalars=1,
        ),
        at, *att_pieces, *proj_near, *proj_far, doc_rows, vec_one,
    )

    normed_pieces = group_of(normed_low)
    hid_f = shape_of((tp * ROWS, hidden), f32)
    hid_b = shape_of((tp * ROWS, hidden), bf16)
    ffn_weights = (g_up.x, g_up.other, g_down.x, g_down.other)
    normed_group, slope, act_low, keep, give = run(
        lambda *ins: call(
            partial(up_kernel, (0, 1)), ins, [group_out, hid_f, hid_b, wide_f, wide_b], scalars=1,
        ),
        at, *normed_pieces[:2], *ffn_weights, my_upb,
    )
    meet = Meet().near_pair(keep, give)
    normed_group, slope, act_low, keep, give = run(
        lambda *ins: call(
            partial(up_kernel, (2, 3)), ins, [group_out, hid_f, hid_b, wide_f, wide_b], scalars=1,
            alias={8: 0, 9: 1, 10: 2},
        ),
        at, *normed_pieces[2:], *ffn_weights, my_upb, normed_group, slope, act_low,
    )
    meet.far_pair(keep, give).send()
    (slope,) = run(lambda *ins: call(slope_kernel, ins, [hid_f]), slope)
    encoded, d_ffn, d_resid_two, sums_two = run(
        lambda *ins: call(
            second_norm_kernel, ins,
            [shape_of((1, SLOTS, D), bf16), wide_b, wide_f, shape_of((3, D), f32)],
        ),
        *meet.terms(), normed_one, grad_in, live_row, vec_two,
    )

    d_ffn_pieces = group_of(d_ffn)
    ffn_weights = (g_down.x, g_down.other, g_up.x, g_up.other)
    sums_out = shape_of((2, hidden), f32)
    d_ffn_group, d_pre, d_up_bias, keep, give = run(
        lambda *ins: call(
            partial(down_back_kernel, (0, 1)), ins,
            [group_out, hid_b, sums_out, wide_f, wide_b], scalars=1,
        ),
        at, *d_ffn_pieces[:2], *ffn_weights, slope,
    )
    meet = Meet().near_pair(keep, give)
    d_ffn_group, d_pre, d_up_bias, keep, give = run(
        lambda *ins: call(
            partial(down_back_kernel, (2, 3)), ins,
            [group_out, hid_b, sums_out, wide_f, wide_b], scalars=1,
            alias={8: 0, 9: 1, 10: 2},
        ),
        at, *d_ffn_pieces[2:], *ffn_weights, slope, d_ffn_group, d_pre, d_up_bias,
    )
    meet.far_pair(keep, give)

    def half_grad(left, right, near):
        out = shape_of((D // 2, right.shape[1]), bf16)
        (made,) = run(lambda *ins: call(partial(half_grad_kernel, near), ins, [out]), left, right)
        return made

    meet.send()
    give = half_grad(d_ffn_group, act_low, False)
    s_down = Scatter(run, (give,), "dp", X_Z, given=give).send()
    give = half_grad(normed_group, d_pre, False)
    s_up = Scatter(run, (give,), "dp", Z_X, given=give).send()
    s_down.own(half_grad(d_ffn_group, act_low, True))
    s_up.own(half_grad(normed_group, d_pre, True))

    d_branch, d_resid_one, sums_one, a0, a1, a2 = run(
        lambda *ins: call(
            partial(first_back_kernel, width), ins,
            [wide_b, wide_f, shape_of((3, D), f32), doc_out, doc_out, pair_out],
            [pltpu.VMEM((ROWS, D), bf16)], scalars=1,
        ),
        at, *meet.terms(), d_resid_two, hat_one, scale_one, vec_one, *proj_near, *proj_far,
    )
    far = swap(a2, by_y)
    got_c = swap(a1, by_c)
    parts = run(
        lambda *ins: call(
            partial(proj_grad_kernel, width), ins, [col_out] * 4, scalars=1, cost=1.3
        ),
        at, attended, d_branch,
    )
    meet_proj = Meet().near_pair(parts[0], parts[1]).far_pair(parts[2], parts[3])
    grids = shape_of((3, NB, heads * NB), f32)
    room = [pltpu.VMEM((heads * ROWS, ROWS), bf16), pltpu.VMEM((ROWS, heads * NB), bf16)]
    d_qkv, d_sums, d_grid = run(
        lambda *ins: call(
            partial(attend_back_kernel, heads, (0, 1), False), ins,
            [qkv_out, shape_of((tp, 3 * width), f32), grids], room, cost=10,
        ),
        qkv, probs, a0, got_c, notes,
    )
    got_far = swap(second(far), by_c)
    meet_proj.send()
    d_qkv, d_sums, d_grid, d_ext = run(
        lambda *ins: call(
            partial(attend_back_kernel, heads, (2, 3), True), ins,
            [qkv_out, shape_of((tp, 3 * width), f32), grids, shape_of((3 * heads, 2 * NB), f32)],
            room,
            alias={5: 0, 6: 1, 7: 2},
        ),
        qkv, probs, far, got_far, notes, d_qkv, d_sums, d_grid,
    )

    def with_proj(k, c, y, small):
        p = (k.astype(f32) + c.astype(f32) + y.astype(f32)).astype(bf16)
        return jnp.concatenate([p, small], axis=-1).astype(f32)

    give = half_grad(group, d_qkv, False)
    s_first = Scatter(run, (give,), "dp", Z_X, given=give).send()
    run.wait(s_up.other, s_down.other)
    s_up.take().send()
    s_down.take().send()
    s_first.own(half_grad(group, d_qkv, True))
    plains = [pltpu.VMEM((24, D), f32)] * 2
    (small_grads,) = run(
        lambda *ins: call(
            partial(small_grads_kernel, heads, n_dev), ins, [shape_of((D, 128), bf16)],
            flats + plains, scalars=1,
        ),
        at, d_ext, d_sums, d_up_bias, sums_one, sums_two,
    )
    parts = run(
        lambda *ins: call(
            partial(tokens_back_kernel, width), ins, [wide_f, wide_b, wide_f, wide_b], scalars=1
        ),
        at, d_qkv, g_first.x, g_first.other,
    )
    meet_tok = Meet().near_pair(parts[0], parts[1]).far_pair(parts[2], parts[3])
    s_second = Scatter(
        run, (*meet_proj.terms(), small_grads), "dp", Z_X, base=with_proj
    ).send()
    s_up.take().send()
    s_first.take().send()
    run.wait(s_first.other)
    s_first.take().send()
    meet_tok.send()
    run.wait(s_up.other, s_down.other, s_second.other, s_first.other)
    s_second.take().send()
    s_down.take().send()

    def columns_back(scatters):
        sums = [x.sum().reshape(tp, rows, -1) for x in scatters]
        out = shape_of((2, rows, sum(x.shape[2] for x in sums)), bf16)

        def fn(at, *refs):
            for target, c in ((refs[-2], 1 - at[0] % 2), (refs[-1], at[0] % 2)):
                for y in range(2):
                    target[y] = jnp.concatenate([ref[2 * y + c] for ref in refs[:-2]], axis=1)

        return Exchange(run, at, *run(lambda *ins: call(fn, ins, [out, out], scalars=1), at, *sums))

    def whole_rows(exchanged, groups, widths, smalls):
        outs = [shape_of((rows, tp * g * w), f32) for g, w in zip(groups, widths)]
        ends = [shape_of((1, n * rows), f32) for n in smalls]

        def fn(at, mine, other, *refs):
            outs, ends = refs[: len(groups)], refs[len(groups) :]
            total = None
            for near, ref in ((True, mine), (False, other)):
                for n in range(2):
                    start, f = 0, source_of(at, near, n)
                    for out, g, w in zip(outs, groups, widths):
                        for i in range(g):
                            place = pl.multiple_of((i * tp + f) * w, w)
                            out[:, pl.ds(place, w)] = ref[n, :, start : start + w].astype(f32)
                            start += w
                    if ends:
                        part = ref[n, :, start:].astype(f32)
                        total = part if total is None else total + part
            if ends:
                small_outs(total, ends)

        return run(
            lambda *ins: call(fn, ins, outs + ends, scalars=1), at, exchanged.mine, exchanged.other
        )

    s_up.take()
    s_first.take()
    x_up = columns_back([s_up, s_first]).turn()
    s_second.take().send()
    run.wait(s_down.other, s_second.other, meet_tok.far, x_up.other)
    s_down.take()
    s_second.take()
    x_rest = columns_back([s_down, s_second])
    out_f = shape_of((1, SLOTS, D), f32)
    grad_tokens = run(
        lambda *ins: glue(
            lambda d, k, c, y: (
                d[...] + k[...] + c[...].astype(f32) + y[...].astype(f32)
            )[:SLOTS][None],
            [out_f], *ins,
        ),
        d_resid_one, *meet_tok.terms(),
    )
    x_rest.turn()
    grad_up, grad_qkv = whole_rows(x_up, (1, 3), (hidden, width), ())
    grad_down, grad_proj, *out = whole_rows(
        x_rest, (1, 1), (hidden, width), (1,) * 6 + (2, 6, 4)
    )
    out = [x.reshape(-1) for x in out]
    return (
        encoded,
        grad_tokens,
        grad_qkv,
        out[6],
        grad_proj,
        out[0],
        out[1],
        out[2],
        out[7],
        grad_up,
        out[8],
        grad_down,
        out[3],
        out[4],
        out[5],
    )


def solution(mesh):
    split = ("dp", "fsdp")
    one, two, three = P(split), P(split, None), P(split, None, None)
    return jax.shard_map(
        local,
        mesh=mesh,
        in_specs=(
            three, three, one, two, two, two, two, one, two, one, one, one, one, two, one, two,
            one, one, one,
        ),
        out_specs=(
            three, three, two, one, two, one, one, one, one, two, one, two, one, one, one,
        ),
        check_vma=False,
    )
```

```python
from functools import partial

import jax
import jax.numpy as jnp
from jax import lax
from jax.experimental import pallas as pl
from jax.experimental.pallas import tpu as pltpu
from jax.sharding import PartitionSpec as P

D = 1024
H = 16
HD = 64
FF = 4096
NB = 128
TEXT = 120
SLOTS = 169
ROWS = 176
NEGATIVE = -1e30
EPSILON = 1e-05

f32 = jnp.float32
bf16 = jnp.bfloat16


def shape_of(shape, kind):
    return jax.ShapeDtypeStruct(tuple(shape), kind)


def call(kernel, ins, outs, scratch=(), scalars=0, alias=None, vmem=16, cost=0):
    spaces = [pltpu.SMEM] * scalars + [pltpu.VMEM] * (len(ins) - scalars)
    return pl.pallas_call(
        kernel,
        in_specs=[pl.BlockSpec(memory_space=m) for m in spaces],
        out_specs=[pl.BlockSpec(memory_space=pltpu.VMEM) for _ in outs],
        out_shape=list(outs),
        scratch_shapes=list(scratch),
        input_output_aliases=alias or {},
        cost_estimate=pl.CostEstimate(
            flops=int(cost * 1e9), bytes_accessed=0, transcendentals=0
        ),
        compiler_params=pltpu.CompilerParams(vmem_limit_bytes=vmem * 2**20),
    )(*ins)


def glue(fn, outs, *ins, scalars=0):
    def kernel(*refs):
        made = fn(*refs[: len(ins)])
        for out, value in zip(refs[len(ins) :], made if isinstance(made, tuple) else (made,)):
            out[...] = value

    made = call(kernel, ins, outs, scalars=scalars)
    return made[0] if len(outs) == 1 else made


def axis_bits(axis):
    bits, b = [], lax.axis_size(axis) // 2
    while b >= 1:
        bits.append((axis, b))
        b //= 2
    return bits


def swap(x, bit):
    axis, b = bit
    return lax.ppermute(x, axis, [(i, i ^ b) for i in range(lax.axis_size(axis))])


def side(bit):
    axis, b = bit
    return (lax.axis_index(axis) // b) % 2


def pair_up(mine, other, bit, pos):
    one = side(bit) == 1
    return jnp.stack([jnp.where(one, other, mine), jnp.where(one, mine, other)], axis=pos)


class Order:
    def __init__(self):
        self.last = ()

    def tie(self, args):
        if not self.last:
            return args
        return lax.optimization_barrier(tuple(args) + self.last)[: len(args)]

    def wait(self, *arrays):
        self.last = self.last + arrays

    def __call__(self, fn, *args):
        out = fn(*self.tie(args))
        self.last = tuple(jax.tree.leaves(out))
        return out


def after(x, *earlier):
    return lax.optimization_barrier((x,) + earlier)[0]


def high_bits(axis, order):
    bits = axis_bits(axis)
    return [bits[i] for i in order]


class Gather:
    def __init__(self, run, x, axis, order):
        self.run, self.x = run, x
        self.bits = axis_bits(axis)[3:][::-1] + high_bits(axis, order)
        while len(self.bits) > 3:
            self.send().join()

    def send(self, *earlier):
        self.other = swap(after(self.x, *earlier), self.bits[0])
        return self

    def join(self):
        bit = self.bits.pop(0)
        if len(self.bits) >= 3:
            self.x = self.run(
                lambda m, o: pair_up(m, o, bit, 0).reshape(-1, m.shape[1]), self.x, self.other
            )
        else:
            r, c = self.x.shape

            def join(m, o, out):
                out[:r], out[r:] = m[...], o[...]

            (self.x,) = self.run(
                lambda *ins: call(join, ins, [shape_of((2 * r, c), bf16)]), self.x, self.other
            )
        return self


class Scatter:
    def __init__(self, run, arrays, axis, order, walk=None, base=None, given=None):
        self.run = run
        self.high, rest = high_bits(axis, order), axis_bits(axis)[3:]
        have = self.high[::-1] + rest
        self.order = (high_bits(axis, walk) if walk else self.high[::-1]) + rest
        self.low = len(rest)
        if given is not None:
            have = [bit for bit in have if bit != self.order[0]]
            given = given.reshape((2,) * len(have) + (-1, given.shape[-1]))
        self.given = given
        arrays = tuple(a.reshape((2,) * len(have) + (-1, a.shape[-1])) for a in arrays)
        self.terms = [(arrays, have, [], base or (lambda x: x.astype(f32)))]

    def own(self, array):
        arrays, *rest = self.terms[0]
        self.terms[0] = ((array.reshape(arrays[0].shape),), *rest)

    def flat(self):
        return [a for arrays, *unused in self.terms for a in arrays]

    def value(self, flat, extra=()):
        flat, total = list(flat), None
        for arrays, have, cuts, base in self.terms:
            chosen = dict(list(cuts) + list(extra))
            at = tuple(
                slice(None) if bit not in chosen
                else (0 if chosen[bit] else 1) if bit in self.high
                else side(bit) if chosen[bit] else 1 - side(bit)
                for bit in have
            )
            part = base(*[flat.pop(0)[at] for unused in arrays])
            total = part if total is None else total + part
        return total

    def sum(self, extra=()):
        flat = self.flat()
        fn = lambda *f: self.value(f, extra).astype(bf16)
        if self.low:
            return self.run(fn, *flat)
        out = jax.eval_shape(fn, *flat)
        return self.run(lambda *f: glue(fn, [out], *f), *flat)

    def send(self, *earlier):
        bit = self.order[0]
        out = self.given if self.given is not None else self.sum([(bit, False)])
        self.other = swap(after(out, *earlier), bit)
        return self

    def take(self):
        bit = self.order.pop(0)
        for arrays, have, cuts, base in self.terms:
            if self.given is None:
                cuts.append((bit, True))
        self.given = None
        self.terms.append(((self.other,), list(self.order_left()), [], lambda x: x.astype(f32)))
        while 0 < len(self.order) <= self.low:
            self.send().take()
        return self

    def order_left(self):
        arrays, have, cuts, base = self.terms[0]
        gone = [bit for bit, keep in cuts]
        return [bit for bit in have if bit not in gone]


class Exchange:
    def __init__(self, run, at, give, keep):
        self.run, self.at, self.keep = run, at, keep
        self.other = swap(give, axis_bits("fsdp")[1])

    def turn(self, *earlier):
        def fn(at, keep, got, give, mine):
            y, c = at[0] // 2, at[0] % 2
            give[c], give[1 - c] = keep[1 - y], got[1 - y]
            mine[c], mine[1 - c] = keep[y], got[y]

        out = shape_of(self.keep.shape, self.keep.dtype)
        give, self.mine = self.run(
            lambda *ins: call(fn, ins, [out, out], scalars=1), self.at, self.keep, self.other
        )
        self.other = swap(after(give, *earlier), axis_bits("fsdp")[0])
        return self


def source_of(at, near, n):
    y = at[0] // 2
    return (y if near else 1 - y) * 2 + n


def dot_nn(a, b):
    return jnp.dot(a, b, preferred_element_type=f32)


def dot_nt(a, b):
    return lax.dot_general(a, b, (((1,), (1,)), ((), ())), preferred_element_type=f32)


def dot_tn(a, b):
    return lax.dot_general(a, b, (((0,), (0,)), ((), ())), preferred_element_type=f32)


def call_docs(kernel, docs, ins, in_whole, outs):
    def spec(a, whole):
        n = len(a.shape)
        if whole:
            return pl.BlockSpec(tuple(a.shape), lambda d: (0,) * n)
        return pl.BlockSpec((1,) + tuple(a.shape[1:]), lambda d: (d,) + (0,) * (n - 1))

    return pl.pallas_call(
        kernel,
        grid=(docs,),
        in_specs=[spec(a, w) for a, w in zip(ins, in_whole)],
        out_specs=[spec(a, False) for a in outs],
        out_shape=list(outs),
        cost_estimate=pl.CostEstimate(flops=0, bytes_accessed=0, transcendentals=0),
        compiler_params=pltpu.CompilerParams(vmem_limit_bytes=16 * 2**20),
    )(*ins)


def at_block(ref, me, j, size):
    return pl.ds(pl.multiple_of((me ^ j) * size, size), size)


BLOCK = D // 8
Z_X = (0, 1, 2)
X_Z = (0, 2, 1)
X_FIRST = (2, 1, 0)


def far_block(place, q, order):
    away = sum(((q >> n) & 1) * (4 >> bit) for n, bit in enumerate(order))
    return pl.ds(pl.multiple_of((place ^ away) * BLOCK, BLOCK), BLOCK)


def relative(src, dst, place, order, rows):
    for q in range(8):
        dst[rows, q * BLOCK : (q + 1) * BLOCK] = src[:, far_block(place, q, order)]


def doc_at(j):
    return slice(j * ROWS, (j + 1) * ROWS)


def hot_rows(notes, flip=False):
    buckets = lax.broadcasted_iota(jnp.int32, (NB, ROWS), 0).astype(f32)
    if flip:
        buckets = (NB - 1) - buckets
    return [(notes[r : r + 1, :ROWS] == buckets).astype(f32).astype(bf16) for r in (12, 9, 10)]


ROW_QV, ROW_TABLES, ROW_UP = 6, 7, 9
TILE_ROWS = 16


def pack_kernel(*refs):
    *smalls, out_ref = refs
    rows = smalls[0].shape[1]
    tile = jnp.zeros(out_ref.shape, f32)
    row = lax.broadcasted_iota(jnp.int32, out_ref.shape, 0)
    qv, tables, up = smalls[6:]
    parts = list(smalls[:6]) + [qv] + [tables.at[:, 3 * n * rows : 3 * (n + 1) * rows] for n in range(2)]
    for n, ref in enumerate(parts + [up]):
        value = ref[...].astype(f32)
        wide = jnp.concatenate(
            [value, jnp.zeros((1, 128 - value.shape[1]), f32)], axis=1
        ) if value.shape[1] < 128 else value
        tile = jnp.where(row == n, jnp.broadcast_to(wide, out_ref.shape), tile)
    out_ref[...] = tile.astype(bf16)


def unpack_kernel(heads, count, at_ref, all_ref, ext_ref, add_ref, up_ref, one_ref, two_ref, qv_ref, tab_ref, upb_ref):
    me, place = at_ref[0], at_ref[1]
    rows, width, low = D // count, heads * HD, count // 32
    for d in range(count):
        q = place ^ (d // (4 * low))
        block = (q * low + (d // 4) % low) * 4 + (me ^ (d % 4))
        place_of = pl.ds(pl.multiple_of(block * TILE_ROWS, TILE_ROWS), TILE_ROWS)
        tile = all_ref[place_of, :].astype(f32)
        at = slice(d * rows, (d + 1) * rows)
        one_ref[:, at] = tile[0:3, :rows]
        two_ref[:, at] = tile[3:6, :rows]
        qv_ref[:, 2 * d * rows : 2 * (d + 1) * rows] = tile[ROW_QV : ROW_QV + 1, : 2 * rows]
        for n in range(2):
            start = (2 * d + n) * 3 * rows
            row = tile[ROW_TABLES + n : ROW_TABLES + n + 1, : 3 * rows]
            tab_ref[:, start : start + 3 * rows] = row
        upb_ref[:, 4 * d * rows : 4 * (d + 1) * rows] = tile[ROW_UP : ROW_UP + 1, : 4 * rows]
    start = pl.multiple_of(me * width, width)
    add_ref[:, :width] = qv_ref[:, pl.ds(start, width)]
    add_ref[:, width : 2 * width] = jnp.zeros((1, width), f32)
    add_ref[:, 2 * width :] = qv_ref[:, pl.ds(D + start, width)]
    hidden = up_ref.shape[1]
    up_ref[...] = upb_ref[:, pl.ds(pl.multiple_of(me * hidden, hidden), hidden)]
    half = NB // 2
    for k in range(3):
        for h in range(heads):
            n = k * heads + h
            row = tab_ref[:, pl.ds(pl.multiple_of((k * H + me * heads + h) * NB, NB), NB)]
            ext_ref[n : n + 1, :half] = jnp.broadcast_to(row[:, :1], (1, half))
            ext_ref[n : n + 1, half : half + NB] = row
            ext_ref[n : n + 1, half + NB :] = jnp.broadcast_to(row[:, NB - 1 :], (1, half))


PIECES = 18


def small_grads_kernel(
    heads, count, at_ref, ext_ref, sums_ref, up_ref, one_ref, two_ref, out_ref,
    qv_ref, tab_ref, upb_ref, plain_ref, order_ref,
):
    me = at_ref[0]
    rows, width = D // count, heads * HD
    for ref in (qv_ref, tab_ref, upb_ref, plain_ref):
        ref[...] = jnp.zeros_like(ref)
    start = pl.multiple_of(me * width, width)
    sums = jnp.sum(sums_ref[...], axis=0, keepdims=True)
    qv_ref[:, pl.ds(start, width)] = sums[:, :width]
    qv_ref[:, pl.ds(D + start, width)] = sums[:, 2 * width :]
    hidden = up_ref.shape[1]
    upb_ref[:, pl.ds(pl.multiple_of(me * hidden, hidden), hidden)] = jnp.sum(
        up_ref[...], axis=0, keepdims=True
    )
    half = NB // 2
    lane = lax.broadcasted_iota(jnp.int32, (1, NB), 1)
    for k in range(3):
        for h in range(heads):
            row = ext_ref[k * heads + h : k * heads + h + 1, :]
            low = jnp.sum(row[:, :half], axis=1, keepdims=True)
            high = jnp.sum(row[:, half + NB :], axis=1, keepdims=True)
            grad = row[:, half : half + NB] + jnp.where(lane == 0, low, 0.0)
            grad = grad + jnp.where(lane == NB - 1, high, 0.0)
            tab_ref[:, pl.ds(pl.multiple_of((k * H + me * heads + h) * NB, NB), NB)] = grad
    plain_ref[0:3, :] = one_ref[...]
    plain_ref[3:6, :] = two_ref[...]
    for d in range(count):
        at = slice(d * rows, (d + 1) * rows)
        row = 6
        for ref, times in ((qv_ref, 2), (tab_ref, 6), (upb_ref, 4)):
            for n in range(times):
                begin = (d * times + n) * rows
                plain_ref[row : row + 1, at] = ref[:, begin : begin + rows]
                row += 1
    relative(plain_ref, order_ref, at_ref[1], Z_X, slice(None))
    shape = (plain_ref.shape[0], 128)
    same = lax.broadcasted_iota(jnp.int32, shape, 0) == lax.broadcasted_iota(jnp.int32, shape, 1)
    out_ref[...] = dot_tn(order_ref[...].astype(bf16), same.astype(f32).astype(bf16)).astype(bf16)


def small_outs(total, outs):
    rows = total.shape[0]
    shape = (rows, rows)
    same = lax.broadcasted_iota(jnp.int32, shape, 0) == lax.broadcasted_iota(jnp.int32, shape, 1)
    turned = lax.dot_general(
        total, same.astype(f32), (((0,), (0,)), ((), ())),
        precision=lax.Precision.HIGHEST, preferred_element_type=f32,
    )
    row = 0
    for out in outs:
        for n in range(out.shape[1] // rows):
            out[:, n * rows : (n + 1) * rows] = turned[row : row + 1, :]
            row += 1


def bias_kernel(heads, notes_ref, ext_ref, out_ref):
    notes = notes_ref[0].astype(f32)
    hots = hot_rows(notes)
    every_hot = jnp.concatenate(hots, axis=0)
    live = notes[11:12, :ROWS] > 0.5
    for h in range(heads):
        codes = []
        for k in range(3):
            row = ext_ref[k * heads + h : k * heads + h + 1, :]
            spread = jnp.broadcast_to(row, (NB, 2 * NB))
            skew = pltpu.roll(spread, NB, 1, stride=1, stride_axis=0)
            codes.append(dot_tn(hots[k], skew[:, :NB].astype(bf16)).astype(bf16))
        total = dot_nn(jnp.concatenate(codes, axis=1), every_hot)
        out_ref[0, h] = jnp.where(live, total, NEGATIVE)


def softmax_rows(q, k, bias):
    s = dot_nt(q, k) * 0.125 + bias
    e = jnp.exp(s - jnp.max(s, axis=-1, keepdims=True))
    return e * (1.0 / jnp.sum(e, axis=-1, keepdims=True))


def attend_kernel(heads, pair, at_ref, d0, d1, near_ref, far_ref, add_ref, bias_ref, *rest):
    group_ref, qkv_ref, probs_ref, mixed_ref = rest[-4:]
    width = heads * HD
    for j, piece in zip(pair, (d0, d1)):
        relative(piece, group_ref, at_ref[1], Z_X, doc_at(j))
    both = slice(pair[0] * ROWS, (pair[1] + 1) * ROWS)
    for n in range(3):
        at = slice(n * width, (n + 1) * width)
        qkv = dot_nn(group_ref[both, : D // 2], near_ref[:, at])
        qkv = qkv + dot_nn(group_ref[both, D // 2 :], far_ref[:, at])
        qkv_ref[both, at] = (qkv + add_ref[:, at]).astype(bf16)
    for n, j in enumerate(pair):
        outs = []
        for h in range(heads):
            q = qkv_ref[doc_at(j), h * HD : (h + 1) * HD]
            k = qkv_ref[doc_at(j), width + h * HD : width + (h + 1) * HD]
            v = qkv_ref[doc_at(j), 2 * width + h * HD : 2 * width + (h + 1) * HD]
            probs = softmax_rows(q, k, bias_ref[j, h])
            probs_ref[j, h] = probs
            outs.append(dot_nn(probs.astype(bf16), v).astype(bf16))
        mixed_ref[n] = jnp.concatenate(outs, axis=1)


def norm_parts(values):
    average = jnp.mean(values, axis=-1, keepdims=True)
    centred = values - average
    spread = jnp.mean(centred * centred, axis=-1, keepdims=True)
    scale = lax.rsqrt(spread + EPSILON)
    return centred * scale, scale


def norm_back(grad, gain, hat, scale):
    scaled = grad * gain
    first = jnp.mean(scaled, axis=-1, keepdims=True)
    second = jnp.mean(scaled * hat, axis=-1, keepdims=True)
    return (scaled - first - hat * second) * scale


def first_norm_kernel(
    width, at_ref, a0, a1, a2, a3, *rest
):
    near, far = rest[:4], rest[4:8]
    tokens_ref, vec_ref, att_ref, low_ref, normed_ref, hat_ref, scale_ref, branch_ref, plain_ref = rest[8:]
    me = at_ref[0]
    for j, piece in enumerate((a0[0], a1[...], a2[0], a3[...])):
        plain_ref[:, at_block(plain_ref, me, j, width)] = piece
    relative(plain_ref, att_ref, at_ref[1], Z_X, slice(None))
    left, right = att_ref[:, : D // 2], att_ref[:, D // 2 :]
    for j in range(4):
        branch_ref[:, at_block(branch_ref, me, j, width)] = dot_nn(left, near[j][...]) + dot_nn(
            right, far[j][...]
        )
    resid = tokens_ref[...].astype(f32) + branch_ref[...] + vec_ref[0:1, :]
    hat, scale = norm_parts(resid)
    normed = hat * vec_ref[1:2, :] + vec_ref[2:3, :]
    low_ref[...] = normed.astype(bf16)
    normed_ref[...] = normed
    hat_ref[...] = hat
    scale_ref[...] = scale


def parts_back(left, near_ref, far_ref, outs, place, order):
    for q in range(0, 8, 2):
        ref = near_ref if q < 4 else far_ref
        at = slice((q % 4) * BLOCK, (q % 4 + 2) * BLOCK)
        part = dot_nt(left, ref[at, :])
        for n, out in enumerate(outs):
            for half in range(2):
                block = part[doc_at(n), half * BLOCK : (half + 1) * BLOCK]
                out[:, far_block(place, q + half, order)] = block.astype(out.dtype)


def half_grad_kernel(near, left_ref, right_ref, out_ref):
    left = left_ref[:, : D // 2] if near else left_ref[:, D // 2 :]

    def tile(n):
        at = pl.ds(pl.multiple_of(n * TILE, TILE), TILE)
        out_ref[:, at] = dot_tn(left, right_ref[:, at]).astype(bf16)

    steps = right_ref.shape[1] // TILE
    if near:
        pl.loop(0, steps)(tile)
    else:
        for n in range(steps):
            tile(n)


def normal_below(u):
    return 0.5 + 0.5 * lax.erf(u * (0.5**0.5))


def slope_kernel(pre_ref, slope_ref):
    for n in range(pre_ref.shape[1] // TILE):
        at = slice(n * TILE, (n + 1) * TILE)
        u = pre_ref[:, at]
        density = jnp.exp(-0.5 * u * u) * ((2 * jnp.pi) ** -0.5)
        slope_ref[:, at] = normal_below(u) + u * density


TILE = 256


def up_kernel(pair, at_ref, x0, x1, up_near, up_far, down_near, down_far, add_ref, *rest):
    group_ref, slope_ref, act_ref, keep_ref, give_ref = rest[-5:]
    for j, piece in zip(pair, (x0, x1)):
        relative(piece, group_ref, at_ref[1], Z_X, doc_at(j))
    both = slice(pair[0] * ROWS, (pair[1] + 1) * ROWS)
    for n in range(act_ref.shape[1] // TILE):
        at = slice(n * TILE, (n + 1) * TILE)
        pre = dot_nn(group_ref[both, : D // 2], up_near[:, at])
        pre = pre + dot_nn(group_ref[both, D // 2 :], up_far[:, at]) + add_ref[:, at]
        slope_ref[both, at] = pre
        act_ref[both, at] = (pre * normal_below(pre)).astype(bf16)
    parts_back(act_ref[both, :], down_near, down_far, (keep_ref, give_ref), at_ref[1], X_Z)


def down_back_kernel(pair, at_ref, g0, g1, down_near, down_far, up_near, up_far, slope_ref, *rest):
    group_ref, dpre_ref, sums_ref, keep_ref, give_ref = rest[-5:]
    for j, piece in zip(pair, (g0, g1)):
        relative(piece, group_ref, at_ref[1], X_Z, doc_at(j))
    both = slice(pair[0] * ROWS, (pair[1] + 1) * ROWS)
    for n in range(dpre_ref.shape[1] // TILE):
        at = slice(n * TILE, (n + 1) * TILE)
        d_act = dot_nn(group_ref[both, : D // 2], down_near[:, at])
        d_act = d_act + dot_nn(group_ref[both, D // 2 :], down_far[:, at])
        d_pre = (d_act * slope_ref[both, at]).astype(bf16)
        dpre_ref[both, at] = d_pre
        sums_ref[pair[0] // 2 : pair[0] // 2 + 1, at] = jnp.sum(d_pre.astype(f32), axis=0, keepdims=True)
    parts_back(dpre_ref[both, :], up_near, up_far, (keep_ref, give_ref), at_ref[1], Z_X)


def second_norm_kernel(
    keep_ref, got_c, got_y, normed_ref, grad_ref, live_ref, vec_ref,
    enc_ref, dffn_ref, dres_ref, sums_ref,
):
    ffn = keep_ref[...] + got_c[...].astype(f32) + got_y[...].astype(f32) + vec_ref[0:1, :]
    hat, scale = norm_parts(normed_ref[...] + ffn)
    ones = jnp.ones((8, 128), bf16)
    live = dot_tn(live_ref[...].astype(bf16), ones)[:, :1]
    gain = vec_ref[1:2, :]
    enc = ((hat * gain + vec_ref[2:3, :]) * live).astype(bf16)
    enc_ref[0] = enc[:SLOTS]
    grad = grad_ref[...].astype(f32) * live
    d_resid = norm_back(grad, gain, hat, scale)
    dres_ref[...] = d_resid
    low = d_resid.astype(bf16)
    dffn_ref[...] = low
    sums_ref[0:1, :] = jnp.sum(low.astype(f32), axis=0, keepdims=True)
    sums_ref[1:2, :] = jnp.sum(grad * hat, axis=0, keepdims=True)
    sums_ref[2:3, :] = jnp.sum(grad, axis=0, keepdims=True)


def first_back_kernel(width, at_ref, keep_ref, got_c, got_y, dres_ref, hat_ref, scale_ref, vec_ref, *rest):
    near, far = rest[:4], rest[4:8]
    branch_ref, done_ref, sums_ref, a0_ref, a1_ref, a2_ref, plain_ref = rest[8:]
    me = at_ref[0]
    hat = hat_ref[...]
    grad = dres_ref[...] + keep_ref[...] + got_c[...].astype(f32) + got_y[...].astype(f32)
    d_one = norm_back(grad, vec_ref[1:2, :], hat, scale_ref[...])
    done_ref[...] = d_one
    low = d_one.astype(bf16)
    branch_ref[...] = low
    sums_ref[0:1, :] = jnp.sum(low.astype(f32), axis=0, keepdims=True)
    sums_ref[1:2, :] = jnp.sum(grad * hat, axis=0, keepdims=True)
    sums_ref[2:3, :] = jnp.sum(grad, axis=0, keepdims=True)
    for n, proj in enumerate((near, far)):
        total = None
        for j in range(4):
            part = dot_nt(branch_ref[:, at_block(branch_ref, me, j, width)], proj[j][...])
            total = part if total is None else total + part
        for q in range(4):
            plain_ref[:, far_block(at_ref[1], 4 * n + q, Z_X)] = total[
                :, q * BLOCK : (q + 1) * BLOCK
            ].astype(bf16)
    for i, out in enumerate((a0_ref, a1_ref, a2_ref.at[0], a2_ref.at[1])):
        out[...] = plain_ref[:, at_block(plain_ref, me, i, width)]


def proj_grad_kernel(width, at_ref, att_ref, branch_ref, *outs):
    me = at_ref[0]
    att = att_ref[...]
    for j, out in enumerate(outs):
        out[...] = dot_tn(att, branch_ref[:, at_block(branch_ref, me, j, width)]).astype(bf16)


def attend_back_kernel(heads, pair, last, qkv_ref, probs_ref, g0, g1, notes_ref, *rest):
    ds_ref, wide_ref = rest[-2:]
    dqkv_ref, sums_ref, grid_ref = rest[-6:-3] if last else rest[-5:-2]
    width = heads * HD
    for j, grad_ref in zip(pair, (g0.at[0] if last else g0, g1)):
        notes = notes_ref[j].astype(f32)
        hots = jnp.concatenate(hot_rows(notes), axis=0)
        flipped = hot_rows(notes, flip=True)
        for h in range(heads):
            q = qkv_ref[doc_at(j), h * HD : (h + 1) * HD]
            k = qkv_ref[doc_at(j), width + h * HD : width + (h + 1) * HD]
            v = qkv_ref[doc_at(j), 2 * width + h * HD : 2 * width + (h + 1) * HD]
            g = grad_ref[:, h * HD : (h + 1) * HD]
            p = probs_ref[j, h]
            dp = dot_nt(g, v)
            ds = (p * (dp - jnp.sum(p * dp, axis=-1, keepdims=True))).astype(bf16)
            ds_ref[doc_at(h), :] = ds
            dq = (dot_nn(ds, k) * 0.125).astype(bf16)
            dk = (dot_tn(ds, q) * 0.125).astype(bf16)
            dv = dot_tn(p.astype(bf16), g).astype(bf16)
            for c, d in enumerate((dq, dk, dv)):
                at = slice(c * width + h * HD, c * width + (h + 1) * HD)
                dqkv_ref[doc_at(j), at] = d
        part = dot_nt(ds_ref[...], hots).astype(bf16)
        for n in range(3):
            for h in range(heads):
                wide_ref[:, h * NB : (h + 1) * NB] = part[doc_at(h), n * NB : (n + 1) * NB]
            term = dot_nn(flipped[n], wide_ref[...])
            if j == 0:
                grid_ref[n] = term
            else:
                grid_ref[n] += term
        sums_ref[j : j + 1, :] = jnp.sum(dqkv_ref[doc_at(j), :].astype(f32), axis=0, keepdims=True)
    if last:
        ext_ref = rest[-3]
        for n in range(3 * heads):
            block = grid_ref[n // heads, :, (n % heads) * NB : (n % heads + 1) * NB]
            wide = jnp.concatenate([block, jnp.zeros((NB, NB), f32)], axis=1)
            skew = pltpu.roll(wide, 1, 1, stride=1, stride_axis=0)
            ext_ref[n : n + 1, :] = jnp.sum(skew, axis=0, keepdims=True)


def tokens_back_kernel(width, at_ref, d_ref, near_ref, far_ref, *outs):
    for q in range(0, 8, 2):
        ref = near_ref if q < 4 else far_ref
        at = slice((q % 4) * BLOCK, (q % 4 + 2) * BLOCK)
        part = dot_nt(d_ref[...], ref[at, : 3 * width])
        for n, out in enumerate(outs):
            for half in range(2):
                block = part[doc_at(n), half * BLOCK : (half + 1) * BLOCK]
                out[:, far_block(at_ref[1], q + half, Z_X)] = block.astype(out.dtype)


def pad_rows(x):
    return jnp.pad(x, ((0, ROWS - SLOTS), (0, 0)))


def local(
    tokens,
    out_grad,
    text_len,
    x_bucket,
    y_bucket,
    patch_mask,
    qkv_weight,
    qv_bias,
    proj_weight,
    proj_bias,
    first_gain,
    first_shift,
    rel_tables,
    up_weight,
    up_bias,
    down_weight,
    down_bias,
    second_gain,
    second_shift,
):
    inner = axis_bits("fsdp")
    outer = axis_bits("dp")
    tp = 4
    by_y, by_c = inner
    dpn = lax.axis_size("dp")
    n_dev = tp * dpn
    rows = D // n_dev
    heads = H // tp
    width = heads * HD
    hidden = FF // tp
    me = lax.axis_index("fsdp")
    place = lax.axis_index("dp") // (dpn // 8)
    at = jnp.stack([me, place]).astype(jnp.int32)
    run = Order()
    run.wait(at)
    doc_out = shape_of((ROWS, width), bf16)

    def group_of(own):
        far = swap(own, by_y)
        return own, swap(own, by_c), far, swap(far, by_c)

    def second(pair):
        return run(lambda p: glue(lambda ref: ref[1], [doc_out], p), pair)

    def trade(p1, far):
        return swap(p1, by_c), far, swap(second(far), by_c)

    class Meet:
        def near_pair(self, keep, give):
            self.keep, self.near = keep, swap(give, by_c)
            return self

        def far_pair(self, keep, give):
            self.held, self.both = keep, swap(give, by_c)
            return self

        def send(self):
            out = shape_of(self.held.shape, bf16)
            fn = lambda k, g: (k[...].astype(f32) + g[...].astype(f32)).astype(bf16)
            both = run(lambda *ins: glue(fn, [out], *ins), self.held, self.both)
            self.far = swap(both, by_y)
            return self

        def terms(self):
            return self.keep, self.near, self.far

    def column_blocks(shards, groups):
        widths = [a.shape[1] // (g * tp) for a, g in zip(shards, groups)]
        out = shape_of((2, rows, sum(w * g for w, g in zip(widths, groups))), bf16)

        def fn(at, *refs):
            for target, c in ((refs[-2], 1 - at[0] % 2), (refs[-1], at[0] % 2)):
                for y in range(2):
                    start = 0
                    for ref, w, g in zip(refs, widths, groups):
                        for n in range(g):
                            place = pl.multiple_of((n * tp + 2 * y + c) * w, w)
                            target[y, :, start : start + w] = ref[:, pl.ds(place, w)]
                            start += w

        return Exchange(
            run, at,
            *run(lambda *ins: call(fn, ins, [out, out], scalars=1), at, *shards),
        )

    def block_rows(exchanged, parts):
        cols = exchanged.mine.shape[2] // parts

        def fn(at, mine, other, *outs):
            for near, ref in ((True, mine), (False, other)):
                for n in range(2):
                    for p, out in enumerate(outs):
                        out[source_of(at, near, n)] = ref[n, :, p * cols : (p + 1) * cols]

        outs = run(
            lambda *ins: call(fn, ins, [shape_of((tp, rows, cols), bf16)] * parts, scalars=1),
            at, exchanged.mine, exchanged.other,
        )
        return [o.reshape(tp * rows, cols) for o in outs]

    ex_first = column_blocks((qkv_weight, proj_weight), (3, 1))

    smalls = [
        proj_bias, first_gain, first_shift, down_bias, second_gain, second_shift,
        qv_bias, rel_tables, up_bias,
    ]
    flats = [pltpu.VMEM((1, n), f32) for n in (2 * D, 3 * H * NB, FF)]

    places = jnp.arange(TEXT, dtype=jnp.int32)
    live_own = jnp.concatenate(
        [places[None, :] < text_len[:, None], patch_mask > 0], axis=1
    ).astype(f32)

    def document(tokens, x_bucket, y_bucket, live):
        pad_cols = ((0, 0), (0, D - SLOTS))
        positions = (jnp.arange(SLOTS, dtype=jnp.int32) * NB // SLOTS)[None]
        return jnp.concatenate(
            [
                tokens[0],
                jnp.pad(x_bucket.astype(bf16), pad_cols),
                jnp.pad(y_bucket.astype(bf16), pad_cols),
                jnp.pad(live.astype(bf16), pad_cols),
                jnp.pad(positions.astype(bf16), pad_cols),
                jnp.zeros((ROWS - SLOTS - 4, D), bf16),
            ],
            axis=0,
        )

    ex_ffn = column_blocks((up_weight, down_weight), (1, 1))
    ex_first.turn()
    ex_ffn.turn(ex_first.other)
    doc_rows = run(document, tokens, x_bucket, y_bucket, live_own)
    (packed,) = run(
        lambda *ins: call(pack_kernel, [x[None] for x in ins], [shape_of((TILE_ROWS, 128), bf16)]),
        *smalls,
    )

    def beside(m, o):
        r = m.shape[0]

        def join(m, o, out):
            out[:r], out[r:] = m[...], o[...]

        return run(lambda *ins: call(join, ins, [shape_of((2 * r, 128), bf16)]), m, o)[0]

    small_near = swap(packed, by_c)
    grad_in, live_row = run(
        lambda g, l: (pad_rows(g[0]), jnp.pad(l, ((0, 7), (0, ROWS - SLOTS)))), out_grad, live_own
    )
    pair = beside(packed, small_near)
    small_far = swap(pair, by_y)
    g_first = Gather(run, *block_rows(ex_first, 1), "dp", Z_X).send()
    g_small = Gather(run, beside(pair, small_far), "dp", X_FIRST).send()
    doc_far = swap(after(doc_rows, ex_ffn.other, small_far), by_y)
    doc_near = swap(doc_rows, by_c)
    up_own, down_own = block_rows(ex_ffn, 2)
    g_small.join().send()
    g_small.join().send()
    g_down = Gather(run, down_own, "dp", X_Z)
    g_first.join().send()
    g_down.send(g_first.x)
    doc_pieces = (doc_rows, doc_near, doc_far, swap(after(doc_far, g_first.x), by_c))

    def take_notes(*refs):
        for n in range(4):
            refs[4][n] = refs[n][ROWS - 16 :, : 2 * NB]

    (notes,) = run(
        lambda *ins: call(take_notes, ins, [shape_of((tp, 16, 2 * NB), bf16)]), *doc_pieces
    )
    run.wait(g_small.other)
    g_down.join()
    g_first.join().send()
    g_down.send()
    g_up = Gather(run, up_own, "dp", Z_X).send(g_down.x)
    ext, qkv_bias, my_upb, vec_one, vec_two = run(
        lambda *ins: call(
            partial(unpack_kernel, heads, n_dev), ins,
            [
                shape_of((3 * heads, 2 * NB), f32), shape_of((1, 3 * width), f32),
                shape_of((1, hidden), f32), shape_of((3, D), f32), shape_of((3, D), f32),
            ],
            flats, scalars=1,
        ),
        at, beside(g_small.x, g_small.other),
    )

    (bias,) = run(
        lambda *ins: call_docs(
            partial(bias_kernel, heads), tp, ins, [False, True],
            [shape_of((tp, heads, ROWS, ROWS), f32)],
        ),
        notes, ext,
    )
    g_up.join().send()
    col_out = shape_of((D, width), bf16)
    half_out = shape_of((D // 2, width), bf16)

    def proj_part(rows_of):
        return group_of(
            run(lambda w: glue(lambda ref: ref[:, 3 * width :], [half_out], w), rows_of)
        )

    proj_near = proj_part(g_first.x)
    g_up.join()
    run.wait(*proj_near)

    proj_far = proj_part(g_first.other)
    pair_out = shape_of((2, ROWS, width), bf16)
    group_out = shape_of((tp * ROWS, D), bf16)
    qkv_out = shape_of((tp * ROWS, 3 * width), bf16)
    probs_out = shape_of((tp, heads, ROWS, ROWS), f32)
    group, qkv, probs, far = run(
        lambda *ins: call(
            partial(attend_kernel, heads, (2, 3)), ins,
            [group_out, qkv_out, probs_out, pair_out], scalars=1,
        ),
        at, *doc_pieces[2:], g_first.x, g_first.other, qkv_bias, bias,
    )
    mixed_far = swap(far, by_y)
    g_up.send(g_first.other)
    g_down.join().send()
    group, qkv, probs, near = run(
        lambda *ins: call(
            partial(attend_kernel, heads, (0, 1)), ins,
            [group_out, qkv_out, probs_out, pair_out], scalars=1,
            alias={7: 0, 8: 1, 9: 2},
        ),
        at, *doc_pieces[:2], g_first.x, g_first.other, qkv_bias, bias, group, qkv, probs,
    )
    att_pieces = (near, *trade(second(near), mixed_far))

    wide_f = shape_of((ROWS, D), f32)
    wide_b = shape_of((ROWS, D), bf16)
    attended, normed_low, normed_one, hat_one, scale_one = run(
        lambda *ins: call(
            partial(first_norm_kernel, width), ins,
            [wide_b, wide_b, wide_f, wide_f, shape_of((ROWS, 1), f32)],
            [pltpu.VMEM((ROWS, D), f32), pltpu.VMEM((ROWS, D), bf16)], scalars=1,
        ),
        at, *att_pieces, *proj_near, *proj_far, doc_rows, vec_one,
    )

    normed_pieces = group_of(normed_low)
    hid_f = shape_of((tp * ROWS, hidden), f32)
    hid_b = shape_of((tp * ROWS, hidden), bf16)
    ffn_weights = (g_up.x, g_up.other, g_down.x, g_down.other)
    normed_group, slope, act_low, keep, give = run(
        lambda *ins: call(
            partial(up_kernel, (0, 1)), ins, [group_out, hid_f, hid_b, wide_f, wide_b], scalars=1,
        ),
        at, *normed_pieces[:2], *ffn_weights, my_upb,
    )
    meet = Meet().near_pair(keep, give)
    normed_group, slope, act_low, keep, give = run(
        lambda *ins: call(
            partial(up_kernel, (2, 3)), ins, [group_out, hid_f, hid_b, wide_f, wide_b], scalars=1,
            alias={8: 0, 9: 1, 10: 2},
        ),
        at, *normed_pieces[2:], *ffn_weights, my_upb, normed_group, slope, act_low,
    )
    meet.far_pair(keep, give).send()
    (slope,) = run(lambda *ins: call(slope_kernel, ins, [hid_f]), slope)
    encoded, d_ffn, d_resid_two, sums_two = run(
        lambda *ins: call(
            second_norm_kernel, ins,
            [shape_of((1, SLOTS, D), bf16), wide_b, wide_f, shape_of((3, D), f32)],
        ),
        *meet.terms(), normed_one, grad_in, live_row, vec_two,
    )

    d_ffn_pieces = group_of(d_ffn)
    ffn_weights = (g_down.x, g_down.other, g_up.x, g_up.other)
    sums_out = shape_of((2, hidden), f32)
    d_ffn_group, d_pre, d_up_bias, keep, give = run(
        lambda *ins: call(
            partial(down_back_kernel, (0, 1)), ins,
            [group_out, hid_b, sums_out, wide_f, wide_b], scalars=1,
        ),
        at, *d_ffn_pieces[:2], *ffn_weights, slope,
    )
    meet = Meet().near_pair(keep, give)
    d_ffn_group, d_pre, d_up_bias, keep, give = run(
        lambda *ins: call(
            partial(down_back_kernel, (2, 3)), ins,
            [group_out, hid_b, sums_out, wide_f, wide_b], scalars=1,
            alias={8: 0, 9: 1, 10: 2},
        ),
        at, *d_ffn_pieces[2:], *ffn_weights, slope, d_ffn_group, d_pre, d_up_bias,
    )
    meet.far_pair(keep, give)

    def half_grad(left, right, near):
        out = shape_of((D // 2, right.shape[1]), bf16)
        (made,) = run(lambda *ins: call(partial(half_grad_kernel, near), ins, [out]), left, right)
        return made

    meet.send()
    give = half_grad(d_ffn_group, act_low, False)
    s_down = Scatter(run, (give,), "dp", X_Z, given=give).send()
    give = half_grad(normed_group, d_pre, False)
    s_up = Scatter(run, (give,), "dp", Z_X, given=give).send()
    s_down.own(half_grad(d_ffn_group, act_low, True))
    s_up.own(half_grad(normed_group, d_pre, True))

    d_branch, d_resid_one, sums_one, a0, a1, a2 = run(
        lambda *ins: call(
            partial(first_back_kernel, width), ins,
            [wide_b, wide_f, shape_of((3, D), f32), doc_out, doc_out, pair_out],
            [pltpu.VMEM((ROWS, D), bf16)], scalars=1,
        ),
        at, *meet.terms(), d_resid_two, hat_one, scale_one, vec_one, *proj_near, *proj_far,
    )
    far = swap(a2, by_y)
    got_c = swap(a1, by_c)
    parts = run(
        lambda *ins: call(
            partial(proj_grad_kernel, width), ins, [col_out] * 4, scalars=1, cost=1.3
        ),
        at, attended, d_branch,
    )
    meet_proj = Meet().near_pair(parts[0], parts[1]).far_pair(parts[2], parts[3])
    grids = shape_of((3, NB, heads * NB), f32)
    room = [pltpu.VMEM((heads * ROWS, ROWS), bf16), pltpu.VMEM((ROWS, heads * NB), bf16)]
    d_qkv, d_sums, d_grid = run(
        lambda *ins: call(
            partial(attend_back_kernel, heads, (0, 1), False), ins,
            [qkv_out, shape_of((tp, 3 * width), f32), grids], room, cost=6,
        ),
        qkv, probs, a0, got_c, notes,
    )
    got_far = swap(second(far), by_c)
    meet_proj.send()
    d_qkv, d_sums, d_grid, d_ext = run(
        lambda *ins: call(
            partial(attend_back_kernel, heads, (2, 3), True), ins,
            [qkv_out, shape_of((tp, 3 * width), f32), grids, shape_of((3 * heads, 2 * NB), f32)],
            room,
            alias={5: 0, 6: 1, 7: 2},
        ),
        qkv, probs, far, got_far, notes, d_qkv, d_sums, d_grid,
    )

    def with_proj(k, c, y, small):
        p = (k.astype(f32) + c.astype(f32) + y.astype(f32)).astype(bf16)
        return jnp.concatenate([p, small], axis=-1).astype(f32)

    give = half_grad(group, d_qkv, False)
    s_first = Scatter(run, (give,), "dp", Z_X, given=give).send()
    run.wait(s_up.other, s_down.other)
    s_up.take().send()
    s_down.take().send()
    s_first.own(half_grad(group, d_qkv, True))
    plains = [pltpu.VMEM((24, D), f32)] * 2
    (small_grads,) = run(
        lambda *ins: call(
            partial(small_grads_kernel, heads, n_dev), ins, [shape_of((D, 128), bf16)],
            flats + plains, scalars=1,
        ),
        at, d_ext, d_sums, d_up_bias, sums_one, sums_two,
    )
    parts = run(
        lambda *ins: call(
            partial(tokens_back_kernel, width), ins, [wide_f, wide_b, wide_f, wide_b], scalars=1
        ),
        at, d_qkv, g_first.x, g_first.other,
    )
    meet_tok = Meet().near_pair(parts[0], parts[1]).far_pair(parts[2], parts[3])
    s_second = Scatter(
        run, (*meet_proj.terms(), small_grads), "dp", Z_X, base=with_proj
    ).send()
    s_up.take().send()
    s_first.take().send()
    run.wait(s_first.other)
    s_first.take().send()
    meet_tok.send()
    run.wait(s_up.other, s_down.other, s_second.other, s_first.other)
    s_second.take().send()
    s_down.take().send()

    def columns_back(scatters):
        sums = [x.sum().reshape(tp, rows, -1) for x in scatters]
        out = shape_of((2, rows, sum(x.shape[2] for x in sums)), bf16)

        def fn(at, *refs):
            for target, c in ((refs[-2], 1 - at[0] % 2), (refs[-1], at[0] % 2)):
                for y in range(2):
                    target[y] = jnp.concatenate([ref[2 * y + c] for ref in refs[:-2]], axis=1)

        return Exchange(run, at, *run(lambda *ins: call(fn, ins, [out, out], scalars=1), at, *sums))

    def whole_rows(exchanged, groups, widths, smalls):
        outs = [shape_of((rows, tp * g * w), f32) for g, w in zip(groups, widths)]
        ends = [shape_of((1, n * rows), f32) for n in smalls]

        def fn(at, mine, other, *refs):
            outs, ends = refs[: len(groups)], refs[len(groups) :]
            total = None
            for near, ref in ((True, mine), (False, other)):
                for n in range(2):
                    start, f = 0, source_of(at, near, n)
                    for out, g, w in zip(outs, groups, widths):
                        for i in range(g):
                            place = pl.multiple_of((i * tp + f) * w, w)
                            out[:, pl.ds(place, w)] = ref[n, :, start : start + w].astype(f32)
                            start += w
                    if ends:
                        part = ref[n, :, start:].astype(f32)
                        total = part if total is None else total + part
            if ends:
                small_outs(total, ends)

        return run(
            lambda *ins: call(fn, ins, outs + ends, scalars=1), at, exchanged.mine, exchanged.other
        )

    s_up.take()
    s_first.take()
    x_up = columns_back([s_up, s_first]).turn()
    s_second.take().send()
    run.wait(s_down.other, s_second.other, meet_tok.far, x_up.other)
    s_down.take()
    s_second.take()
    x_rest = columns_back([s_down, s_second])
    out_f = shape_of((1, SLOTS, D), f32)
    grad_tokens = run(
        lambda *ins: glue(
            lambda d, k, c, y: (
                d[...] + k[...] + c[...].astype(f32) + y[...].astype(f32)
            )[:SLOTS][None],
            [out_f], *ins,
        ),
        d_resid_one, *meet_tok.terms(),
    )
    x_rest.turn()
    grad_up, grad_qkv = whole_rows(x_up, (1, 3), (hidden, width), ())
    grad_down, grad_proj, *out = whole_rows(
        x_rest, (1, 1), (hidden, width), (1,) * 6 + (2, 6, 4)
    )
    out = [x.reshape(-1) for x in out]
    return (
        encoded,
        grad_tokens,
        grad_qkv,
        out[6],
        grad_proj,
        out[0],
        out[1],
        out[2],
        out[7],
        grad_up,
        out[8],
        grad_down,
        out[3],
        out[4],
        out[5],
    )


def solution(mesh):
    split = ("dp", "fsdp")
    one, two, three = P(split), P(split, None), P(split, None, None)
    return jax.shard_map(
        local,
        mesh=mesh,
        in_specs=(
            three, three, one, two, two, two, two, one, two, one, one, one, one, two, one, two,
            one, one, one,
        ),
        out_specs=(
            three, three, two, one, two, one, one, one, one, two, one, two, one, one, one,
        ),
        check_vma=False,
    )
```

```python
from functools import partial

import jax
import jax.numpy as jnp
from jax import lax
from jax.experimental import pallas as pl
from jax.experimental.pallas import tpu as pltpu
from jax.sharding import PartitionSpec as P

D = 1024
H = 16
HD = 64
FF = 4096
NB = 128
TEXT = 120
SLOTS = 169
ROWS = 176
NEGATIVE = -1e30
EPSILON = 1e-05

f32 = jnp.float32
bf16 = jnp.bfloat16


def shape_of(shape, kind):
    return jax.ShapeDtypeStruct(tuple(shape), kind)


def call(kernel, ins, outs, scratch=(), scalars=0, alias=None, vmem=16, cost=0):
    spaces = [pltpu.SMEM] * scalars + [pltpu.VMEM] * (len(ins) - scalars)
    return pl.pallas_call(
        kernel,
        in_specs=[pl.BlockSpec(memory_space=m) for m in spaces],
        out_specs=[pl.BlockSpec(memory_space=pltpu.VMEM) for _ in outs],
        out_shape=list(outs),
        scratch_shapes=list(scratch),
        input_output_aliases=alias or {},
        cost_estimate=pl.CostEstimate(
            flops=int(cost * 1e9), bytes_accessed=0, transcendentals=0
        ),
        compiler_params=pltpu.CompilerParams(vmem_limit_bytes=vmem * 2**20),
    )(*ins)


def glue(fn, outs, *ins, scalars=0):
    def kernel(*refs):
        made = fn(*refs[: len(ins)])
        for out, value in zip(refs[len(ins) :], made if isinstance(made, tuple) else (made,)):
            out[...] = value

    made = call(kernel, ins, outs, scalars=scalars)
    return made[0] if len(outs) == 1 else made


def axis_bits(axis):
    bits, b = [], lax.axis_size(axis) // 2
    while b >= 1:
        bits.append((axis, b))
        b //= 2
    return bits


def swap(x, bit):
    axis, b = bit
    return lax.ppermute(x, axis, [(i, i ^ b) for i in range(lax.axis_size(axis))])


def side(bit):
    axis, b = bit
    return (lax.axis_index(axis) // b) % 2


def pair_up(mine, other, bit, pos):
    one = side(bit) == 1
    return jnp.stack([jnp.where(one, other, mine), jnp.where(one, mine, other)], axis=pos)


class Order:
    def __init__(self):
        self.last = ()

    def tie(self, args):
        if not self.last:
            return args
        return lax.optimization_barrier(tuple(args) + self.last)[: len(args)]

    def wait(self, *arrays):
        self.last = self.last + arrays

    def __call__(self, fn, *args):
        out = fn(*self.tie(args))
        self.last = tuple(jax.tree.leaves(out))
        return out


def after(x, *earlier):
    return lax.optimization_barrier((x,) + earlier)[0]


def high_bits(axis, order):
    bits = axis_bits(axis)
    return [bits[i] for i in order]


class Gather:
    def __init__(self, run, x, axis, order):
        self.run, self.x = run, x
        self.bits = axis_bits(axis)[3:][::-1] + high_bits(axis, order)
        while len(self.bits) > 3:
            self.send().join()

    def send(self, *earlier):
        self.other = swap(after(self.x, *earlier), self.bits[0])
        return self

    def join(self):
        bit = self.bits.pop(0)
        if len(self.bits) >= 3:
            self.x = self.run(
                lambda m, o: pair_up(m, o, bit, 0).reshape(-1, m.shape[1]), self.x, self.other
            )
        else:
            r, c = self.x.shape

            def join(m, o, out):
                out[:r], out[r:] = m[...], o[...]

            (self.x,) = self.run(
                lambda *ins: call(join, ins, [shape_of((2 * r, c), bf16)]), self.x, self.other
            )
        return self


class Scatter:
    def __init__(self, run, arrays, axis, order, walk=None, base=None, given=None):
        self.run = run
        self.high, rest = high_bits(axis, order), axis_bits(axis)[3:]
        have = self.high[::-1] + rest
        self.order = (high_bits(axis, walk) if walk else self.high[::-1]) + rest
        self.low = len(rest)
        if given is not None:
            have = [bit for bit in have if bit != self.order[0]]
            given = given.reshape((2,) * len(have) + (-1, given.shape[-1]))
        self.given = given
        arrays = tuple(a.reshape((2,) * len(have) + (-1, a.shape[-1])) for a in arrays)
        self.terms = [(arrays, have, [], base or (lambda x: x.astype(f32)))]

    def own(self, array):
        arrays, *rest = self.terms[0]
        self.terms[0] = ((array.reshape(arrays[0].shape),), *rest)

    def flat(self):
        return [a for arrays, *unused in self.terms for a in arrays]

    def value(self, flat, extra=()):
        flat, total = list(flat), None
        for arrays, have, cuts, base in self.terms:
            chosen = dict(list(cuts) + list(extra))
            at = tuple(
                slice(None) if bit not in chosen
                else (0 if chosen[bit] else 1) if bit in self.high
                else side(bit) if chosen[bit] else 1 - side(bit)
                for bit in have
            )
            part = base(*[flat.pop(0)[at] for unused in arrays])
            total = part if total is None else total + part
        return total

    def sum(self, extra=()):
        flat = self.flat()
        fn = lambda *f: self.value(f, extra).astype(bf16)
        if self.low:
            return self.run(fn, *flat)
        out = jax.eval_shape(fn, *flat)
        return self.run(lambda *f: glue(fn, [out], *f), *flat)

    def send(self, *earlier):
        bit = self.order[0]
        out = self.given if self.given is not None else self.sum([(bit, False)])
        self.other = swap(after(out, *earlier), bit)
        return self

    def take(self):
        bit = self.order.pop(0)
        for arrays, have, cuts, base in self.terms:
            if self.given is None:
                cuts.append((bit, True))
        self.given = None
        self.terms.append(((self.other,), list(self.order_left()), [], lambda x: x.astype(f32)))
        while 0 < len(self.order) <= self.low:
            self.send().take()
        return self

    def order_left(self):
        arrays, have, cuts, base = self.terms[0]
        gone = [bit for bit, keep in cuts]
        return [bit for bit in have if bit not in gone]


class Exchange:
    def __init__(self, run, at, give, keep):
        self.run, self.at, self.keep = run, at, keep
        self.other = swap(give, axis_bits("fsdp")[1])

    def turn(self, *earlier):
        def fn(at, keep, got, give, mine):
            y, c = at[0] // 2, at[0] % 2
            give[c], give[1 - c] = keep[1 - y], got[1 - y]
            mine[c], mine[1 - c] = keep[y], got[y]

        out = shape_of(self.keep.shape, self.keep.dtype)
        give, self.mine = self.run(
            lambda *ins: call(fn, ins, [out, out], scalars=1), self.at, self.keep, self.other
        )
        self.other = swap(after(give, *earlier), axis_bits("fsdp")[0])
        return self


def source_of(at, near, n):
    y = at[0] // 2
    return (y if near else 1 - y) * 2 + n


def dot_nn(a, b):
    return jnp.dot(a, b, preferred_element_type=f32)


def dot_nt(a, b):
    return lax.dot_general(a, b, (((1,), (1,)), ((), ())), preferred_element_type=f32)


def dot_tn(a, b):
    return lax.dot_general(a, b, (((0,), (0,)), ((), ())), preferred_element_type=f32)


def call_docs(kernel, docs, ins, in_whole, outs):
    def spec(a, whole):
        n = len(a.shape)
        if whole:
            return pl.BlockSpec(tuple(a.shape), lambda d: (0,) * n)
        return pl.BlockSpec((1,) + tuple(a.shape[1:]), lambda d: (d,) + (0,) * (n - 1))

    return pl.pallas_call(
        kernel,
        grid=(docs,),
        in_specs=[spec(a, w) for a, w in zip(ins, in_whole)],
        out_specs=[spec(a, False) for a in outs],
        out_shape=list(outs),
        cost_estimate=pl.CostEstimate(flops=0, bytes_accessed=0, transcendentals=0),
        compiler_params=pltpu.CompilerParams(vmem_limit_bytes=16 * 2**20),
    )(*ins)


def at_block(ref, me, j, size):
    return pl.ds(pl.multiple_of((me ^ j) * size, size), size)


BLOCK = D // 8
Z_X = (0, 1, 2)
X_Z = (0, 2, 1)
X_FIRST = (2, 1, 0)


def far_block(place, q, order):
    away = sum(((q >> n) & 1) * (4 >> bit) for n, bit in enumerate(order))
    return pl.ds(pl.multiple_of((place ^ away) * BLOCK, BLOCK), BLOCK)


def relative(src, dst, place, order, rows):
    for q in range(8):
        dst[rows, q * BLOCK : (q + 1) * BLOCK] = src[:, far_block(place, q, order)]


def doc_at(j):
    return slice(j * ROWS, (j + 1) * ROWS)


def hot_rows(notes, flip=False):
    buckets = lax.broadcasted_iota(jnp.int32, (NB, ROWS), 0).astype(f32)
    if flip:
        buckets = (NB - 1) - buckets
    return [(notes[r : r + 1, :ROWS] == buckets).astype(f32).astype(bf16) for r in (12, 9, 10)]


ROW_QV, ROW_TABLES, ROW_UP = 6, 7, 9
TILE_ROWS = 16


def pack_kernel(*refs):
    *smalls, out_ref = refs
    rows = smalls[0].shape[1]
    tile = jnp.zeros(out_ref.shape, f32)
    row = lax.broadcasted_iota(jnp.int32, out_ref.shape, 0)
    qv, tables, up = smalls[6:]
    parts = list(smalls[:6]) + [qv] + [tables.at[:, 3 * n * rows : 3 * (n + 1) * rows] for n in range(2)]
    for n, ref in enumerate(parts + [up]):
        value = ref[...].astype(f32)
        wide = jnp.concatenate(
            [value, jnp.zeros((1, 128 - value.shape[1]), f32)], axis=1
        ) if value.shape[1] < 128 else value
        tile = jnp.where(row == n, jnp.broadcast_to(wide, out_ref.shape), tile)
    out_ref[...] = tile.astype(bf16)


def unpack_kernel(heads, count, at_ref, all_ref, ext_ref, add_ref, up_ref, one_ref, two_ref, qv_ref, tab_ref, upb_ref):
    me, place = at_ref[0], at_ref[1]
    rows, width, low = D // count, heads * HD, count // 32
    for d in range(count):
        q = place ^ (d // (4 * low))
        block = (q * low + (d // 4) % low) * 4 + (me ^ (d % 4))
        place_of = pl.ds(pl.multiple_of(block * TILE_ROWS, TILE_ROWS), TILE_ROWS)
        tile = all_ref[place_of, :].astype(f32)
        at = slice(d * rows, (d + 1) * rows)
        one_ref[:, at] = tile[0:3, :rows]
        two_ref[:, at] = tile[3:6, :rows]
        qv_ref[:, 2 * d * rows : 2 * (d + 1) * rows] = tile[ROW_QV : ROW_QV + 1, : 2 * rows]
        for n in range(2):
            start = (2 * d + n) * 3 * rows
            row = tile[ROW_TABLES + n : ROW_TABLES + n + 1, : 3 * rows]
            tab_ref[:, start : start + 3 * rows] = row
        upb_ref[:, 4 * d * rows : 4 * (d + 1) * rows] = tile[ROW_UP : ROW_UP + 1, : 4 * rows]
    start = pl.multiple_of(me * width, width)
    add_ref[:, :width] = qv_ref[:, pl.ds(start, width)]
    add_ref[:, width : 2 * width] = jnp.zeros((1, width), f32)
    add_ref[:, 2 * width :] = qv_ref[:, pl.ds(D + start, width)]
    hidden = up_ref.shape[1]
    up_ref[...] = upb_ref[:, pl.ds(pl.multiple_of(me * hidden, hidden), hidden)]
    half = NB // 2
    for k in range(3):
        for h in range(heads):
            n = k * heads + h
            row = tab_ref[:, pl.ds(pl.multiple_of((k * H + me * heads + h) * NB, NB), NB)]
            ext_ref[n : n + 1, :half] = jnp.broadcast_to(row[:, :1], (1, half))
            ext_ref[n : n + 1, half : half + NB] = row
            ext_ref[n : n + 1, half + NB :] = jnp.broadcast_to(row[:, NB - 1 :], (1, half))


PIECES = 18


def small_grads_kernel(
    heads, count, at_ref, ext_ref, sums_ref, up_ref, one_ref, two_ref, out_ref,
    qv_ref, tab_ref, upb_ref, plain_ref, order_ref,
):
    me = at_ref[0]
    rows, width = D // count, heads * HD
    for ref in (qv_ref, tab_ref, upb_ref, plain_ref):
        ref[...] = jnp.zeros_like(ref)
    start = pl.multiple_of(me * width, width)
    sums = jnp.sum(sums_ref[...], axis=0, keepdims=True)
    qv_ref[:, pl.ds(start, width)] = sums[:, :width]
    qv_ref[:, pl.ds(D + start, width)] = sums[:, 2 * width :]
    hidden = up_ref.shape[1]
    upb_ref[:, pl.ds(pl.multiple_of(me * hidden, hidden), hidden)] = jnp.sum(
        up_ref[...], axis=0, keepdims=True
    )
    half = NB // 2
    lane = lax.broadcasted_iota(jnp.int32, (1, NB), 1)
    for k in range(3):
        for h in range(heads):
            row = ext_ref[k * heads + h : k * heads + h + 1, :]
            low = jnp.sum(row[:, :half], axis=1, keepdims=True)
            high = jnp.sum(row[:, half + NB :], axis=1, keepdims=True)
            grad = row[:, half : half + NB] + jnp.where(lane == 0, low, 0.0)
            grad = grad + jnp.where(lane == NB - 1, high, 0.0)
            tab_ref[:, pl.ds(pl.multiple_of((k * H + me * heads + h) * NB, NB), NB)] = grad
    plain_ref[0:3, :] = one_ref[...]
    plain_ref[3:6, :] = two_ref[...]
    for d in range(count):
        at = slice(d * rows, (d + 1) * rows)
        row = 6
        for ref, times in ((qv_ref, 2), (tab_ref, 6), (upb_ref, 4)):
            for n in range(times):
                begin = (d * times + n) * rows
                plain_ref[row : row + 1, at] = ref[:, begin : begin + rows]
                row += 1
    relative(plain_ref, order_ref, at_ref[1], Z_X, slice(None))
    shape = (plain_ref.shape[0], 128)
    same = lax.broadcasted_iota(jnp.int32, shape, 0) == lax.broadcasted_iota(jnp.int32, shape, 1)
    out_ref[...] = dot_tn(order_ref[...].astype(bf16), same.astype(f32).astype(bf16)).astype(bf16)


def small_outs(total, outs):
    rows = total.shape[0]
    shape = (rows, rows)
    same = lax.broadcasted_iota(jnp.int32, shape, 0) == lax.broadcasted_iota(jnp.int32, shape, 1)
    turned = lax.dot_general(
        total, same.astype(f32), (((0,), (0,)), ((), ())),
        precision=lax.Precision.HIGHEST, preferred_element_type=f32,
    )
    row = 0
    for out in outs:
        for n in range(out.shape[1] // rows):
            out[:, n * rows : (n + 1) * rows] = turned[row : row + 1, :]
            row += 1


def bias_kernel(heads, notes_ref, ext_ref, out_ref):
    notes = notes_ref[0].astype(f32)
    hots = hot_rows(notes)
    every_hot = jnp.concatenate(hots, axis=0)
    live = notes[11:12, :ROWS] > 0.5
    for h in range(heads):
        codes = []
        for k in range(3):
            row = ext_ref[k * heads + h : k * heads + h + 1, :]
            spread = jnp.broadcast_to(row, (NB, 2 * NB))
            skew = pltpu.roll(spread, NB, 1, stride=1, stride_axis=0)
            codes.append(dot_tn(hots[k], skew[:, :NB].astype(bf16)).astype(bf16))
        total = dot_nn(jnp.concatenate(codes, axis=1), every_hot)
        out_ref[0, h] = jnp.where(live, total, NEGATIVE)


def softmax_rows(q, k, bias):
    s = dot_nt(q, k) * 0.125 + bias
    e = jnp.exp(s - jnp.max(s, axis=-1, keepdims=True))
    return e * (1.0 / jnp.sum(e, axis=-1, keepdims=True))


def attend_kernel(heads, pair, at_ref, d0, d1, near_ref, far_ref, add_ref, bias_ref, *rest):
    group_ref, qkv_ref, probs_ref, mixed_ref = rest[-4:]
    width = heads * HD
    for j, piece in zip(pair, (d0, d1)):
        relative(piece, group_ref, at_ref[1], Z_X, doc_at(j))
    both = slice(pair[0] * ROWS, (pair[1] + 1) * ROWS)
    for n in range(3):
        at = slice(n * width, (n + 1) * width)
        qkv = dot_nn(group_ref[both, : D // 2], near_ref[:, at])
        qkv = qkv + dot_nn(group_ref[both, D // 2 :], far_ref[:, at])
        qkv_ref[both, at] = (qkv + add_ref[:, at]).astype(bf16)
    for n, j in enumerate(pair):
        outs = []
        for h in range(heads):
            q = qkv_ref[doc_at(j), h * HD : (h + 1) * HD]
            k = qkv_ref[doc_at(j), width + h * HD : width + (h + 1) * HD]
            v = qkv_ref[doc_at(j), 2 * width + h * HD : 2 * width + (h + 1) * HD]
            probs = softmax_rows(q, k, bias_ref[j, h])
            probs_ref[j, h] = probs
            outs.append(dot_nn(probs.astype(bf16), v).astype(bf16))
        mixed_ref[n] = jnp.concatenate(outs, axis=1)


def norm_parts(values):
    average = jnp.mean(values, axis=-1, keepdims=True)
    centred = values - average
    spread = jnp.mean(centred * centred, axis=-1, keepdims=True)
    scale = lax.rsqrt(spread + EPSILON)
    return centred * scale, scale


def norm_back(grad, gain, hat, scale):
    scaled = grad * gain
    first = jnp.mean(scaled, axis=-1, keepdims=True)
    second = jnp.mean(scaled * hat, axis=-1, keepdims=True)
    return (scaled - first - hat * second) * scale


def first_norm_kernel(
    width, at_ref, a0, a1, a2, a3, *rest
):
    near, far = rest[:4], rest[4:8]
    tokens_ref, vec_ref, att_ref, low_ref, normed_ref, hat_ref, scale_ref, branch_ref, plain_ref = rest[8:]
    me = at_ref[0]
    for j, piece in enumerate((a0[0], a1[...], a2[0], a3[...])):
        plain_ref[:, at_block(plain_ref, me, j, width)] = piece
    relative(plain_ref, att_ref, at_ref[1], Z_X, slice(None))
    left, right = att_ref[:, : D // 2], att_ref[:, D // 2 :]
    for j in range(4):
        branch_ref[:, at_block(branch_ref, me, j, width)] = dot_nn(left, near[j][...]) + dot_nn(
            right, far[j][...]
        )
    resid = tokens_ref[...].astype(f32) + branch_ref[...] + vec_ref[0:1, :]
    hat, scale = norm_parts(resid)
    normed = hat * vec_ref[1:2, :] + vec_ref[2:3, :]
    low_ref[...] = normed.astype(bf16)
    normed_ref[...] = normed
    hat_ref[...] = hat
    scale_ref[...] = scale


def parts_back(left, near_ref, far_ref, outs, place, order):
    for q in range(0, 8, 2):
        ref = near_ref if q < 4 else far_ref
        at = slice((q % 4) * BLOCK, (q % 4 + 2) * BLOCK)
        part = dot_nt(left, ref[at, :])
        for n, out in enumerate(outs):
            for half in range(2):
                block = part[doc_at(n), half * BLOCK : (half + 1) * BLOCK]
                out[:, far_block(place, q + half, order)] = block.astype(out.dtype)


def half_grad_kernel(near, left_ref, right_ref, out_ref):
    left = left_ref[:, : D // 2] if near else left_ref[:, D // 2 :]

    def tile(n):
        at = pl.ds(pl.multiple_of(n * TILE, TILE), TILE)
        out_ref[:, at] = dot_tn(left, right_ref[:, at]).astype(bf16)

    steps = right_ref.shape[1] // TILE
    if near:
        pl.loop(0, steps)(tile)
    else:
        for n in range(steps):
            tile(n)


def normal_below(u):
    return 0.5 + 0.5 * lax.erf(u * (0.5**0.5))


def slope_kernel(pre_ref, slope_ref):
    for n in range(pre_ref.shape[1] // TILE):
        at = slice(n * TILE, (n + 1) * TILE)
        u = pre_ref[:, at]
        density = jnp.exp(-0.5 * u * u) * ((2 * jnp.pi) ** -0.5)
        slope_ref[:, at] = normal_below(u) + u * density


TILE = 256


def up_kernel(pair, at_ref, x0, x1, up_near, up_far, down_near, down_far, add_ref, *rest):
    group_ref, slope_ref, act_ref, keep_ref, give_ref = rest[-5:]
    for j, piece in zip(pair, (x0, x1)):
        relative(piece, group_ref, at_ref[1], Z_X, doc_at(j))
    both = slice(pair[0] * ROWS, (pair[1] + 1) * ROWS)
    for n in range(act_ref.shape[1] // TILE):
        at = slice(n * TILE, (n + 1) * TILE)
        pre = dot_nn(group_ref[both, : D // 2], up_near[:, at])
        pre = pre + dot_nn(group_ref[both, D // 2 :], up_far[:, at]) + add_ref[:, at]
        slope_ref[both, at] = pre
        act_ref[both, at] = (pre * normal_below(pre)).astype(bf16)
    parts_back(act_ref[both, :], down_near, down_far, (keep_ref, give_ref), at_ref[1], X_Z)


def down_back_kernel(pair, at_ref, g0, g1, down_near, down_far, up_near, up_far, slope_ref, *rest):
    group_ref, dpre_ref, sums_ref, keep_ref, give_ref = rest[-5:]
    for j, piece in zip(pair, (g0, g1)):
        relative(piece, group_ref, at_ref[1], X_Z, doc_at(j))
    both = slice(pair[0] * ROWS, (pair[1] + 1) * ROWS)
    for n in range(dpre_ref.shape[1] // TILE):
        at = slice(n * TILE, (n + 1) * TILE)
        d_act = dot_nn(group_ref[both, : D // 2], down_near[:, at])
        d_act = d_act + dot_nn(group_ref[both, D // 2 :], down_far[:, at])
        d_pre = (d_act * slope_ref[both, at]).astype(bf16)
        dpre_ref[both, at] = d_pre
        sums_ref[pair[0] // 2 : pair[0] // 2 + 1, at] = jnp.sum(d_pre.astype(f32), axis=0, keepdims=True)
    parts_back(dpre_ref[both, :], up_near, up_far, (keep_ref, give_ref), at_ref[1], Z_X)


def second_norm_kernel(
    keep_ref, got_c, got_y, normed_ref, grad_ref, live_ref, vec_ref,
    enc_ref, dffn_ref, dres_ref, sums_ref,
):
    ffn = keep_ref[...] + got_c[...].astype(f32) + got_y[...].astype(f32) + vec_ref[0:1, :]
    hat, scale = norm_parts(normed_ref[...] + ffn)
    ones = jnp.ones((8, 128), bf16)
    live = dot_tn(live_ref[...].astype(bf16), ones)[:, :1]
    gain = vec_ref[1:2, :]
    enc = ((hat * gain + vec_ref[2:3, :]) * live).astype(bf16)
    enc_ref[0] = enc[:SLOTS]
    grad = grad_ref[...].astype(f32) * live
    d_resid = norm_back(grad, gain, hat, scale)
    dres_ref[...] = d_resid
    low = d_resid.astype(bf16)
    dffn_ref[...] = low
    sums_ref[0:1, :] = jnp.sum(low.astype(f32), axis=0, keepdims=True)
    sums_ref[1:2, :] = jnp.sum(grad * hat, axis=0, keepdims=True)
    sums_ref[2:3, :] = jnp.sum(grad, axis=0, keepdims=True)


def first_back_kernel(width, at_ref, keep_ref, got_c, got_y, dres_ref, hat_ref, scale_ref, vec_ref, *rest):
    near, far = rest[:4], rest[4:8]
    branch_ref, done_ref, sums_ref, a0_ref, a1_ref, a2_ref, plain_ref = rest[8:]
    me = at_ref[0]
    hat = hat_ref[...]
    grad = dres_ref[...] + keep_ref[...] + got_c[...].astype(f32) + got_y[...].astype(f32)
    d_one = norm_back(grad, vec_ref[1:2, :], hat, scale_ref[...])
    done_ref[...] = d_one
    low = d_one.astype(bf16)
    branch_ref[...] = low
    sums_ref[0:1, :] = jnp.sum(low.astype(f32), axis=0, keepdims=True)
    sums_ref[1:2, :] = jnp.sum(grad * hat, axis=0, keepdims=True)
    sums_ref[2:3, :] = jnp.sum(grad, axis=0, keepdims=True)
    for n, proj in enumerate((near, far)):
        total = None
        for j in range(4):
            part = dot_nt(branch_ref[:, at_block(branch_ref, me, j, width)], proj[j][...])
            total = part if total is None else total + part
        for q in range(4):
            plain_ref[:, far_block(at_ref[1], 4 * n + q, Z_X)] = total[
                :, q * BLOCK : (q + 1) * BLOCK
            ].astype(bf16)
    for i, out in enumerate((a0_ref, a1_ref, a2_ref.at[0], a2_ref.at[1])):
        out[...] = plain_ref[:, at_block(plain_ref, me, i, width)]


def proj_grad_kernel(width, at_ref, att_ref, branch_ref, *outs):
    me = at_ref[0]
    att = att_ref[...]
    for j, out in enumerate(outs):
        out[...] = dot_tn(att, branch_ref[:, at_block(branch_ref, me, j, width)]).astype(bf16)


def attend_back_kernel(heads, pair, last, qkv_ref, probs_ref, g0, g1, notes_ref, *rest):
    ds_ref, wide_ref = rest[-2:]
    dqkv_ref, sums_ref, grid_ref = rest[-6:-3] if last else rest[-5:-2]
    width = heads * HD
    for j, grad_ref in zip(pair, (g0.at[0] if last else g0, g1)):
        notes = notes_ref[j].astype(f32)
        hots = jnp.concatenate(hot_rows(notes), axis=0)
        flipped = hot_rows(notes, flip=True)
        for h in range(heads):
            q = qkv_ref[doc_at(j), h * HD : (h + 1) * HD]
            k = qkv_ref[doc_at(j), width + h * HD : width + (h + 1) * HD]
            v = qkv_ref[doc_at(j), 2 * width + h * HD : 2 * width + (h + 1) * HD]
            g = grad_ref[:, h * HD : (h + 1) * HD]
            p = probs_ref[j, h]
            dp = dot_nt(g, v)
            ds = (p * (dp - jnp.sum(p * dp, axis=-1, keepdims=True))).astype(bf16)
            ds_ref[doc_at(h), :] = ds
            dq = (dot_nn(ds, k) * 0.125).astype(bf16)
            dk = (dot_tn(ds, q) * 0.125).astype(bf16)
            dv = dot_tn(p.astype(bf16), g).astype(bf16)
            for c, d in enumerate((dq, dk, dv)):
                at = slice(c * width + h * HD, c * width + (h + 1) * HD)
                dqkv_ref[doc_at(j), at] = d
        part = dot_nt(ds_ref[...], hots).astype(bf16)
        for n in range(3):
            for h in range(heads):
                wide_ref[:, h * NB : (h + 1) * NB] = part[doc_at(h), n * NB : (n + 1) * NB]
            term = dot_nn(flipped[n], wide_ref[...])
            if j == 0:
                grid_ref[n] = term
            else:
                grid_ref[n] += term
        sums_ref[j : j + 1, :] = jnp.sum(dqkv_ref[doc_at(j), :].astype(f32), axis=0, keepdims=True)
    if last:
        ext_ref = rest[-3]
        for n in range(3 * heads):
            block = grid_ref[n // heads, :, (n % heads) * NB : (n % heads + 1) * NB]
            wide = jnp.concatenate([block, jnp.zeros((NB, NB), f32)], axis=1)
            skew = pltpu.roll(wide, 1, 1, stride=1, stride_axis=0)
            ext_ref[n : n + 1, :] = jnp.sum(skew, axis=0, keepdims=True)


def tokens_back_kernel(width, at_ref, d_ref, near_ref, far_ref, *outs):
    for q in range(0, 8, 2):
        ref = near_ref if q < 4 else far_ref
        at = slice((q % 4) * BLOCK, (q % 4 + 2) * BLOCK)
        part = dot_nt(d_ref[...], ref[at, : 3 * width])
        for n, out in enumerate(outs):
            for half in range(2):
                block = part[doc_at(n), half * BLOCK : (half + 1) * BLOCK]
                out[:, far_block(at_ref[1], q + half, Z_X)] = block.astype(out.dtype)


def pad_rows(x):
    return jnp.pad(x, ((0, ROWS - SLOTS), (0, 0)))


def local(
    tokens,
    out_grad,
    text_len,
    x_bucket,
    y_bucket,
    patch_mask,
    qkv_weight,
    qv_bias,
    proj_weight,
    proj_bias,
    first_gain,
    first_shift,
    rel_tables,
    up_weight,
    up_bias,
    down_weight,
    down_bias,
    second_gain,
    second_shift,
):
    inner = axis_bits("fsdp")
    outer = axis_bits("dp")
    tp = 4
    by_y, by_c = inner
    dpn = lax.axis_size("dp")
    n_dev = tp * dpn
    rows = D // n_dev
    heads = H // tp
    width = heads * HD
    hidden = FF // tp
    me = lax.axis_index("fsdp")
    place = lax.axis_index("dp") // (dpn // 8)
    at = jnp.stack([me, place]).astype(jnp.int32)
    run = Order()
    run.wait(at)
    doc_out = shape_of((ROWS, width), bf16)

    def group_of(own):
        far = swap(own, by_y)
        return own, swap(own, by_c), far, swap(far, by_c)

    def second(pair):
        return run(lambda p: glue(lambda ref: ref[1], [doc_out], p), pair)

    def trade(p1, far):
        return swap(p1, by_c), far, swap(second(far), by_c)

    class Meet:
        def near_pair(self, keep, give):
            self.keep, self.near = keep, swap(give, by_c)
            return self

        def far_pair(self, keep, give):
            self.held, self.both = keep, swap(give, by_c)
            return self

        def send(self):
            out = shape_of(self.held.shape, bf16)
            fn = lambda k, g: (k[...].astype(f32) + g[...].astype(f32)).astype(bf16)
            both = run(lambda *ins: glue(fn, [out], *ins), self.held, self.both)
            self.far = swap(both, by_y)
            return self

        def terms(self):
            return self.keep, self.near, self.far

    def column_blocks(shards, groups):
        widths = [a.shape[1] // (g * tp) for a, g in zip(shards, groups)]
        out = shape_of((2, rows, sum(w * g for w, g in zip(widths, groups))), bf16)

        def fn(at, *refs):
            for target, c in ((refs[-2], 1 - at[0] % 2), (refs[-1], at[0] % 2)):
                for y in range(2):
                    start = 0
                    for ref, w, g in zip(refs, widths, groups):
                        for n in range(g):
                            place = pl.multiple_of((n * tp + 2 * y + c) * w, w)
                            target[y, :, start : start + w] = ref[:, pl.ds(place, w)]
                            start += w

        return Exchange(
            run, at,
            *run(lambda *ins: call(fn, ins, [out, out], scalars=1), at, *shards),
        )

    def block_rows(exchanged, parts):
        cols = exchanged.mine.shape[2] // parts

        def fn(at, mine, other, *outs):
            for near, ref in ((True, mine), (False, other)):
                for n in range(2):
                    for p, out in enumerate(outs):
                        out[source_of(at, near, n)] = ref[n, :, p * cols : (p + 1) * cols]

        outs = run(
            lambda *ins: call(fn, ins, [shape_of((tp, rows, cols), bf16)] * parts, scalars=1),
            at, exchanged.mine, exchanged.other,
        )
        return [o.reshape(tp * rows, cols) for o in outs]

    ex_first = column_blocks((qkv_weight, proj_weight), (3, 1))

    smalls = [
        proj_bias, first_gain, first_shift, down_bias, second_gain, second_shift,
        qv_bias, rel_tables, up_bias,
    ]
    flats = [pltpu.VMEM((1, n), f32) for n in (2 * D, 3 * H * NB, FF)]

    places = jnp.arange(TEXT, dtype=jnp.int32)
    live_own = jnp.concatenate(
        [places[None, :] < text_len[:, None], patch_mask > 0], axis=1
    ).astype(f32)

    def document(tokens, x_bucket, y_bucket, live):
        pad_cols = ((0, 0), (0, D - SLOTS))
        positions = (jnp.arange(SLOTS, dtype=jnp.int32) * NB // SLOTS)[None]
        return jnp.concatenate(
            [
                tokens[0],
                jnp.pad(x_bucket.astype(bf16), pad_cols),
                jnp.pad(y_bucket.astype(bf16), pad_cols),
                jnp.pad(live.astype(bf16), pad_cols),
                jnp.pad(positions.astype(bf16), pad_cols),
                jnp.zeros((ROWS - SLOTS - 4, D), bf16),
            ],
            axis=0,
        )

    ex_ffn = column_blocks((up_weight, down_weight), (1, 1))
    ex_first.turn()
    ex_ffn.turn(ex_first.other)
    doc_rows = run(document, tokens, x_bucket, y_bucket, live_own)
    (packed,) = run(
        lambda *ins: call(pack_kernel, [x[None] for x in ins], [shape_of((TILE_ROWS, 128), bf16)]),
        *smalls,
    )

    def beside(m, o):
        r = m.shape[0]

        def join(m, o, out):
            out[:r], out[r:] = m[...], o[...]

        return run(lambda *ins: call(join, ins, [shape_of((2 * r, 128), bf16)]), m, o)[0]

    small_near = swap(packed, by_c)
    grad_in, live_row = run(
        lambda g, l: (pad_rows(g[0]), jnp.pad(l, ((0, 7), (0, ROWS - SLOTS)))), out_grad, live_own
    )
    pair = beside(packed, small_near)
    small_far = swap(pair, by_y)
    g_first = Gather(run, *block_rows(ex_first, 1), "dp", Z_X).send()
    g_small = Gather(run, beside(pair, small_far), "dp", X_FIRST).send()
    doc_far = swap(after(doc_rows, ex_ffn.other, small_far), by_y)
    doc_near = swap(doc_rows, by_c)
    up_own, down_own = block_rows(ex_ffn, 2)
    g_small.join().send()
    g_small.join().send()
    g_down = Gather(run, down_own, "dp", X_Z)
    g_first.join().send()
    g_down.send(g_first.x)
    doc_pieces = (doc_rows, doc_near, doc_far, swap(after(doc_far, g_first.x), by_c))

    def take_notes(*refs):
        for n in range(4):
            refs[4][n] = refs[n][ROWS - 16 :, : 2 * NB]

    (notes,) = run(
        lambda *ins: call(take_notes, ins, [shape_of((tp, 16, 2 * NB), bf16)]), *doc_pieces
    )
    run.wait(g_small.other)
    g_down.join()
    g_first.join().send()
    g_down.send()
    g_up = Gather(run, up_own, "dp", Z_X).send(g_down.x)
    ext, qkv_bias, my_upb, vec_one, vec_two = run(
        lambda *ins: call(
            partial(unpack_kernel, heads, n_dev), ins,
            [
                shape_of((3 * heads, 2 * NB), f32), shape_of((1, 3 * width), f32),
                shape_of((1, hidden), f32), shape_of((3, D), f32), shape_of((3, D), f32),
            ],
            flats, scalars=1,
        ),
        at, beside(g_small.x, g_small.other),
    )

    (bias,) = run(
        lambda *ins: call_docs(
            partial(bias_kernel, heads), tp, ins, [False, True],
            [shape_of((tp, heads, ROWS, ROWS), f32)],
        ),
        notes, ext,
    )
    g_up.join().send()
    col_out = shape_of((D, width), bf16)
    half_out = shape_of((D // 2, width), bf16)

    def proj_part(rows_of):
        return group_of(
            run(lambda w: glue(lambda ref: ref[:, 3 * width :], [half_out], w), rows_of)
        )

    proj_near = proj_part(g_first.x)
    g_up.join()
    run.wait(*proj_near)

    proj_far = proj_part(g_first.other)
    pair_out = shape_of((2, ROWS, width), bf16)
    group_out = shape_of((tp * ROWS, D), bf16)
    qkv_out = shape_of((tp * ROWS, 3 * width), bf16)
    probs_out = shape_of((tp, heads, ROWS, ROWS), f32)
    group, qkv, probs, far = run(
        lambda *ins: call(
            partial(attend_kernel, heads, (2, 3)), ins,
            [group_out, qkv_out, probs_out, pair_out], scalars=1,
        ),
        at, *doc_pieces[2:], g_first.x, g_first.other, qkv_bias, bias,
    )
    mixed_far = swap(far, by_y)
    g_up.send(g_first.other)
    g_down.join().send()
    group, qkv, probs, near = run(
        lambda *ins: call(
            partial(attend_kernel, heads, (0, 1)), ins,
            [group_out, qkv_out, probs_out, pair_out], scalars=1,
            alias={7: 0, 8: 1, 9: 2},
        ),
        at, *doc_pieces[:2], g_first.x, g_first.other, qkv_bias, bias, group, qkv, probs,
    )
    att_pieces = (near, *trade(second(near), mixed_far))

    wide_f = shape_of((ROWS, D), f32)
    wide_b = shape_of((ROWS, D), bf16)
    attended, normed_low, normed_one, hat_one, scale_one = run(
        lambda *ins: call(
            partial(first_norm_kernel, width), ins,
            [wide_b, wide_b, wide_f, wide_f, shape_of((ROWS, 1), f32)],
            [pltpu.VMEM((ROWS, D), f32), pltpu.VMEM((ROWS, D), bf16)], scalars=1,
        ),
        at, *att_pieces, *proj_near, *proj_far, doc_rows, vec_one,
    )

    normed_pieces = group_of(normed_low)
    hid_f = shape_of((tp * ROWS, hidden), f32)
    hid_b = shape_of((tp * ROWS, hidden), bf16)
    ffn_weights = (g_up.x, g_up.other, g_down.x, g_down.other)
    normed_group, slope, act_low, keep, give = run(
        lambda *ins: call(
            partial(up_kernel, (0, 1)), ins, [group_out, hid_f, hid_b, wide_f, wide_b], scalars=1,
        ),
        at, *normed_pieces[:2], *ffn_weights, my_upb,
    )
    meet = Meet().near_pair(keep, give)
    normed_group, slope, act_low, keep, give = run(
        lambda *ins: call(
            partial(up_kernel, (2, 3)), ins, [group_out, hid_f, hid_b, wide_f, wide_b], scalars=1,
            alias={8: 0, 9: 1, 10: 2},
        ),
        at, *normed_pieces[2:], *ffn_weights, my_upb, normed_group, slope, act_low,
    )
    meet.far_pair(keep, give).send()
    (slope,) = run(lambda *ins: call(slope_kernel, ins, [hid_f]), slope)
    encoded, d_ffn, d_resid_two, sums_two = run(
        lambda *ins: call(
            second_norm_kernel, ins,
            [shape_of((1, SLOTS, D), bf16), wide_b, wide_f, shape_of((3, D), f32)],
        ),
        *meet.terms(), normed_one, grad_in, live_row, vec_two,
    )

    d_ffn_pieces = group_of(d_ffn)
    ffn_weights = (g_down.x, g_down.other, g_up.x, g_up.other)
    sums_out = shape_of((2, hidden), f32)
    d_ffn_group, d_pre, d_up_bias, keep, give = run(
        lambda *ins: call(
            partial(down_back_kernel, (0, 1)), ins,
            [group_out, hid_b, sums_out, wide_f, wide_b], scalars=1,
        ),
        at, *d_ffn_pieces[:2], *ffn_weights, slope,
    )
    meet = Meet().near_pair(keep, give)
    d_ffn_group, d_pre, d_up_bias, keep, give = run(
        lambda *ins: call(
            partial(down_back_kernel, (2, 3)), ins,
            [group_out, hid_b, sums_out, wide_f, wide_b], scalars=1,
            alias={8: 0, 9: 1, 10: 2},
        ),
        at, *d_ffn_pieces[2:], *ffn_weights, slope, d_ffn_group, d_pre, d_up_bias,
    )
    meet.far_pair(keep, give)

    def half_grad(left, right, near):
        out = shape_of((D // 2, right.shape[1]), bf16)
        (made,) = run(lambda *ins: call(partial(half_grad_kernel, near), ins, [out]), left, right)
        return made

    give = half_grad(d_ffn_group, act_low, False)
    meet.send()
    s_down = Scatter(run, (give,), "dp", X_Z, given=give).send()
    give = half_grad(normed_group, d_pre, False)
    s_up = Scatter(run, (give,), "dp", Z_X, given=give).send()
    s_down.own(half_grad(d_ffn_group, act_low, True))
    s_up.own(half_grad(normed_group, d_pre, True))

    d_branch, d_resid_one, sums_one, a0, a1, a2 = run(
        lambda *ins: call(
            partial(first_back_kernel, width), ins,
            [wide_b, wide_f, shape_of((3, D), f32), doc_out, doc_out, pair_out],
            [pltpu.VMEM((ROWS, D), bf16)], scalars=1,
        ),
        at, *meet.terms(), d_resid_two, hat_one, scale_one, vec_one, *proj_near, *proj_far,
    )
    far = swap(a2, by_y)
    got_c = swap(a1, by_c)
    parts = run(
        lambda *ins: call(
            partial(proj_grad_kernel, width), ins, [col_out] * 4, scalars=1, cost=1.3
        ),
        at, attended, d_branch,
    )
    meet_proj = Meet().near_pair(parts[0], parts[1]).far_pair(parts[2], parts[3])
    grids = shape_of((3, NB, heads * NB), f32)
    room = [pltpu.VMEM((heads * ROWS, ROWS), bf16), pltpu.VMEM((ROWS, heads * NB), bf16)]
    d_qkv, d_sums, d_grid = run(
        lambda *ins: call(
            partial(attend_back_kernel, heads, (0, 1), False), ins,
            [qkv_out, shape_of((tp, 3 * width), f32), grids], room, cost=6,
        ),
        qkv, probs, a0, got_c, notes,
    )
    got_far = swap(second(far), by_c)
    meet_proj.send()
    d_qkv, d_sums, d_grid, d_ext = run(
        lambda *ins: call(
            partial(attend_back_kernel, heads, (2, 3), True), ins,
            [qkv_out, shape_of((tp, 3 * width), f32), grids, shape_of((3 * heads, 2 * NB), f32)],
            room,
            alias={5: 0, 6: 1, 7: 2},
        ),
        qkv, probs, far, got_far, notes, d_qkv, d_sums, d_grid,
    )

    def with_proj(k, c, y, small):
        p = (k.astype(f32) + c.astype(f32) + y.astype(f32)).astype(bf16)
        return jnp.concatenate([p, small], axis=-1).astype(f32)

    give = half_grad(group, d_qkv, False)
    s_first = Scatter(run, (give,), "dp", Z_X, given=give).send()
    run.wait(s_up.other, s_down.other)
    s_up.take().send()
    s_down.take().send()
    s_first.own(half_grad(group, d_qkv, True))
    plains = [pltpu.VMEM((24, D), f32)] * 2
    (small_grads,) = run(
        lambda *ins: call(
            partial(small_grads_kernel, heads, n_dev), ins, [shape_of((D, 128), bf16)],
            flats + plains, scalars=1,
        ),
        at, d_ext, d_sums, d_up_bias, sums_one, sums_two,
    )
    parts = run(
        lambda *ins: call(
            partial(tokens_back_kernel, width), ins, [wide_f, wide_b, wide_f, wide_b], scalars=1
        ),
        at, d_qkv, g_first.x, g_first.other,
    )
    meet_tok = Meet().near_pair(parts[0], parts[1]).far_pair(parts[2], parts[3])
    s_second = Scatter(
        run, (*meet_proj.terms(), small_grads), "dp", Z_X, base=with_proj
    ).send()
    s_up.take().send()
    s_first.take().send()
    run.wait(s_first.other)
    s_first.take().send()
    meet_tok.send()
    run.wait(s_up.other, s_down.other, s_second.other, s_first.other)
    s_second.take().send()
    s_down.take().send()

    def columns_back(scatters):
        sums = [x.sum().reshape(tp, rows, -1) for x in scatters]
        out = shape_of((2, rows, sum(x.shape[2] for x in sums)), bf16)

        def fn(at, *refs):
            for target, c in ((refs[-2], 1 - at[0] % 2), (refs[-1], at[0] % 2)):
                for y in range(2):
                    target[y] = jnp.concatenate([ref[2 * y + c] for ref in refs[:-2]], axis=1)

        return Exchange(run, at, *run(lambda *ins: call(fn, ins, [out, out], scalars=1), at, *sums))

    def whole_rows(exchanged, groups, widths, smalls):
        outs = [shape_of((rows, tp * g * w), f32) for g, w in zip(groups, widths)]
        ends = [shape_of((1, n * rows), f32) for n in smalls]

        def fn(at, mine, other, *refs):
            outs, ends = refs[: len(groups)], refs[len(groups) :]
            total = None
            for near, ref in ((True, mine), (False, other)):
                for n in range(2):
                    start, f = 0, source_of(at, near, n)
                    for out, g, w in zip(outs, groups, widths):
                        for i in range(g):
                            place = pl.multiple_of((i * tp + f) * w, w)
                            out[:, pl.ds(place, w)] = ref[n, :, start : start + w].astype(f32)
                            start += w
                    if ends:
                        part = ref[n, :, start:].astype(f32)
                        total = part if total is None else total + part
            if ends:
                small_outs(total, ends)

        return run(
            lambda *ins: call(fn, ins, outs + ends, scalars=1), at, exchanged.mine, exchanged.other
        )

    s_up.take()
    s_first.take()
    x_up = columns_back([s_up, s_first]).turn()
    s_second.take().send()
    run.wait(s_down.other, s_second.other, meet_tok.far, x_up.other)
    s_down.take()
    s_second.take()
    x_rest = columns_back([s_down, s_second])
    out_f = shape_of((1, SLOTS, D), f32)
    grad_tokens = run(
        lambda *ins: glue(
            lambda d, k, c, y: (
                d[...] + k[...] + c[...].astype(f32) + y[...].astype(f32)
            )[:SLOTS][None],
            [out_f], *ins,
        ),
        d_resid_one, *meet_tok.terms(),
    )
    x_rest.turn()
    grad_up, grad_qkv = whole_rows(x_up, (1, 3), (hidden, width), ())
    grad_down, grad_proj, *out = whole_rows(
        x_rest, (1, 1), (hidden, width), (1,) * 6 + (2, 6, 4)
    )
    out = [x.reshape(-1) for x in out]
    return (
        encoded,
        grad_tokens,
        grad_qkv,
        out[6],
        grad_proj,
        out[0],
        out[1],
        out[2],
        out[7],
        grad_up,
        out[8],
        grad_down,
        out[3],
        out[4],
        out[5],
    )


def solution(mesh):
    split = ("dp", "fsdp")
    one, two, three = P(split), P(split, None), P(split, None, None)
    return jax.shard_map(
        local,
        mesh=mesh,
        in_specs=(
            three, three, one, two, two, two, two, one, two, one, one, one, one, two, one, two,
            one, one, one,
        ),
        out_specs=(
            three, three, two, one, two, one, one, one, one, two, one, two, one, one, one,
        ),
        check_vma=False,
    )
```
